32 devices in a mesh: groups: 2 (over y), gz: 4 (over z), dev: 2 (over x), xy: 2 (over core).
Axes of the slice: x: 2, y: 2, z: 4, core: 2. Of those that a mesh axis runs over, the one named last changes fastest.
Arguments:
- fields: float32 [12, 8, 64, 256], P('groups', 'dev', 'gz', 'xy'), parts along dimension 0, may hold values from -6 to 6
- spectra: float32 [24, 8, 64, 256], P('groups', 'dev', 'gz', 'xy'), parts along dimension 0, may hold values from -6 to 6
- permittivity: float32 [16, 64, 256], P(('groups', 'dev'), 'gz', 'xy'), parts along dimension 0, may hold values from 1 to 12
- phase_start: float32 [2], P('groups'), parts along dimension 0, may hold values from -3.140625 to 3.140625
- wall_owner: int32 [4, 4], P('gz'), may hold values from 0 to 3, as said below
- cap_owner: int32 [2, 32], replicated, may hold values from 0 to 3, as said below
- dir_index: int32 [2048], replicated, may hold values from 0 to 4095
- target: float32 [4096], P('groups'), parts along dimension 0, may hold values from 1 to 12
- aim_mask: int32 [4096], P('groups'), parts along dimension 0, may hold values 0 or 1
Outputs:
- fields_out: float32 [12, 8, 64, 256], P('groups', 'dev', 'gz', 'xy'), parts along dimension 0
- spectra_out: float32 [24, 8, 64, 256], P('groups', 'dev', 'gz', 'xy'), parts along dimension 0
- owned_currents: float32 [8, 2, 2, 20, 128], P(('groups', 'gz'), 'dev', 'xy'), parts along dimension 0
- intensity: float32 [4096], P(('groups', 'gz', 'dev', 'xy')), parts along dimension 0
- adjoint_currents: float32 [8, 2, 2, 36, 128], P(('groups', 'gz'), 'dev', 'xy'), parts along dimension 0
The draws below stay inside these ranges and needn't reach their ends.
There are 2 independent parts, one for each index of `groups`. The reference program is written for one: setup_inputs(seed, part) draws one part's arguments, and reference() takes and returns one part's arrays. A program takes and returns all parts, laid end to end along the dimension named above; an argument that names none is the same for every part. Nothing has to cross between parts.
Inputs may be any that keep to these rules, and one draw needn't show every extreme that they name: `wall_owner`: entry [s, j] names the index of gz that owns wall patch j of slab s; every index owns exactly 4 wall patches of a column, and a slab gives one index at most 1 of them. `cap_owner`: row 0 names the owner on gz of each patch of the lower cap, row 1 of the upper cap; each index owns exactly 8 patches of each cap, so that every index owns exactly 20 patches of a column.
All inputs are finite; a program needn't handle non-finite values.
Results may differ from the reference program's by a relative error of at most 0.0003.
Values sent between devices are 32-bit elements; how exact they have to be, the bound alone decides.
A program may use at most 64 MiB of HBM per device.

```python
import math
import jax
import jax.numpy as jnp
from jax import lax

CX = 128
CY = 4
CZ = 16
PATCH = 16
XB = 8
ZB = 4
STEPS = 3
NDIR = 2048
THETAS = 64
NX = 256
NY = 8
NZ = 64
WALLP = 4
CAPP = 32
OWNED = 20
NSURF = 5120
N_GZ = 4
N_DEV = 2
N_XY = 2


def draw_wall_owner(key, part):
    offsets = jax.random.permutation(jax.random.fold_in(key, 11), N_GZ)
    sources = jnp.arange(N_GZ, dtype=jnp.int32)
    patches = jnp.arange(WALLP, dtype=jnp.int32)
    return ((sources[:, None] + offsets[patches % N_GZ][None, :]) % N_GZ).astype(jnp.int32)


def draw_cap_owner(key, part):
    lower = jax.random.permutation(jax.random.fold_in(key, 21), CAPP) % N_GZ
    upper = jax.random.permutation(jax.random.fold_in(key, 22), CAPP) % N_GZ
    return jnp.stack([lower, upper]).astype(jnp.int32)


def with_ends(entries, stream_key, low, high):
    longest = entries.shape.index(max(entries.shape))
    spots = []
    for shift in (0, 1):
        where = [jax.random.randint(jax.random.fold_in(stream_key, axis), (), 0, length) for axis, length in enumerate(entries.shape)]
        where[longest] = (where[longest] + shift) % entries.shape[longest]
        spots.append(tuple(where))
    return entries.at[spots[0]].set(low).at[spots[1]].set(high)


def levels(own_key, dims, cuts, least, top_value):
    factor_of = 1.0
    for axis_at, shards_of in cuts:
        heights = jax.random.uniform(jax.random.fold_in(jax.random.fold_in(own_key, 6), axis_at), (shards_of,), jnp.float32, least / len(cuts), top_value / len(cuts))
        factor_of = factor_of * jnp.repeat(jnp.exp(heights), dims[axis_at] // shards_of).reshape((-1,) + (1,) * (len(dims) - 1 - axis_at))
    return factor_of


def gaussian(stream_key, shape, deviation, limit, shards=(), held_as=jnp.bfloat16):
    drawn = deviation * jax.random.normal(stream_key, shape, jnp.float32)
    if shards:
        drawn = drawn * levels(stream_key, shape, shards, -0.22, 0.18)
    return jnp.clip(drawn, -limit, limit).astype(held_as)


def setup_inputs(seed: int = 0, part: int = 0) -> dict:
    streams_of = jax.random.split(jax.random.key(seed), 10)
    own_keys = jax.random.split(jax.random.fold_in(streams_of[9], part), 10)
    return {
        "fields": gaussian(own_keys[0], (6, NY, NZ, NX), 1.0, 6.0, ((1, 2), (2, 4), (3, 2)), jnp.float32),
        "spectra": gaussian(own_keys[1], (12, NY, NZ, NX), 1.0, 6.0, ((1, 2), (2, 4), (3, 2)), jnp.float32),
        "permittivity": jnp.clip(jnp.exp(math.log(12.0) - 2.4849066 * jax.random.uniform(own_keys[2], (NY, NZ, NX), jnp.float32) ** levels(own_keys[2], (NY, NZ, NX), ((0, 2), (1, 4), (2, 2)), -0.2, 0.2)), 1.0, 12.0),
        "phase_start": jnp.clip(jax.random.uniform(own_keys[3], (1,), jnp.float32, -3.140625, 3.140625), -3.140625, 3.140625),
        "wall_owner": draw_wall_owner(jax.random.fold_in(streams_of[9], 71), part),
        "cap_owner": draw_cap_owner(jax.random.fold_in(streams_of[9], 71), part),
        "dir_index": with_ends(jax.random.randint(streams_of[6], (NDIR,), 0, THETAS * THETAS), jax.random.fold_in(streams_of[6], 1), 0, (THETAS * THETAS) - 1).astype(jnp.int32),
        "target": jnp.clip(jax.random.uniform(own_keys[7], (NDIR,), jnp.float32, 1.0, 12.0), 1.0, 12.0),
        "aim_mask": with_ends((jax.random.randint(own_keys[8], (NDIR,), 0, 4) < 3).astype(jnp.int32), jax.random.fold_in(own_keys[8], 1), 0, 1),
    }


COURANT = 0.5
ANGULAR_STEP = 0.3
WAVE_NUMBER = 0.6
HIGHEST = lax.Precision.HIGHEST
CURRENT_SIGNS = (-1.0, 1.0, 1.0, -1.0)
X_PICKS = (5, 4, 2, 1)
Z_PICKS = (4, 3, 1, 0)

def ahead_diff(values, axis_number):
    length = values.shape[axis_number]
    shifted = jnp.concatenate([lax.slice_in_dim(values, 1, length, axis=axis_number), jnp.zeros_like(lax.slice_in_dim(values, 0, 1, axis=axis_number))], axis=axis_number)
    return shifted - values

def behind_diff(values, axis_number):
    length = values.shape[axis_number]
    shifted = jnp.concatenate([jnp.zeros_like(lax.slice_in_dim(values, 0, 1, axis=axis_number)), lax.slice_in_dim(values, 0, length - 1, axis=axis_number)], axis=axis_number)
    return values - shifted

def spectral_update(spectra_now, electric, magnetic, phase_start, step_number):
    angle_half = phase_start[0] + ANGULAR_STEP * (step_number + 0.5)
    angle_full = phase_start[0] + ANGULAR_STEP * (step_number + 1.0)
    return jnp.concatenate([spectra_now[0:3] + electric * jnp.cos(angle_full), spectra_now[3:6] + magnetic * jnp.cos(angle_half), spectra_now[6:9] - electric * jnp.sin(angle_full), spectra_now[9:12] - magnetic * jnp.sin(angle_half)])

def face_values(spectral_plane, facing, chosen):
    real_part = [CURRENT_SIGNS[number] * facing * spectral_plane[chosen[number]] for number in range(4)]
    imag_part = [CURRENT_SIGNS[number] * facing * spectral_plane[6 + chosen[number]] for number in range(4)]
    return jnp.stack(real_part + imag_part)

def to_vectors(record_values, x_flag):
    z_flag = 1.0 - x_flag
    stacked_rows = []
    for offset in (0, 4):
        tangent_one = record_values[offset]
        tangent_two = record_values[offset + 1]
        moment_one = record_values[offset + 2]
        moment_two = record_values[offset + 3]
        stacked_rows += [z_flag * tangent_one, x_flag * tangent_one + z_flag * tangent_two, x_flag * tangent_two, z_flag * moment_one, x_flag * moment_one + z_flag * moment_two, x_flag * moment_two]
    return jnp.stack(stacked_rows)

def to_record(gradient, x_flag):
    z_flag = 1.0 - x_flag
    stacked_rows = []
    for offset in (0, 6):
        stacked_rows += [x_flag * gradient[offset + 1] + z_flag * gradient[offset], x_flag * gradient[offset + 2] + z_flag * gradient[offset + 1], x_flag * gradient[offset + 4] + z_flag * gradient[offset + 3], x_flag * gradient[offset + 5] + z_flag * gradient[offset + 4]]
    return jnp.stack(stacked_rows)

def direction_frames(dir_index):
    polar_row = (dir_index // THETAS).astype(jnp.float32)
    azimuth_col = (dir_index % THETAS).astype(jnp.float32)
    polar_angle = jnp.pi * (polar_row + 0.5) / THETAS
    azimuth = 2.0 * jnp.pi * azimuth_col / THETAS
    sin_polar = jnp.sin(polar_angle)
    cos_polar = jnp.cos(polar_angle)
    sin_azim = jnp.sin(azimuth)
    cos_azim = jnp.cos(azimuth)
    unit_vectors = jnp.stack([sin_polar * cos_azim, sin_polar * sin_azim, cos_polar], axis=1)
    theta_hat = jnp.stack([cos_polar * cos_azim, cos_polar * sin_azim, -sin_polar], axis=1)
    phi_hat = jnp.stack([-sin_azim, cos_azim, jnp.zeros_like(sin_azim)], axis=1)
    return (unit_vectors, theta_hat, phi_hat)

def steering(unit_block, positions):
    angle_table = WAVE_NUMBER * (positions[0][:, None] * unit_block[None, :, 0] + positions[1][:, None] * unit_block[None, :, 1] + positions[2][:, None] * unit_block[None, :, 2])
    return (jnp.cos(angle_table), jnp.sin(angle_table))

def far_block(unit_block, currents, positions):
    cosine_table, sine_table = steering(unit_block, positions)
    real_part = jnp.dot(currents[:6], cosine_table, precision=HIGHEST) - jnp.dot(currents[6:], sine_table, precision=HIGHEST)
    imag_part = jnp.dot(currents[:6], sine_table, precision=HIGHEST) + jnp.dot(currents[6:], cosine_table, precision=HIGHEST)
    return jnp.concatenate([real_part, imag_part], axis=0)

def adjoint_block(unit_block, slope_block, positions):
    cosine_table, sine_table = steering(unit_block, positions)
    real_part = jnp.dot(slope_block[:6], cosine_table.T, precision=HIGHEST) + jnp.dot(slope_block[6:], sine_table.T, precision=HIGHEST)
    imag_part = jnp.dot(slope_block[6:], cosine_table.T, precision=HIGHEST) - jnp.dot(slope_block[:6], sine_table.T, precision=HIGHEST)
    return jnp.concatenate([real_part, imag_part], axis=0)

def intensity_and_slope(far_total, theta_hat, phi_hat, target, aim_mask):
    theta_rows = theta_hat.T
    phi_rows = phi_hat.T

    def project(vectors, frame_rows):
        return lax.optimization_barrier(jnp.sum(vectors * frame_rows, axis=0))
    e_theta_re = -(project(far_total[3:6], phi_rows) + project(far_total[0:3], theta_rows))
    e_phi_re = project(far_total[3:6], theta_rows) - project(far_total[0:3], phi_rows)
    e_theta_im = -(project(far_total[9:12], phi_rows) + project(far_total[6:9], theta_rows))
    e_phi_im = project(far_total[9:12], theta_rows) - project(far_total[6:9], phi_rows)
    intensity = e_theta_re * e_theta_re + e_theta_im * e_theta_im + e_phi_re * e_phi_re + e_phi_im * e_phi_im
    residual = aim_mask.astype(jnp.float32) * (intensity - target)
    slope_theta_re = 2.0 * residual * e_theta_re
    slope_phi_re = 2.0 * residual * e_phi_re
    slope_theta_im = 2.0 * residual * e_theta_im
    slope_phi_im = 2.0 * residual * e_phi_im
    n_re = -slope_theta_re * theta_rows - slope_phi_re * phi_rows
    l_re = -slope_theta_re * phi_rows + slope_phi_re * theta_rows
    n_im = -slope_theta_im * theta_rows - slope_phi_im * phi_rows
    l_im = -slope_theta_im * phi_rows + slope_phi_im * theta_rows
    return (intensity, jnp.concatenate([n_re, l_re, n_im, l_im], axis=0))

def arrange(wall_values, cap_values):
    walls = wall_values.reshape(N_XY, 8, N_DEV, CY, N_GZ, CZ).transpose(4, 2, 0, 1, 3, 5)
    walls = walls.reshape(N_GZ, N_DEV, N_XY, 8, WALLP, PATCH).transpose(0, 1, 2, 4, 3, 5).reshape(N_GZ, N_DEV, N_XY, WALLP, 8 * PATCH)
    caps = cap_values.reshape(2, 8, N_DEV, CY, N_XY, CX).transpose(0, 2, 4, 1, 3, 5)
    caps = caps.reshape(2, N_DEV, N_XY, 8, CAPP, PATCH).transpose(0, 1, 2, 4, 3, 5).reshape(2, N_DEV, N_XY, CAPP, 8 * PATCH)
    middle = jnp.zeros((N_GZ - 2, N_DEV, N_XY, CAPP, 8 * PATCH), jnp.float32)
    cap_rows = jnp.concatenate([caps[0:1], middle, caps[1:2]], axis=0)
    return jnp.concatenate([walls, cap_rows], axis=3)

def gather_owned(records, wall_owner, cap_owner):
    flat_walls = records[:, :, :, :WALLP].transpose(0, 3, 1, 2, 4).reshape(N_GZ * WALLP, N_DEV, N_XY, 8 * PATCH)
    caps_lower = records[0, :, :, WALLP:].transpose(2, 0, 1, 3)
    caps_upper = records[N_GZ - 1, :, :, WALLP:].transpose(2, 0, 1, 3)
    flat_records = jnp.concatenate([flat_walls, caps_lower, caps_upper], axis=0)
    owner_flat = jnp.concatenate([wall_owner.reshape(N_GZ * WALLP), cap_owner[0], cap_owner[1]]).astype(jnp.int32)
    total = N_GZ * WALLP + 2 * CAPP
    flat_order = jnp.arange(total, dtype=jnp.int32)
    earlier_same = (owner_flat[:, None] == owner_flat[None, :]) & (flat_order[None, :] < flat_order[:, None])
    slot_rank = lax.optimization_barrier(jnp.sum(earlier_same.astype(jnp.int32), axis=1)).astype(jnp.int32)
    owner_range = jnp.arange(N_GZ, dtype=jnp.int32)
    place_range = jnp.arange(OWNED, dtype=jnp.int32)
    matches = (owner_flat[None, None, :] == owner_range[:, None, None]) & (slot_rank[None, None, :] == place_range[None, :, None])
    selector = jnp.where(matches, 1.0, 0.0).astype(jnp.float32)
    return jnp.einsum('okg,gdhr->odhkr', selector, flat_records, precision=HIGHEST)

def reference(fields, spectra, permittivity, phase_start, wall_owner, cap_owner, dir_index, target, aim_mask):
    step_rate = COURANT / permittivity
    electric_list = [fields[0], fields[1], fields[2]]
    magnetic_list = [fields[3], fields[4], fields[5]]
    spectra_now = spectra
    for step_number in range(STEPS):
        magn_x = magnetic_list[0] - COURANT * (ahead_diff(electric_list[2], 0) - ahead_diff(electric_list[1], 1))
        magn_y = magnetic_list[1] - COURANT * (ahead_diff(electric_list[0], 1) - ahead_diff(electric_list[2], 2))
        magn_z = magnetic_list[2] - COURANT * (ahead_diff(electric_list[1], 2) - ahead_diff(electric_list[0], 0))
        magnetic_list = [magn_x, magn_y, magn_z]
        elec_x = electric_list[0] + step_rate * (behind_diff(magn_z, 0) - behind_diff(magn_y, 1))
        elec_y = electric_list[1] + step_rate * (behind_diff(magn_x, 1) - behind_diff(magn_z, 2))
        elec_z = electric_list[2] + step_rate * (behind_diff(magn_y, 2) - behind_diff(magn_x, 0))
        electric_list = [elec_x, elec_y, elec_z]
        spectra_now = spectral_update(spectra_now, jnp.stack(electric_list), jnp.stack(magnetic_list), phase_start, step_number)
    fields_out = jnp.stack(electric_list + magnetic_list)
    wall_values = jnp.stack([face_values(spectra_now[:, :, :, XB], -1.0, X_PICKS), face_values(spectra_now[:, :, :, NX - 1 - XB], 1.0, X_PICKS)])
    cap_values = jnp.stack([face_values(spectra_now[:, :, ZB, :], -1.0, Z_PICKS), face_values(spectra_now[:, :, NZ - 1 - ZB, :], 1.0, Z_PICKS)])
    records = arrange(wall_values, cap_values)
    owned_currents = gather_owned(records, wall_owner, cap_owner)
    wall_points = 2 * NY * NZ
    cap_points = 2 * NY * NX
    point_values = jnp.concatenate([wall_values.transpose(1, 0, 2, 3).reshape(8, wall_points), cap_values.transpose(1, 0, 2, 3).reshape(8, cap_points)], axis=1)
    x_flag = jnp.concatenate([jnp.ones((wall_points,), jnp.float32), jnp.zeros((cap_points,), jnp.float32)])
    y_grid = jnp.arange(NY, dtype=jnp.float32) - (NY - 1) / 2.0
    z_grid = jnp.arange(NZ, dtype=jnp.float32) - (NZ - 1) / 2.0
    x_grid = jnp.arange(NX, dtype=jnp.float32) - (NX - 1) / 2.0
    wall_x = jnp.array([XB, NX - 1 - XB], dtype=jnp.float32) - (NX - 1) / 2.0
    cap_z = jnp.array([ZB, NZ - 1 - ZB], dtype=jnp.float32) - (NZ - 1) / 2.0
    wall_shape = (2, NY, NZ)
    cap_shape = (2, NY, NX)
    wall_positions = jnp.stack([jnp.broadcast_to(wall_x[:, None, None], wall_shape), jnp.broadcast_to(y_grid[None, :, None], wall_shape), jnp.broadcast_to(z_grid[None, None, :], wall_shape)]).reshape(3, wall_points)
    cap_positions = jnp.stack([jnp.broadcast_to(x_grid[None, None, :], cap_shape), jnp.broadcast_to(y_grid[None, :, None], cap_shape), jnp.broadcast_to(cap_z[:, None, None], cap_shape)]).reshape(3, cap_points)
    positions = jnp.concatenate([wall_positions, cap_positions], axis=1)
    norm_scale = 1.0 / math.sqrt(2.0 * NSURF)
    currents = to_vectors(point_values, x_flag) * norm_scale
    unit_vectors, theta_hat, phi_hat = direction_frames(dir_index)
    block_rows = 128
    unit_blocks = unit_vectors.reshape(NDIR // block_rows, block_rows, 3)

    def far_of_block(unit_block):
        return far_block(unit_block, currents, positions)
    far_total = lax.map(far_of_block, unit_blocks).transpose(1, 0, 2).reshape(12, NDIR)
    intensity, slope_total = intensity_and_slope(far_total, theta_hat, phi_hat, target, aim_mask)
    slope_blocks = slope_total.reshape(12, NDIR // block_rows, block_rows).transpose(1, 0, 2)

    def add_block(carry_sum, pieces):
        return (carry_sum + adjoint_block(pieces[0], pieces[1], positions), None)
    gradient, ignored = lax.scan(add_block, jnp.zeros((12, NSURF), jnp.float32), (unit_blocks, slope_blocks))
    point_adjoint = to_record(gradient * norm_scale, x_flag)
    adjoint_walls = point_adjoint[:, :wall_points].reshape(8, 2, NY, NZ).transpose(1, 0, 2, 3)
    adjoint_caps = point_adjoint[:, wall_points:].reshape(8, 2, NY, NX).transpose(1, 0, 2, 3)
    adjoint_currents = arrange(adjoint_walls, adjoint_caps)
    return (fields_out, spectra_now, owned_currents, intensity, adjoint_currents)
```

```python
import functools
import math

import jax
import jax.numpy as jnp
from jax import lax
from jax.experimental import pallas as pl
from jax.experimental.pallas import tpu as pltpu
from jax.sharding import PartitionSpec as P

PATCH = 16
XB = 8
ZB = 4
STEPS = 3
THETAS = 64
COURANT = 0.5
ANGULAR_STEP = 0.3
WAVE_NUMBER = 0.6
LANES = 128
HIGHEST = lax.Precision.HIGHEST
CURRENT_SIGNS = (-1.0, 1.0, 1.0, -1.0)
X_PICKS = (5, 4, 2, 1)
Z_PICKS = (4, 3, 1, 0)
MESH = pl.DeviceIdType.MESH
AXES = ("dev", "gz", "xy")
F32 = jnp.float32
BF16 = jnp.bfloat16


def iota(shape, dim):
    return lax.broadcasted_iota(jnp.int32, shape, dim)


def sincos(turns):
    half = (turns - jnp.floor(turns + 0.5)) * math.pi
    sq = half * half
    sin_h = half * (1.0 + sq * (-1.0 / 6 + sq * (1.0 / 120 + sq * (-1.0 / 5040 + sq * (1.0 / 362880 - sq * (1.0 / 39916800))))))
    cos_h = 1.0 + sq * (-0.5 + sq * (1.0 / 24 + sq * (-1.0 / 720 + sq * (1.0 / 40320 + sq * (-1.0 / 3628800 + sq * (1.0 / 479001600))))))
    return 2.0 * sin_h * cos_h, 1.0 - 2.0 * sin_h * sin_h


def split(values):
    high = values.astype(BF16)
    return high, (values - high.astype(F32)).astype(BF16)


def block_transpose(tile):
    on_diagonal = (iota(tile.shape, 1) // PATCH) == iota(tile.shape, 0)
    total = jnp.where(on_diagonal, tile, 0.0)
    for k in range(1, 8):
        turned = pltpu.roll(tile, PATCH * k, 1)
        total = total + pltpu.roll(jnp.where(on_diagonal, turned, 0.0), 8 - k, 0)
    return total


def kernel(
    sizes,
    fields_in, spectra_in, permit_in, phase_in, wall_owner_in, cap_owner_in, dirs_in, target_in, aim_in,
    fields_out, spectra_out, owned_out, intensity_out, adjoint_out,
    send_y, send_z, send_x, got_y, got_z, got_x,
    fields, spectra, permit, phase, wall_owner, cap_owner, dirs, target, aim,
    geo, weights, phases, table_hi, table_lo, cap_plane, lhs,
    parts_out, parts_in, totals, walls, caps,
    halo_send, halo_got, part_send, part_got, total_send, total_got, wall_send, wall_got, cap_send, cap_got, loads,
):
    slabs, devs, xys = sizes
    peers = slabs * devs * xys
    size_y, size_z, size_x = permit.shape
    chunks = dirs.shape[0]
    ratio = peers // chunks
    across = devs * xys
    per = max(1, chunks // (2 * across))
    owners = chunks // per
    groups = 2 * size_y
    half_rows = 8 * size_y
    all_rows = 2 * half_rows
    gz, dev, xy = lax.axis_index("gz"), lax.axis_index("dev"), lax.axis_index("xy")
    me = (gz * devs + dev) * xys + xy
    place = {"dev": dev, "gz": gz, "xy": xy}
    count = {"dev": devs, "gz": slabs, "xy": xys}

    def ident(flat):
        return {"gz": flat // (devs * xys), "dev": (flat // xys) % devs, "xy": flat % xys}

    barrier = pltpu.get_barrier_semaphore()

    def greet(k, carry):
        pl.semaphore_signal(barrier, inc=1, device_id=ident((me + k) % peers), device_id_type=MESH)
        return carry

    lax.fori_loop(1, peers, greet, 0)

    loading = [
        pltpu.make_async_copy(source, held, loads.at[number])
        for number, (source, held) in enumerate((
            (fields_in, fields), (dirs_in, dirs), (phase_in, phase), (permit_in, permit), (spectra_in, spectra),
            (wall_owner_in, wall_owner), (cap_owner_in, cap_owner), (target_in, target), (aim_in, aim),
        ))
    ]
    for copy in loading:
        copy.start()

    for copy in loading[1:3]:
        copy.wait()
    index = dirs[...]
    sin_t, cos_t = sincos(((index // THETAS).astype(F32) + 0.5) * (0.5 / THETAS))
    sin_f, cos_f = sincos((index % THETAS).astype(F32) * (1.0 / THETAS))
    wave = WAVE_NUMBER / (2.0 * math.pi)
    for slot, values in enumerate((
        wave * sin_t * cos_f, wave * sin_t * sin_f, wave * cos_t,
        cos_t * cos_f, cos_t * sin_f, -sin_t, -sin_f, cos_f,
    )):
        geo[slot] = values

    grid_x, grid_y, grid_z = size_x * xys, size_y * devs, size_z * slabs
    x_first = (xy * size_x).astype(F32) - (grid_x - 1) / 2.0
    y_first = (dev * size_y).astype(F32) - (grid_y - 1) / 2.0
    z_first = (gz * size_z).astype(F32) - (grid_z - 1) / 2.0
    x_wall = jnp.where(xy == 0, XB, size_x - 1 - XB)
    z_cap = jnp.where(gz == 0, ZB, size_z - 1 - ZB)
    x_face = x_first + x_wall.astype(F32)
    z_face = z_first + z_cap.astype(F32)
    facing_x = jnp.where(xy == 0, -1.0, 1.0)
    facing_z = jnp.where(gz == 0, -1.0, 1.0)
    is_end = jnp.logical_or(gz == 0, gz == slabs - 1)
    end_weight = jnp.where(is_end, 1.0, 0.0)
    norm = 1.0 / math.sqrt(2.0 * (2 * grid_y * grid_z + 2 * grid_y * grid_x))

    def make_tables(j, carry):
        def row(slot):
            return geo[slot, pl.ds(j, 1), :]

        ux, uy, uz = row(0), row(1), row(2)
        blocks = size_x // 8
        far_s, far_c = sincos((iota((blocks, LANES), 0).astype(F32) * 8.0 + x_first) * ux)
        near_s, near_c = sincos(iota((8, LANES), 0).astype(F32) * ux)
        far_s, far_c = far_s[:, None, :], far_c[:, None, :]
        near_s, near_c = near_s[None], near_c[None]
        cos_x = (far_c * near_c - far_s * near_s).reshape(size_x, LANES)
        sin_x = (far_s * near_c + far_c * near_s).reshape(size_x, LANES)
        sin_z, cos_z = sincos((iota((size_z, LANES), 0).astype(F32) + z_first) * uz)
        for at, (x_part, z_part) in enumerate(((cos_x, cos_z), (sin_x, sin_z))):
            lanes = pl.ds(at * LANES, LANES)
            x_high, x_low = split(x_part)
            z_high, z_low = split(z_part)
            table_hi[j, pl.ds(0, size_x), lanes] = x_high
            table_lo[j, pl.ds(0, size_x), lanes] = x_low
            table_hi[j, pl.ds(size_x, 8 * size_z), lanes] = jnp.concatenate([z_high] * 8, axis=0)
            table_lo[j, pl.ds(size_x, 8 * size_z), lanes] = jnp.concatenate([z_low] * 8, axis=0)
        which = iota((groups, LANES), 0)
        cell_y = (which % size_y).astype(F32) + y_first
        sin_g, cos_g = sincos(cell_y * uy + jnp.where(which < size_y, z_face * uz, x_face * ux))
        phases[j, 0] = cos_g
        phases[j, 1] = sin_g
        kind = iota((8, LANES), 0) % 4

        def pattern(a, b, c, d):
            return jnp.where(kind == 0, a, jnp.where(kind == 1, b, jnp.where(kind == 2, c, d)))

        tx, ty, tz, fx, fy = row(3), row(4), row(5), row(6), row(7)
        weights[j, 0] = pattern(-tx, -ty, -fx, -fy)
        weights[j, 1] = pattern(-fx, -fy, tx, ty)
        weights[j, 2] = pattern(-ty, -tz, -fy, jnp.zeros_like(fy))
        weights[j, 3] = pattern(-fy, jnp.zeros_like(fy), ty, tz)
        return carry

    windows = 2 * STEPS

    def tables_of(window):
        lax.fori_loop(window * chunks // windows, (window + 1) * chunks // windows, make_tables, 0)

    order = iota((8, LANES), 0).astype(F32)
    run_s, run_c = sincos((phase[0] + 0.5 * ANGULAR_STEP * (order + 1.0)) * (0.5 / math.pi))

    for number, (axis, got) in enumerate(zip(AXES, (got_y, got_z, got_x))):
        @pl.when(place[axis] == count[axis] - 1)
        def _():
            for window in range(0, windows, 2):
                got[window] = jnp.zeros(got.shape[1:], F32)

        @pl.when(place[axis] == 0)
        def _():
            for window in range(1, windows, 2):
                got[window] = jnp.zeros(got.shape[1:], F32)

    loading[0].wait()
    pl.semaphore_wait(barrier, peers - 1)

    lane = iota((size_z, LANES), 1)
    lane3 = iota((size_y, size_z, LANES), 2)
    row3 = iota((size_y, size_z, LANES), 1)

    def halo_copies(window):
        step = -1 if window % 2 == 0 else 1
        copies = []
        for number, (axis, source, landing) in enumerate(
            zip(AXES, (send_y, send_z, send_x), (got_y, got_z, got_x))
        ):
            mine, total = place[axis], count[axis]
            copy = pltpu.make_async_remote_copy(
                src_ref=source.at[window],
                dst_ref=landing.at[window],
                send_sem=halo_send.at[window, number],
                recv_sem=halo_got.at[window, number],
                device_id={axis: (mine + step + total) % total},
                device_id_type=MESH,
            )
            if step < 0:
                copies.append((copy, mine > 0, mine < total - 1))
            else:
                copies.append((copy, mine < total - 1, mine > 0))
        return copies

    def start_halo(window, for_y, for_z, for_x):
        ahead = window % 2 == 0
        at_y, at_z = (0, 0) if ahead else (size_y - 1, size_z - 1)
        for k in range(2):
            send_y[window, k] = for_y[k][at_y]
            send_z[window, k] = for_z[k][:, at_z : at_z + 1, :]
        copies = halo_copies(window)
        for copy, sends, receives in copies[:2]:
            @pl.when(sends)
            def _():
                copy.start()
        packed = jnp.zeros((size_z, LANES), F32)
        for k in range(2):
            for y in range(size_y):
                spot = k * size_y + y
                amount = spot if ahead else (spot + 1) % LANES
                value = for_x[k][y]
                turned = pltpu.roll(value, amount, 1) if amount else value
                packed = jnp.where(lane == spot, turned, packed)
        send_x[window] = packed
        copy, sends, receives = copies[2]

        @pl.when(sends)
        def _():
            copy.start()

    def wait_halo(window):
        for copy, sends, receives in halo_copies(window):
            @pl.when(receives)
            def _():
                copy.wait_recv()

    def inner(ahead, axis, value):
        if axis == 0:
            none = jnp.zeros_like(value[:1])
            if ahead:
                return jnp.concatenate([value[1:], none], axis=0) - value
            return value - jnp.concatenate([none, value[:-1]], axis=0)
        length = value.shape[axis]
        spots = row3 if axis == 1 else lane3
        if ahead:
            return jnp.where(spots == length - 1, 0.0, pltpu.roll(value, length - 1, axis)) - value
        return value - jnp.where(spots == 0, 0.0, pltpu.roll(value, 1, axis))

    def edge_y(window, k):
        other = got_y[window, k][None]
        none = jnp.zeros((size_y - 1, size_z, LANES), F32)
        return jnp.concatenate([none, other] if window % 2 == 0 else [other, none], axis=0)

    def edge_z(window, k):
        return jnp.where(row3 == (size_z - 1 if window % 2 == 0 else 0), got_z[window, k], 0.0)

    def edge_x(window, k):
        landed = got_x[window]
        edges = []
        for y in range(size_y):
            spot = k * size_y + y
            amount = (LANES - 1 - spot) if window % 2 == 0 else (LANES - spot) % LANES
            edges.append(pltpu.roll(landed, amount, 1) if amount else landed)
        return jnp.where(lane3 == (size_x - 1 if window % 2 == 0 else 0), jnp.stack(edges, axis=0), 0.0)

    ex, ey, ez = fields[0], fields[1], fields[2]
    start_halo(0, (ez, ex), (ey, ex), (ez, ey))
    loading[3].wait()
    rate = COURANT / permit[...]
    for copy in loading[4:]:
        copy.wait()
    hx, hy, hz = fields[3], fields[4], fields[5]
    spec_from = spectra
    for n in range(STEPS):
        window = 2 * n
        hx = hx - COURANT * (inner(True, 0, ez) - inner(True, 1, ey))
        hy = hy - COURANT * (inner(True, 1, ex) - inner(True, 2, ez))
        hz = hz - COURANT * (inner(True, 2, ey) - inner(True, 0, ex))
        tables_of(window)
        wait_halo(window)
        hx = hx - COURANT * (edge_y(window, 0) - edge_z(window, 0))
        hy = hy - COURANT * (edge_z(window, 1) - edge_x(window, 0))
        hz = hz - COURANT * (edge_x(window, 1) - edge_y(window, 1))
        window = 2 * n + 1
        start_halo(window, (hz, hx), (hy, hx), (hz, hy))
        half_c, half_s = run_c[2 * n : 2 * n + 1, :], run_s[2 * n : 2 * n + 1, :]
        for c, value in enumerate((hx, hy, hz)):
            spectra_out[3 + c] = spec_from[3 + c] + value * half_c
            spectra_out[9 + c] = spec_from[9 + c] - value * half_s
        ex = ex + rate * (inner(False, 0, hz) - inner(False, 1, hy))
        ey = ey + rate * (inner(False, 1, hx) - inner(False, 2, hz))
        ez = ez + rate * (inner(False, 2, hy) - inner(False, 0, hx))
        tables_of(window)
        wait_halo(window)
        ex = ex - rate * (edge_y(window, 0) - edge_z(window, 0))
        ey = ey - rate * (edge_z(window, 1) - edge_x(window, 0))
        ez = ez - rate * (edge_x(window, 1) - edge_y(window, 1))
        if n < STEPS - 1:
            start_halo(window + 1, (ez, ex), (ey, ex), (ez, ey))
        full_c, full_s = run_c[2 * n + 1 : 2 * n + 2, :], run_s[2 * n + 1 : 2 * n + 2, :]
        for c, value in enumerate((ex, ey, ez)):
            spectra_out[c] = spec_from[c] + value * full_c
            spectra_out[6 + c] = spec_from[6 + c] - value * full_s
        spec_from = spectra_out
    for c, value in enumerate((ex, ey, ez, hx, hy, hz)):
        fields_out[c] = value

    own_walls = walls.at[gz]
    lane_block = iota((8, LANES), 1) // PATCH
    sub = iota((8, LANES), 0)
    own_block = lane_block == sub
    z_row = iota((size_z, LANES), 0)
    own_walls[...] = jnp.zeros((8, LANES), F32)
    for y in range(size_y):
        spread = jnp.zeros((size_z, LANES), F32)
        for c in range(8):
            k = c % 4
            from_c = X_PICKS[k] + (6 if c >= 4 else 0)
            column = jnp.sum(jnp.where(lane == x_wall, spectra_out[from_c, y], 0.0), axis=1, keepdims=True)
            spread = jnp.where(lane == c * PATCH + z_row, column * (CURRENT_SIGNS[k] * facing_x), spread)
        record = jnp.sum(spread, axis=0, keepdims=True)
        own_walls[pl.ds(y, 1), :] = record
        for c in range(8):
            k = c % 4
            from_c = Z_PICKS[k] + (6 if c >= 4 else 0)
            low = spectra_out[from_c, y, pl.ds(ZB, 1), :]
            high = spectra_out[from_c, y, pl.ds(size_z - 1 - ZB, 1), :]
            picked = jnp.where(gz == 0, low, high) * (CURRENT_SIGNS[k] * facing_z * end_weight)
            cap_plane[pl.ds(8 * y + c, 1), :] = picked
        wall_hi, wall_lo = split(jnp.where(own_block, record, 0.0) * norm)
        cap_hi, cap_lo = split(cap_plane[pl.ds(8 * y, 8), :] * norm)
        none = jnp.zeros((8, LANES), BF16)
        for at, (cap_part, wall_part) in enumerate(((cap_hi, wall_hi), (cap_lo, wall_lo))):
            first = at * all_rows + 8 * y
            lhs[pl.ds(first, 8), :] = jnp.concatenate([cap_part, none], axis=1)
            lhs[pl.ds(first + half_rows, 8), :] = jnp.concatenate([none, wall_part], axis=1)

    lanes8 = iota((1, LANES), 1)
    owner_row = jnp.zeros((1, LANES), F32)
    for p in range(size_y):
        owner_row = jnp.where(lanes8 == 8 * gz + p, (wall_owner[0, p] + 1).astype(F32), owner_row)
    own_walls[pl.ds(size_y, 1), :] = owner_row

    def wall_copy(k):
        return pltpu.make_async_remote_copy(
            src_ref=walls.at[gz],
            dst_ref=walls.at[gz],
            send_sem=wall_send.at[k],
            recv_sem=wall_got.at[gz],
            device_id={"gz": (gz + k) % slabs},
            device_id_type=MESH,
        )

    def wall_landing(s):
        return pltpu.make_async_remote_copy(
            src_ref=walls.at[s], dst_ref=walls.at[s], send_sem=wall_send.at[0], recv_sem=wall_got.at[s],
            device_id={"gz": (gz + 1) % slabs}, device_id_type=MESH,
        )

    def cap_copy(k, at):
        return pltpu.make_async_remote_copy(
            src_ref=caps.at[at],
            dst_ref=caps.at[at],
            send_sem=cap_send.at[k],
            recv_sem=cap_got.at[at],
            device_id={"gz": (gz + k) % slabs},
            device_id_type=MESH,
        )

    sign = jnp.where(sub < 4, -1.0, 1.0)

    def far_of(j):
        rows = lhs[...]
        by_high = jnp.dot(rows, table_hi[j], preferred_element_type=F32)
        by_low = jnp.dot(rows[:all_rows], table_lo[j], preferred_element_type=F32)
        product = by_high[:all_rows] + by_high[all_rows:] + by_low
        theta = jnp.zeros((8, LANES), F32)
        phi = jnp.zeros((8, LANES), F32)
        for face in range(2):
            sum_c = jnp.zeros((8, LANES), F32)
            sum_s = jnp.zeros((8, LANES), F32)
            for y in range(size_y):
                g = face * size_y + y
                tile = product[8 * g : 8 * g + 8]
                tile = tile[:, :LANES] + sign * pltpu.roll(tile[:, LANES:], 4, 0)
                sum_c = sum_c + tile * phases[j, 0, pl.ds(g, 1), :]
                sum_s = sum_s + tile * phases[j, 1, pl.ds(g, 1), :]
            far = sum_c + sign * pltpu.roll(sum_s, 4, 0)
            theta = theta + weights[j, 2 * face] * far
            phi = phi + weights[j, 2 * face + 1] * far

        def four(values):
            pairs = values + pltpu.roll(values, 7, 0)
            return pairs + pltpu.roll(pairs, 6, 0)

        both = jnp.where(sub % 4 == 1, pltpu.roll(four(phi), 1, 0), four(theta))
        parts_out[j] = jnp.where(sub < 2, both, pltpu.roll(both, 6, 0))[:4]

    bunch = per * max(1, 4 // per)
    together = bunch // per
    upper = jnp.where(gz >= slabs // 2, 1, 0)
    near = (upper * across + dev * xys + xy) % owners

    def partner(number):
        other, bit = 0, 1
        while bit < owners:
            other = other + bit * ((near // bit + number // bit) % 2)
            bit *= 2
        return other

    def flat_of(owner):
        return (slabs // 2 - 1) * across + owner

    def part_copy(owner, source):
        return pltpu.make_async_remote_copy(
            src_ref=parts_out.at[pl.ds(owner * per, per)],
            dst_ref=parts_in.at[source],
            send_sem=part_send.at[owner],
            recv_sem=part_got.at[source],
            device_id=ident(flat_of(owner)),
            device_id_type=MESH,
        )

    mine = me - flat_of(0)
    leads = jnp.logical_and(mine >= 0, mine < owners)

    def far_and_send(number, carry):
        several = [partner(owners - 1 - together * number - m) for m in range(together)]
        for owner in several:
            for m in range(per):
                far_of(owner * per + m)
        for owner in several:
            @pl.when(owner != mine)
            def _():
                part_copy(owner, me).start()

        return carry

    lax.fori_loop(0, owners // together, far_and_send, 0)

    for k in range(1, slabs):
        wall_copy(k).start()
    for at, holder in enumerate((0, slabs - 1)):
        @pl.when(gz == holder)
        def _():
            for y in range(size_y):
                caps[at, pl.ds(8 * y, 8), :] = block_transpose(cap_plane[pl.ds(8 * y, 8), :])
            for k in range(1, slabs):
                cap_copy(k, at).start()

    def each_peer(act):
        def body(k, carry):
            act(k)
            return carry

        lax.fori_loop(1, peers, body, 0)

    def total_copy(k, owner):
        return pltpu.make_async_remote_copy(
            src_ref=totals.at[pl.ds(owner * per, per)],
            dst_ref=totals.at[pl.ds(owner * per, per)],
            send_sem=total_send.at[k],
            recv_sem=total_got.at[owner],
            device_id=ident((me + k) % peers),
            device_id_type=MESH,
        )

    @pl.when(leads)
    def _():
        parts_in[me] = parts_out[pl.ds(mine * per, per)]
        each_peer(lambda k: part_copy(0, (me + k) % peers).wait_recv())
        totals[pl.ds(mine * per, per)] = jnp.sum(parts_in[...], axis=0)
        each_peer(lambda k: total_copy(peers - k, mine).start())

    def choose(mine, share, records):
        length = mine.shape[1]
        before = jnp.where(iota((length, length), 0) < iota((length, length), 1), 1.0, 0.0).astype(BF16)
        ones = jnp.broadcast_to(jnp.where(mine, 1.0, 0.0), (8, length))
        rank = jnp.dot(ones.astype(BF16), before, preferred_element_type=F32)
        wanted = iota((8, length), 0).astype(F32)
        chooser = jnp.where(rank == wanted, ones, 0.0)
        return jnp.dot(chooser, records, precision=HIGHEST, preferred_element_type=F32)[:share]

    def choose_owned():
        for s in range(slabs):
            @pl.when(s != gz)
            def _():
                wall_landing(s).wait_recv()
        for at, holder in enumerate((0, slabs - 1)):
            @pl.when(gz != holder)
            def _():
                cap_copy(1, at).wait_recv()
        all_walls = walls[...]
        owner_all = jnp.sum(all_walls[:, size_y : size_y + 1, :], axis=0)[:, : 8 * slabs]
        cap_share = (owned_out.shape[0] - size_y) // 2
        owned_out[pl.ds(0, size_y), 0, :] = choose(
            owner_all == (gz + 1).astype(F32), size_y, all_walls.reshape(8 * slabs, LANES)
        )
        for at in range(2):
            owned_out[pl.ds(size_y + at * cap_share, cap_share), 0, :] = choose(
                cap_owner[pl.ds(at, 1), :] == gz, cap_share, caps[at]
            )

    def intensity_of(field):
        return jnp.sum(field * field, axis=0, keepdims=True)

    def slope_of(j):
        field = totals[j]
        residual = aim[pl.ds(j, 1), :].astype(F32) * (intensity_of(field) - target[pl.ds(j, 1), :])
        return 2.0 * residual * field

    def adjoint_of(j):
        slope = slope_of(j)
        by_theta = jnp.where(sub < 4, slope[0:1], slope[2:3])
        by_phi = jnp.where(sub < 4, slope[1:2], slope[3:4])
        tiles = []
        for face in range(2):
            vector = weights[j, 2 * face] * by_theta + weights[j, 2 * face + 1] * by_phi
            turned = -sign * pltpu.roll(vector, 4, 0)
            for y in range(size_y):
                g = face * size_y + y
                tile = vector * phases[j, 0, pl.ds(g, 1), :] + turned * phases[j, 1, pl.ds(g, 1), :]
                tiles.append(jnp.concatenate([tile, -sign * pltpu.roll(tile, 4, 0)], axis=1))
        rows = jnp.concatenate(tiles, axis=0)
        high, low = split(rows)
        both = jnp.concatenate([high, low], axis=0)
        across = (((1,), (1,)), ((), ()))
        by_high = lax.dot_general(both, table_hi[j], across, preferred_element_type=F32)
        by_low = lax.dot_general(high, table_lo[j], across, preferred_element_type=F32)
        return by_high[:all_rows] + by_high[all_rows:] + by_low

    def adjoint_some(number, total):
        several = [partner(together * number + m) for m in range(together)]
        for owner in several:
            @pl.when(owner != mine)
            def _():
                total_copy(1, owner).wait_recv()

        for owner in several:
            for m in range(per):
                total = total + adjoint_of(owner * per + m)
        return total

    rounds = owners // together
    gradient = lax.fori_loop(0, rounds // 2, adjoint_some, jnp.zeros((all_rows, size_x + 8 * size_z), F32))
    choose_owned()
    gradient = lax.fori_loop(rounds // 2, rounds, adjoint_some, gradient)
    intensity_out[...] = intensity_of(totals[me // ratio])
    for y in range(size_y):
        wall = gradient[half_rows + 8 * y : half_rows + 8 * y + 8, size_x:]
        adjoint_out[pl.ds(y, 1), 0, :] = jnp.sum(jnp.where(own_block, wall, 0.0), axis=0, keepdims=True) * norm
        cap = block_transpose(gradient[8 * y : 8 * y + 8, :size_x] * (norm * end_weight))
        adjoint_out[pl.ds(size_y + 8 * y, 8), 0, :] = cap

    for window in range(windows):
        for copy, sends, receives in halo_copies(window):
            @pl.when(sends)
            def _():
                copy.wait_send()

    def part_sent(owner, carry):
        @pl.when(owner != mine)
        def _():
            part_copy(owner, me).wait_send()

        return carry

    lax.fori_loop(0, owners, part_sent, 0)
    for k in range(1, slabs):
        wall_copy(k).wait_send()
    for at, holder in enumerate((0, slabs - 1)):
        @pl.when(gz == holder)
        def _():
            for k in range(1, slabs):
                cap_copy(k, at).wait_send()

    @pl.when(leads)
    def _():
        each_peer(lambda k: total_copy(k, mine).wait_send())


def write_out(*refs):
    copies = [pltpu.make_async_copy(refs[i], refs[5 + i], refs[10].at[i]) for i in range(5)]
    for copy in copies:
        copy.start()
    for copy in copies:
        copy.wait()


def local(fields, spectra, permittivity, phase_start, wall_owner, cap_owner, dir_index, target, aim_mask):
    slabs, devs, xys = (lax.axis_size(a) for a in ("gz", "dev", "xy"))
    peers = slabs * devs * xys
    size_y, size_z, size_x = permittivity.shape
    assert size_z == PATCH and size_x == LANES and size_y == 4
    directions = dir_index.shape[0]
    chunks = directions // LANES
    ratio = peers // chunks
    per = max(1, chunks // (2 * devs * xys))
    owners = chunks // per
    share = directions // peers
    cap_count = size_y * size_x // PATCH
    owned = size_y + 2 * (cap_count // slabs)
    rows = 16 * size_y
    depth = size_x + 8 * size_z
    windows = 2 * STEPS
    vmem = pl.BlockSpec(memory_space=pltpu.VMEM)
    anywhere = pl.BlockSpec(memory_space=pl.ANY)
    dma = pltpu.SemaphoreType.DMA
    outs = pl.pallas_call(
        functools.partial(kernel, (slabs, devs, xys)),
        out_shape=(
            pltpu.VMEM(fields.shape, F32),
            pltpu.VMEM(spectra.shape, F32),
            pltpu.VMEM((owned, 1, LANES), F32),
            pltpu.VMEM((1, LANES), F32),
            pltpu.VMEM((size_y + cap_count, 1, LANES), F32),
        ),
        in_specs=[anywhere] * 9,
        out_specs=(vmem,) * 5,
        scratch_shapes=[
            pltpu.VMEM((windows, 2, size_z, LANES), F32),
            pltpu.VMEM((windows, 2, size_y, 1, LANES), F32),
            pltpu.VMEM((windows, size_z, LANES), F32),
            pltpu.VMEM((windows, 2, size_z, LANES), F32),
            pltpu.VMEM((windows, 2, size_y, 1, LANES), F32),
            pltpu.VMEM((windows, size_z, LANES), F32),
            pltpu.VMEM(fields.shape, F32),
            pltpu.VMEM(spectra.shape, F32),
            pltpu.VMEM(permittivity.shape, F32),
            pltpu.SMEM((1,), F32),
            pltpu.SMEM(wall_owner.shape, jnp.int32),
            pltpu.VMEM(cap_owner.shape, jnp.int32),
            pltpu.VMEM((chunks, LANES), jnp.int32),
            pltpu.VMEM((chunks, LANES), F32),
            pltpu.VMEM((chunks, LANES), jnp.int32),
            pltpu.VMEM((8, chunks, LANES), F32),
            pltpu.VMEM((chunks, 4, 8, LANES), F32),
            pltpu.VMEM((chunks, 2, 2 * size_y, LANES), F32),
            pltpu.VMEM((chunks, depth, 2 * LANES), BF16),
            pltpu.VMEM((chunks, depth, 2 * LANES), BF16),
            pltpu.VMEM((8 * size_y, LANES), F32),
            pltpu.VMEM((2 * rows, depth), BF16),
            pltpu.VMEM((chunks, 4, LANES), F32),
            pltpu.VMEM((peers, per, 4, LANES), F32),
            pltpu.VMEM((chunks, 4, LANES), F32),
            pltpu.VMEM((slabs, 8, LANES), F32),
            pltpu.VMEM((2, cap_count, LANES), F32),
            dma((windows, 3)), dma((windows, 3)),
            dma((owners,)), dma((peers,)),
            dma((peers,)), dma((owners,)),
            dma((slabs,)), dma((slabs,)),
            dma((slabs,)), dma((2,)),
            dma((9,)),
        ],
        compiler_params=pltpu.CompilerParams(collective_id=0, has_side_effects=True),
    )(
        fields, spectra, permittivity, phase_start, wall_owner, cap_owner,
        dir_index.reshape(chunks, LANES), target.reshape(chunks, LANES), aim_mask.reshape(chunks, LANES),
    )
    held = (fields.shape, spectra.shape, (owned, 1, LANES), (1, LANES), (size_y + cap_count, 1, LANES))
    fields_new, spectra_new, owned_rows, intensity, adjoint = pl.pallas_call(
        write_out,
        out_shape=tuple(jax.ShapeDtypeStruct(shape, F32) for shape in held),
        in_specs=[pl.BlockSpec(memory_space=pltpu.VMEM)] * 5,
        out_specs=(pl.BlockSpec(memory_space=pl.ANY),) * 5,
        scratch_shapes=[dma((5,))],
    )(*(pltpu.with_memory_space_constraint(out, pltpu.VMEM) for out in outs))
    owned_rows = owned_rows.reshape(1, 1, owned, 1, LANES).transpose(0, 1, 3, 2, 4)
    adjoint = adjoint.reshape(1, 1, size_y + cap_count, 1, LANES).transpose(0, 1, 3, 2, 4)
    intensity = intensity.reshape(LANES)
    if ratio > 1:
        me = (lax.axis_index("gz") * devs + lax.axis_index("dev")) * xys + lax.axis_index("xy")
        intensity = lax.dynamic_slice_in_dim(intensity, (me % ratio) * share, share, 0)
    return (fields_new, spectra_new, owned_rows, intensity, adjoint)


def solution(mesh):
    placed = (
        P("groups", "dev", "gz", "xy"),
        P("groups", "dev", "gz", "xy"),
        P(("groups", "dev"), "gz", "xy"),
        P("groups"),
        P("gz", None),
        P(),
        P(),
        P("groups"),
        P("groups"),
    )
    return jax.shard_map(
        local,
        mesh=mesh,
        in_specs=placed,
        out_specs=(
            P("groups", "dev", "gz", "xy"),
            P("groups", "dev", "gz", "xy"),
            P(("groups", "gz"), "dev", "xy", None, None),
            P(("groups", "gz", "dev", "xy")),
            P(("groups", "gz"), "dev", "xy", None, None),
        ),
        check_vma=False,
    )
```

```python
import functools
import math

import jax
import jax.numpy as jnp
from jax import lax
from jax.experimental import pallas as pl
from jax.experimental.pallas import tpu as pltpu
from jax.sharding import PartitionSpec as P

PATCH = 16
XB = 8
ZB = 4
STEPS = 3
THETAS = 64
COURANT = 0.5
ANGULAR_STEP = 0.3
WAVE_NUMBER = 0.6
LANES = 128
HIGHEST = lax.Precision.HIGHEST
CURRENT_SIGNS = (-1.0, 1.0, 1.0, -1.0)
X_PICKS = (5, 4, 2, 1)
Z_PICKS = (4, 3, 1, 0)
MESH = pl.DeviceIdType.MESH
AXES = ("dev", "gz", "xy")
F32 = jnp.float32
BF16 = jnp.bfloat16


def iota(shape, dim):
    return lax.broadcasted_iota(jnp.int32, shape, dim)


def sincos(turns):
    half = (turns - jnp.floor(turns + 0.5)) * math.pi
    sq = half * half
    sin_h = half * (1.0 + sq * (-1.0 / 6 + sq * (1.0 / 120 + sq * (-1.0 / 5040 + sq * (1.0 / 362880 - sq * (1.0 / 39916800))))))
    cos_h = 1.0 + sq * (-0.5 + sq * (1.0 / 24 + sq * (-1.0 / 720 + sq * (1.0 / 40320 + sq * (-1.0 / 3628800 + sq * (1.0 / 479001600))))))
    return 2.0 * sin_h * cos_h, 1.0 - 2.0 * sin_h * sin_h


def split(values):
    high = values.astype(BF16)
    return high, (values - high.astype(F32)).astype(BF16)


def block_transpose(tile):
    on_diagonal = (iota(tile.shape, 1) // PATCH) == iota(tile.shape, 0)
    total = jnp.where(on_diagonal, tile, 0.0)
    for k in range(1, 8):
        turned = pltpu.roll(tile, PATCH * k, 1)
        total = total + pltpu.roll(jnp.where(on_diagonal, turned, 0.0), 8 - k, 0)
    return total


def kernel(
    sizes,
    fields_in, spectra_in, permit_in, phase_in, wall_owner_in, cap_owner_in, dirs_in, target_in, aim_in,
    fields_out, spectra_out, owned_out, intensity_out, adjoint_out,
    out_yu, out_yd, out_zu, out_zd, out_xu, out_xd,
    in_yu, in_yd, in_zu, in_zd, in_xu, in_xd, in_zy, in_yz, in_yx, in_zx, in_xz, in_xy,
    fields, spectra, permit, phase, wall_owner, cap_owner, dirs, target, aim,
    geo, weights, phases, table_hi, table_lo, cap_plane, lhs,
    parts_out, parts_in, totals, walls, caps,
    halo_send, halo_got, part_send, part_got, total_send, total_got, wall_send, wall_got, cap_send, cap_got, loads, chain,
):
    slabs, devs, xys = sizes
    peers = slabs * devs * xys
    size_y, size_z, size_x = permit.shape
    chunks = dirs.shape[0]
    ratio = peers // chunks
    across = devs * xys
    per = max(1, chunks // (2 * across))
    owners = chunks // per
    groups = 2 * size_y
    half_rows = 8 * size_y
    all_rows = 2 * half_rows
    gz, dev, xy = lax.axis_index("gz"), lax.axis_index("dev"), lax.axis_index("xy")
    me = (gz * devs + dev) * xys + xy
    place = {"dev": dev, "gz": gz, "xy": xy}
    count = {"dev": devs, "gz": slabs, "xy": xys}

    def ident(flat):
        return {"gz": flat // (devs * xys), "dev": (flat // xys) % devs, "xy": flat % xys}

    barrier = pltpu.get_barrier_semaphore()

    for away in (1, -1, 0):
        @pl.when(jnp.logical_and(gz + away >= 0, gz + away < slabs))
        def _():
            def greet(k, carry):
                spot = (dev * xys + xy + k) % across
                to = {"gz": gz + away, "dev": spot // xys, "xy": spot % xys}
                pl.semaphore_signal(barrier, inc=1, device_id=to, device_id_type=MESH)
                return carry

            lax.fori_loop(0 if away else 1, across, greet, 0)

    beside = jnp.where(gz > 0, across, 0) + jnp.where(gz < slabs - 1, across, 0) + across - 1

    def pass_on():
        for at, away in enumerate((1, -1)):
            @pl.when(jnp.logical_and(gz + away >= 0, gz + away < slabs))
            def _():
                to = {"gz": gz + away, "dev": dev, "xy": xy}
                pl.semaphore_signal(chain.at[at], inc=1, device_id=to, device_id_type=MESH)

    def hear():
        for at, away in enumerate((1, -1)):
            @pl.when(jnp.logical_and(gz - away >= 0, gz - away < slabs))
            def _():
                pl.semaphore_wait(chain.at[at], 1)

    loading = [
        pltpu.make_async_copy(source, held, loads.at[number])
        for number, (source, held) in enumerate((
            (fields_in, fields), (dirs_in, dirs), (phase_in, phase), (permit_in, permit), (spectra_in, spectra),
            (wall_owner_in, wall_owner), (cap_owner_in, cap_owner), (target_in, target), (aim_in, aim),
        ))
    ]
    for copy in loading:
        copy.start()

    def geometry():
        index = dirs[...]
        sin_t, cos_t = sincos(((index // THETAS).astype(F32) + 0.5) * (0.5 / THETAS))
        sin_f, cos_f = sincos((index % THETAS).astype(F32) * (1.0 / THETAS))
        wave = WAVE_NUMBER / (2.0 * math.pi)
        for slot, values in enumerate((
            wave * sin_t * cos_f, wave * sin_t * sin_f, wave * cos_t,
            cos_t * cos_f, cos_t * sin_f, -sin_t, -sin_f, cos_f,
        )):
            geo[slot] = values

    grid_x, grid_y, grid_z = size_x * xys, size_y * devs, size_z * slabs
    x_first = (xy * size_x).astype(F32) - (grid_x - 1) / 2.0
    y_first = (dev * size_y).astype(F32) - (grid_y - 1) / 2.0
    z_first = (gz * size_z).astype(F32) - (grid_z - 1) / 2.0
    x_wall = jnp.where(xy == 0, XB, size_x - 1 - XB)
    z_cap = jnp.where(gz == 0, ZB, size_z - 1 - ZB)
    x_face = x_first + x_wall.astype(F32)
    z_face = z_first + z_cap.astype(F32)
    facing_x = jnp.where(xy == 0, -1.0, 1.0)
    facing_z = jnp.where(gz == 0, -1.0, 1.0)
    is_end = jnp.logical_or(gz == 0, gz == slabs - 1)
    end_weight = jnp.where(is_end, 1.0, 0.0)
    norm = 1.0 / math.sqrt(2.0 * (2 * grid_y * grid_z + 2 * grid_y * grid_x))

    def make_tables(j, carry):
        def row(slot):
            return geo[slot, pl.ds(j, 1), :]

        ux, uy, uz = row(0), row(1), row(2)
        blocks = size_x // 8
        far_s, far_c = sincos((iota((blocks, LANES), 0).astype(F32) * 8.0 + x_first) * ux)
        near_s, near_c = sincos(iota((8, LANES), 0).astype(F32) * ux)
        far_s, far_c = far_s[:, None, :], far_c[:, None, :]
        near_s, near_c = near_s[None], near_c[None]
        cos_x = (far_c * near_c - far_s * near_s).reshape(size_x, LANES)
        sin_x = (far_s * near_c + far_c * near_s).reshape(size_x, LANES)
        sin_z, cos_z = sincos((iota((size_z, LANES), 0).astype(F32) + z_first) * uz)
        for at, (x_part, z_part) in enumerate(((cos_x, cos_z), (sin_x, sin_z))):
            lanes = pl.ds(at * LANES, LANES)
            x_high, x_low = split(x_part)
            z_high, z_low = split(z_part)
            table_hi[j, pl.ds(0, size_x), lanes] = x_high
            table_lo[j, pl.ds(0, size_x), lanes] = x_low
            table_hi[j, pl.ds(size_x, 8 * size_z), lanes] = jnp.concatenate([z_high] * 8, axis=0)
            table_lo[j, pl.ds(size_x, 8 * size_z), lanes] = jnp.concatenate([z_low] * 8, axis=0)
        which = iota((groups, LANES), 0)
        cell_y = (which % size_y).astype(F32) + y_first
        sin_g, cos_g = sincos(cell_y * uy + jnp.where(which < size_y, z_face * uz, x_face * ux))
        phases[j, 0] = cos_g
        phases[j, 1] = sin_g
        kind = iota((8, LANES), 0) % 4

        def pattern(a, b, c, d):
            return jnp.where(kind == 0, a, jnp.where(kind == 1, b, jnp.where(kind == 2, c, d)))

        tx, ty, tz, fx, fy = row(3), row(4), row(5), row(6), row(7)
        weights[j, 0] = pattern(-tx, -ty, -fx, -fy)
        weights[j, 1] = pattern(-fx, -fy, tx, ty)
        weights[j, 2] = pattern(-ty, -tz, -fy, jnp.zeros_like(fy))
        weights[j, 3] = pattern(-fy, jnp.zeros_like(fy), ty, tz)
        return carry

    windows = STEPS

    def tables_of(window):
        lax.fori_loop(window * chunks // windows, (window + 1) * chunks // windows, make_tables, 0)

    lane = iota((size_z, LANES), 1)
    lane3 = iota((size_y, size_z, LANES), 2)
    row3 = iota((size_y, size_z, LANES), 1)

    messages = (
        (in_yu, {"dev": 1}), (in_yd, {"dev": -1}), (in_zu, {"gz": 1}), (in_zd, {"gz": -1}),
        (in_zy, {"gz": -1, "dev": 1}), (in_yz, {"dev": -1, "gz": 1}),
        (in_xu, {"xy": 1}), (in_xd, {"xy": -1}),
        (in_yx, {"dev": 1, "xy": -1}), (in_zx, {"gz": 1, "xy": -1}), (in_xz, {"xy": 1, "gz": -1}), (in_xy, {"xy": 1, "dev": -1}),
    )
    plain = 6

    def within(move, sign):
        inside = True
        for axis, step in move.items():
            spot = place[axis] + sign * step
            inside = jnp.logical_and(inside, jnp.logical_and(spot >= 0, spot < count[axis]))
        return inside

    def first_of(n):
        return (0, 5) if n == 0 else (5 + 3 * (n - 1), 3)

    def views(n):
        start, length = first_of(n)
        planes, pair = pl.ds(start, length), pl.ds(2 * n, 2)
        low, high = pl.ds(0, 8), pl.ds(size_z - 8, 8)
        return (
            (out_yu.at[planes], in_yu.at[planes]), (out_yd.at[pair], in_yd.at[pair]),
            (out_zu.at[planes], in_zu.at[planes]), (out_zd.at[pair], in_zd.at[pair]),
            (out_zd.at[2 * n, size_y - 1], in_zy.at[n]), (out_yd.at[2 * n, high], in_yz.at[n]),
            (out_xu.at[n], in_xu.at[n]), (out_xd.at[n], in_xd.at[n]),
            (out_xd.at[n], in_yx.at[n]), (out_xd.at[n, high], in_zx.at[n]),
            (out_xu.at[n, low], in_xz.at[n]), (out_xu.at[n], in_xy.at[n]),
        )

    def halo_copy(n, number, source, landing):
        to = {axis: (place[axis] + step + count[axis]) % count[axis] for axis, step in messages[number][1].items()}
        return pltpu.make_async_remote_copy(
            src_ref=source,
            dst_ref=landing,
            send_sem=halo_send.at[number],
            recv_sem=halo_got.at[n % 2, number],
            device_id=to,
            device_id_type=MESH,
        )

    def start_halo(n, numbers):
        for number in numbers:
            @pl.when(within(messages[number][1], 1))
            def _():
                halo_copy(n, number, *views(n)[number]).start()

    def wait_halo(n):
        for number in range(len(messages)):
            @pl.when(within(messages[number][1], -1))
            def _():
                halo_copy(n, number, *views(n)[number]).wait_recv()

    def pack(values, high):
        packed = jnp.zeros((size_z, LANES), F32)
        for k, value in enumerate(values):
            for y in range(size_y):
                spot = k * size_y + y
                amount = (spot + 1) % LANES if high else spot
                turned = pltpu.roll(value[y], amount, 1) if amount else value[y]
                packed = jnp.where(lane == spot, turned, packed)
        return packed

    def stage(n, ex, ey, ez, for_y, for_z, for_x):
        start, _ = first_of(n)
        for k, value in enumerate((ex, ey, ez) + for_y):
            out_yu[start + k] = value[size_y - 1]
        for k, value in enumerate((ez, ex)):
            out_yd[2 * n + k] = value[0]
        for k, value in enumerate((ex, ey, ez) + for_z):
            out_zu[start + k] = value[:, size_z - 1 : size_z, :]
        for k, value in enumerate((ey, ex)):
            out_zd[2 * n + k] = value[:, 0:1, :]
        yield
        out_xu[n] = pack((ex, ey, ez) + for_x, True)
        out_xd[n] = pack((ez, ey), False)
        yield

    for landing, move in messages:
        @pl.when(jnp.logical_not(within(move, -1)))
        def _():
            landing[...] = jnp.zeros(landing.shape, F32)

    def inner(ahead, axis, value):
        if axis == 0:
            none = jnp.zeros_like(value[:1])
            if ahead:
                return jnp.concatenate([value[1:], none], axis=0) - value
            return value - jnp.concatenate([none, value[:-1]], axis=0)
        length = value.shape[axis]
        spots = row3 if axis == 1 else lane3
        if ahead:
            return jnp.where(spots == length - 1, 0.0, pltpu.roll(value, length - 1, axis)) - value
        return value - jnp.where(spots == 0, 0.0, pltpu.roll(value, 1, axis))

    none = jnp.zeros((size_y - 1, size_z, LANES), F32)

    def at_y(plane, ahead):
        return jnp.concatenate([none, plane[None]] if ahead else [plane[None], none], axis=0)

    def at_z(rows, ahead):
        return jnp.where(row3 == (size_z - 1 if ahead else 0), rows, 0.0)

    def at_x(packed, k, ahead):
        edges = []
        for y in range(size_y):
            spot = k * size_y + y
            amount = (LANES - 1 - spot) if ahead else (LANES - spot) % LANES
            edges.append(pltpu.roll(packed, amount, 1) if amount else packed)
        return jnp.where(lane3 == (size_x - 1 if ahead else 0), jnp.stack(edges, axis=0), 0.0)

    def turn(value, by, axis):
        return pltpu.roll(value, by % value.shape[axis], axis)

    row2 = iota((size_z, LANES), 0)
    lane_row = iota((size_y, 1, LANES), 2)
    half_y = jnp.where(dev > 0, COURANT, 0.0)
    half_z = jnp.where(gz > 0, COURANT, 0.0)
    half_x = jnp.where(xy > 0, COURANT, 0.0)

    loading[0].wait()
    ex, ey, ez = fields[0], fields[1], fields[2]
    hx, hy, hz = fields[3], fields[4], fields[5]
    for _ in stage(0, ex, ey, ez, (hx, hz), (hx, hy), (hy, hz)):
        pass
    pl.semaphore_wait(barrier, beside)
    start_halo(0, range(len(messages)))
    pass_on()
    for copy in loading[1:3]:
        copy.wait()
    geometry()
    run_s, run_c = sincos((phase[0] + 0.5 * ANGULAR_STEP * (iota((8, LANES), 0).astype(F32) + 1.0)) * (0.5 / math.pi))
    loading[3].wait()
    rate = COURANT / permit[...]
    for copy in loading[4:]:
        copy.wait()
    spec_from = spectra
    for n in range(STEPS):
        hx = hx - COURANT * (inner(True, 0, ez) - inner(True, 1, ey))
        hy = hy - COURANT * (inner(True, 1, ex) - inner(True, 2, ez))
        hz = hz - COURANT * (inner(True, 2, ey) - inner(True, 0, ex))
        tables_of(n)
        if n == 1:
            def relay(k, carry):
                hear()
                pass_on()
                return carry

            lax.fori_loop(0, slabs - 3, relay, 0)
        wait_halo(n)
        start, _ = first_of(n)
        xp = in_xd[n]
        hx = hx - COURANT * (at_y(in_yd[2 * n], True) - at_z(in_zd[2 * n], True))
        hy = hy - COURANT * (at_z(in_zd[2 * n + 1], True) - at_x(xp, 0, True))
        hz = hz - COURANT * (at_x(xp, 1, True) - at_y(in_yd[2 * n + 1], True))

        ax, ay, az = in_yu[start], in_yu[start + 1], in_yu[start + 2]
        bx, by, bz = in_zu[start], in_zu[start + 1], in_zu[start + 2]
        c_ex, own = in_xu[n], out_xd[n]
        if n == 0:
            y_hx, y_hz = in_yu[3], in_yu[4]
            z_hx, z_hy = in_zu[3], in_zu[4]
            x_hy, x_hz = turn(c_ex, -3 * size_y, 1), turn(c_ex, -4 * size_y, 1)
        ay_z = jnp.where(row2 == size_z - 1, in_zy[n], turn(ay, -1, 0))
        ay_x = jnp.where(lane == size_x - 1, turn(in_yx[n], -2 * size_y, 1), turn(ay, -1, 1))
        y_hx = y_hx - half_y * ((ez[0] - az) - (ay_z - ay))
        y_hz = y_hz - half_y * ((ay_x - ay) - (ex[0] - ax))
        bz_y = jnp.concatenate([bz[1:], in_yz[n, 7:8, :][None]], axis=0)
        corner = in_zx[n, 7:8, :]
        bz_x = jnp.stack([turn(corner, -1 - y, 1) for y in range(size_y)], axis=0)
        bz_x = jnp.where(lane_row == size_x - 1, bz_x, jnp.stack([turn(bz[y], -1, 1) for y in range(size_y)], axis=0))
        z_hx = z_hx - half_z * ((bz_y - bz) - (ey[:, 0:1, :] - by))
        z_hy = z_hy - half_z * ((ex[:, 0:1, :] - bx) - (bz_x - bz))
        c_z = jnp.where(row2 == size_z - 1, in_xz[n, 0:1, :], turn(c_ex, -1, 0))
        c_y = jnp.where(lane == size_y - 1, turn(in_xy[n], size_y - 1, 1), turn(c_ex, -1, 1))
        x_hy = x_hy - half_x * ((c_z - c_ex) - (own - turn(c_ex, -2 * size_y, 1)))
        x_hz = x_hz - half_x * ((turn(own, -size_y, 1) - turn(c_ex, -size_y, 1)) - (c_y - c_ex))

        ex = ex + rate * (inner(False, 0, hz) - inner(False, 1, hy))
        ey = ey + rate * (inner(False, 1, hx) - inner(False, 2, hz))
        ez = ez + rate * (inner(False, 2, hy) - inner(False, 0, hx))
        ex = ex - rate * (at_y(y_hz, False) - at_z(z_hy, False))
        ey = ey - rate * (at_z(z_hx, False) - at_x(x_hz, 0, False))
        ez = ez - rate * (at_x(x_hy, 0, False) - at_y(y_hx, False))
        if n < STEPS - 1:
            staging = stage(n + 1, ex, ey, ez, (), (), ())
            next(staging)
            start_halo(n + 1, range(plain))
            next(staging)
            start_halo(n + 1, range(plain, len(messages)))
        half_c, half_s = run_c[2 * n : 2 * n + 1, :], run_s[2 * n : 2 * n + 1, :]
        for c, value in enumerate((hx, hy, hz)):
            spectra_out[3 + c] = spec_from[3 + c] + value * half_c
            spectra_out[9 + c] = spec_from[9 + c] - value * half_s
        full_c, full_s = run_c[2 * n + 1 : 2 * n + 2, :], run_s[2 * n + 1 : 2 * n + 2, :]
        for c, value in enumerate((ex, ey, ez)):
            spectra_out[c] = spec_from[c] + value * full_c
            spectra_out[6 + c] = spec_from[6 + c] - value * full_s
        spec_from = spectra_out
    for c, value in enumerate((ex, ey, ez, hx, hy, hz)):
        fields_out[c] = value

    own_walls = walls.at[gz]
    lane_block = iota((8, LANES), 1) // PATCH
    sub = iota((8, LANES), 0)
    own_block = lane_block == sub
    z_row = iota((size_z, LANES), 0)
    own_walls[...] = jnp.zeros((8, LANES), F32)
    for y in range(size_y):
        spread = jnp.zeros((size_z, LANES), F32)
        for c in range(8):
            k = c % 4
            from_c = X_PICKS[k] + (6 if c >= 4 else 0)
            column = jnp.sum(jnp.where(lane == x_wall, spectra_out[from_c, y], 0.0), axis=1, keepdims=True)
            spread = jnp.where(lane == c * PATCH + z_row, column * (CURRENT_SIGNS[k] * facing_x), spread)
        record = jnp.sum(spread, axis=0, keepdims=True)
        own_walls[pl.ds(y, 1), :] = record
        for c in range(8):
            k = c % 4
            from_c = Z_PICKS[k] + (6 if c >= 4 else 0)
            low = spectra_out[from_c, y, pl.ds(ZB, 1), :]
            high = spectra_out[from_c, y, pl.ds(size_z - 1 - ZB, 1), :]
            picked = jnp.where(gz == 0, low, high) * (CURRENT_SIGNS[k] * facing_z * end_weight)
            cap_plane[pl.ds(8 * y + c, 1), :] = picked
        wall_hi, wall_lo = split(jnp.where(own_block, record, 0.0) * norm)
        cap_hi, cap_lo = split(cap_plane[pl.ds(8 * y, 8), :] * norm)
        none = jnp.zeros((8, LANES), BF16)
        for at, (cap_part, wall_part) in enumerate(((cap_hi, wall_hi), (cap_lo, wall_lo))):
            first = at * all_rows + 8 * y
            lhs[pl.ds(first, 8), :] = jnp.concatenate([cap_part, none], axis=1)
            lhs[pl.ds(first + half_rows, 8), :] = jnp.concatenate([none, wall_part], axis=1)

    lanes8 = iota((1, LANES), 1)
    owner_row = jnp.zeros((1, LANES), F32)
    for p in range(size_y):
        owner_row = jnp.where(lanes8 == 8 * gz + p, (wall_owner[0, p] + 1).astype(F32), owner_row)
    own_walls[pl.ds(size_y, 1), :] = owner_row

    def wall_copy(k, ref=None):
        held = walls.at[gz] if ref is None else ref
        return pltpu.make_async_remote_copy(
            src_ref=held,
            dst_ref=held,
            send_sem=wall_send,
            recv_sem=wall_got,
            device_id={"gz": (gz + k) % slabs},
            device_id_type=MESH,
        )

    def cap_copy(k, at):
        return pltpu.make_async_remote_copy(
            src_ref=caps.at[at],
            dst_ref=caps.at[at],
            send_sem=cap_send.at[k - 1],
            recv_sem=cap_got.at[at],
            device_id={"gz": (gz + k) % slabs},
            device_id_type=MESH,
        )

    sign = jnp.where(sub < 4, -1.0, 1.0)

    def far_of(j):
        rows = lhs[...]
        by_high = jnp.dot(rows, table_hi[j], preferred_element_type=F32)
        by_low = jnp.dot(rows[:all_rows], table_lo[j], preferred_element_type=F32)
        product = by_high[:all_rows] + by_high[all_rows:] + by_low
        theta = jnp.zeros((8, LANES), F32)
        phi = jnp.zeros((8, LANES), F32)
        for face in range(2):
            sum_c = jnp.zeros((8, LANES), F32)
            sum_s = jnp.zeros((8, LANES), F32)
            for y in range(size_y):
                g = face * size_y + y
                tile = product[8 * g : 8 * g + 8]
                tile = tile[:, :LANES] + sign * pltpu.roll(tile[:, LANES:], 4, 0)
                sum_c = sum_c + tile * phases[j, 0, pl.ds(g, 1), :]
                sum_s = sum_s + tile * phases[j, 1, pl.ds(g, 1), :]
            far = sum_c + sign * pltpu.roll(sum_s, 4, 0)
            theta = theta + weights[j, 2 * face] * far
            phi = phi + weights[j, 2 * face + 1] * far

        def four(values):
            pairs = values + pltpu.roll(values, 7, 0)
            return pairs + pltpu.roll(pairs, 6, 0)

        both = jnp.where(sub % 4 == 1, pltpu.roll(four(phi), 1, 0), four(theta))
        parts_out[j] = jnp.where(sub < 2, both, pltpu.roll(both, 6, 0))[:4]

    bunch = per * max(1, 4 // per)
    together = bunch // per
    upper = jnp.where(gz >= slabs // 2, 1, 0)
    near = (upper * across + dev * xys + xy) % owners

    def partner(number):
        other, bit = 0, 1
        while bit < owners:
            other = other + bit * ((near // bit + number // bit) % 2)
            bit *= 2
        return other

    def flat_of(owner):
        return (slabs // 2 - 1) * across + owner

    def part_copy(owner, source):
        return pltpu.make_async_remote_copy(
            src_ref=parts_out.at[pl.ds(owner * per, per)],
            dst_ref=parts_in.at[source],
            send_sem=part_send,
            recv_sem=part_got,
            device_id=ident(flat_of(owner)),
            device_id_type=MESH,
        )

    mine = me - flat_of(0)
    leads = jnp.logical_and(mine >= 0, mine < owners)

    def far_and_send(number, carry):
        several = [partner(owners - 1 - together * number - m) for m in range(together)]
        for owner in several:
            for m in range(per):
                far_of(owner * per + m)
        for owner in several:
            @pl.when(owner != mine)
            def _():
                part_copy(owner, me).start()

        return carry

    hear()
    lax.fori_loop(0, owners // together, far_and_send, 0)

    for k in range(1, slabs):
        wall_copy(k).start()
    for at, holder in enumerate((0, slabs - 1)):
        @pl.when(gz == holder)
        def _():
            for y in range(size_y):
                caps[at, pl.ds(8 * y, 8), :] = block_transpose(cap_plane[pl.ds(8 * y, 8), :])
            for k in range(1, slabs):
                cap_copy(k, at).start()

    def each_peer(act):
        def body(k, carry):
            act(k)
            return carry

        lax.fori_loop(1, peers, body, 0)

    def total_copy(k, owner, ref=None):
        held = totals.at[pl.ds(owner * per, per)] if ref is None else ref
        return pltpu.make_async_remote_copy(
            src_ref=held,
            dst_ref=held,
            send_sem=total_send,
            recv_sem=total_got.at[owner // together],
            device_id=ident((me + k) % peers),
            device_id_type=MESH,
        )

    @pl.when(leads)
    def _():
        everyone = parts_in.at[pl.ds(0, peers - 1)]
        pltpu.make_async_remote_copy(
            src_ref=everyone, dst_ref=everyone, send_sem=part_send, recv_sem=part_got, device_id={"gz": gz}, device_id_type=MESH
        ).wait_recv()
        parts_in[me] = parts_out[pl.ds(mine * per, per)]
        totals[pl.ds(mine * per, per)] = jnp.sum(parts_in[...], axis=0)
        each_peer(lambda k: total_copy(peers - k, mine).start())

    def choose(mine, share, records):
        length = mine.shape[1]
        before = jnp.where(iota((length, length), 0) < iota((length, length), 1), 1.0, 0.0).astype(BF16)
        ones = jnp.broadcast_to(jnp.where(mine, 1.0, 0.0), (8, length))
        rank = jnp.dot(ones.astype(BF16), before, preferred_element_type=F32)
        wanted = iota((8, length), 0).astype(F32)
        chooser = jnp.where(rank == wanted, ones, 0.0)
        return jnp.dot(chooser, records, precision=HIGHEST, preferred_element_type=F32)[:share]

    def choose_owned():
        wall_copy(1, walls.at[pl.ds(0, slabs - 1)]).wait_recv()
        for at, holder in enumerate((0, slabs - 1)):
            @pl.when(gz != holder)
            def _():
                cap_copy(1, at).wait_recv()
        all_walls = walls[...]
        owner_all = jnp.sum(all_walls[:, size_y : size_y + 1, :], axis=0)[:, : 8 * slabs]
        cap_share = (owned_out.shape[0] - size_y) // 2
        owned_out[pl.ds(0, size_y), 0, :] = choose(
            owner_all == (gz + 1).astype(F32), size_y, all_walls.reshape(8 * slabs, LANES)
        )
        for at in range(2):
            owned_out[pl.ds(size_y + at * cap_share, cap_share), 0, :] = choose(
                cap_owner[pl.ds(at, 1), :] == gz, cap_share, caps[at]
            )

    def intensity_of(field):
        return jnp.sum(field * field, axis=0, keepdims=True)

    def slope_of(j):
        field = totals[j]
        residual = aim[pl.ds(j, 1), :].astype(F32) * (intensity_of(field) - target[pl.ds(j, 1), :])
        return 2.0 * residual * field

    def adjoint_of(j):
        slope = slope_of(j)
        by_theta = jnp.where(sub < 4, slope[0:1], slope[2:3])
        by_phi = jnp.where(sub < 4, slope[1:2], slope[3:4])
        tiles = []
        for face in range(2):
            vector = weights[j, 2 * face] * by_theta + weights[j, 2 * face + 1] * by_phi
            turned = -sign * pltpu.roll(vector, 4, 0)
            for y in range(size_y):
                g = face * size_y + y
                tile = vector * phases[j, 0, pl.ds(g, 1), :] + turned * phases[j, 1, pl.ds(g, 1), :]
                tiles.append(jnp.concatenate([tile, -sign * pltpu.roll(tile, 4, 0)], axis=1))
        rows = jnp.concatenate(tiles, axis=0)
        high, low = split(rows)
        both = jnp.concatenate([high, low], axis=0)
        across = (((1,), (1,)), ((), ()))
        by_high = lax.dot_general(both, table_hi[j], across, preferred_element_type=F32)
        by_low = lax.dot_general(high, table_lo[j], across, preferred_element_type=F32)
        return by_high[:all_rows] + by_high[all_rows:] + by_low

    def adjoint_some(number, total):
        several = [partner(together * number + m) for m in range(together)]
        batch = several[0] // together
        ours = jnp.logical_and(leads, mine // together == batch)

        @pl.when(jnp.logical_not(ours))
        def _():
            total_copy(1, several[0], totals.at[pl.ds(batch * bunch, bunch)]).wait_recv()

        if together > 1:
            @pl.when(ours)
            def _():
                total_copy(1, several[0], totals.at[pl.ds(batch * bunch, bunch - per)]).wait_recv()

        for owner in several:
            for m in range(per):
                total = total + adjoint_of(owner * per + m)
        return total

    rounds = owners // together
    gradient = lax.fori_loop(0, rounds // 2, adjoint_some, jnp.zeros((all_rows, size_x + 8 * size_z), F32))
    choose_owned()
    gradient = lax.fori_loop(rounds // 2, rounds, adjoint_some, gradient)
    intensity_out[...] = intensity_of(totals[me // ratio])
    for y in range(size_y):
        wall = gradient[half_rows + 8 * y : half_rows + 8 * y + 8, size_x:]
        adjoint_out[pl.ds(y, 1), 0, :] = jnp.sum(jnp.where(own_block, wall, 0.0), axis=0, keepdims=True) * norm
        cap = block_transpose(gradient[8 * y : 8 * y + 8, :size_x] * (norm * end_weight))
        adjoint_out[pl.ds(size_y + 8 * y, 8), 0, :] = cap

    for number, (landing, move) in enumerate(messages):
        @pl.when(within(move, 1))
        def _():
            halo_copy(0, number, landing, landing).wait_send()

    def parts_sent(ref):
        pltpu.make_async_remote_copy(
            src_ref=ref, dst_ref=ref, send_sem=part_send, recv_sem=part_got, device_id={"gz": gz}, device_id_type=MESH
        ).wait_send()

    @pl.when(leads)
    def _():
        parts_sent(parts_out.at[pl.ds(0, (owners - 1) * per)])
        total_copy(1, 0, parts_in.at[pl.ds(0, peers - 1)]).wait_send()

    @pl.when(jnp.logical_not(leads))
    def _():
        parts_sent(parts_out)

    wall_copy(1, walls.at[pl.ds(0, slabs - 1)]).wait_send()
    for at, holder in enumerate((0, slabs - 1)):
        @pl.when(gz == holder)
        def _():
            for k in range(1, slabs):
                cap_copy(k, at).wait_send()


def write_out(*refs):
    copies = [pltpu.make_async_copy(refs[i], refs[5 + i], refs[10].at[i]) for i in range(5)]
    for copy in copies:
        copy.start()
    for copy in copies:
        copy.wait()


def local(fields, spectra, permittivity, phase_start, wall_owner, cap_owner, dir_index, target, aim_mask):
    slabs, devs, xys = (lax.axis_size(a) for a in ("gz", "dev", "xy"))
    peers = slabs * devs * xys
    size_y, size_z, size_x = permittivity.shape
    assert size_z == PATCH and size_x == LANES and size_y == 4
    directions = dir_index.shape[0]
    chunks = directions // LANES
    ratio = peers // chunks
    per = max(1, chunks // (2 * devs * xys))
    owners = chunks // per
    share = directions // peers
    cap_count = size_y * size_x // PATCH
    owned = size_y + 2 * (cap_count // slabs)
    rows = 16 * size_y
    depth = size_x + 8 * size_z
    planes, pairs = 5 + 3 * (STEPS - 1), 2 * STEPS
    halos = (
        (planes, size_z, LANES), (pairs, size_z, LANES), (planes, size_y, 1, LANES), (pairs, size_y, 1, LANES),
        (STEPS, size_z, LANES), (STEPS, size_z, LANES),
        (STEPS, 1, LANES), (STEPS, 8, LANES), (STEPS, size_z, LANES), (STEPS, 8, LANES), (STEPS, 8, LANES), (STEPS, size_z, LANES),
    )
    vmem = pl.BlockSpec(memory_space=pltpu.VMEM)
    anywhere = pl.BlockSpec(memory_space=pl.ANY)
    dma = pltpu.SemaphoreType.DMA
    outs = pl.pallas_call(
        functools.partial(kernel, (slabs, devs, xys)),
        out_shape=(
            pltpu.VMEM(fields.shape, F32),
            pltpu.VMEM(spectra.shape, F32),
            pltpu.VMEM((owned, 1, LANES), F32),
            pltpu.VMEM((1, LANES), F32),
            pltpu.VMEM((size_y + cap_count, 1, LANES), F32),
        ),
        in_specs=[anywhere] * 9,
        out_specs=(vmem,) * 5,
        scratch_shapes=[
            *(pltpu.VMEM(shape, F32) for shape in halos[:6]),
            *(pltpu.VMEM(shape, F32) for shape in halos),
            pltpu.VMEM(fields.shape, F32),
            pltpu.VMEM(spectra.shape, F32),
            pltpu.VMEM(permittivity.shape, F32),
            pltpu.SMEM((1,), F32),
            pltpu.SMEM(wall_owner.shape, jnp.int32),
            pltpu.VMEM(cap_owner.shape, jnp.int32),
            pltpu.VMEM((chunks, LANES), jnp.int32),
            pltpu.VMEM((chunks, LANES), F32),
            pltpu.VMEM((chunks, LANES), jnp.int32),
            pltpu.VMEM((8, chunks, LANES), F32),
            pltpu.VMEM((chunks, 4, 8, LANES), F32),
            pltpu.VMEM((chunks, 2, 2 * size_y, LANES), F32),
            pltpu.VMEM((chunks, depth, 2 * LANES), BF16),
            pltpu.VMEM((chunks, depth, 2 * LANES), BF16),
            pltpu.VMEM((8 * size_y, LANES), F32),
            pltpu.VMEM((2 * rows, depth), BF16),
            pltpu.VMEM((chunks, 4, LANES), F32),
            pltpu.VMEM((peers, per, 4, LANES), F32),
            pltpu.VMEM((chunks, 4, LANES), F32),
            pltpu.VMEM((slabs, 8, LANES), F32),
            pltpu.VMEM((2, cap_count, LANES), F32),
            dma((len(halos),)), dma((2, len(halos))),
            dma, dma,
            dma, dma((owners // max(1, 4 // per),)),
            dma, dma,
            dma((slabs - 1,)), dma((2,)),
            dma((9,)), pltpu.SemaphoreType.REGULAR((2,)),
        ],
        compiler_params=pltpu.CompilerParams(collective_id=0, has_side_effects=True),
    )(
        fields, spectra, permittivity, phase_start, wall_owner, cap_owner,
        dir_index.reshape(chunks, LANES), target.reshape(chunks, LANES), aim_mask.reshape(chunks, LANES),
    )
    held = (fields.shape, spectra.shape, (owned, 1, LANES), (1, LANES), (size_y + cap_count, 1, LANES))
    fields_new, spectra_new, owned_rows, intensity, adjoint = pl.pallas_call(
        write_out,
        out_shape=tuple(jax.ShapeDtypeStruct(shape, F32) for shape in held),
        in_specs=[pl.BlockSpec(memory_space=pltpu.VMEM)] * 5,
        out_specs=(pl.BlockSpec(memory_space=pl.ANY),) * 5,
        scratch_shapes=[dma((5,))],
    )(*(pltpu.with_memory_space_constraint(out, pltpu.VMEM) for out in outs))
    owned_rows = owned_rows.reshape(1, 1, owned, 1, LANES).transpose(0, 1, 3, 2, 4)
    adjoint = adjoint.reshape(1, 1, size_y + cap_count, 1, LANES).transpose(0, 1, 3, 2, 4)
    intensity = intensity.reshape(LANES)
    if ratio > 1:
        me = (lax.axis_index("gz") * devs + lax.axis_index("dev")) * xys + lax.axis_index("xy")
        intensity = lax.dynamic_slice_in_dim(intensity, (me % ratio) * share, share, 0)
    return (fields_new, spectra_new, owned_rows, intensity, adjoint)


def solution(mesh):
    placed = (
        P("groups", "dev", "gz", "xy"),
        P("groups", "dev", "gz", "xy"),
        P(("groups", "dev"), "gz", "xy"),
        P("groups"),
        P("gz", None),
        P(),
        P(),
        P("groups"),
        P("groups"),
    )
    return jax.shard_map(
        local,
        mesh=mesh,
        in_specs=placed,
        out_specs=(
            P("groups", "dev", "gz", "xy"),
            P("groups", "dev", "gz", "xy"),
            P(("groups", "gz"), "dev", "xy", None, None),
            P(("groups", "gz", "dev", "xy")),
            P(("groups", "gz"), "dev", "xy", None, None),
        ),
        check_vma=False,
    )
```

```python
import functools
import math

import jax
import jax.numpy as jnp
from jax import lax
from jax.experimental import pallas as pl
from jax.experimental.pallas import tpu as pltpu
from jax.sharding import PartitionSpec as P

PATCH = 16
XB = 8
ZB = 4
STEPS = 3
THETAS = 64
COURANT = 0.5
ANGULAR_STEP = 0.3
WAVE_NUMBER = 0.6
LANES = 128
HIGHEST = lax.Precision.HIGHEST
CURRENT_SIGNS = (-1.0, 1.0, 1.0, -1.0)
X_PICKS = (5, 4, 2, 1)
Z_PICKS = (4, 3, 1, 0)
MESH = pl.DeviceIdType.MESH
AXES = ("dev", "gz", "xy")
F32 = jnp.float32
BF16 = jnp.bfloat16


def iota(shape, dim):
    return lax.broadcasted_iota(jnp.int32, shape, dim)


def sincos(turns):
    half = (turns - jnp.floor(turns + 0.5)) * math.pi
    sq = half * half
    sin_h = half * (1.0 + sq * (-1.0 / 6 + sq * (1.0 / 120 + sq * (-1.0 / 5040 + sq * (1.0 / 362880 - sq * (1.0 / 39916800))))))
    cos_h = 1.0 + sq * (-0.5 + sq * (1.0 / 24 + sq * (-1.0 / 720 + sq * (1.0 / 40320 + sq * (-1.0 / 3628800 + sq * (1.0 / 479001600))))))
    return 2.0 * sin_h * cos_h, 1.0 - 2.0 * sin_h * sin_h


def split(values):
    high = values.astype(BF16)
    return high, (values - high.astype(F32)).astype(BF16)


def arrival_rows(n, size_y, size_z):
    length = 5 if n == 0 else 3
    return (length + 2) * (size_z + size_y) + 1 + 3 * 8 + 4 * size_z


def block_transpose(tile):
    on_diagonal = (iota(tile.shape, 1) // PATCH) == iota(tile.shape, 0)
    total = jnp.where(on_diagonal, tile, 0.0)
    for k in range(1, 8):
        turned = pltpu.roll(tile, PATCH * k, 1)
        total = total + pltpu.roll(jnp.where(on_diagonal, turned, 0.0), 8 - k, 0)
    return total


def kernel(
    sizes,
    fields_in, spectra_in, permit_in, phase_in, wall_owner_in, cap_owner_in, dirs_in, target_in, aim_in,
    fields_out, spectra_out, owned_out, intensity_out, adjoint_out,
    out_yu, out_yd, out_zu, out_zd, out_xu, out_xd,
    in_yu, in_yd, in_zu, in_zd, in_xu, in_xd, in_zy, in_yz, in_yx, in_zx, in_xz, in_xy, blank, blank_rows, arrivals,
    fields, spectra, permit, phase, wall_owner, cap_owner, dirs, target, aim,
    geo, weights, phases, table_hi, table_lo, cap_plane, lhs,
    parts_out, parts_in, totals, walls, caps,
    halo_send, halo_got, part_send, part_got, total_send, total_got, wall_send, wall_got, cap_send, cap_got, loads, chain,
):
    slabs, devs, xys = sizes
    peers = slabs * devs * xys
    size_y, size_z, size_x = permit.shape
    chunks = dirs.shape[0]
    ratio = peers // chunks
    across = devs * xys
    per = max(1, chunks // (2 * across))
    owners = chunks // per
    groups = 2 * size_y
    half_rows = 8 * size_y
    all_rows = 2 * half_rows
    gz, dev, xy = lax.axis_index("gz"), lax.axis_index("dev"), lax.axis_index("xy")
    me = (gz * devs + dev) * xys + xy
    place = {"dev": dev, "gz": gz, "xy": xy}
    count = {"dev": devs, "gz": slabs, "xy": xys}

    def ident(flat):
        return {"gz": flat // (devs * xys), "dev": (flat // xys) % devs, "xy": flat % xys}

    pltpu.make_async_copy(fields_in, fields, loads.at[0]).start()
    barrier = pltpu.get_barrier_semaphore()

    for away in (1, -1, 0):
        @pl.when(jnp.logical_and(gz + away >= 0, gz + away < slabs))
        def _():
            def greet(k, carry):
                spot = (dev * xys + xy + k) % across
                to = {"gz": gz + away, "dev": spot // xys, "xy": spot % xys}
                pl.semaphore_signal(barrier, inc=1, device_id=to, device_id_type=MESH)
                return carry

            lax.fori_loop(0 if away else 1, across, greet, 0)

    beside = jnp.where(gz > 0, across, 0) + jnp.where(gz < slabs - 1, across, 0) + across - 1

    def pass_on():
        for at, away in enumerate((1, -1)):
            @pl.when(jnp.logical_and(gz + away >= 0, gz + away < slabs))
            def _():
                to = {"gz": gz + away, "dev": dev, "xy": xy}
                pl.semaphore_signal(chain.at[at], inc=1, device_id=to, device_id_type=MESH)

    def hear():
        for at, away in enumerate((1, -1)):
            @pl.when(jnp.logical_and(gz - away >= 0, gz - away < slabs))
            def _():
                pl.semaphore_wait(chain.at[at], 1)

    loading = [
        pltpu.make_async_copy(source, held, loads.at[number])
        for number, (source, held) in enumerate((
            (fields_in, fields), (dirs_in, dirs), (phase_in, phase), (permit_in, permit), (spectra_in, spectra),
            (wall_owner_in, wall_owner), (cap_owner_in, cap_owner), (target_in, target), (aim_in, aim),
        ))
    ]
    for copy in loading[1:]:
        copy.start()

    def geometry():
        index = dirs[...]
        sin_t, cos_t = sincos(((index // THETAS).astype(F32) + 0.5) * (0.5 / THETAS))
        sin_f, cos_f = sincos((index % THETAS).astype(F32) * (1.0 / THETAS))
        wave = WAVE_NUMBER / (2.0 * math.pi)
        for slot, values in enumerate((
            wave * sin_t * cos_f, wave * sin_t * sin_f, wave * cos_t,
            cos_t * cos_f, cos_t * sin_f, -sin_t, -sin_f, cos_f,
        )):
            geo[slot] = values

    grid_x, grid_y, grid_z = size_x * xys, size_y * devs, size_z * slabs
    x_first = (xy * size_x).astype(F32) - (grid_x - 1) / 2.0
    y_first = (dev * size_y).astype(F32) - (grid_y - 1) / 2.0
    z_first = (gz * size_z).astype(F32) - (grid_z - 1) / 2.0
    x_wall = jnp.where(xy == 0, XB, size_x - 1 - XB)
    z_cap = jnp.where(gz == 0, ZB, size_z - 1 - ZB)
    x_face = x_first + x_wall.astype(F32)
    z_face = z_first + z_cap.astype(F32)
    facing_x = jnp.where(xy == 0, -1.0, 1.0)
    facing_z = jnp.where(gz == 0, -1.0, 1.0)
    is_end = jnp.logical_or(gz == 0, gz == slabs - 1)
    end_weight = jnp.where(is_end, 1.0, 0.0)
    norm = 1.0 / math.sqrt(2.0 * (2 * grid_y * grid_z + 2 * grid_y * grid_x))

    def make_tables(j, carry):
        def row(slot):
            return geo[slot, pl.ds(j, 1), :]

        ux, uy, uz = row(0), row(1), row(2)
        blocks = size_x // 8
        far_s, far_c = sincos((iota((blocks, LANES), 0).astype(F32) * 8.0 + x_first) * ux)
        near_s, near_c = sincos(iota((8, LANES), 0).astype(F32) * ux)
        far_s, far_c = far_s[:, None, :], far_c[:, None, :]
        near_s, near_c = near_s[None], near_c[None]
        cos_x = (far_c * near_c - far_s * near_s).reshape(size_x, LANES)
        sin_x = (far_s * near_c + far_c * near_s).reshape(size_x, LANES)
        sin_z, cos_z = sincos((iota((size_z, LANES), 0).astype(F32) + z_first) * uz)
        for at, (x_part, z_part) in enumerate(((cos_x, cos_z), (sin_x, sin_z))):
            lanes = pl.ds(at * LANES, LANES)
            x_high, x_low = split(x_part)
            z_high, z_low = split(z_part)
            table_hi[j, pl.ds(0, size_x), lanes] = x_high
            table_lo[j, pl.ds(0, size_x), lanes] = x_low
            table_hi[j, pl.ds(size_x, 8 * size_z), lanes] = jnp.concatenate([z_high] * 8, axis=0)
            table_lo[j, pl.ds(size_x, 8 * size_z), lanes] = jnp.concatenate([z_low] * 8, axis=0)
        which = iota((groups, LANES), 0)
        cell_y = (which % size_y).astype(F32) + y_first
        sin_g, cos_g = sincos(cell_y * uy + jnp.where(which < size_y, z_face * uz, x_face * ux))
        phases[j, 0] = cos_g
        phases[j, 1] = sin_g
        kind = iota((8, LANES), 0) % 4

        def pattern(a, b, c, d):
            return jnp.where(kind == 0, a, jnp.where(kind == 1, b, jnp.where(kind == 2, c, d)))

        tx, ty, tz, fx, fy = row(3), row(4), row(5), row(6), row(7)
        weights[j, 0] = pattern(-tx, -ty, -fx, -fy)
        weights[j, 1] = pattern(-fx, -fy, tx, ty)
        weights[j, 2] = pattern(-ty, -tz, -fy, jnp.zeros_like(fy))
        weights[j, 3] = pattern(-fy, jnp.zeros_like(fy), ty, tz)
        return carry

    windows = STEPS

    def tables_of(window):
        lax.fori_loop(window * chunks // windows, (window + 1) * chunks // windows, make_tables, 0)

    lane = iota((size_z, LANES), 1)
    lane3 = iota((size_y, size_z, LANES), 2)
    row3 = iota((size_y, size_z, LANES), 1)

    messages = (
        (in_yu, {"dev": 1}), (in_yd, {"dev": -1}), (in_zu, {"gz": 1}), (in_zd, {"gz": -1}),
        (in_zy, {"gz": -1, "dev": 1}), (in_yz, {"dev": -1, "gz": 1}),
        (in_xu, {"xy": 1}), (in_xd, {"xy": -1}),
        (in_yx, {"dev": 1, "xy": -1}), (in_zx, {"gz": 1, "xy": -1}), (in_xz, {"xy": 1, "gz": -1}), (in_xy, {"xy": 1, "dev": -1}),
    )

    def within(move, sign):
        inside = True
        for axis, step in move.items():
            spot = place[axis] + sign * step
            inside = jnp.logical_and(inside, jnp.logical_and(spot >= 0, spot < count[axis]))
        return inside

    def first_of(n):
        return (0, 5) if n == 0 else (5 + 3 * (n - 1), 3)

    def views(n):
        start, length = first_of(n)
        planes, pair = pl.ds(start, length), pl.ds(2 * n, 2)
        low, high = pl.ds(0, 8), pl.ds(size_z - 8, 8)
        return (
            (out_yu.at[planes], in_yu.at[planes]), (out_yd.at[pair], in_yd.at[pair]),
            (out_zu.at[planes], in_zu.at[planes]), (out_zd.at[pair], in_zd.at[pair]),
            (out_zd.at[2 * n, size_y - 1], in_zy.at[n]), (out_yd.at[2 * n, high], in_yz.at[n]),
            (out_xu.at[n], in_xu.at[n]), (out_xd.at[n], in_xd.at[n]),
            (out_xd.at[n], in_yx.at[n]), (out_xd.at[n, high], in_zx.at[n]),
            (out_xu.at[n, low], in_xz.at[n]), (out_xu.at[n], in_xy.at[n]),
        )

    def halo_copy(n, number, source, landing):
        to = {axis: (place[axis] + step + count[axis]) % count[axis] for axis, step in messages[number][1].items()}
        return pltpu.make_async_remote_copy(
            src_ref=source,
            dst_ref=landing,
            send_sem=halo_send.at[number],
            recv_sem=halo_got.at[n],
            device_id=to,
            device_id_type=MESH,
        )

    def start_halo(n, numbers):
        for number in numbers:
            @pl.when(within(messages[number][1], 1))
            def _():
                halo_copy(n, number, *views(n)[number]).start()

    def fill_halo(n):
        length = first_of(n)[1]
        planes, pair, rows, row_pair = blank.at[pl.ds(0, length)], blank.at[pl.ds(0, 2)], blank_rows.at[pl.ds(0, length)], blank_rows.at[pl.ds(0, 2)]
        plane, tile = blank.at[0], blank.at[0, pl.ds(0, 8)]
        sources = (planes, pair, rows, row_pair, blank_rows.at[0, 0], tile, plane, plane, plane, tile, tile, plane)
        for number, source in enumerate(sources):
            @pl.when(jnp.logical_not(within(messages[number][1], -1)))
            def _():
                pltpu.make_async_copy(source, views(n)[number][1], halo_got.at[n]).start()

    def wait_halo(n):
        everything = arrivals.at[pl.ds(0, arrival_rows(n, size_y, size_z))]
        pltpu.make_async_copy(everything, everything, halo_got.at[n]).wait()

    def pack(values, high):
        packed = jnp.zeros((size_z, LANES), F32)
        for k, value in enumerate(values):
            for y in range(size_y):
                spot = k * size_y + y
                amount = (spot + 1) % LANES if high else spot
                turned = pltpu.roll(value[y], amount, 1) if amount else value[y]
                packed = jnp.where(lane == spot, turned, packed)
        return packed

    def stage(n, ex, ey, ez, for_y, for_z, for_x):
        start, _ = first_of(n)
        for k, value in enumerate((ex, ey, ez) + for_y):
            out_yu[start + k] = value[size_y - 1]
        for k, value in enumerate((ez, ex)):
            out_yd[2 * n + k] = value[0]
        for k, value in enumerate((ex, ey, ez) + for_z):
            out_zu[start + k] = value[:, size_z - 1 : size_z, :]
        for k, value in enumerate((ey, ex)):
            out_zd[2 * n + k] = value[:, 0:1, :]
        yield
        out_xu[n] = pack((ex, ey, ez) + for_x, True)
        out_xd[n] = pack((ez, ey), False)
        yield

    blank[...] = jnp.zeros(blank.shape, F32)
    blank_rows[...] = jnp.zeros(blank_rows.shape, F32)

    def inner(ahead, axis, value):
        if axis == 0:
            none = jnp.zeros_like(value[:1])
            if ahead:
                return jnp.concatenate([value[1:], none], axis=0) - value
            return value - jnp.concatenate([none, value[:-1]], axis=0)
        length = value.shape[axis]
        spots = row3 if axis == 1 else lane3
        if ahead:
            return jnp.where(spots == length - 1, 0.0, pltpu.roll(value, length - 1, axis)) - value
        return value - jnp.where(spots == 0, 0.0, pltpu.roll(value, 1, axis))

    none = jnp.zeros((size_y - 1, size_z, LANES), F32)

    def at_y(plane, ahead):
        return jnp.concatenate([none, plane[None]] if ahead else [plane[None], none], axis=0)

    def at_z(rows, ahead):
        return jnp.where(row3 == (size_z - 1 if ahead else 0), rows, 0.0)

    def at_x(packed, k, ahead):
        edges = []
        for y in range(size_y):
            spot = k * size_y + y
            amount = (LANES - 1 - spot) if ahead else (LANES - spot) % LANES
            edges.append(pltpu.roll(packed, amount, 1) if amount else packed)
        return jnp.where(lane3 == (size_x - 1 if ahead else 0), jnp.stack(edges, axis=0), 0.0)

    def turn(value, by, axis):
        return pltpu.roll(value, by % value.shape[axis], axis)

    row2 = iota((size_z, LANES), 0)
    lane_row = iota((size_y, 1, LANES), 2)
    half_y = jnp.where(dev > 0, COURANT, 0.0)
    half_z = jnp.where(gz > 0, COURANT, 0.0)
    half_x = jnp.where(xy > 0, COURANT, 0.0)

    loading[0].wait()
    ex, ey, ez = fields[0], fields[1], fields[2]
    hx, hy, hz = fields[3], fields[4], fields[5]
    for _ in stage(0, ex, ey, ez, (hx, hz), (hx, hy), (hy, hz)):
        pass
    pl.semaphore_wait(barrier, beside)
    start_halo(0, (4, 5, 8, 11, 9, 10, 0, 1, 2, 3, 6, 7))
    fill_halo(0)
    pass_on()
    for copy in loading[1:3]:
        copy.wait()
    geometry()
    run_s, run_c = sincos((phase[0] + 0.5 * ANGULAR_STEP * (iota((8, LANES), 0).astype(F32) + 1.0)) * (0.5 / math.pi))
    for n in range(1, STEPS):
        fill_halo(n)
    loading[3].wait()
    rate = COURANT / permit[...]
    for copy in loading[4:]:
        copy.wait()
    spec_from = spectra
    for n in range(STEPS):
        hx = hx - COURANT * (inner(True, 0, ez) - inner(True, 1, ey))
        hy = hy - COURANT * (inner(True, 1, ex) - inner(True, 2, ez))
        hz = hz - COURANT * (inner(True, 2, ey) - inner(True, 0, ex))
        tables_of(n)
        if n == 1:
            def relay(k, carry):
                hear()
                pass_on()
                return carry

            lax.fori_loop(0, slabs - 3, relay, 0)
        wait_halo(n)
        start, _ = first_of(n)
        xp = in_xd[n]
        hx = hx - COURANT * (at_y(in_yd[2 * n], True) - at_z(in_zd[2 * n], True))
        hy = hy - COURANT * (at_z(in_zd[2 * n + 1], True) - at_x(xp, 0, True))
        hz = hz - COURANT * (at_x(xp, 1, True) - at_y(in_yd[2 * n + 1], True))

        ax, ay, az = in_yu[start], in_yu[start + 1], in_yu[start + 2]
        bx, by, bz = in_zu[start], in_zu[start + 1], in_zu[start + 2]
        c_ex, own = in_xu[n], out_xd[n]
        if n == 0:
            y_hx, y_hz = in_yu[3], in_yu[4]
            z_hx, z_hy = in_zu[3], in_zu[4]
            x_hy, x_hz = turn(c_ex, -3 * size_y, 1), turn(c_ex, -4 * size_y, 1)
        ay_z = jnp.where(row2 == size_z - 1, in_zy[n], turn(ay, -1, 0))
        ay_x = jnp.where(lane == size_x - 1, turn(in_yx[n], -2 * size_y, 1), turn(ay, -1, 1))
        y_hx = y_hx - half_y * ((ez[0] - az) - (ay_z - ay))
        y_hz = y_hz - half_y * ((ay_x - ay) - (ex[0] - ax))
        bz_y = jnp.concatenate([bz[1:], in_yz[n, 7:8, :][None]], axis=0)
        corner = in_zx[n, 7:8, :]
        bz_x = jnp.stack([turn(corner, -1 - y, 1) for y in range(size_y)], axis=0)
        bz_x = jnp.where(lane_row == size_x - 1, bz_x, jnp.stack([turn(bz[y], -1, 1) for y in range(size_y)], axis=0))
        z_hx = z_hx - half_z * ((bz_y - bz) - (ey[:, 0:1, :] - by))
        z_hy = z_hy - half_z * ((ex[:, 0:1, :] - bx) - (bz_x - bz))
        c_z = jnp.where(row2 == size_z - 1, in_xz[n, 0:1, :], turn(c_ex, -1, 0))
        c_y = jnp.where(lane == size_y - 1, turn(in_xy[n], size_y - 1, 1), turn(c_ex, -1, 1))
        x_hy = x_hy - half_x * ((c_z - c_ex) - (own - turn(c_ex, -2 * size_y, 1)))
        x_hz = x_hz - half_x * ((turn(own, -size_y, 1) - turn(c_ex, -size_y, 1)) - (c_y - c_ex))

        ex = ex + rate * (inner(False, 0, hz) - inner(False, 1, hy))
        ey = ey + rate * (inner(False, 1, hx) - inner(False, 2, hz))
        ez = ez + rate * (inner(False, 2, hy) - inner(False, 0, hx))
        ex = ex - rate * (at_y(y_hz, False) - at_z(z_hy, False))
        ey = ey - rate * (at_z(z_hx, False) - at_x(x_hz, 0, False))
        ez = ez - rate * (at_x(x_hy, 0, False) - at_y(y_hx, False))
        if n < STEPS - 1:
            staging = stage(n + 1, ex, ey, ez, (), (), ())
            next(staging)
            start_halo(n + 1, (4, 5, 0, 1, 2, 3))
            next(staging)
            start_halo(n + 1, (8, 11, 9, 10, 6, 7))
        half_c, half_s = run_c[2 * n : 2 * n + 1, :], run_s[2 * n : 2 * n + 1, :]
        for c, value in enumerate((hx, hy, hz)):
            spectra_out[3 + c] = spec_from[3 + c] + value * half_c
            spectra_out[9 + c] = spec_from[9 + c] - value * half_s
        full_c, full_s = run_c[2 * n + 1 : 2 * n + 2, :], run_s[2 * n + 1 : 2 * n + 2, :]
        for c, value in enumerate((ex, ey, ez)):
            spectra_out[c] = spec_from[c] + value * full_c
            spectra_out[6 + c] = spec_from[6 + c] - value * full_s
        spec_from = spectra_out
    for c, value in enumerate((ex, ey, ez, hx, hy, hz)):
        fields_out[c] = value

    own_walls = walls.at[gz]
    lane_block = iota((8, LANES), 1) // PATCH
    sub = iota((8, LANES), 0)
    own_block = lane_block == sub
    z_row = iota((size_z, LANES), 0)
    own_walls[...] = jnp.zeros((8, LANES), F32)
    for y in range(size_y):
        spread = jnp.zeros((size_z, LANES), F32)
        for c in range(8):
            k = c % 4
            from_c = X_PICKS[k] + (6 if c >= 4 else 0)
            column = jnp.sum(jnp.where(lane == x_wall, spectra_out[from_c, y], 0.0), axis=1, keepdims=True)
            spread = jnp.where(lane == c * PATCH + z_row, column * (CURRENT_SIGNS[k] * facing_x), spread)
        record = jnp.sum(spread, axis=0, keepdims=True)
        own_walls[pl.ds(y, 1), :] = record
        for c in range(8):
            k = c % 4
            from_c = Z_PICKS[k] + (6 if c >= 4 else 0)
            low = spectra_out[from_c, y, pl.ds(ZB, 1), :]
            high = spectra_out[from_c, y, pl.ds(size_z - 1 - ZB, 1), :]
            picked = jnp.where(gz == 0, low, high) * (CURRENT_SIGNS[k] * facing_z * end_weight)
            cap_plane[pl.ds(8 * y + c, 1), :] = picked
        wall_hi, wall_lo = split(jnp.where(own_block, record, 0.0) * norm)
        cap_hi, cap_lo = split(cap_plane[pl.ds(8 * y, 8), :] * norm)
        none = jnp.zeros((8, LANES), BF16)
        for at, (cap_part, wall_part) in enumerate(((cap_hi, wall_hi), (cap_lo, wall_lo))):
            first = at * all_rows + 8 * y
            lhs[pl.ds(first, 8), :] = jnp.concatenate([cap_part, none], axis=1)
            lhs[pl.ds(first + half_rows, 8), :] = jnp.concatenate([none, wall_part], axis=1)

    lanes8 = iota((1, LANES), 1)
    owner_row = jnp.zeros((1, LANES), F32)
    for p in range(size_y):
        owner_row = jnp.where(lanes8 == 8 * gz + p, (wall_owner[0, p] + 1).astype(F32), owner_row)
    own_walls[pl.ds(size_y, 1), :] = owner_row

    def wall_copy(k, ref=None):
        held = walls.at[gz] if ref is None else ref
        return pltpu.make_async_remote_copy(
            src_ref=held,
            dst_ref=held,
            send_sem=wall_send,
            recv_sem=wall_got,
            device_id={"gz": (gz + k) % slabs},
            device_id_type=MESH,
        )

    def cap_copy(k, at):
        return pltpu.make_async_remote_copy(
            src_ref=caps.at[at],
            dst_ref=caps.at[at],
            send_sem=cap_send,
            recv_sem=cap_got.at[at],
            device_id={"gz": (gz + k) % slabs},
            device_id_type=MESH,
        )

    sign = jnp.where(sub < 4, -1.0, 1.0)

    def far_of(j):
        rows = lhs[...]
        by_high = jnp.dot(rows, table_hi[j], preferred_element_type=F32)
        by_low = jnp.dot(rows[:all_rows], table_lo[j], preferred_element_type=F32)
        product = by_high[:all_rows] + by_high[all_rows:] + by_low
        theta = jnp.zeros((8, LANES), F32)
        phi = jnp.zeros((8, LANES), F32)
        for face in range(2):
            sum_c = jnp.zeros((8, LANES), F32)
            sum_s = jnp.zeros((8, LANES), F32)
            for y in range(size_y):
                g = face * size_y + y
                tile = product[8 * g : 8 * g + 8]
                tile = tile[:, :LANES] + sign * pltpu.roll(tile[:, LANES:], 4, 0)
                sum_c = sum_c + tile * phases[j, 0, pl.ds(g, 1), :]
                sum_s = sum_s + tile * phases[j, 1, pl.ds(g, 1), :]
            far = sum_c + sign * pltpu.roll(sum_s, 4, 0)
            theta = theta + weights[j, 2 * face] * far
            phi = phi + weights[j, 2 * face + 1] * far

        def four(values):
            pairs = values + pltpu.roll(values, 7, 0)
            return pairs + pltpu.roll(pairs, 6, 0)

        both = jnp.where(sub % 4 == 1, pltpu.roll(four(phi), 1, 0), four(theta))
        parts_out[j] = jnp.where(sub < 2, both, pltpu.roll(both, 6, 0))[:4]

    bunch = per * max(1, 4 // per)
    together = bunch // per
    upper = jnp.where(gz >= slabs // 2, 1, 0)
    near = (upper * across + dev * xys + xy) % owners

    def partner(number):
        other, bit = 0, 1
        while bit < owners:
            other = other + bit * ((near // bit + number // bit) % 2)
            bit *= 2
        return other

    def flat_of(owner):
        return (slabs // 2 - 1) * across + owner

    def part_copy(owner, source):
        return pltpu.make_async_remote_copy(
            src_ref=parts_out.at[pl.ds(owner * per, per)],
            dst_ref=parts_in.at[source],
            send_sem=part_send,
            recv_sem=part_got,
            device_id=ident(flat_of(owner)),
            device_id_type=MESH,
        )

    mine = me - flat_of(0)
    leads = jnp.logical_and(mine >= 0, mine < owners)

    def far_and_send(number, carry):
        several = [partner(owners - 1 - together * number - m) for m in range(together)]
        for owner in several:
            for m in range(per):
                far_of(owner * per + m)
        for owner in several:
            @pl.when(owner != mine)
            def _():
                part_copy(owner, me).start()

        return carry

    hear()
    lax.fori_loop(0, owners // together, far_and_send, 0)

    for k in range(1, slabs):
        wall_copy(k).start()
    for at, holder in enumerate((0, slabs - 1)):
        @pl.when(gz == holder)
        def _():
            for y in range(size_y):
                caps[at, pl.ds(8 * y, 8), :] = block_transpose(cap_plane[pl.ds(8 * y, 8), :])
            for k in range(1, slabs):
                cap_copy(k, at).start()

    def total_copy(k, owner, ref=None):
        held = totals.at[pl.ds(owner * per, per)] if ref is None else ref
        return pltpu.make_async_remote_copy(
            src_ref=held,
            dst_ref=held,
            send_sem=total_send,
            recv_sem=total_got.at[owner // together],
            device_id=ident((me + k) % peers),
            device_id_type=MESH,
        )

    @pl.when(leads)
    def _():
        everyone = parts_in.at[pl.ds(0, peers - 1)]
        pltpu.make_async_remote_copy(
            src_ref=everyone, dst_ref=everyone, send_sem=part_send, recv_sem=part_got, device_id={"gz": gz}, device_id_type=MESH
        ).wait_recv()
        parts_in[me] = parts_out[pl.ds(mine * per, per)]
        totals[pl.ds(mine * per, per)] = jnp.sum(parts_in[...], axis=0)
        for k in sorted(range(slabs), key=lambda k: -min(k, slabs - k)):
            row = (gz + k) % slabs * across

            def send(r, carry):
                to = row + (dev * xys + xy + r) % across

                @pl.when(to != me)
                def _():
                    total_copy((to - me + peers) % peers, mine).start()

                return carry

            lax.fori_loop(0, across, send, 0, unroll=across <= 4)


    def choose(mine, share, records):
        length = mine.shape[1]
        before = jnp.where(iota((length, length), 0) < iota((length, length), 1), 1.0, 0.0).astype(BF16)
        ones = jnp.broadcast_to(jnp.where(mine, 1.0, 0.0), (8, length))
        rank = jnp.dot(ones.astype(BF16), before, preferred_element_type=F32)
        wanted = iota((8, length), 0).astype(F32)
        chooser = jnp.where(rank == wanted, ones, 0.0)
        return jnp.dot(chooser, records, precision=HIGHEST, preferred_element_type=F32)[:share]

    def choose_owned():
        wall_copy(1, walls.at[pl.ds(0, slabs - 1)]).wait_recv()
        for at, holder in enumerate((0, slabs - 1)):
            @pl.when(gz != holder)
            def _():
                cap_copy(1, at).wait_recv()
        all_walls = walls[...]
        owner_all = jnp.sum(all_walls[:, size_y : size_y + 1, :], axis=0)[:, : 8 * slabs]
        cap_share = (owned_out.shape[0] - size_y) // 2
        owned_out[pl.ds(0, size_y), 0, :] = choose(
            owner_all == (gz + 1).astype(F32), size_y, all_walls.reshape(8 * slabs, LANES)
        )
        for at in range(2):
            owned_out[pl.ds(size_y + at * cap_share, cap_share), 0, :] = choose(
                cap_owner[pl.ds(at, 1), :] == gz, cap_share, caps[at]
            )

    def intensity_of(field):
        return jnp.sum(field * field, axis=0, keepdims=True)

    def slope_of(j):
        field = totals[j]
        residual = aim[pl.ds(j, 1), :].astype(F32) * (intensity_of(field) - target[pl.ds(j, 1), :])
        return 2.0 * residual * field

    def adjoint_of(j):
        slope = slope_of(j)
        by_theta = jnp.where(sub < 4, slope[0:1], slope[2:3])
        by_phi = jnp.where(sub < 4, slope[1:2], slope[3:4])
        tiles = []
        for face in range(2):
            vector = weights[j, 2 * face] * by_theta + weights[j, 2 * face + 1] * by_phi
            turned = -sign * pltpu.roll(vector, 4, 0)
            for y in range(size_y):
                g = face * size_y + y
                tile = vector * phases[j, 0, pl.ds(g, 1), :] + turned * phases[j, 1, pl.ds(g, 1), :]
                tiles.append(jnp.concatenate([tile, -sign * pltpu.roll(tile, 4, 0)], axis=1))
        rows = jnp.concatenate(tiles, axis=0)
        high, low = split(rows)
        both = jnp.concatenate([high, low], axis=0)
        across = (((1,), (1,)), ((), ()))
        by_high = lax.dot_general(both, table_hi[j], across, preferred_element_type=F32)
        by_low = lax.dot_general(high, table_lo[j], across, preferred_element_type=F32)
        return by_high[:all_rows] + by_high[all_rows:] + by_low

    def adjoint_some(number, total):
        several = [partner(together * number + m) for m in range(together)]
        batch = several[0] // together
        ours = jnp.logical_and(leads, mine // together == batch)

        @pl.when(jnp.logical_not(ours))
        def _():
            total_copy(1, several[0], totals.at[pl.ds(batch * bunch, bunch)]).wait_recv()

        if together > 1:
            @pl.when(ours)
            def _():
                total_copy(1, several[0], totals.at[pl.ds(batch * bunch, bunch - per)]).wait_recv()

        for owner in several:
            for m in range(per):
                total = total + adjoint_of(owner * per + m)
        return total

    rounds = owners // together
    choose_owned()
    gradient = lax.fori_loop(0, rounds, adjoint_some, jnp.zeros((all_rows, size_x + 8 * size_z), F32))
    intensity_out[...] = intensity_of(totals[me // ratio])
    for y in range(size_y):
        wall = gradient[half_rows + 8 * y : half_rows + 8 * y + 8, size_x:]
        adjoint_out[pl.ds(y, 1), 0, :] = jnp.sum(jnp.where(own_block, wall, 0.0), axis=0, keepdims=True) * norm
        cap = block_transpose(gradient[8 * y : 8 * y + 8, :size_x] * (norm * end_weight))
        adjoint_out[pl.ds(size_y + 8 * y, 8), 0, :] = cap

    for number, (landing, move) in enumerate(messages):
        @pl.when(within(move, 1))
        def _():
            halo_copy(0, number, landing, landing).wait_send()

    def parts_sent(ref):
        pltpu.make_async_remote_copy(
            src_ref=ref, dst_ref=ref, send_sem=part_send, recv_sem=part_got, device_id={"gz": gz}, device_id_type=MESH
        ).wait_send()

    @pl.when(leads)
    def _():
        parts_sent(parts_out.at[pl.ds(0, (owners - 1) * per)])
        total_copy(1, 0, parts_in.at[pl.ds(0, peers - 1)]).wait_send()

    @pl.when(jnp.logical_not(leads))
    def _():
        parts_sent(parts_out)

    wall_copy(1, walls.at[pl.ds(0, slabs - 1)]).wait_send()
    for at, holder in enumerate((0, slabs - 1)):
        @pl.when(gz == holder)
        def _():
            sent = weights.at[pl.ds(0, slabs - 1)]
            pltpu.make_async_copy(sent, sent, cap_send).wait()


def write_out(*refs):
    copies = [pltpu.make_async_copy(refs[i], refs[5 + i], refs[10].at[i]) for i in range(5)]
    for copy in copies:
        copy.start()
    for copy in copies:
        copy.wait()


def local(fields, spectra, permittivity, phase_start, wall_owner, cap_owner, dir_index, target, aim_mask):
    slabs, devs, xys = (lax.axis_size(a) for a in ("gz", "dev", "xy"))
    peers = slabs * devs * xys
    size_y, size_z, size_x = permittivity.shape
    assert size_z == PATCH and size_x == LANES and size_y == 4
    directions = dir_index.shape[0]
    chunks = directions // LANES
    ratio = peers // chunks
    per = max(1, chunks // (2 * devs * xys))
    owners = chunks // per
    share = directions // peers
    cap_count = size_y * size_x // PATCH
    owned = size_y + 2 * (cap_count // slabs)
    rows = 16 * size_y
    depth = size_x + 8 * size_z
    planes, pairs = 5 + 3 * (STEPS - 1), 2 * STEPS
    halos = (
        (planes, size_z, LANES), (pairs, size_z, LANES), (planes, size_y, 1, LANES), (pairs, size_y, 1, LANES),
        (STEPS, size_z, LANES), (STEPS, size_z, LANES),
        (STEPS, 1, LANES), (STEPS, 8, LANES), (STEPS, size_z, LANES), (STEPS, 8, LANES), (STEPS, 8, LANES), (STEPS, size_z, LANES),
    )
    vmem = pl.BlockSpec(memory_space=pltpu.VMEM)
    anywhere = pl.BlockSpec(memory_space=pl.ANY)
    dma = pltpu.SemaphoreType.DMA
    outs = pl.pallas_call(
        functools.partial(kernel, (slabs, devs, xys)),
        out_shape=(
            pltpu.VMEM(fields.shape, F32),
            pltpu.VMEM(spectra.shape, F32),
            pltpu.VMEM((owned, 1, LANES), F32),
            pltpu.VMEM((1, LANES), F32),
            pltpu.VMEM((size_y + cap_count, 1, LANES), F32),
        ),
        in_specs=[anywhere] * 9,
        out_specs=(vmem,) * 5,
        scratch_shapes=[
            *(pltpu.VMEM(shape, F32) for shape in halos[:6]),
            *(pltpu.VMEM(shape, F32) for shape in halos),
            pltpu.VMEM((5, size_z, LANES), F32),
            pltpu.VMEM((5, size_y, 1, LANES), F32),
            pltpu.VMEM((arrival_rows(0, size_y, size_z), 1, LANES), F32),
            pltpu.VMEM(fields.shape, F32),
            pltpu.VMEM(spectra.shape, F32),
            pltpu.VMEM(permittivity.shape, F32),
            pltpu.SMEM((1,), F32),
            pltpu.SMEM(wall_owner.shape, jnp.int32),
            pltpu.VMEM(cap_owner.shape, jnp.int32),
            pltpu.VMEM((chunks, LANES), jnp.int32),
            pltpu.VMEM((chunks, LANES), F32),
            pltpu.VMEM((chunks, LANES), jnp.int32),
            pltpu.VMEM((8, chunks, LANES), F32),
            pltpu.VMEM((chunks, 4, 8, LANES), F32),
            pltpu.VMEM((chunks, 2, 2 * size_y, LANES), F32),
            pltpu.VMEM((chunks, depth, 2 * LANES), BF16),
            pltpu.VMEM((chunks, depth, 2 * LANES), BF16),
            pltpu.VMEM((8 * size_y, LANES), F32),
            pltpu.VMEM((2 * rows, depth), BF16),
            pltpu.VMEM((chunks, 4, LANES), F32),
            pltpu.VMEM((peers, per, 4, LANES), F32),
            pltpu.VMEM((chunks, 4, LANES), F32),
            pltpu.VMEM((slabs, 8, LANES), F32),
            pltpu.VMEM((2, cap_count, LANES), F32),
            dma((len(halos),)), dma((STEPS,)),
            dma, dma,
            dma, dma((owners // max(1, 4 // per),)),
            dma, dma,
            dma, dma((2,)),
            dma((9,)), pltpu.SemaphoreType.REGULAR((2,)),
        ],
        compiler_params=pltpu.CompilerParams(collective_id=0, has_side_effects=True),
    )(
        fields, spectra, permittivity, phase_start, wall_owner, cap_owner,
        dir_index.reshape(chunks, LANES), target.reshape(chunks, LANES), aim_mask.reshape(chunks, LANES),
    )
    held = (fields.shape, spectra.shape, (owned, 1, LANES), (1, LANES), (size_y + cap_count, 1, LANES))
    fields_new, spectra_new, owned_rows, intensity, adjoint = pl.pallas_call(
        write_out,
        out_shape=tuple(jax.ShapeDtypeStruct(shape, F32) for shape in held),
        in_specs=[pl.BlockSpec(memory_space=pltpu.VMEM)] * 5,
        out_specs=(pl.BlockSpec(memory_space=pl.ANY),) * 5,
        scratch_shapes=[dma((5,))],
    )(*(pltpu.with_memory_space_constraint(out, pltpu.VMEM) for out in outs))
    owned_rows = owned_rows.reshape(1, 1, owned, 1, LANES).transpose(0, 1, 3, 2, 4)
    adjoint = adjoint.reshape(1, 1, size_y + cap_count, 1, LANES).transpose(0, 1, 3, 2, 4)
    intensity = intensity.reshape(LANES)
    if ratio > 1:
        me = (lax.axis_index("gz") * devs + lax.axis_index("dev")) * xys + lax.axis_index("xy")
        intensity = lax.dynamic_slice_in_dim(intensity, (me % ratio) * share, share, 0)
    return (fields_new, spectra_new, owned_rows, intensity, adjoint)


def solution(mesh):
    placed = (
        P("groups", "dev", "gz", "xy"),
        P("groups", "dev", "gz", "xy"),
        P(("groups", "dev"), "gz", "xy"),
        P("groups"),
        P("gz", None),
        P(),
        P(),
        P("groups"),
        P("groups"),
    )
    return jax.shard_map(
        local,
        mesh=mesh,
        in_specs=placed,
        out_specs=(
            P("groups", "dev", "gz", "xy"),
            P("groups", "dev", "gz", "xy"),
            P(("groups", "gz"), "dev", "xy", None, None),
            P(("groups", "gz", "dev", "xy")),
            P(("groups", "gz"), "dev", "xy", None, None),
        ),
        check_vma=False,
    )
```

```python
import functools
import math

import jax
import jax.numpy as jnp
from jax import lax
from jax.experimental import pallas as pl
from jax.experimental.pallas import tpu as pltpu
from jax.sharding import PartitionSpec as P

PATCH = 16
XB = 8
ZB = 4
STEPS = 3
THETAS = 64
COURANT = 0.5
ANGULAR_STEP = 0.3
WAVE_NUMBER = 0.6
LANES = 128
HIGHEST = lax.Precision.HIGHEST
CURRENT_SIGNS = (-1.0, 1.0, 1.0, -1.0)
X_PICKS = (5, 4, 2, 1)
Z_PICKS = (4, 3, 1, 0)
MESH = pl.DeviceIdType.MESH
AXES = ("dev", "gz", "xy")
F32 = jnp.float32
BF16 = jnp.bfloat16


def iota(shape, dim):
    return lax.broadcasted_iota(jnp.int32, shape, dim)


def sincos(turns):
    half = (turns - jnp.floor(turns + 0.5)) * math.pi
    sq = half * half
    sin_h = half * (1.0 + sq * (-1.0 / 6 + sq * (1.0 / 120 + sq * (-1.0 / 5040 + sq * (1.0 / 362880 - sq * (1.0 / 39916800))))))
    cos_h = 1.0 + sq * (-0.5 + sq * (1.0 / 24 + sq * (-1.0 / 720 + sq * (1.0 / 40320 + sq * (-1.0 / 3628800 + sq * (1.0 / 479001600))))))
    return 2.0 * sin_h * cos_h, 1.0 - 2.0 * sin_h * sin_h


def split(values):
    high = values.astype(BF16)
    return high, (values - high.astype(F32)).astype(BF16)


def arrival_rows(n, size_y, size_z):
    length = 5 if n == 0 else 3
    return (length + 2) * (size_z + size_y) + 1 + 3 * 8 + 4 * size_z


def block_transpose(tile):
    on_diagonal = (iota(tile.shape, 1) // PATCH) == iota(tile.shape, 0)
    total = jnp.where(on_diagonal, tile, 0.0)
    for k in range(1, 8):
        turned = pltpu.roll(tile, PATCH * k, 1)
        total = total + pltpu.roll(jnp.where(on_diagonal, turned, 0.0), 8 - k, 0)
    return total


def kernel(
    sizes,
    fields_in, spectra_in, permit_in, phase_in, wall_owner_in, cap_owner_in, dirs_in, target_in, aim_in,
    fields_out, spectra_out, owned_out, intensity_out, adjoint_out,
    out_yu, out_yd, out_zu, out_zd, out_xu, out_xd,
    in_yu, in_yd, in_zu, in_zd, in_xu, in_xd, in_zy, in_yz, in_yx, in_zx, in_xz, in_xy, blank, blank_rows, arrivals,
    out_w, out_x, land_w, land_x, cap_e, cap_h, cap_r, empty, cap_sum,
    fields, spectra, permit, phase, wall_owner, cap_owner, dirs, target, aim,
    geo, weights, phases, table_hi, table_lo, cap_plane, lhs,
    parts_out, parts_in, totals, walls, caps,
    halo_send, halo_got, part_send, part_got, total_send, total_got, wall_send, wall_got, cap_send, cap_got, loads, chain, region_send, region_got,
):
    slabs, devs, xys = sizes
    peers = slabs * devs * xys
    size_y, size_z, size_x = permit.shape
    chunks = dirs.shape[0]
    ratio = peers // chunks
    across = devs * xys
    per = max(1, chunks // (2 * across))
    owners = chunks // per
    groups = 2 * size_y
    half_rows = 8 * size_y
    all_rows = 2 * half_rows
    gz, dev, xy = lax.axis_index("gz"), lax.axis_index("dev"), lax.axis_index("xy")
    me = (gz * devs + dev) * xys + xy
    place = {"dev": dev, "gz": gz, "xy": xy}
    count = {"dev": devs, "gz": slabs, "xy": xys}

    def ident(flat):
        return {"gz": flat // (devs * xys), "dev": (flat // xys) % devs, "xy": flat % xys}

    pltpu.make_async_copy(fields_in, fields, loads.at[0]).start()
    barrier = pltpu.get_barrier_semaphore()

    for away in (1, -1, 0):
        @pl.when(jnp.logical_and(gz + away >= 0, gz + away < slabs))
        def _():
            def greet(k, carry):
                spot = (dev * xys + xy + k) % across
                to = {"gz": gz + away, "dev": spot // xys, "xy": spot % xys}
                pl.semaphore_signal(barrier, inc=1, device_id=to, device_id_type=MESH)
                return carry

            lax.fori_loop(0 if away else 1, across, greet, 0)

    beside = jnp.where(gz > 0, across, 0) + jnp.where(gz < slabs - 1, across, 0) + across - 1

    def pass_on():
        for at, away in enumerate((1, -1)):
            @pl.when(jnp.logical_and(gz + away >= 0, gz + away < slabs))
            def _():
                to = {"gz": gz + away, "dev": dev, "xy": xy}
                pl.semaphore_signal(chain.at[at], inc=1, device_id=to, device_id_type=MESH)

    def hear():
        for at, away in enumerate((1, -1)):
            @pl.when(jnp.logical_and(gz - away >= 0, gz - away < slabs))
            def _():
                pl.semaphore_wait(chain.at[at], 1)

    loading = [
        pltpu.make_async_copy(source, held, loads.at[number])
        for number, (source, held) in enumerate((
            (fields_in, fields), (dirs_in, dirs), (phase_in, phase), (permit_in, permit), (spectra_in, spectra),
            (wall_owner_in, wall_owner), (cap_owner_in, cap_owner), (target_in, target), (aim_in, aim),
        ))
    ]
    for copy in loading[1:]:
        copy.start()

    def geometry():
        index = dirs[...]
        sin_t, cos_t = sincos(((index // THETAS).astype(F32) + 0.5) * (0.5 / THETAS))
        sin_f, cos_f = sincos((index % THETAS).astype(F32) * (1.0 / THETAS))
        wave = WAVE_NUMBER / (2.0 * math.pi)
        for slot, values in enumerate((
            wave * sin_t * cos_f, wave * sin_t * sin_f, wave * cos_t,
            cos_t * cos_f, cos_t * sin_f, -sin_t, -sin_f, cos_f,
        )):
            geo[slot] = values

    grid_x, grid_y, grid_z = size_x * xys, size_y * devs, size_z * slabs
    x_first = (xy * size_x).astype(F32) - (grid_x - 1) / 2.0
    y_first = (dev * size_y).astype(F32) - (grid_y - 1) / 2.0
    z_first = (gz * size_z).astype(F32) - (grid_z - 1) / 2.0
    x_wall = jnp.where(xy == 0, XB, size_x - 1 - XB)
    z_cap = jnp.where(gz == 0, ZB, size_z - 1 - ZB)
    x_face = x_first + x_wall.astype(F32)
    z_face = z_first + z_cap.astype(F32)
    facing_x = jnp.where(xy == 0, -1.0, 1.0)
    facing_z = jnp.where(gz == 0, -1.0, 1.0)
    is_end = jnp.logical_or(gz == 0, gz == slabs - 1)
    end_weight = jnp.where(is_end, 1.0, 0.0)
    norm = 1.0 / math.sqrt(2.0 * (2 * grid_y * grid_z + 2 * grid_y * grid_x))

    def make_tables(j, carry):
        def row(slot):
            return geo[slot, pl.ds(j, 1), :]

        ux, uy, uz = row(0), row(1), row(2)
        blocks = size_x // 8
        far_s, far_c = sincos((iota((blocks, LANES), 0).astype(F32) * 8.0 + x_first) * ux)
        near_s, near_c = sincos(iota((8, LANES), 0).astype(F32) * ux)
        far_s, far_c = far_s[:, None, :], far_c[:, None, :]
        near_s, near_c = near_s[None], near_c[None]
        cos_x = (far_c * near_c - far_s * near_s).reshape(size_x, LANES)
        sin_x = (far_s * near_c + far_c * near_s).reshape(size_x, LANES)
        sin_z, cos_z = sincos((iota((size_z, LANES), 0).astype(F32) + z_first) * uz)
        for at, (x_part, z_part) in enumerate(((cos_x, cos_z), (sin_x, sin_z))):
            lanes = pl.ds(at * LANES, LANES)
            x_high, x_low = split(x_part)
            z_high, z_low = split(z_part)
            table_hi[j, pl.ds(0, size_x), lanes] = x_high
            table_lo[j, pl.ds(0, size_x), lanes] = x_low
            table_hi[j, pl.ds(size_x, 8 * size_z), lanes] = jnp.concatenate([z_high] * 8, axis=0)
            table_lo[j, pl.ds(size_x, 8 * size_z), lanes] = jnp.concatenate([z_low] * 8, axis=0)
        which = iota((groups, LANES), 0)
        cell_y = (which % size_y).astype(F32) + y_first
        sin_g, cos_g = sincos(cell_y * uy + jnp.where(which < size_y, z_face * uz, x_face * ux))
        phases[j, 0] = cos_g
        phases[j, 1] = sin_g
        kind = iota((8, LANES), 0) % 4

        def pattern(a, b, c, d):
            return jnp.where(kind == 0, a, jnp.where(kind == 1, b, jnp.where(kind == 2, c, d)))

        tx, ty, tz, fx, fy = row(3), row(4), row(5), row(6), row(7)
        weights[j, 0] = pattern(-tx, -ty, -fx, -fy)
        weights[j, 1] = pattern(-fx, -fy, tx, ty)
        weights[j, 2] = pattern(-ty, -tz, -fy, jnp.zeros_like(fy))
        weights[j, 3] = pattern(-fy, jnp.zeros_like(fy), ty, tz)
        return carry

    windows = STEPS

    def tables_of(window):
        lax.fori_loop(window * chunks // windows, (window + 1) * chunks // windows, make_tables, 0)

    lane = iota((size_z, LANES), 1)
    lane3 = iota((size_y, size_z, LANES), 2)
    row3 = iota((size_y, size_z, LANES), 1)

    messages = (
        (in_yu, {"dev": 1}), (in_yd, {"dev": -1}), (in_zu, {"gz": 1}), (in_zd, {"gz": -1}),
        (in_zy, {"gz": -1, "dev": 1}), (in_yz, {"dev": -1, "gz": 1}),
        (in_xu, {"xy": 1}), (in_xd, {"xy": -1}),
        (in_yx, {"dev": 1, "xy": -1}), (in_zx, {"gz": 1, "xy": -1}), (in_xz, {"xy": 1, "gz": -1}), (in_xy, {"xy": 1, "dev": -1}),
    )

    def within(move, sign):
        inside = True
        for axis, step in move.items():
            spot = place[axis] + sign * step
            inside = jnp.logical_and(inside, jnp.logical_and(spot >= 0, spot < count[axis]))
        return inside

    def first_of(n):
        return (0, 5) if n == 0 else (5 + 3 * (n - 1), 3)

    def views(n):
        start, length = first_of(n)
        planes, pair = pl.ds(start, length), pl.ds(2 * n, 2)
        low, high = pl.ds(0, 8), pl.ds(size_z - 8, 8)
        return (
            (out_yu.at[planes], in_yu.at[planes]), (out_yd.at[pair], in_yd.at[pair]),
            (out_zu.at[planes], in_zu.at[planes]), (out_zd.at[pair], in_zd.at[pair]),
            (out_zd.at[2 * n, size_y - 1], in_zy.at[n]), (out_yd.at[2 * n, high], in_yz.at[n]),
            (out_xu.at[n], in_xu.at[n]), (out_xd.at[n], in_xd.at[n]),
            (out_xd.at[n], in_yx.at[n]), (out_xd.at[n, high], in_zx.at[n]),
            (out_xu.at[n, low], in_xz.at[n]), (out_xu.at[n], in_xy.at[n]),
        )

    def halo_copy(n, number, source, landing):
        to = {axis: (place[axis] + step + count[axis]) % count[axis] for axis, step in messages[number][1].items()}
        return pltpu.make_async_remote_copy(
            src_ref=source,
            dst_ref=landing,
            send_sem=halo_send.at[number],
            recv_sem=halo_got.at[n],
            device_id=to,
            device_id_type=MESH,
        )

    def start_halo(n, numbers):
        for number in numbers:
            @pl.when(within(messages[number][1], 1))
            def _():
                halo_copy(n, number, *views(n)[number]).start()

    def fill_halo(n):
        length = first_of(n)[1]
        planes, pair, rows, row_pair = blank.at[pl.ds(0, length)], blank.at[pl.ds(0, 2)], blank_rows.at[pl.ds(0, length)], blank_rows.at[pl.ds(0, 2)]
        plane, tile = blank.at[0], blank.at[0, pl.ds(0, 8)]
        sources = (planes, pair, rows, row_pair, blank_rows.at[0, 0], tile, plane, plane, plane, tile, tile, plane)
        for number, source in enumerate(sources):
            @pl.when(jnp.logical_not(within(messages[number][1], -1)))
            def _():
                pltpu.make_async_copy(source, views(n)[number][1], halo_got.at[n]).start()

    def wait_halo(n):
        everything = arrivals.at[pl.ds(0, arrival_rows(n, size_y, size_z))]
        pltpu.make_async_copy(everything, everything, halo_got.at[n]).wait()

    def pack(values, high):
        packed = jnp.zeros((size_z, LANES), F32)
        for k, value in enumerate(values):
            for y in range(size_y):
                spot = k * size_y + y
                amount = (spot + 1) % LANES if high else spot
                turned = pltpu.roll(value[y], amount, 1) if amount else value[y]
                packed = jnp.where(lane == spot, turned, packed)
        return packed

    def stage(n, ex, ey, ez, for_y, for_z, for_x):
        start, _ = first_of(n)
        for k, value in enumerate((ex, ey, ez) + for_y):
            out_yu[start + k] = value[size_y - 1]
        for k, value in enumerate((ez, ex)):
            out_yd[2 * n + k] = value[0]
        for k, value in enumerate((ex, ey, ez) + for_z):
            out_zu[start + k] = value[:, size_z - 1 : size_z, :]
        for k, value in enumerate((ey, ex)):
            out_zd[2 * n + k] = value[:, 0:1, :]
        yield
        out_xu[n] = pack((ex, ey, ez) + for_x, True)
        out_xd[n] = pack((ez, ey), False)
        yield

    blank[...] = jnp.zeros(blank.shape, F32)
    blank_rows[...] = jnp.zeros(blank_rows.shape, F32)

    def inner(ahead, axis, value):
        if axis == 0:
            none = jnp.zeros_like(value[:1])
            if ahead:
                return jnp.concatenate([value[1:], none], axis=0) - value
            return value - jnp.concatenate([none, value[:-1]], axis=0)
        length = value.shape[axis]
        spots = row3 if axis == 1 else lane3
        if ahead:
            return jnp.where(spots == length - 1, 0.0, pltpu.roll(value, length - 1, axis)) - value
        return value - jnp.where(spots == 0, 0.0, pltpu.roll(value, 1, axis))

    none = jnp.zeros((size_y - 1, size_z, LANES), F32)

    def at_y(plane, ahead):
        return jnp.concatenate([none, plane[None]] if ahead else [plane[None], none], axis=0)

    def at_z(rows, ahead):
        return jnp.where(row3 == (size_z - 1 if ahead else 0), rows, 0.0)

    def at_x(packed, k, ahead):
        edges = []
        for y in range(size_y):
            spot = k * size_y + y
            amount = (LANES - 1 - spot) if ahead else (LANES - spot) % LANES
            edges.append(pltpu.roll(packed, amount, 1) if amount else packed)
        return jnp.where(lane3 == (size_x - 1 if ahead else 0), jnp.stack(edges, axis=0), 0.0)

    def turn(value, by, axis):
        return pltpu.roll(value, by % value.shape[axis], axis)

    row2 = iota((size_z, LANES), 0)
    lane_row = iota((size_y, 1, LANES), 2)
    half_y = jnp.where(dev > 0, COURANT, 0.0)
    half_z = jnp.where(gz > 0, COURANT, 0.0)
    half_x = jnp.where(xy > 0, COURANT, 0.0)

    zt = pl.multiple_of(jnp.where(gz == 0, 0, size_z - 8), 8)
    depth = STEPS
    extent = size_y + 2 * depth
    quarter = 8 * size_y
    low_tile, high_tile = pl.ds(0, 8), pl.ds(size_z - 8, 8)

    regions = []
    for a in (1, -1, 0):
        for b in (1, -1, 0):
            if a or b:
                source = out_w if b == 0 else out_w.at[:, high_tile if b > 0 else low_tile]
                rows = pl.ds(8, size_z) if b == 0 else pl.ds(0 if b > 0 else size_z + 8, 8)
                landing = land_w.at[1 - a, :, rows]
                nothing = blank.at[pl.ds(0, 2)] if b == 0 else empty.at[0, pl.ds(0, 2)]
                regions.append((0, {"dev": a, "gz": b}, source, landing, landing, nothing))
    for a in (1, -1, 0):
        for flip in (0, 1):
            if a or flip:
                to = {"dev": a, "flip": flip}
                regions.append((1, to, out_x, land_x.at[1 - a, xy], land_x.at[1 - a, (xy + flip) % 2], empty.at[0, pl.ds(0, 2)]))
    for at, a in enumerate((1, -1)):
        three = pl.ds(size_y - depth, depth) if a > 0 else pl.ds(0, depth)
        two = pl.ds(size_y - 2, 2) if a > 0 else pl.ds(0, 2)
        h_planes = three if a > 0 else two
        h_landing = cap_h.at[at] if a > 0 else cap_h.at[at, :, two]
        tile = pl.ds(zt, 8)
        for source, landing, nothing in (
            (fields_in.at[pl.ds(0, 3), three, tile], cap_e.at[at], empty),
            (fields_in.at[pl.ds(3, 3), h_planes, tile], h_landing, empty if a > 0 else empty.at[:, two]),
            (permit_in.at[two, tile], cap_r.at[at], empty.at[0, pl.ds(0, 2)]),
        ):
            regions.append((2, {"dev": a}, source, landing, landing, nothing))

    def region_inside(move, sign):
        return within({axis: step for axis, step in move.items() if axis != "flip" and step}, sign)

    def region_copy(number):
        kind, move, source, landing, _, _ = regions[number]
        to = {axis: (place[axis] + step + count[axis]) % count[axis] for axis, step in move.items() if axis != "flip"}
        if move.get("flip"):
            to["xy"] = (xy + 1) % 2
        return pltpu.make_async_remote_copy(
            src_ref=source,
            dst_ref=landing,
            send_sem=region_send.at[number],
            recv_sem=region_got.at[min(kind, 1)],
            device_id=to,
            device_id_type=MESH,
        )

    def region_when(number, sign):
        inside = region_inside(regions[number][1], sign)
        return jnp.logical_and(inside, is_end) if regions[number][0] else inside

    def start_regions(kinds):
        for number, region in enumerate(regions):
            if region[0] in kinds:
                @pl.when(region_when(number, 1))
                def _():
                    region_copy(number).start()

    def fill_regions():
        for number, (kind, move, _, _, landing, nothing) in enumerate(regions):
            missing = jnp.logical_not(region_inside(move, -1))

            @pl.when(jnp.logical_and(missing, is_end) if kind else missing)
            def _():
                pltpu.make_async_copy(nothing, landing, region_got.at[min(kind, 1)]).start()

    def wait_region(which):
        length = (10 * size_z) if which == 0 else 80 + 296
        everything = arrivals.at[pl.ds(0, length)]
        pltpu.make_async_copy(everything, everything, region_got.at[which]).wait()

    def window(slots, amount_of):
        rows = slots[0].shape[1]
        spot = iota((rows, LANES), 1)
        packs = []
        for part in range(2):
            packed = jnp.full((rows, LANES), COURANT, F32)
            for c in range(4 * part, min(4 * part + 4, len(slots))):
                for y in range(size_y):
                    base = quarter * (c % 4) + 8 * y
                    turned = pltpu.roll(slots[c][y], amount_of(base), 1)
                    packed = jnp.where(jnp.logical_and(spot >= base, spot < base + 8), turned, packed)
            packs.append(packed)
        return packs

    empty[...] = jnp.zeros(empty.shape, F32)
    pl.semaphore_wait(barrier, beside)
    start_regions((2,))
    pass_on()
    loading[0].wait()
    loading[3].wait()
    permit[...] = COURANT / permit[...]
    own = window([fields[c] for c in range(6)] + [permit[...]], lambda base: (base - (x_wall - 4) + 2 * LANES) % LANES)
    for part in range(2):
        out_w[part] = own[part]
        land_w[1, part, pl.ds(8, size_z), :] = own[part]

    @pl.when(is_end)
    def _():
        tile = pl.ds(zt, 8)
        packs = window([fields[c, :, tile, :] for c in range(6)] + [permit[:, tile, :]], lambda base: (base + 4) % LANES)
        left = iota((8, LANES), 1) % 8 < 4
        mine_half = jnp.where(xy == 0, 1.0, 0.0)
        for part in range(2):
            kept = packs[part] * jnp.where(left, mine_half, 1.0 - mine_half)
            out_x[part] = kept
            land_x[1, xy, part] = kept

    @pl.when(jnp.logical_not(is_end))
    def _():
        land_x[...] = jnp.zeros(land_x.shape, F32)

    start_regions((1, 0))
    for _ in stage(0, *(fields[c] for c in range(3)), (fields[3], fields[5]), (fields[3], fields[4]), (fields[4], fields[5])):
        pass
    start_halo(0, (4, 5, 8, 11, 9, 10, 0, 1, 2, 3, 6, 7))
    fill_regions()
    for n in range(STEPS):
        fill_halo(n)
    for copy in loading[1:3]:
        copy.wait()
    geometry()
    run_s, run_c = sincos((phase[0] + 0.5 * ANGULAR_STEP * (iota((8, LANES), 0).astype(F32) + 1.0)) * (0.5 / math.pi))
    for n in range(STEPS):
        tables_of(n)

    def relay(k, carry):
        hear()
        pass_on()
        return carry

    lax.fori_loop(0, slabs - 3, relay, 0)
    for copy in loading[4:]:
        copy.wait()

    def half_of(n):
        return run_c[2 * n : 2 * n + 1, :], run_s[2 * n : 2 * n + 1, :]

    def full_of(n):
        return run_c[2 * n + 1 : 2 * n + 2, :], run_s[2 * n + 1 : 2 * n + 2, :]

    wait_region(0)

    @pl.when(is_end)
    def _():
        wait_region(1)

    tall = size_z + 16
    spot = iota((tall + 8, LANES), 1)
    joined = [
        [jnp.concatenate([land_w[dy, part], land_x[dy, 0, part] + land_x[dy, 1, part]], axis=0) for part in range(2)]
        for dy in range(3)
    ]
    held = []
    for c in range(8):
        value = jnp.zeros((tall + 8, LANES), F32)
        first = 0
        for dy, planes in enumerate((depth, size_y, depth)):
            start = quarter * (c % 4) + (8 * (size_y - depth) if dy == 0 else 0)
            chosen = jnp.logical_and(spot >= first, spot < first + 8 * planes)
            value = jnp.where(chosen, turn(joined[dy][c // 4], first - start, 1), value)
            first += 8 * planes
        held.append(value)
    ex, ey, ez, hx, hy, hz, r, k = held
    border_e, border_h = [], []
    sums = [jnp.zeros((size_z, LANES), F32) for _ in range(8)]
    for n in range(STEPS):
        border_e.append((ez[tall:], ey[tall:]))
        hx = hx - k * ((turn(ez, -8, 1) - ez) - (turn(ey, -1, 0) - ey))
        hy = hy - k * ((turn(ex, -1, 0) - ex) - (turn(ez, -1, 1) - ez))
        hz = hz - k * ((turn(ey, -1, 1) - ey) - (turn(ex, -8, 1) - ex))
        border_h.append((hz[tall:], hy[tall:]))
        ex = ex + r * ((hz - turn(hz, 8, 1)) - (hy - turn(hy, 1, 0)))
        ey = ey + r * ((hx - turn(hx, 1, 0)) - (hz - turn(hz, 1, 1)))
        ez = ez + r * ((hy - turn(hy, 1, 1)) - (hx - turn(hx, 8, 1)))
        for at, (value, (co, si)) in enumerate(((hz, half_of(n)), (hy, half_of(n)), (ez, full_of(n)), (ey, full_of(n)))):
            value = value[8 : 8 + size_z]
            sums[at] = sums[at] + value * co
            sums[4 + at] = sums[4 + at] - value * si

    cap_sum[...] = jnp.zeros(cap_sum.shape, F32)

    @pl.when(is_end)
    def _():
        tile = pl.ds(zt, 8)
        eight = iota((8, LANES), 1)
        left, right = jnp.where(xy == 0, 1.0, 0.0), jnp.where(xy == 0, 0.0, 1.0)
        behind, ahead = jnp.where(dev > 0, COURANT, 0.0), jnp.where(dev < devs - 1, COURANT, 0.0)

        def rate_of(eps):
            there = eps > 0.0
            return jnp.where(there, COURANT / jnp.where(there, eps, 1.0), 0.0)

        e = [[cap_e[0, c, i] for i in range(3)] + [fields[c, y, tile, :] for y in range(size_y)] + [cap_e[1, c, i] for i in range(3)] for c in range(3)]
        h = [[cap_h[0, c, i] for i in range(3)] + [fields[3 + c, y, tile, :] for y in range(size_y)] + [cap_h[1, c, i] for i in range(2)] for c in range(3)]
        rates = [None] + [rate_of(cap_r[0, i]) for i in range(2)] + [permit[y, tile, :] for y in range(size_y)] + [rate_of(cap_r[1, i]) for i in range(2)]
        coefs = [behind] * depth + [COURANT] * size_y + [ahead] * depth

        def next_x(value, border, i):
            return jnp.where(eight == LANES - 1, turn(border, LANES - 1 - (8 * i + 4), 1), turn(value, -1, 1))

        def last_x(value, border, i):
            return jnp.where(eight == 0, turn(border, -(8 * i + 3), 1), turn(value, 1, 1))

        totals_of = [[jnp.zeros((8, LANES), F32) for _ in range(8)] for _ in range(size_y)]
        for n in range(STEPS):
            bz, by = (value * left for value in border_e[n])
            fx, fy, fz = [list(v) for v in h]
            for i in range(n, extent - 1 - n):
                xs, ys, zs = e[0][i], e[1][i], e[2][i]
                fx[i] = h[0][i] - coefs[i] * ((e[2][i + 1] - zs) - (turn(ys, -1, 0) - ys))
                fy[i] = h[1][i] - coefs[i] * ((turn(xs, -1, 0) - xs) - (next_x(zs, bz, i) - zs))
                fz[i] = h[2][i] - coefs[i] * ((next_x(ys, by, i) - ys) - (e[0][i + 1] - xs))
            h = [fx, fy, fz]
            bz, by = (value * right for value in border_h[n])
            gx, gy, gz_ = [list(v) for v in e]
            for i in range(n + 1, extent - 1 - n):
                xs, ys, zs = h[0][i], h[1][i], h[2][i]
                gx[i] = e[0][i] + rates[i] * ((zs - h[2][i - 1]) - (ys - turn(ys, 1, 0)))
                gy[i] = e[1][i] + rates[i] * ((xs - turn(xs, 1, 0)) - (zs - last_x(zs, bz, i)))
                gz_[i] = e[2][i] + rates[i] * ((ys - last_x(ys, by, i)) - (xs - h[0][i - 1]))
            e = [gx, gy, gz_]
            for y in range(size_y):
                i = depth + y
                for at, (value, (co, si)) in enumerate(((h[1][i], half_of(n)), (h[0][i], half_of(n)), (e[1][i], full_of(n)), (e[0][i], full_of(n)))):
                    totals_of[y][at] = totals_of[y][at] + value * co
                    totals_of[y][4 + at] = totals_of[y][4 + at] - value * si
        for y in range(size_y):
            for c in range(8):
                value = totals_of[y][c]
                cap_sum[pl.ds(8 * y + c, 1), :] = jnp.where(gz == 0, value[ZB : ZB + 1], value[7 - ZB : 8 - ZB])

    def advance(n, ghosts):
        fields_from, spec_from = (fields, spectra) if n == 0 else (fields_out, spectra_out)
        ex, ey, ez, hx, hy, hz = (fields_from[c] for c in range(6))
        rate = permit[...]
        hx = hx - COURANT * (inner(True, 0, ez) - inner(True, 1, ey))
        hy = hy - COURANT * (inner(True, 1, ex) - inner(True, 2, ez))
        hz = hz - COURANT * (inner(True, 2, ey) - inner(True, 0, ex))
        wait_halo(n)
        start, _ = first_of(n)
        xp = in_xd[n]
        hx = hx - COURANT * (at_y(in_yd[2 * n], True) - at_z(in_zd[2 * n], True))
        hy = hy - COURANT * (at_z(in_zd[2 * n + 1], True) - at_x(xp, 0, True))
        hz = hz - COURANT * (at_x(xp, 1, True) - at_y(in_yd[2 * n + 1], True))

        ax, ay, az = in_yu[start], in_yu[start + 1], in_yu[start + 2]
        bx, by, bz = in_zu[start], in_zu[start + 1], in_zu[start + 2]
        c_ex, own = in_xu[n], out_xd[n]
        if n == 0:
            y_hx, y_hz = in_yu[3], in_yu[4]
            z_hx, z_hy = in_zu[3], in_zu[4]
            x_hy, x_hz = turn(c_ex, -3 * size_y, 1), turn(c_ex, -4 * size_y, 1)
        else:
            y_hx, y_hz, z_hx, z_hy, x_hy, x_hz = ghosts
        ay_z = jnp.where(row2 == size_z - 1, in_zy[n], turn(ay, -1, 0))
        ay_x = jnp.where(lane == size_x - 1, turn(in_yx[n], -2 * size_y, 1), turn(ay, -1, 1))
        y_hx = y_hx - half_y * ((ez[0] - az) - (ay_z - ay))
        y_hz = y_hz - half_y * ((ay_x - ay) - (ex[0] - ax))
        bz_y = jnp.concatenate([bz[1:], in_yz[n, 7:8, :][None]], axis=0)
        corner = in_zx[n, 7:8, :]
        bz_x = jnp.stack([turn(corner, -1 - y, 1) for y in range(size_y)], axis=0)
        bz_x = jnp.where(lane_row == size_x - 1, bz_x, jnp.stack([turn(bz[y], -1, 1) for y in range(size_y)], axis=0))
        z_hx = z_hx - half_z * ((bz_y - bz) - (ey[:, 0:1, :] - by))
        z_hy = z_hy - half_z * ((ex[:, 0:1, :] - bx) - (bz_x - bz))
        c_z = jnp.where(row2 == size_z - 1, in_xz[n, 0:1, :], turn(c_ex, -1, 0))
        c_y = jnp.where(lane == size_y - 1, turn(in_xy[n], size_y - 1, 1), turn(c_ex, -1, 1))
        x_hy = x_hy - half_x * ((c_z - c_ex) - (own - turn(c_ex, -2 * size_y, 1)))
        x_hz = x_hz - half_x * ((turn(own, -size_y, 1) - turn(c_ex, -size_y, 1)) - (c_y - c_ex))

        ex = ex + rate * (inner(False, 0, hz) - inner(False, 1, hy))
        ey = ey + rate * (inner(False, 1, hx) - inner(False, 2, hz))
        ez = ez + rate * (inner(False, 2, hy) - inner(False, 0, hx))
        ex = ex - rate * (at_y(y_hz, False) - at_z(z_hy, False))
        ey = ey - rate * (at_z(z_hx, False) - at_x(x_hz, 0, False))
        ez = ez - rate * (at_x(x_hy, 0, False) - at_y(y_hx, False))
        if n < STEPS - 1:
            staging = stage(n + 1, ex, ey, ez, (), (), ())
            next(staging)
            start_halo(n + 1, (4, 5, 0, 1, 2, 3))
            next(staging)
            start_halo(n + 1, (8, 11, 9, 10, 6, 7))
        half_c, half_s = run_c[2 * n : 2 * n + 1, :], run_s[2 * n : 2 * n + 1, :]
        for c, value in enumerate((hx, hy, hz)):
            spectra_out[3 + c] = spec_from[3 + c] + value * half_c
            spectra_out[9 + c] = spec_from[9 + c] - value * half_s
        full_c, full_s = run_c[2 * n + 1 : 2 * n + 2, :], run_s[2 * n + 1 : 2 * n + 2, :]
        for c, value in enumerate((ex, ey, ez)):
            spectra_out[c] = spec_from[c] + value * full_c
            spectra_out[6 + c] = spec_from[6 + c] - value * full_s
        for c, value in enumerate((ex, ey, ez, hx, hy, hz)):
            fields_out[c] = value
        return y_hx, y_hz, z_hx, z_hy, x_hy, x_hz

    own_walls = walls.at[gz]
    lane_block = iota((8, LANES), 1) // PATCH
    sub = iota((8, LANES), 0)
    own_block = lane_block == sub
    z_row = iota((size_z, LANES), 0)
    own_walls[...] = jnp.zeros((8, LANES), F32)
    for y in range(size_y):
        spread = jnp.zeros((size_z, LANES), F32)
        for c in range(8):
            k = c % 4
            from_c = X_PICKS[k] + (6 if c >= 4 else 0)
            column = jnp.where(lane == x_wall, spectra[from_c, y], 0.0) + jnp.where(lane == 8 * (depth + y) + 4, sums[c], 0.0)
            column = jnp.sum(column, axis=1, keepdims=True)
            spread = jnp.where(lane == c * PATCH + z_row, column * (CURRENT_SIGNS[k] * facing_x), spread)
        record = jnp.sum(spread, axis=0, keepdims=True)
        own_walls[pl.ds(y, 1), :] = record
        for c in range(8):
            k = c % 4
            from_c = Z_PICKS[k] + (6 if c >= 4 else 0)
            low = spectra[from_c, y, pl.ds(ZB, 1), :]
            high = spectra[from_c, y, pl.ds(size_z - 1 - ZB, 1), :]
            picked = (jnp.where(gz == 0, low, high) + cap_sum[pl.ds(8 * y + c, 1), :]) * (CURRENT_SIGNS[k] * facing_z * end_weight)
            cap_plane[pl.ds(8 * y + c, 1), :] = picked
        wall_hi, wall_lo = split(jnp.where(own_block, record, 0.0) * norm)
        cap_hi, cap_lo = split(cap_plane[pl.ds(8 * y, 8), :] * norm)
        nil = jnp.zeros((8, LANES), BF16)
        for at, (cap_part, wall_part) in enumerate(((cap_hi, wall_hi), (cap_lo, wall_lo))):
            first = at * all_rows + 8 * y
            lhs[pl.ds(first, 8), :] = jnp.concatenate([cap_part, nil], axis=1)
            lhs[pl.ds(first + half_rows, 8), :] = jnp.concatenate([nil, wall_part], axis=1)

    lanes8 = iota((1, LANES), 1)
    owner_row = jnp.zeros((1, LANES), F32)
    for p in range(size_y):
        owner_row = jnp.where(lanes8 == 8 * gz + p, (wall_owner[0, p] + 1).astype(F32), owner_row)
    own_walls[pl.ds(size_y, 1), :] = owner_row

    def wall_copy(k, ref=None):
        held = walls.at[gz] if ref is None else ref
        return pltpu.make_async_remote_copy(
            src_ref=held,
            dst_ref=held,
            send_sem=wall_send,
            recv_sem=wall_got,
            device_id={"gz": (gz + k) % slabs},
            device_id_type=MESH,
        )

    def cap_copy(k, at):
        return pltpu.make_async_remote_copy(
            src_ref=caps.at[at],
            dst_ref=caps.at[at],
            send_sem=cap_send,
            recv_sem=cap_got.at[at],
            device_id={"gz": (gz + k) % slabs},
            device_id_type=MESH,
        )

    sign = jnp.where(sub < 4, -1.0, 1.0)

    def far_of(j):
        rows = lhs[...]
        by_high = jnp.dot(rows, table_hi[j], preferred_element_type=F32)
        by_low = jnp.dot(rows[:all_rows], table_lo[j], preferred_element_type=F32)
        product = by_high[:all_rows] + by_high[all_rows:] + by_low
        theta = jnp.zeros((8, LANES), F32)
        phi = jnp.zeros((8, LANES), F32)
        for face in range(2):
            sum_c = jnp.zeros((8, LANES), F32)
            sum_s = jnp.zeros((8, LANES), F32)
            for y in range(size_y):
                g = face * size_y + y
                tile = product[8 * g : 8 * g + 8]
                tile = tile[:, :LANES] + sign * pltpu.roll(tile[:, LANES:], 4, 0)
                sum_c = sum_c + tile * phases[j, 0, pl.ds(g, 1), :]
                sum_s = sum_s + tile * phases[j, 1, pl.ds(g, 1), :]
            far = sum_c + sign * pltpu.roll(sum_s, 4, 0)
            theta = theta + weights[j, 2 * face] * far
            phi = phi + weights[j, 2 * face + 1] * far

        def four(values):
            pairs = values + pltpu.roll(values, 7, 0)
            return pairs + pltpu.roll(pairs, 6, 0)

        both = jnp.where(sub % 4 == 1, pltpu.roll(four(phi), 1, 0), four(theta))
        parts_out[j] = jnp.where(sub < 2, both, pltpu.roll(both, 6, 0))[:4]

    bunch = per * max(1, 4 // per)
    together = bunch // per
    upper = jnp.where(gz >= slabs // 2, 1, 0)
    near = (upper * across + dev * xys + xy) % owners

    def partner(number):
        other, bit = 0, 1
        while bit < owners:
            other = other + bit * ((near // bit + number // bit) % 2)
            bit *= 2
        return other

    def flat_of(owner):
        return (slabs // 2 - 1) * across + owner

    def part_copy(owner, source):
        return pltpu.make_async_remote_copy(
            src_ref=parts_out.at[pl.ds(owner * per, per)],
            dst_ref=parts_in.at[source],
            send_sem=part_send,
            recv_sem=part_got,
            device_id=ident(flat_of(owner)),
            device_id_type=MESH,
        )

    mine = me - flat_of(0)
    leads = jnp.logical_and(mine >= 0, mine < owners)

    def far_and_send(number, carry):
        several = [partner(owners - 1 - together * number - m) for m in range(together)]
        for owner in several:
            for m in range(per):
                far_of(owner * per + m)
        for owner in several:
            @pl.when(owner != mine)
            def _():
                part_copy(owner, me).start()

        return carry

    hear()
    lax.fori_loop(0, owners // together, far_and_send, 0)

    for k in range(1, slabs):
        wall_copy(k).start()
    for at, holder in enumerate((0, slabs - 1)):
        @pl.when(gz == holder)
        def _():
            for y in range(size_y):
                caps[at, pl.ds(8 * y, 8), :] = block_transpose(cap_plane[pl.ds(8 * y, 8), :])
            for k in range(1, slabs):
                cap_copy(k, at).start()

    def total_copy(k, owner, ref=None):
        held = totals.at[pl.ds(owner * per, per)] if ref is None else ref
        return pltpu.make_async_remote_copy(
            src_ref=held,
            dst_ref=held,
            send_sem=total_send,
            recv_sem=total_got.at[owner // together],
            device_id=ident((me + k) % peers),
            device_id_type=MESH,
        )

    ghosts = advance(0, None)

    @pl.when(leads)
    def _():
        everyone = parts_in.at[pl.ds(0, peers - 1)]
        pltpu.make_async_remote_copy(
            src_ref=everyone, dst_ref=everyone, send_sem=part_send, recv_sem=part_got, device_id={"gz": gz}, device_id_type=MESH
        ).wait_recv()
        parts_in[me] = parts_out[pl.ds(mine * per, per)]
        totals[pl.ds(mine * per, per)] = jnp.sum(parts_in[...], axis=0)
        for k in sorted(range(slabs), key=lambda k: -min(k, slabs - k)):
            row = (gz + k) % slabs * across

            def send(r, carry):
                to = row + (dev * xys + xy + r) % across

                @pl.when(to != me)
                def _():
                    total_copy((to - me + peers) % peers, mine).start()

                return carry

            lax.fori_loop(0, across, send, 0, unroll=across <= 4)


    def choose(mine, share, records):
        length = mine.shape[1]
        before = jnp.where(iota((length, length), 0) < iota((length, length), 1), 1.0, 0.0).astype(BF16)
        ones = jnp.broadcast_to(jnp.where(mine, 1.0, 0.0), (8, length))
        rank = jnp.dot(ones.astype(BF16), before, preferred_element_type=F32)
        wanted = iota((8, length), 0).astype(F32)
        chooser = jnp.where(rank == wanted, ones, 0.0)
        return jnp.dot(chooser, records, precision=HIGHEST, preferred_element_type=F32)[:share]

    def choose_owned():
        wall_copy(1, walls.at[pl.ds(0, slabs - 1)]).wait_recv()
        for at, holder in enumerate((0, slabs - 1)):
            @pl.when(gz != holder)
            def _():
                cap_copy(1, at).wait_recv()
        all_walls = walls[...]
        owner_all = jnp.sum(all_walls[:, size_y : size_y + 1, :], axis=0)[:, : 8 * slabs]
        cap_share = (owned_out.shape[0] - size_y) // 2
        owned_out[pl.ds(0, size_y), 0, :] = choose(
            owner_all == (gz + 1).astype(F32), size_y, all_walls.reshape(8 * slabs, LANES)
        )
        for at in range(2):
            owned_out[pl.ds(size_y + at * cap_share, cap_share), 0, :] = choose(
                cap_owner[pl.ds(at, 1), :] == gz, cap_share, caps[at]
            )

    def intensity_of(field):
        return jnp.sum(field * field, axis=0, keepdims=True)

    def slope_of(j):
        field = totals[j]
        residual = aim[pl.ds(j, 1), :].astype(F32) * (intensity_of(field) - target[pl.ds(j, 1), :])
        return 2.0 * residual * field

    def adjoint_of(j):
        slope = slope_of(j)
        by_theta = jnp.where(sub < 4, slope[0:1], slope[2:3])
        by_phi = jnp.where(sub < 4, slope[1:2], slope[3:4])
        tiles = []
        for face in range(2):
            vector = weights[j, 2 * face] * by_theta + weights[j, 2 * face + 1] * by_phi
            turned = -sign * pltpu.roll(vector, 4, 0)
            for y in range(size_y):
                g = face * size_y + y
                tile = vector * phases[j, 0, pl.ds(g, 1), :] + turned * phases[j, 1, pl.ds(g, 1), :]
                tiles.append(jnp.concatenate([tile, -sign * pltpu.roll(tile, 4, 0)], axis=1))
        rows = jnp.concatenate(tiles, axis=0)
        high, low = split(rows)
        both = jnp.concatenate([high, low], axis=0)
        across = (((1,), (1,)), ((), ()))
        by_high = lax.dot_general(both, table_hi[j], across, preferred_element_type=F32)
        by_low = lax.dot_general(high, table_lo[j], across, preferred_element_type=F32)
        return by_high[:all_rows] + by_high[all_rows:] + by_low

    def adjoint_some(number, total):
        several = [partner(together * number + m) for m in range(together)]
        batch = several[0] // together
        ours = jnp.logical_and(leads, mine // together == batch)

        @pl.when(jnp.logical_not(ours))
        def _():
            total_copy(1, several[0], totals.at[pl.ds(batch * bunch, bunch)]).wait_recv()

        if together > 1:
            @pl.when(ours)
            def _():
                total_copy(1, several[0], totals.at[pl.ds(batch * bunch, bunch - per)]).wait_recv()

        for owner in several:
            for m in range(per):
                total = total + adjoint_of(owner * per + m)
        return total

    rounds = owners // together
    ghosts = advance(1, ghosts)
    choose_owned()
    gradient = lax.fori_loop(0, rounds, adjoint_some, jnp.zeros((all_rows, size_x + 8 * size_z), F32))
    intensity_out[...] = intensity_of(totals[me // ratio])
    advance(2, ghosts)
    for y in range(size_y):
        wall = gradient[half_rows + 8 * y : half_rows + 8 * y + 8, size_x:]
        adjoint_out[pl.ds(y, 1), 0, :] = jnp.sum(jnp.where(own_block, wall, 0.0), axis=0, keepdims=True) * norm
        cap = block_transpose(gradient[8 * y : 8 * y + 8, :size_x] * (norm * end_weight))
        adjoint_out[pl.ds(size_y + 8 * y, 8), 0, :] = cap

    for number, (landing, move) in enumerate(messages):
        @pl.when(within(move, 1))
        def _():
            halo_copy(0, number, landing, landing).wait_send()

    for number in range(len(regions)):
        @pl.when(region_when(number, 1))
        def _():
            region_copy(number).wait_send()

    def parts_sent(ref):
        pltpu.make_async_remote_copy(
            src_ref=ref, dst_ref=ref, send_sem=part_send, recv_sem=part_got, device_id={"gz": gz}, device_id_type=MESH
        ).wait_send()

    @pl.when(leads)
    def _():
        parts_sent(parts_out.at[pl.ds(0, (owners - 1) * per)])
        total_copy(1, 0, parts_in.at[pl.ds(0, peers - 1)]).wait_send()

    @pl.when(jnp.logical_not(leads))
    def _():
        parts_sent(parts_out)

    wall_copy(1, walls.at[pl.ds(0, slabs - 1)]).wait_send()
    for at, holder in enumerate((0, slabs - 1)):
        @pl.when(gz == holder)
        def _():
            sent = weights.at[pl.ds(0, slabs - 1)]
            pltpu.make_async_copy(sent, sent, cap_send).wait()


def write_out(*refs):
    copies = [pltpu.make_async_copy(refs[i], refs[5 + i], refs[10].at[i]) for i in range(5)]
    for copy in copies:
        copy.start()
    for copy in copies:
        copy.wait()


def local(fields, spectra, permittivity, phase_start, wall_owner, cap_owner, dir_index, target, aim_mask):
    slabs, devs, xys = (lax.axis_size(a) for a in ("gz", "dev", "xy"))
    peers = slabs * devs * xys
    size_y, size_z, size_x = permittivity.shape
    assert size_z == PATCH and size_x == LANES and size_y == 4 and xys == 2
    directions = dir_index.shape[0]
    chunks = directions // LANES
    ratio = peers // chunks
    per = max(1, chunks // (2 * devs * xys))
    owners = chunks // per
    share = directions // peers
    cap_count = size_y * size_x // PATCH
    owned = size_y + 2 * (cap_count // slabs)
    rows = 16 * size_y
    depth = size_x + 8 * size_z
    planes, pairs = 5 + 3 * (STEPS - 1), 2 * STEPS
    halos = (
        (planes, size_z, LANES), (pairs, size_z, LANES), (planes, size_y, 1, LANES), (pairs, size_y, 1, LANES),
        (STEPS, size_z, LANES), (STEPS, size_z, LANES),
        (STEPS, 1, LANES), (STEPS, 8, LANES), (STEPS, size_z, LANES), (STEPS, 8, LANES), (STEPS, 8, LANES), (STEPS, size_z, LANES),
    )
    vmem = pl.BlockSpec(memory_space=pltpu.VMEM)
    anywhere = pl.BlockSpec(memory_space=pl.ANY)
    dma = pltpu.SemaphoreType.DMA
    outs = pl.pallas_call(
        functools.partial(kernel, (slabs, devs, xys)),
        out_shape=(
            pltpu.VMEM(fields.shape, F32),
            pltpu.VMEM(spectra.shape, F32),
            pltpu.VMEM((owned, 1, LANES), F32),
            pltpu.VMEM((1, LANES), F32),
            pltpu.VMEM((size_y + cap_count, 1, LANES), F32),
        ),
        in_specs=[anywhere] * 9,
        out_specs=(vmem,) * 5,
        scratch_shapes=[
            *(pltpu.VMEM(shape, F32) for shape in halos[:6]),
            *(pltpu.VMEM(shape, F32) for shape in halos),
            pltpu.VMEM((5, size_z, LANES), F32),
            pltpu.VMEM((5, size_y, 1, LANES), F32),
            pltpu.VMEM((376, 1, LANES), F32),
            pltpu.VMEM((2, size_z, LANES), F32),
            pltpu.VMEM((2, 8, LANES), F32),
            pltpu.VMEM((3, 2, size_z + 16, LANES), F32),
            pltpu.VMEM((3, 2, 2, 8, LANES), F32),
            pltpu.VMEM((2, 3, 3, 8, LANES), F32),
            pltpu.VMEM((2, 3, 3, 8, LANES), F32),
            pltpu.VMEM((2, 2, 8, LANES), F32),
            pltpu.VMEM((3, 3, 8, LANES), F32),
            pltpu.VMEM((8 * size_y, LANES), F32),
            pltpu.VMEM(fields.shape, F32),
            pltpu.VMEM(spectra.shape, F32),
            pltpu.VMEM(permittivity.shape, F32),
            pltpu.SMEM((1,), F32),
            pltpu.SMEM(wall_owner.shape, jnp.int32),
            pltpu.VMEM(cap_owner.shape, jnp.int32),
            pltpu.VMEM((chunks, LANES), jnp.int32),
            pltpu.VMEM((chunks, LANES), F32),
            pltpu.VMEM((chunks, LANES), jnp.int32),
            pltpu.VMEM((8, chunks, LANES), F32),
            pltpu.VMEM((chunks, 4, 8, LANES), F32),
            pltpu.VMEM((chunks, 2, 2 * size_y, LANES), F32),
            pltpu.VMEM((chunks, depth, 2 * LANES), BF16),
            pltpu.VMEM((chunks, depth, 2 * LANES), BF16),
            pltpu.VMEM((8 * size_y, LANES), F32),
            pltpu.VMEM((2 * rows, depth), BF16),
            pltpu.VMEM((chunks, 4, LANES), F32),
            pltpu.VMEM((peers, per, 4, LANES), F32),
            pltpu.VMEM((chunks, 4, LANES), F32),
            pltpu.VMEM((slabs, 8, LANES), F32),
            pltpu.VMEM((2, cap_count, LANES), F32),
            dma((len(halos),)), dma((STEPS,)),
            dma, dma,
            dma, dma((owners // max(1, 4 // per),)),
            dma, dma,
            dma, dma((2,)),
            dma((9,)), pltpu.SemaphoreType.REGULAR((2,)), dma((19,)), dma((2,)),
        ],
        compiler_params=pltpu.CompilerParams(collective_id=0, has_side_effects=True),
    )(
        fields, spectra, permittivity, phase_start, wall_owner, cap_owner,
        dir_index.reshape(chunks, LANES), target.reshape(chunks, LANES), aim_mask.reshape(chunks, LANES),
    )
    held = (fields.shape, spectra.shape, (owned, 1, LANES), (1, LANES), (size_y + cap_count, 1, LANES))
    fields_new, spectra_new, owned_rows, intensity, adjoint = pl.pallas_call(
        write_out,
        out_shape=tuple(jax.ShapeDtypeStruct(shape, F32) for shape in held),
        in_specs=[pl.BlockSpec(memory_space=pltpu.VMEM)] * 5,
        out_specs=(pl.BlockSpec(memory_space=pl.ANY),) * 5,
        scratch_shapes=[dma((5,))],
    )(*(pltpu.with_memory_space_constraint(out, pltpu.VMEM) for out in outs))
    owned_rows = owned_rows.reshape(1, 1, owned, 1, LANES).transpose(0, 1, 3, 2, 4)
    adjoint = adjoint.reshape(1, 1, size_y + cap_count, 1, LANES).transpose(0, 1, 3, 2, 4)
    intensity = intensity.reshape(LANES)
    if ratio > 1:
        me = (lax.axis_index("gz") * devs + lax.axis_index("dev")) * xys + lax.axis_index("xy")
        intensity = lax.dynamic_slice_in_dim(intensity, (me % ratio) * share, share, 0)
    return (fields_new, spectra_new, owned_rows, intensity, adjoint)


def solution(mesh):
    placed = (
        P("groups", "dev", "gz", "xy"),
        P("groups", "dev", "gz", "xy"),
        P(("groups", "dev"), "gz", "xy"),
        P("groups"),
        P("gz", None),
        P(),
        P(),
        P("groups"),
        P("groups"),
    )
    return jax.shard_map(
        local,
        mesh=mesh,
        in_specs=placed,
        out_specs=(
            P("groups", "dev", "gz", "xy"),
            P("groups", "dev", "gz", "xy"),
            P(("groups", "gz"), "dev", "xy", None, None),
            P(("groups", "gz", "dev", "xy")),
            P(("groups", "gz"), "dev", "xy", None, None),
        ),
        check_vma=False,
    )
```

```python
import functools
import math

import jax
import jax.numpy as jnp
from jax import lax
from jax.experimental import pallas as pl
from jax.experimental.pallas import tpu as pltpu
from jax.sharding import PartitionSpec as P

PATCH = 16
XB = 8
ZB = 4
STEPS = 3
THETAS = 64
COURANT = 0.5
ANGULAR_STEP = 0.3
WAVE_NUMBER = 0.6
LANES = 128
HIGHEST = lax.Precision.HIGHEST
CURRENT_SIGNS = (-1.0, 1.0, 1.0, -1.0)
X_PICKS = (5, 4, 2, 1)
Z_PICKS = (4, 3, 1, 0)
MESH = pl.DeviceIdType.MESH
AXES = ("dev", "gz", "xy")
F32 = jnp.float32
BF16 = jnp.bfloat16


def iota(shape, dim):
    return lax.broadcasted_iota(jnp.int32, shape, dim)


def sincos(turns):
    half = (turns - jnp.floor(turns + 0.5)) * math.pi
    sq = half * half
    sin_h = half * (1.0 + sq * (-1.0 / 6 + sq * (1.0 / 120 + sq * (-1.0 / 5040 + sq * (1.0 / 362880 - sq * (1.0 / 39916800))))))
    cos_h = 1.0 + sq * (-0.5 + sq * (1.0 / 24 + sq * (-1.0 / 720 + sq * (1.0 / 40320 + sq * (-1.0 / 3628800 + sq * (1.0 / 479001600))))))
    return 2.0 * sin_h * cos_h, 1.0 - 2.0 * sin_h * sin_h


def split(values):
    high = values.astype(BF16)
    return high, (values - high.astype(F32)).astype(BF16)


def arrival_rows(n, size_y, size_z):
    length = 5 if n == 0 else 3
    return (length + 2) * (size_z + size_y) + 1 + 3 * 8 + 4 * size_z


def stagger(tile, by):
    row = iota(tile.shape, 0)
    for bit in (1, 2, 4):
        tile = jnp.where(row // bit % 2 == 1, pltpu.roll(tile, by * bit % LANES, 1), tile)
    return tile


def block_transpose(tile):
    on_diagonal = (iota(tile.shape, 1) // PATCH) == iota(tile.shape, 0)
    total = jnp.where(on_diagonal, tile, 0.0)
    for k in range(1, 8):
        turned = pltpu.roll(tile, PATCH * k, 1)
        total = total + pltpu.roll(jnp.where(on_diagonal, turned, 0.0), 8 - k, 0)
    return total


def kernel(
    sizes,
    fields_in, spectra_in, permit_in, phase_in, wall_owner_in, cap_owner_in, dirs_in, target_in, aim_in,
    fields_out, spectra_out, owned_out, intensity_out, adjoint_out,
    out_yu, out_yd, out_zu, out_zd, out_xu, out_xd,
    in_yu, in_yd, in_zu, in_zd, in_xu, in_xd, in_zy, in_yz, in_yx, in_zx, in_xz, in_xy, blank, blank_rows, arrivals,
    out_w, out_x, land_w, land_x, cap_e, cap_h, cap_r, empty, cap_sum,
    fields, spectra, permit, phase, wall_owner, cap_owner, dirs, target, aim,
    geo, weights, phases, table_hi, table_lo, cap_plane, lhs,
    parts_out, parts_in, totals, walls, caps,
    halo_send, halo_got, part_send, part_got, total_send, total_got, wall_send, wall_got, cap_send, cap_got, loads, chain, region_got,
):
    slabs, devs, xys = sizes
    peers = slabs * devs * xys
    size_y, size_z, size_x = permit.shape
    chunks = dirs.shape[0]
    ratio = peers // chunks
    across = devs * xys
    per = max(1, chunks // (2 * across))
    owners = chunks // per
    groups = 2 * size_y
    half_rows = 8 * size_y
    all_rows = 2 * half_rows
    gz, dev, xy = lax.axis_index("gz"), lax.axis_index("dev"), lax.axis_index("xy")
    me = (gz * devs + dev) * xys + xy
    place = {"dev": dev, "gz": gz, "xy": xy}
    count = {"dev": devs, "gz": slabs, "xy": xys}

    def ident(flat):
        return {"gz": flat // (devs * xys), "dev": (flat // xys) % devs, "xy": flat % xys}

    pltpu.make_async_copy(fields_in, fields, loads.at[0]).start()
    barrier = pltpu.get_barrier_semaphore()

    for away in (1, -1, 0):
        @pl.when(jnp.logical_and(gz + away >= 0, gz + away < slabs))
        def _():
            def greet(k, carry):
                spot = (dev * xys + xy + k) % across
                to = {"gz": gz + away, "dev": spot // xys, "xy": spot % xys}
                pl.semaphore_signal(barrier, inc=1, device_id=to, device_id_type=MESH)
                return carry

            lax.fori_loop(0 if away else 1, across, greet, 0)

    beside = jnp.where(gz > 0, across, 0) + jnp.where(gz < slabs - 1, across, 0) + across - 1

    def pass_on():
        for at, away in enumerate((1, -1)):
            @pl.when(jnp.logical_and(gz + away >= 0, gz + away < slabs))
            def _():
                to = {"gz": gz + away, "dev": dev, "xy": xy}
                pl.semaphore_signal(chain.at[at], inc=1, device_id=to, device_id_type=MESH)

    def hear():
        for at, away in enumerate((1, -1)):
            @pl.when(jnp.logical_and(gz - away >= 0, gz - away < slabs))
            def _():
                pl.semaphore_wait(chain.at[at], 1)

    loading = [
        pltpu.make_async_copy(source, held, loads.at[number])
        for number, (source, held) in enumerate((
            (fields_in, fields), (dirs_in, dirs), (phase_in, phase), (permit_in, permit), (spectra_in, spectra),
            (wall_owner_in, wall_owner), (cap_owner_in, cap_owner), (target_in, target), (aim_in, aim),
        ))
    ]
    for copy in loading[1:]:
        copy.start()

    def geometry():
        index = dirs[...]
        sin_t, cos_t = sincos(((index // THETAS).astype(F32) + 0.5) * (0.5 / THETAS))
        sin_f, cos_f = sincos((index % THETAS).astype(F32) * (1.0 / THETAS))
        wave = WAVE_NUMBER / (2.0 * math.pi)
        for slot, values in enumerate((
            wave * sin_t * cos_f, wave * sin_t * sin_f, wave * cos_t,
            cos_t * cos_f, cos_t * sin_f, -sin_t, -sin_f, cos_f,
        )):
            geo[slot] = values

    grid_x, grid_y, grid_z = size_x * xys, size_y * devs, size_z * slabs
    x_first = (xy * size_x).astype(F32) - (grid_x - 1) / 2.0
    y_first = (dev * size_y).astype(F32) - (grid_y - 1) / 2.0
    z_first = (gz * size_z).astype(F32) - (grid_z - 1) / 2.0
    x_wall = jnp.where(xy == 0, XB, size_x - 1 - XB)
    z_cap = jnp.where(gz == 0, ZB, size_z - 1 - ZB)
    x_face = x_first + x_wall.astype(F32)
    z_face = z_first + z_cap.astype(F32)
    facing_x = jnp.where(xy == 0, -1.0, 1.0)
    facing_z = jnp.where(gz == 0, -1.0, 1.0)
    is_end = jnp.logical_or(gz == 0, gz == slabs - 1)
    end_weight = jnp.where(is_end, 1.0, 0.0)
    norm = 1.0 / math.sqrt(2.0 * (2 * grid_y * grid_z + 2 * grid_y * grid_x))

    def make_tables(j, carry):
        def row(slot):
            return geo[slot, pl.ds(j, 1), :]

        ux, uy, uz = row(0), row(1), row(2)
        blocks = size_x // 8
        far_s, far_c = sincos((iota((blocks, LANES), 0).astype(F32) * 8.0 + x_first) * ux)
        near_s, near_c = sincos(iota((8, LANES), 0).astype(F32) * ux)
        far_s, far_c = far_s[:, None, :], far_c[:, None, :]
        near_s, near_c = near_s[None], near_c[None]
        cos_x = (far_c * near_c - far_s * near_s).reshape(size_x, LANES)
        sin_x = (far_s * near_c + far_c * near_s).reshape(size_x, LANES)
        sin_z, cos_z = sincos((iota((size_z, LANES), 0).astype(F32) + z_first) * uz)
        for at, (x_part, z_part) in enumerate(((cos_x, cos_z), (sin_x, sin_z))):
            lanes = pl.ds(at * LANES, LANES)
            x_high, x_low = split(x_part)
            z_high, z_low = split(z_part)
            table_hi[j, pl.ds(0, size_x), lanes] = x_high
            table_lo[j, pl.ds(0, size_x), lanes] = x_low
            table_hi[j, pl.ds(size_x, size_z), lanes] = z_high
            table_lo[j, pl.ds(size_x, size_z), lanes] = z_low
        which = iota((groups, LANES), 0)
        cell_y = (which % size_y).astype(F32) + y_first
        sin_g, cos_g = sincos(cell_y * uy + jnp.where(which < size_y, z_face * uz, x_face * ux))
        phases[j, 0] = cos_g
        phases[j, 1] = sin_g
        kind = iota((8, LANES), 0) % 4

        def pattern(a, b, c, d):
            return jnp.where(kind == 0, a, jnp.where(kind == 1, b, jnp.where(kind == 2, c, d)))

        tx, ty, tz, fx, fy = row(3), row(4), row(5), row(6), row(7)
        weights[j, 0] = pattern(-tx, -ty, -fx, -fy)
        weights[j, 1] = pattern(-fx, -fy, tx, ty)
        weights[j, 2] = pattern(-ty, -tz, -fy, jnp.zeros_like(fy))
        weights[j, 3] = pattern(-fy, jnp.zeros_like(fy), ty, tz)
        return carry

    windows = STEPS

    def tables_of(window):
        lax.fori_loop(window * chunks // windows, (window + 1) * chunks // windows, make_tables, 0)

    lane = iota((size_z, LANES), 1)
    lane3 = iota((size_y, size_z, LANES), 2)
    row3 = iota((size_y, size_z, LANES), 1)

    messages = (
        (in_yu, {"dev": 1}), (in_yd, {"dev": -1}), (in_zu, {"gz": 1}), (in_zd, {"gz": -1}),
        (in_zy, {"gz": -1, "dev": 1}), (in_yz, {"dev": -1, "gz": 1}),
        (in_xu, {"xy": 1}), (in_xd, {"xy": -1}),
        (in_yx, {"dev": 1, "xy": -1}), (in_zx, {"gz": 1, "xy": -1}), (in_xz, {"xy": 1, "gz": -1}), (in_xy, {"xy": 1, "dev": -1}),
    )

    def within(move, sign):
        inside = True
        for axis, step in move.items():
            spot = place[axis] + sign * step
            inside = jnp.logical_and(inside, jnp.logical_and(spot >= 0, spot < count[axis]))
        return inside

    def first_of(n):
        return (0, 5) if n == 0 else (5 + 3 * (n - 1), 3)

    def views(n):
        start, length = first_of(n)
        planes, pair = pl.ds(start, length), pl.ds(2 * n, 2)
        low, high = pl.ds(0, 8), pl.ds(size_z - 8, 8)
        return (
            (out_yu.at[planes], in_yu.at[planes]), (out_yd.at[pair], in_yd.at[pair]),
            (out_zu.at[planes], in_zu.at[planes]), (out_zd.at[pair], in_zd.at[pair]),
            (out_zd.at[2 * n, size_y - 1], in_zy.at[n]), (out_yd.at[2 * n, high], in_yz.at[n]),
            (out_xu.at[n], in_xu.at[n]), (out_xd.at[n], in_xd.at[n]),
            (out_xd.at[n], in_yx.at[n]), (out_xd.at[n, high], in_zx.at[n]),
            (out_xu.at[n, low], in_xz.at[n]), (out_xu.at[n], in_xy.at[n]),
        )

    def halo_copy(n, number, source, landing):
        to = {axis: (place[axis] + step + count[axis]) % count[axis] for axis, step in messages[number][1].items()}
        return pltpu.make_async_remote_copy(
            src_ref=source,
            dst_ref=landing,
            send_sem=halo_send.at[number],
            recv_sem=halo_got.at[n],
            device_id=to,
            device_id_type=MESH,
        )

    def start_halo(n, numbers):
        for number in numbers:
            @pl.when(within(messages[number][1], 1))
            def _():
                halo_copy(n, number, *views(n)[number]).start()

    def fill_halo(n):
        length = first_of(n)[1]
        planes, pair, rows, row_pair = blank.at[pl.ds(0, length)], blank.at[pl.ds(0, 2)], blank_rows.at[pl.ds(0, length)], blank_rows.at[pl.ds(0, 2)]
        plane, tile = blank.at[0], blank.at[0, pl.ds(0, 8)]
        sources = (planes, pair, rows, row_pair, blank_rows.at[0, 0], tile, plane, plane, plane, tile, tile, plane)
        for number, source in enumerate(sources):
            @pl.when(jnp.logical_not(within(messages[number][1], -1)))
            def _():
                pltpu.make_async_copy(source, views(n)[number][1], halo_got.at[n]).start()

    def wait_halo(n):
        everything = arrivals.at[pl.ds(0, arrival_rows(n, size_y, size_z))]
        pltpu.make_async_copy(everything, everything, halo_got.at[n]).wait()

    def pack(values, high):
        packed = jnp.zeros((size_z, LANES), F32)
        for k, value in enumerate(values):
            for y in range(size_y):
                spot = k * size_y + y
                amount = (spot + 1) % LANES if high else spot
                turned = pltpu.roll(value[y], amount, 1) if amount else value[y]
                packed = jnp.where(lane == spot, turned, packed)
        return packed

    def stage(n, ex, ey, ez, for_y, for_z, for_x):
        start, _ = first_of(n)
        for k, value in enumerate((ex, ey, ez) + for_y):
            out_yu[start + k] = value[size_y - 1]
        for k, value in enumerate((ez, ex)):
            out_yd[2 * n + k] = value[0]
        for k, value in enumerate((ex, ey, ez) + for_z):
            out_zu[start + k] = value[:, size_z - 1 : size_z, :]
        for k, value in enumerate((ey, ex)):
            out_zd[2 * n + k] = value[:, 0:1, :]
        yield
        out_xu[n] = pack((ex, ey, ez) + for_x, True)
        out_xd[n] = pack((ez, ey), False)
        yield

    blank[...] = jnp.zeros(blank.shape, F32)
    blank_rows[...] = jnp.zeros(blank_rows.shape, F32)

    def inner(ahead, axis, value):
        if axis == 0:
            none = jnp.zeros_like(value[:1])
            if ahead:
                return jnp.concatenate([value[1:], none], axis=0) - value
            return value - jnp.concatenate([none, value[:-1]], axis=0)
        length = value.shape[axis]
        spots = row3 if axis == 1 else lane3
        if ahead:
            return jnp.where(spots == length - 1, 0.0, pltpu.roll(value, length - 1, axis)) - value
        return value - jnp.where(spots == 0, 0.0, pltpu.roll(value, 1, axis))

    none = jnp.zeros((size_y - 1, size_z, LANES), F32)

    def at_y(plane, ahead):
        return jnp.concatenate([none, plane[None]] if ahead else [plane[None], none], axis=0)

    def at_z(rows, ahead):
        return jnp.where(row3 == (size_z - 1 if ahead else 0), rows, 0.0)

    def at_x(packed, k, ahead):
        edges = []
        for y in range(size_y):
            spot = k * size_y + y
            amount = (LANES - 1 - spot) if ahead else (LANES - spot) % LANES
            edges.append(pltpu.roll(packed, amount, 1) if amount else packed)
        return jnp.where(lane3 == (size_x - 1 if ahead else 0), jnp.stack(edges, axis=0), 0.0)

    def turn(value, by, axis):
        return pltpu.roll(value, by % value.shape[axis], axis)

    row2 = iota((size_z, LANES), 0)
    lane_row = iota((size_y, 1, LANES), 2)
    half_y = jnp.where(dev > 0, COURANT, 0.0)
    half_z = jnp.where(gz > 0, COURANT, 0.0)
    half_x = jnp.where(xy > 0, COURANT, 0.0)

    zt = pl.multiple_of(jnp.where(gz == 0, 0, size_z - 8), 8)
    depth = STEPS
    extent = size_y + 2 * depth
    quarter = 8 * size_y
    low_tile, high_tile = pl.ds(0, 8), pl.ds(size_z - 8, 8)

    regions = []
    for a in (1, -1, 0):
        for b in (1, -1, 0):
            if a or b:
                source = out_w if b == 0 else out_w.at[:, high_tile if b > 0 else low_tile]
                rows = pl.ds(8, size_z) if b == 0 else pl.ds(0 if b > 0 else size_z + 8, 8)
                landing = land_w.at[1 - a, :, rows]
                nothing = blank.at[pl.ds(0, 2)] if b == 0 else empty.at[0, pl.ds(0, 2)]
                regions.append((0, {"dev": a, "gz": b}, source, landing, landing, nothing))
    for a in (1, -1, 0):
        for flip in (0, 1):
            if a or flip:
                to = {"dev": a, "flip": flip}
                regions.append((1, to, out_x, land_x.at[1 - a, xy], land_x.at[1 - a, (xy + flip) % 2], empty.at[0, 0]))
    for at, a in enumerate((1, -1)):
        three = pl.ds(size_y - depth, depth) if a > 0 else pl.ds(0, depth)
        two = pl.ds(size_y - 2, 2) if a > 0 else pl.ds(0, 2)
        h_planes = three if a > 0 else two
        h_landing = cap_h.at[at] if a > 0 else cap_h.at[at, :, two]
        tile = pl.ds(zt, 8)
        for kind, source, landing, nothing in (
            (2, fields_in.at[pl.ds(0, 3), three, tile], cap_e.at[at], empty),
            (3, fields_in.at[pl.ds(3, 3), h_planes, tile], h_landing, empty if a > 0 else empty.at[:, two]),
            (3, permit_in.at[two, tile], cap_r.at[at], empty.at[0, pl.ds(0, 2)]),
        ):
            regions.append((kind, {"dev": a}, source, landing, landing, nothing))

    def group_of(number):
        kind, move = regions[number][:2]
        if kind:
            return len(messages) + 2 + (0 if not move["dev"] else 1 if move["dev"] > 0 else 2)
        for at, (_, other) in enumerate(messages):
            if {axis: step for axis, step in move.items() if step} == other:
                return at
        return len(messages) + (0 if move["dev"] > 0 else 1)

    def region_inside(move, sign):
        return within({axis: step for axis, step in move.items() if axis != "flip" and step}, sign)

    def region_copy(number):
        kind, move, source, landing, _, _ = regions[number]
        to = {axis: (place[axis] + step + count[axis]) % count[axis] for axis, step in move.items() if axis != "flip"}
        if move.get("flip"):
            to["xy"] = (xy + 1) % 2
        return pltpu.make_async_remote_copy(
            src_ref=source,
            dst_ref=landing,
            send_sem=halo_send.at[group_of(number)],
            recv_sem=region_got.at[min(kind, 2)],
            device_id=to,
            device_id_type=MESH,
        )

    def region_when(number, sign):
        inside = region_inside(regions[number][1], sign)
        return jnp.logical_and(inside, is_end) if regions[number][0] else inside

    def start_regions(kinds):
        for number, region in enumerate(regions):
            if region[0] in kinds:
                @pl.when(region_when(number, 1))
                def _():
                    region_copy(number).start()

    def fill_regions():
        for number, (kind, move, _, _, landing, nothing) in enumerate(regions):
            missing = jnp.logical_not(region_inside(move, -1))

            @pl.when(jnp.logical_and(missing, is_end) if kind else missing)
            def _():
                pltpu.make_async_copy(nothing, landing, region_got.at[min(kind, 2)]).start()

    def wait_region(which):
        length = (10 * size_z, 5 * 8, 2 * 9 * 8 + (9 + 6) * 8 + 2 * 2 * 8)[which]
        everything = arrivals.at[pl.ds(0, length)]
        pltpu.make_async_copy(everything, everything, region_got.at[which]).wait()

    def window(slots, amount_of):
        rows = slots[0].shape[1]
        spot = iota((rows, LANES), 1)
        packs = []
        for part in range(2):
            packed = jnp.full((rows, LANES), COURANT, F32)
            for c in range(4 * part, min(4 * part + 4, len(slots))):
                for y in range(size_y):
                    base = quarter * (c % 4) + 8 * y
                    turned = pltpu.roll(slots[c][y], amount_of(base), 1)
                    packed = jnp.where(jnp.logical_and(spot >= base, spot < base + 8), turned, packed)
            packs.append(packed)
        return packs

    empty[...] = jnp.zeros(empty.shape, F32)
    lhs[...] = jnp.zeros(lhs.shape, BF16)
    pl.semaphore_wait(barrier, beside)
    start_regions((2,))
    pass_on()
    loading[0].wait()
    loading[3].wait()
    permit[...] = COURANT / permit[...]
    own = window([fields[c] for c in range(6)] + [permit[...]], lambda base: (base - (x_wall - 4) + 2 * LANES) % LANES)
    for part in range(2):
        out_w[part] = own[part]
        land_w[1, part, pl.ds(8, size_z), :] = own[part]
    start_regions((0,))

    @pl.when(is_end)
    def _():
        tile = pl.ds(zt, 8)
        eight = iota((8, LANES), 1)
        packed = jnp.full((8, LANES), COURANT, F32)
        for c in range(7):
            values = permit[:, tile, :] if c == 6 else fields[c, :, tile, :]
            for y in range(size_y):
                base = quarter * (c % 4) + 8 * y + 4 * (c // 4)
                turned = pltpu.roll(values[y], (base + 4 * (1 - xy)) % LANES, 1)
                packed = jnp.where(jnp.logical_and(eight >= base, eight < base + 4), turned, packed)
        out_x[...] = packed
        land_x[1, xy] = packed

    @pl.when(jnp.logical_not(is_end))
    def _():
        land_x[...] = jnp.zeros(land_x.shape, F32)

    start_regions((1,))
    start_regions((3,))
    for _ in stage(0, *(fields[c] for c in range(3)), (fields[3], fields[5]), (fields[3], fields[4]), (fields[4], fields[5])):
        pass
    start_halo(0, (4, 5, 8, 11, 9, 10, 0, 1, 2, 3, 6, 7))
    fill_regions()
    for n in range(STEPS):
        fill_halo(n)
    for copy in loading[1:3]:
        copy.wait()
    geometry()
    run_s, run_c = sincos((phase[0] + 0.5 * ANGULAR_STEP * (iota((8, LANES), 0).astype(F32) + 1.0)) * (0.5 / math.pi))
    for n in range(STEPS):
        tables_of(n)

    def relay(k, carry):
        hear()
        pass_on()
        return carry

    lax.fori_loop(0, slabs - 3, relay, 0)
    for copy in loading[4:]:
        copy.wait()

    def half_of(n):
        return run_c[2 * n : 2 * n + 1, :], run_s[2 * n : 2 * n + 1, :]

    def full_of(n):
        return run_c[2 * n + 1 : 2 * n + 2, :], run_s[2 * n + 1 : 2 * n + 2, :]

    wait_region(0)

    @pl.when(is_end)
    def _():
        wait_region(1)

    tall = size_z + 16
    low_spot = iota((tall, LANES), 1)
    high_spot = iota((8, LANES), 1)
    held = []
    for c in range(8):
        value = jnp.zeros((tall, LANES), F32)
        border = jnp.zeros((8, LANES), F32)
        first = 0
        for dy, planes in enumerate((depth, size_y, depth)):
            start = quarter * (c % 4) + (8 * (size_y - depth) if dy == 0 else 0)
            last = first + 8 * planes
            chosen = jnp.logical_and(low_spot >= first, low_spot < last)
            value = jnp.where(chosen, turn(land_w[dy, c // 4], first - start, 1), value)
            for side in range(2):
                chosen = jnp.logical_and(jnp.logical_and(high_spot >= first, high_spot < last), high_spot % 8 // 4 == side)
                border = jnp.where(chosen, turn(land_x[dy, side], first - start - 4 * (c // 4) + 4 * side, 1), border)
            first = last
        held.append(jnp.concatenate([value, border], axis=0))
    ex, ey, ez, hx, hy, hz, r, k = held
    border_e, border_h = [], []
    sums = [jnp.zeros((size_z, LANES), F32) for _ in range(8)]
    for n in range(STEPS):
        border_e.append((ez[tall:], ey[tall:]))
        hx = hx - k * ((turn(ez, -8, 1) - ez) - (turn(ey, -1, 0) - ey))
        hy = hy - k * ((turn(ex, -1, 0) - ex) - (turn(ez, -1, 1) - ez))
        hz = hz - k * ((turn(ey, -1, 1) - ey) - (turn(ex, -8, 1) - ex))
        border_h.append((hz[tall:], hy[tall:]))
        ex = ex + r * ((hz - turn(hz, 8, 1)) - (hy - turn(hy, 1, 0)))
        ey = ey + r * ((hx - turn(hx, 1, 0)) - (hz - turn(hz, 1, 1)))
        ez = ez + r * ((hy - turn(hy, 1, 1)) - (hx - turn(hx, 8, 1)))
        for at, (value, (co, si)) in enumerate(((hz, half_of(n)), (hy, half_of(n)), (ez, full_of(n)), (ey, full_of(n)))):
            value = value[8 : 8 + size_z]
            sums[at] = sums[at] + value * co
            sums[4 + at] = sums[4 + at] - value * si

    cap_sum[...] = jnp.zeros(cap_sum.shape, F32)

    @pl.when(is_end)
    def _():
        wait_region(2)
        tile = pl.ds(zt, 8)
        eight = iota((8, LANES), 1)
        left, right = jnp.where(xy == 0, 1.0, 0.0), jnp.where(xy == 0, 0.0, 1.0)
        behind, ahead = jnp.where(dev > 0, COURANT, 0.0), jnp.where(dev < devs - 1, COURANT, 0.0)

        def rate_of(eps):
            there = eps > 0.0
            return jnp.where(there, COURANT / jnp.where(there, eps, 1.0), 0.0)

        e = [[cap_e[0, c, i] for i in range(3)] + [fields[c, y, tile, :] for y in range(size_y)] + [cap_e[1, c, i] for i in range(3)] for c in range(3)]
        h = [[cap_h[0, c, i] for i in range(3)] + [fields[3 + c, y, tile, :] for y in range(size_y)] + [cap_h[1, c, i] for i in range(2)] for c in range(3)]
        rates = [None] + [rate_of(cap_r[0, i]) for i in range(2)] + [permit[y, tile, :] for y in range(size_y)] + [rate_of(cap_r[1, i]) for i in range(2)]
        coefs = [behind] * depth + [COURANT] * size_y + [ahead] * depth

        def next_x(value, border, i):
            return jnp.where(eight == LANES - 1, turn(border, LANES - 1 - (8 * i + 4), 1), turn(value, -1, 1))

        def last_x(value, border, i):
            return jnp.where(eight == 0, turn(border, -(8 * i + 3), 1), turn(value, 1, 1))

        totals_of = [[jnp.zeros((8, LANES), F32) for _ in range(8)] for _ in range(size_y)]
        for n in range(STEPS):
            bz, by = (value * left for value in border_e[n])
            fx, fy, fz = [list(v) for v in h]
            for i in range(n, extent - 1 - n):
                xs, ys, zs = e[0][i], e[1][i], e[2][i]
                fx[i] = h[0][i] - coefs[i] * ((e[2][i + 1] - zs) - (turn(ys, -1, 0) - ys))
                fy[i] = h[1][i] - coefs[i] * ((turn(xs, -1, 0) - xs) - (next_x(zs, bz, i) - zs))
                fz[i] = h[2][i] - coefs[i] * ((next_x(ys, by, i) - ys) - (e[0][i + 1] - xs))
            h = [fx, fy, fz]
            bz, by = (value * right for value in border_h[n])
            gx, gy, gz_ = [list(v) for v in e]
            for i in range(n + 1, extent - 1 - n):
                xs, ys, zs = h[0][i], h[1][i], h[2][i]
                gx[i] = e[0][i] + rates[i] * ((zs - h[2][i - 1]) - (ys - turn(ys, 1, 0)))
                gy[i] = e[1][i] + rates[i] * ((xs - turn(xs, 1, 0)) - (zs - last_x(zs, bz, i)))
                gz_[i] = e[2][i] + rates[i] * ((ys - last_x(ys, by, i)) - (xs - h[0][i - 1]))
            e = [gx, gy, gz_]
            for y in range(size_y):
                i = depth + y
                for at, (value, (co, si)) in enumerate(((h[1][i], half_of(n)), (h[0][i], half_of(n)), (e[1][i], full_of(n)), (e[0][i], full_of(n)))):
                    totals_of[y][at] = totals_of[y][at] + value * co
                    totals_of[y][4 + at] = totals_of[y][4 + at] - value * si
        for y in range(size_y):
            for c in range(8):
                value = totals_of[y][c]
                cap_sum[pl.ds(8 * y + c, 1), :] = jnp.where(gz == 0, value[ZB : ZB + 1], value[7 - ZB : 8 - ZB])

    def advance(n, ghosts):
        fields_from, spec_from = (fields, spectra) if n == 0 else (fields_out, spectra_out)
        ex, ey, ez, hx, hy, hz = (fields_from[c] for c in range(6))
        rate = permit[...]
        hx = hx - COURANT * (inner(True, 0, ez) - inner(True, 1, ey))
        hy = hy - COURANT * (inner(True, 1, ex) - inner(True, 2, ez))
        hz = hz - COURANT * (inner(True, 2, ey) - inner(True, 0, ex))
        wait_halo(n)
        start, _ = first_of(n)
        xp = in_xd[n]
        hx = hx - COURANT * (at_y(in_yd[2 * n], True) - at_z(in_zd[2 * n], True))
        hy = hy - COURANT * (at_z(in_zd[2 * n + 1], True) - at_x(xp, 0, True))
        hz = hz - COURANT * (at_x(xp, 1, True) - at_y(in_yd[2 * n + 1], True))

        ax, ay, az = in_yu[start], in_yu[start + 1], in_yu[start + 2]
        bx, by, bz = in_zu[start], in_zu[start + 1], in_zu[start + 2]
        c_ex, own = in_xu[n], out_xd[n]
        if n == 0:
            y_hx, y_hz = in_yu[3], in_yu[4]
            z_hx, z_hy = in_zu[3], in_zu[4]
            x_hy, x_hz = turn(c_ex, -3 * size_y, 1), turn(c_ex, -4 * size_y, 1)
        else:
            y_hx, y_hz, z_hx, z_hy, x_hy, x_hz = ghosts
        ay_z = jnp.where(row2 == size_z - 1, in_zy[n], turn(ay, -1, 0))
        ay_x = jnp.where(lane == size_x - 1, turn(in_yx[n], -2 * size_y, 1), turn(ay, -1, 1))
        y_hx = y_hx - half_y * ((ez[0] - az) - (ay_z - ay))
        y_hz = y_hz - half_y * ((ay_x - ay) - (ex[0] - ax))
        bz_y = jnp.concatenate([bz[1:], in_yz[n, 7:8, :][None]], axis=0)
        corner = in_zx[n, 7:8, :]
        bz_x = jnp.stack([turn(corner, -1 - y, 1) for y in range(size_y)], axis=0)
        bz_x = jnp.where(lane_row == size_x - 1, bz_x, jnp.stack([turn(bz[y], -1, 1) for y in range(size_y)], axis=0))
        z_hx = z_hx - half_z * ((bz_y - bz) - (ey[:, 0:1, :] - by))
        z_hy = z_hy - half_z * ((ex[:, 0:1, :] - bx) - (bz_x - bz))
        c_z = jnp.where(row2 == size_z - 1, in_xz[n, 0:1, :], turn(c_ex, -1, 0))
        c_y = jnp.where(lane == size_y - 1, turn(in_xy[n], size_y - 1, 1), turn(c_ex, -1, 1))
        x_hy = x_hy - half_x * ((c_z - c_ex) - (own - turn(c_ex, -2 * size_y, 1)))
        x_hz = x_hz - half_x * ((turn(own, -size_y, 1) - turn(c_ex, -size_y, 1)) - (c_y - c_ex))

        ex = ex + rate * (inner(False, 0, hz) - inner(False, 1, hy))
        ey = ey + rate * (inner(False, 1, hx) - inner(False, 2, hz))
        ez = ez + rate * (inner(False, 2, hy) - inner(False, 0, hx))
        ex = ex - rate * (at_y(y_hz, False) - at_z(z_hy, False))
        ey = ey - rate * (at_z(z_hx, False) - at_x(x_hz, 0, False))
        ez = ez - rate * (at_x(x_hy, 0, False) - at_y(y_hx, False))
        if n < STEPS - 1:
            staging = stage(n + 1, ex, ey, ez, (), (), ())
            next(staging)
            start_halo(n + 1, (4, 5, 0, 1, 2, 3))
            next(staging)
            start_halo(n + 1, (8, 11, 9, 10, 6, 7))
        half_c, half_s = run_c[2 * n : 2 * n + 1, :], run_s[2 * n : 2 * n + 1, :]
        for c, value in enumerate((hx, hy, hz)):
            spectra_out[3 + c] = spec_from[3 + c] + value * half_c
            spectra_out[9 + c] = spec_from[9 + c] - value * half_s
        full_c, full_s = run_c[2 * n + 1 : 2 * n + 2, :], run_s[2 * n + 1 : 2 * n + 2, :]
        for c, value in enumerate((ex, ey, ez)):
            spectra_out[c] = spec_from[c] + value * full_c
            spectra_out[6 + c] = spec_from[6 + c] - value * full_s
        for c, value in enumerate((ex, ey, ez, hx, hy, hz)):
            fields_out[c] = value
        return y_hx, y_hz, z_hx, z_hy, x_hy, x_hz

    own_walls = walls.at[gz]
    sub = iota((8, LANES), 0)
    z_row = iota((size_z, LANES), 0)
    own_walls[...] = jnp.zeros((8, LANES), F32)
    for y in range(size_y):
        spread = jnp.zeros((size_z, LANES), F32)
        for c in range(8):
            k = c % 4
            from_c = X_PICKS[k] + (6 if c >= 4 else 0)
            column = jnp.where(lane == x_wall, spectra[from_c, y], 0.0) + jnp.where(lane == 8 * (depth + y) + 4, sums[c], 0.0)
            column = jnp.sum(column, axis=1, keepdims=True)
            spread = jnp.where(lane == c * PATCH + z_row, column * (CURRENT_SIGNS[k] * facing_x), spread)
        record = jnp.sum(spread, axis=0, keepdims=True)
        own_walls[pl.ds(y, 1), :] = record
        for c in range(8):
            k = c % 4
            from_c = Z_PICKS[k] + (6 if c >= 4 else 0)
            low = spectra[from_c, y, pl.ds(ZB, 1), :]
            high = spectra[from_c, y, pl.ds(size_z - 1 - ZB, 1), :]
            picked = (jnp.where(gz == 0, low, high) + cap_sum[pl.ds(8 * y + c, 1), :]) * (CURRENT_SIGNS[k] * facing_z * end_weight)
            cap_plane[pl.ds(8 * y + c, 1), :] = picked
        fanned = stagger(jnp.broadcast_to(record, (8, LANES)), -PATCH)
        wall_hi, wall_lo = split(fanned[:, :size_z] * norm)
        cap_hi, cap_lo = split(cap_plane[pl.ds(8 * y, 8), :] * norm)
        for at, (cap_part, wall_part) in enumerate(((cap_hi, wall_hi), (cap_lo, wall_lo))):
            first = at * all_rows + 8 * y
            lhs[pl.ds(first, 8), pl.ds(0, size_x)] = cap_part
            lhs[pl.ds(first + half_rows, 8), pl.ds(size_x, size_z)] = wall_part

    lanes8 = iota((1, LANES), 1)
    owner_row = jnp.zeros((1, LANES), F32)
    for p in range(size_y):
        owner_row = jnp.where(lanes8 == 8 * gz + p, (wall_owner[0, p] + 1).astype(F32), owner_row)
    own_walls[pl.ds(size_y, 1), :] = owner_row

    def wall_copy(k, ref=None):
        held = walls.at[gz] if ref is None else ref
        return pltpu.make_async_remote_copy(
            src_ref=held,
            dst_ref=held,
            send_sem=wall_send,
            recv_sem=wall_got,
            device_id={"gz": (gz + k) % slabs},
            device_id_type=MESH,
        )

    def cap_copy(k, at):
        return pltpu.make_async_remote_copy(
            src_ref=caps.at[at],
            dst_ref=caps.at[at],
            send_sem=cap_send,
            recv_sem=cap_got.at[at],
            device_id={"gz": (gz + k) % slabs},
            device_id_type=MESH,
        )

    sign = jnp.where(sub < 4, -1.0, 1.0)

    def far_of(j):
        rows = lhs[...]
        by_high = jnp.dot(rows, table_hi[j], preferred_element_type=F32)
        by_low = jnp.dot(rows[:all_rows], table_lo[j], preferred_element_type=F32)
        product = by_high[:all_rows] + by_high[all_rows:] + by_low
        theta = jnp.zeros((8, LANES), F32)
        phi = jnp.zeros((8, LANES), F32)
        for face in range(2):
            sum_c = jnp.zeros((8, LANES), F32)
            sum_s = jnp.zeros((8, LANES), F32)
            for y in range(size_y):
                g = face * size_y + y
                tile = product[8 * g : 8 * g + 8]
                tile = tile[:, :LANES] + sign * pltpu.roll(tile[:, LANES:], 4, 0)
                sum_c = sum_c + tile * phases[j, 0, pl.ds(g, 1), :]
                sum_s = sum_s + tile * phases[j, 1, pl.ds(g, 1), :]
            far = sum_c + sign * pltpu.roll(sum_s, 4, 0)
            theta = theta + weights[j, 2 * face] * far
            phi = phi + weights[j, 2 * face + 1] * far

        def four(values):
            pairs = values + pltpu.roll(values, 7, 0)
            return pairs + pltpu.roll(pairs, 6, 0)

        both = jnp.where(sub % 4 == 1, pltpu.roll(four(phi), 1, 0), four(theta))
        parts_out[j] = jnp.where(sub < 2, both, pltpu.roll(both, 6, 0))[:4]

    bunch = per * max(1, 4 // per)
    together = bunch // per
    upper = jnp.where(gz >= slabs // 2, 1, 0)
    near = (upper * across + dev * xys + xy) % owners

    def partner(number):
        other, bit = 0, 1
        while bit < owners:
            other = other + bit * ((near // bit + number // bit) % 2)
            bit *= 2
        return other

    def flat_of(owner):
        return (slabs // 2 - 1) * across + owner

    def part_copy(owner, source):
        return pltpu.make_async_remote_copy(
            src_ref=parts_out.at[pl.ds(owner * per, per)],
            dst_ref=parts_in.at[source],
            send_sem=part_send,
            recv_sem=part_got,
            device_id=ident(flat_of(owner)),
            device_id_type=MESH,
        )

    mine = me - flat_of(0)
    leads = jnp.logical_and(mine >= 0, mine < owners)

    def far_and_send(number, carry):
        several = [partner(owners - 1 - together * number - m) for m in range(together)]
        for owner in several:
            for m in range(per):
                far_of(owner * per + m)
        for owner in several:
            @pl.when(owner != mine)
            def _():
                part_copy(owner, me).start()

        return carry

    hear()
    lax.fori_loop(0, owners // together, far_and_send, 0)

    for k in range(1, slabs):
        wall_copy(k).start()
    for at, holder in enumerate((0, slabs - 1)):
        @pl.when(gz == holder)
        def _():
            for y in range(size_y):
                caps[at, pl.ds(8 * y, 8), :] = block_transpose(cap_plane[pl.ds(8 * y, 8), :])
            for k in range(1, slabs):
                cap_copy(k, at).start()

    def total_copy(k, owner, ref=None):
        held = totals.at[pl.ds(owner * per, per)] if ref is None else ref
        return pltpu.make_async_remote_copy(
            src_ref=held,
            dst_ref=held,
            send_sem=total_send,
            recv_sem=total_got.at[owner // together],
            device_id=ident((me + k) % peers),
            device_id_type=MESH,
        )

    ghosts = advance(0, None)

    @pl.when(leads)
    def _():
        everyone = parts_in.at[pl.ds(0, peers - 1)]
        pltpu.make_async_remote_copy(
            src_ref=everyone, dst_ref=everyone, send_sem=part_send, recv_sem=part_got, device_id={"gz": gz}, device_id_type=MESH
        ).wait_recv()
        parts_in[me] = parts_out[pl.ds(mine * per, per)]
        totals[pl.ds(mine * per, per)] = jnp.sum(parts_in[...], axis=0)
        for k in sorted(range(slabs), key=lambda k: -min(k, slabs - k)):
            row = (gz + k) % slabs * across

            def send(r, carry):
                to = row + (dev * xys + xy + r) % across

                @pl.when(to != me)
                def _():
                    total_copy((to - me + peers) % peers, mine).start()

                return carry

            lax.fori_loop(0, across, send, 0, unroll=across <= 4)


    def choose(mine, share, records):
        length = mine.shape[1]
        before = jnp.where(iota((length, length), 0) < iota((length, length), 1), 1.0, 0.0).astype(BF16)
        ones = jnp.broadcast_to(jnp.where(mine, 1.0, 0.0), (8, length))
        rank = jnp.dot(ones.astype(BF16), before, preferred_element_type=F32)
        wanted = iota((8, length), 0).astype(F32)
        chooser = jnp.where(rank == wanted, ones, 0.0)
        return jnp.dot(chooser, records, precision=HIGHEST, preferred_element_type=F32)[:share]

    def choose_owned():
        wall_copy(1, walls.at[pl.ds(0, slabs - 1)]).wait_recv()
        for at, holder in enumerate((0, slabs - 1)):
            @pl.when(gz != holder)
            def _():
                cap_copy(1, at).wait_recv()
        all_walls = walls[...]
        owner_all = jnp.sum(all_walls[:, size_y : size_y + 1, :], axis=0)[:, : 8 * slabs]
        cap_share = (owned_out.shape[0] - size_y) // 2
        owned_out[pl.ds(0, size_y), 0, :] = choose(
            owner_all == (gz + 1).astype(F32), size_y, all_walls.reshape(8 * slabs, LANES)
        )
        for at in range(2):
            owned_out[pl.ds(size_y + at * cap_share, cap_share), 0, :] = choose(
                cap_owner[pl.ds(at, 1), :] == gz, cap_share, caps[at]
            )

    def intensity_of(field):
        return jnp.sum(field * field, axis=0, keepdims=True)

    def slope_of(j):
        field = totals[j]
        residual = aim[pl.ds(j, 1), :].astype(F32) * (intensity_of(field) - target[pl.ds(j, 1), :])
        return 2.0 * residual * field

    def adjoint_of(j):
        slope = slope_of(j)
        by_theta = jnp.where(sub < 4, slope[0:1], slope[2:3])
        by_phi = jnp.where(sub < 4, slope[1:2], slope[3:4])
        tiles = []
        for face in range(2):
            vector = weights[j, 2 * face] * by_theta + weights[j, 2 * face + 1] * by_phi
            turned = -sign * pltpu.roll(vector, 4, 0)
            for y in range(size_y):
                g = face * size_y + y
                tile = vector * phases[j, 0, pl.ds(g, 1), :] + turned * phases[j, 1, pl.ds(g, 1), :]
                tiles.append(jnp.concatenate([tile, -sign * pltpu.roll(tile, 4, 0)], axis=1))
        rows = jnp.concatenate(tiles, axis=0)
        high, low = split(rows)
        both = jnp.concatenate([high, low], axis=0)
        across = (((1,), (1,)), ((), ()))
        by_high = lax.dot_general(both, table_hi[j], across, preferred_element_type=F32)
        by_low = lax.dot_general(high, table_lo[j], across, preferred_element_type=F32)
        return by_high[:all_rows] + by_high[all_rows:] + by_low

    def adjoint_wait(number):
        several = [partner(together * number + m) for m in range(together)]
        batch = several[0] // together
        ours = jnp.logical_and(leads, mine // together == batch)

        @pl.when(jnp.logical_not(ours))
        def _():
            total_copy(1, several[0], totals.at[pl.ds(batch * bunch, bunch)]).wait_recv()

        if together > 1:
            @pl.when(ours)
            def _():
                total_copy(1, several[0], totals.at[pl.ds(batch * bunch, bunch - per)]).wait_recv()

        return several

    def adjoint_some(numbers, total):
        several = [owner for number in numbers for owner in adjoint_wait(number)]
        for owner in several:
            for m in range(per):
                total = total + adjoint_of(owner * per + m)
        return total

    rounds = owners // together
    ghosts = advance(1, ghosts)
    choose_owned()
    gradient = adjoint_some((0,), jnp.zeros((all_rows, size_x + size_z), F32))
    gradient = adjoint_some(range(1, rounds), gradient)
    intensity_out[...] = intensity_of(totals[me // ratio])
    advance(2, ghosts)
    for y in range(size_y):
        wall = gradient[half_rows + 8 * y : half_rows + 8 * y + 8, size_x:]
        wall = jnp.concatenate([wall, jnp.zeros((8, LANES - size_z), F32)], axis=1)
        wall = stagger(wall, PATCH)
        adjoint_out[pl.ds(y, 1), 0, :] = jnp.sum(wall, axis=0, keepdims=True) * norm
        cap = block_transpose(gradient[8 * y : 8 * y + 8, :size_x] * (norm * end_weight))
        adjoint_out[pl.ds(size_y + 8 * y, 8), 0, :] = cap

    groups_sent = {}
    for number, (landing, move) in enumerate(messages):
        groups_sent[number] = [within(move, 1), math.prod(landing.shape) // LANES]
    for number, (_, _, source, _, _, _) in enumerate(regions):
        entry = groups_sent.setdefault(group_of(number), [region_when(number, 1), 0])
        entry[1] += math.prod(source.shape) // LANES
    for group, (sent, rows_sent) in groups_sent.items():
        @pl.when(sent)
        def _():
            everything = arrivals.at[pl.ds(0, rows_sent)]
            pltpu.make_async_copy(everything, everything, halo_send.at[group]).wait()

    def parts_sent(ref):
        pltpu.make_async_remote_copy(
            src_ref=ref, dst_ref=ref, send_sem=part_send, recv_sem=part_got, device_id={"gz": gz}, device_id_type=MESH
        ).wait_send()

    @pl.when(leads)
    def _():
        parts_sent(parts_out.at[pl.ds(0, (owners - 1) * per)])
        total_copy(1, 0, parts_in.at[pl.ds(0, peers - 1)]).wait_send()

    @pl.when(jnp.logical_not(leads))
    def _():
        parts_sent(parts_out)

    wall_copy(1, walls.at[pl.ds(0, slabs - 1)]).wait_send()
    for at, holder in enumerate((0, slabs - 1)):
        @pl.when(gz == holder)
        def _():
            sent = weights.at[pl.ds(0, slabs - 1)]
            pltpu.make_async_copy(sent, sent, cap_send).wait()


def write_out(*refs):
    copies = [pltpu.make_async_copy(refs[i], refs[5 + i], refs[10].at[i]) for i in range(5)]
    for copy in copies:
        copy.start()
    for copy in copies:
        copy.wait()


def local(fields, spectra, permittivity, phase_start, wall_owner, cap_owner, dir_index, target, aim_mask):
    slabs, devs, xys = (lax.axis_size(a) for a in ("gz", "dev", "xy"))
    peers = slabs * devs * xys
    size_y, size_z, size_x = permittivity.shape
    assert size_z == PATCH and size_x == LANES and size_y == 4 and xys == 2
    directions = dir_index.shape[0]
    chunks = directions // LANES
    ratio = peers // chunks
    per = max(1, chunks // (2 * devs * xys))
    owners = chunks // per
    share = directions // peers
    cap_count = size_y * size_x // PATCH
    owned = size_y + 2 * (cap_count // slabs)
    rows = 16 * size_y
    depth = size_x + size_z
    planes, pairs = 5 + 3 * (STEPS - 1), 2 * STEPS
    halos = (
        (planes, size_z, LANES), (pairs, size_z, LANES), (planes, size_y, 1, LANES), (pairs, size_y, 1, LANES),
        (STEPS, size_z, LANES), (STEPS, size_z, LANES),
        (STEPS, 1, LANES), (STEPS, 8, LANES), (STEPS, size_z, LANES), (STEPS, 8, LANES), (STEPS, 8, LANES), (STEPS, size_z, LANES),
    )
    vmem = pl.BlockSpec(memory_space=pltpu.VMEM)
    anywhere = pl.BlockSpec(memory_space=pl.ANY)
    dma = pltpu.SemaphoreType.DMA
    outs = pl.pallas_call(
        functools.partial(kernel, (slabs, devs, xys)),
        out_shape=(
            pltpu.VMEM(fields.shape, F32),
            pltpu.VMEM(spectra.shape, F32),
            pltpu.VMEM((owned, 1, LANES), F32),
            pltpu.VMEM((1, LANES), F32),
            pltpu.VMEM((size_y + cap_count, 1, LANES), F32),
        ),
        in_specs=[anywhere] * 9,
        out_specs=(vmem,) * 5,
        scratch_shapes=[
            *(pltpu.VMEM(shape, F32) for shape in halos[:6]),
            *(pltpu.VMEM(shape, F32) for shape in halos),
            pltpu.VMEM((5, size_z, LANES), F32),
            pltpu.VMEM((5, size_y, 1, LANES), F32),
            pltpu.VMEM((376, 1, LANES), F32),
            pltpu.VMEM((2, size_z, LANES), F32),
            pltpu.VMEM((8, LANES), F32),
            pltpu.VMEM((3, 2, size_z + 16, LANES), F32),
            pltpu.VMEM((3, 2, 8, LANES), F32),
            pltpu.VMEM((2, 3, 3, 8, LANES), F32),
            pltpu.VMEM((2, 3, 3, 8, LANES), F32),
            pltpu.VMEM((2, 2, 8, LANES), F32),
            pltpu.VMEM((3, 3, 8, LANES), F32),
            pltpu.VMEM((8 * size_y, LANES), F32),
            pltpu.VMEM(fields.shape, F32),
            pltpu.VMEM(spectra.shape, F32),
            pltpu.VMEM(permittivity.shape, F32),
            pltpu.SMEM((1,), F32),
            pltpu.SMEM(wall_owner.shape, jnp.int32),
            pltpu.VMEM(cap_owner.shape, jnp.int32),
            pltpu.VMEM((chunks, LANES), jnp.int32),
            pltpu.VMEM((chunks, LANES), F32),
            pltpu.VMEM((chunks, LANES), jnp.int32),
            pltpu.VMEM((8, chunks, LANES), F32),
            pltpu.VMEM((chunks, 4, 8, LANES), F32),
            pltpu.VMEM((chunks, 2, 2 * size_y, LANES), F32),
            pltpu.VMEM((chunks, depth, 2 * LANES), BF16),
            pltpu.VMEM((chunks, depth, 2 * LANES), BF16),
            pltpu.VMEM((8 * size_y, LANES), F32),
            pltpu.VMEM((2 * rows, depth), BF16),
            pltpu.VMEM((chunks, 4, LANES), F32),
            pltpu.VMEM((peers, per, 4, LANES), F32),
            pltpu.VMEM((chunks, 4, LANES), F32),
            pltpu.VMEM((slabs, 8, LANES), F32),
            pltpu.VMEM((2, cap_count, LANES), F32),
            dma((len(halos) + 5,)), dma((STEPS,)),
            dma, dma,
            dma, dma((owners // max(1, 4 // per),)),
            dma, dma,
            dma, dma((2,)),
            dma((9,)), pltpu.SemaphoreType.REGULAR((2,)), dma((3,)),
        ],
        compiler_params=pltpu.CompilerParams(collective_id=0, has_side_effects=True),
    )(
        fields, spectra, permittivity, phase_start, wall_owner, cap_owner,
        dir_index.reshape(chunks, LANES), target.reshape(chunks, LANES), aim_mask.reshape(chunks, LANES),
    )
    held = (fields.shape, spectra.shape, (owned, 1, LANES), (1, LANES), (size_y + cap_count, 1, LANES))
    fields_new, spectra_new, owned_rows, intensity, adjoint = pl.pallas_call(
        write_out,
        out_shape=tuple(jax.ShapeDtypeStruct(shape, F32) for shape in held),
        in_specs=[pl.BlockSpec(memory_space=pltpu.VMEM)] * 5,
        out_specs=(pl.BlockSpec(memory_space=pl.ANY),) * 5,
        scratch_shapes=[dma((5,))],
    )(*(pltpu.with_memory_space_constraint(out, pltpu.VMEM) for out in outs))
    owned_rows = owned_rows.reshape(1, 1, owned, 1, LANES).transpose(0, 1, 3, 2, 4)
    adjoint = adjoint.reshape(1, 1, size_y + cap_count, 1, LANES).transpose(0, 1, 3, 2, 4)
    intensity = intensity.reshape(LANES)
    if ratio > 1:
        me = (lax.axis_index("gz") * devs + lax.axis_index("dev")) * xys + lax.axis_index("xy")
        intensity = lax.dynamic_slice_in_dim(intensity, (me % ratio) * share, share, 0)
    return (fields_new, spectra_new, owned_rows, intensity, adjoint)


def solution(mesh):
    placed = (
        P("groups", "dev", "gz", "xy"),
        P("groups", "dev", "gz", "xy"),
        P(("groups", "dev"), "gz", "xy"),
        P("groups"),
        P("gz", None),
        P(),
        P(),
        P("groups"),
        P("groups"),
    )
    return jax.shard_map(
        local,
        mesh=mesh,
        in_specs=placed,
        out_specs=(
            P("groups", "dev", "gz", "xy"),
            P("groups", "dev", "gz", "xy"),
            P(("groups", "gz"), "dev", "xy", None, None),
            P(("groups", "gz", "dev", "xy")),
            P(("groups", "gz"), "dev", "xy", None, None),
        ),
        check_vma=False,
    )
```

```python
import functools
import math

import jax
import jax.numpy as jnp
from jax import lax
from jax.experimental import pallas as pl
from jax.experimental.pallas import tpu as pltpu
from jax.sharding import PartitionSpec as P

PATCH = 16
XB = 8
ZB = 4
STEPS = 3
THETAS = 64
COURANT = 0.5
ANGULAR_STEP = 0.3
WAVE_NUMBER = 0.6
LANES = 128
HIGHEST = lax.Precision.HIGHEST
CURRENT_SIGNS = (-1.0, 1.0, 1.0, -1.0)
X_PICKS = (5, 4, 2, 1)
Z_PICKS = (4, 3, 1, 0)
MESH = pl.DeviceIdType.MESH
AXES = ("dev", "gz", "xy")
F32 = jnp.float32
BF16 = jnp.bfloat16


def iota(shape, dim):
    return lax.broadcasted_iota(jnp.int32, shape, dim)


def sincos(turns):
    half = (turns - jnp.floor(turns + 0.5)) * math.pi
    sq = half * half
    sin_h = half * (1.0 + sq * (-1.0 / 6 + sq * (1.0 / 120 + sq * (-1.0 / 5040 + sq * (1.0 / 362880 - sq * (1.0 / 39916800))))))
    cos_h = 1.0 + sq * (-0.5 + sq * (1.0 / 24 + sq * (-1.0 / 720 + sq * (1.0 / 40320 + sq * (-1.0 / 3628800 + sq * (1.0 / 479001600))))))
    return 2.0 * sin_h * cos_h, 1.0 - 2.0 * sin_h * sin_h


def split(values):
    high = values.astype(BF16)
    return high, (values - high.astype(F32)).astype(BF16)


def arrival_rows(n, size_y, size_z):
    length = 5 if n == 0 else 3
    return (length + 2) * (size_z + size_y) + 1 + 3 * 8 + 4 * size_z


def stagger(tile, by):
    row = iota(tile.shape, 0)
    for bit in (1, 2, 4):
        tile = jnp.where(row // bit % 2 == 1, pltpu.roll(tile, by * bit % LANES, 1), tile)
    return tile


def block_transpose(tile):
    on_diagonal = (iota(tile.shape, 1) // PATCH) == iota(tile.shape, 0)
    total = jnp.where(on_diagonal, tile, 0.0)
    for k in range(1, 8):
        turned = pltpu.roll(tile, PATCH * k, 1)
        total = total + pltpu.roll(jnp.where(on_diagonal, turned, 0.0), 8 - k, 0)
    return total


def kernel(
    sizes,
    fields_in, spectra_in, permit_in, phase_in, wall_owner_in, cap_owner_in, dirs_in, target_in, aim_in,
    fields_out, spectra_out, owned_out, intensity_out, adjoint_out,
    out_yu, out_yd, out_zu, out_zd, out_xu, out_xd,
    in_yu, in_yd, in_zu, in_zd, in_xu, in_xd, in_zy, in_yz, in_yx, in_zx, in_xz, in_xy, blank, blank_rows, arrivals,
    out_w, out_x, land_w, land_x, cap_e, cap_h, cap_r, empty, cap_sum,
    fields, spectra, permit, phase, wall_owner, cap_owner, dirs, target, aim,
    geo, weights, phases, table_hi, table_lo, cap_plane, lhs,
    parts_out, parts_in, totals, walls, caps,
    halo_send, halo_got, part_send, part_got, total_send, total_got, wall_send, wall_got, cap_send, cap_got, loads, chain, region_got,
):
    slabs, devs, xys = sizes
    peers = slabs * devs * xys
    size_y, size_z, size_x = permit.shape
    chunks = dirs.shape[0]
    ratio = peers // chunks
    across = devs * xys
    per = max(1, chunks // (2 * across))
    owners = chunks // per
    groups = 2 * size_y
    half_rows = 8 * size_y
    all_rows = 2 * half_rows
    gz, dev, xy = lax.axis_index("gz"), lax.axis_index("dev"), lax.axis_index("xy")
    me = (gz * devs + dev) * xys + xy
    place = {"dev": dev, "gz": gz, "xy": xy}
    count = {"dev": devs, "gz": slabs, "xy": xys}

    def ident(flat):
        return {"gz": flat // (devs * xys), "dev": (flat // xys) % devs, "xy": flat % xys}

    pltpu.make_async_copy(fields_in, fields, loads.at[0]).start()
    barrier = pltpu.get_barrier_semaphore()

    for away in (1, -1, 0):
        @pl.when(jnp.logical_and(gz + away >= 0, gz + away < slabs))
        def _():
            def greet(k, carry):
                spot = (dev * xys + xy + k) % across
                to = {"gz": gz + away, "dev": spot // xys, "xy": spot % xys}
                pl.semaphore_signal(barrier, inc=1, device_id=to, device_id_type=MESH)
                return carry

            lax.fori_loop(0 if away else 1, across, greet, 0)

    beside = jnp.where(gz > 0, across, 0) + jnp.where(gz < slabs - 1, across, 0) + across - 1

    def pass_on():
        for at, away in enumerate((1, -1)):
            @pl.when(jnp.logical_and(gz + away >= 0, gz + away < slabs))
            def _():
                to = {"gz": gz + away, "dev": dev, "xy": xy}
                pl.semaphore_signal(chain.at[at], inc=1, device_id=to, device_id_type=MESH)

    def hear():
        for at, away in enumerate((1, -1)):
            @pl.when(jnp.logical_and(gz - away >= 0, gz - away < slabs))
            def _():
                pl.semaphore_wait(chain.at[at], 1)

    loading = [
        pltpu.make_async_copy(source, held, loads.at[number])
        for number, (source, held) in enumerate((
            (fields_in, fields), (dirs_in, dirs), (phase_in, phase), (permit_in, permit), (spectra_in, spectra),
            (wall_owner_in, wall_owner), (cap_owner_in, cap_owner), (target_in, target), (aim_in, aim),
        ))
    ]
    for copy in loading[1:]:
        copy.start()

    def geometry():
        index = dirs[...]
        sin_t, cos_t = sincos(((index // THETAS).astype(F32) + 0.5) * (0.5 / THETAS))
        sin_f, cos_f = sincos((index % THETAS).astype(F32) * (1.0 / THETAS))
        wave = WAVE_NUMBER / (2.0 * math.pi)
        for slot, values in enumerate((
            wave * sin_t * cos_f, wave * sin_t * sin_f, wave * cos_t,
            cos_t * cos_f, cos_t * sin_f, -sin_t, -sin_f, cos_f,
        )):
            geo[slot] = values

    grid_x, grid_y, grid_z = size_x * xys, size_y * devs, size_z * slabs
    x_first = (xy * size_x).astype(F32) - (grid_x - 1) / 2.0
    y_first = (dev * size_y).astype(F32) - (grid_y - 1) / 2.0
    z_first = (gz * size_z).astype(F32) - (grid_z - 1) / 2.0
    x_wall = jnp.where(xy == 0, XB, size_x - 1 - XB)
    z_cap = jnp.where(gz == 0, ZB, size_z - 1 - ZB)
    x_face = x_first + x_wall.astype(F32)
    z_face = z_first + z_cap.astype(F32)
    facing_x = jnp.where(xy == 0, -1.0, 1.0)
    facing_z = jnp.where(gz == 0, -1.0, 1.0)
    is_end = jnp.logical_or(gz == 0, gz == slabs - 1)
    end_weight = jnp.where(is_end, 1.0, 0.0)
    norm = 1.0 / math.sqrt(2.0 * (2 * grid_y * grid_z + 2 * grid_y * grid_x))

    def make_tables(j, carry):
        def row(slot):
            return geo[slot, pl.ds(j, 1), :]

        ux, uy, uz = row(0), row(1), row(2)
        blocks = size_x // 8
        far_s, far_c = sincos((iota((blocks, LANES), 0).astype(F32) * 8.0 + x_first) * ux)
        near_s, near_c = sincos(iota((8, LANES), 0).astype(F32) * ux)
        far_s, far_c = far_s[:, None, :], far_c[:, None, :]
        near_s, near_c = near_s[None], near_c[None]
        cos_x = (far_c * near_c - far_s * near_s).reshape(size_x, LANES)
        sin_x = (far_s * near_c + far_c * near_s).reshape(size_x, LANES)
        sin_z, cos_z = sincos((iota((size_z, LANES), 0).astype(F32) + z_first) * uz)
        for at, (x_part, z_part) in enumerate(((cos_x, cos_z), (sin_x, sin_z))):
            lanes = pl.ds(at * LANES, LANES)
            x_high, x_low = split(x_part)
            z_high, z_low = split(z_part)
            table_hi[j, pl.ds(0, size_x), lanes] = x_high
            table_lo[j, pl.ds(0, size_x), lanes] = x_low
            table_hi[j, pl.ds(size_x, size_z), lanes] = z_high
            table_lo[j, pl.ds(size_x, size_z), lanes] = z_low
        which = iota((groups, LANES), 0)
        cell_y = (which % size_y).astype(F32) + y_first
        sin_g, cos_g = sincos(cell_y * uy + jnp.where(which < size_y, z_face * uz, x_face * ux))
        phases[j, 0] = cos_g
        phases[j, 1] = sin_g
        kind = iota((8, LANES), 0) % 4

        def pattern(a, b, c, d):
            return jnp.where(kind == 0, a, jnp.where(kind == 1, b, jnp.where(kind == 2, c, d)))

        tx, ty, tz, fx, fy = row(3), row(4), row(5), row(6), row(7)
        weights[j, 0] = pattern(-tx, -ty, -fx, -fy)
        weights[j, 1] = pattern(-fx, -fy, tx, ty)
        weights[j, 2] = pattern(-ty, -tz, -fy, jnp.zeros_like(fy))
        weights[j, 3] = pattern(-fy, jnp.zeros_like(fy), ty, tz)
        return carry

    windows = STEPS

    def tables_of(window):
        lax.fori_loop(window * chunks // windows, (window + 1) * chunks // windows, make_tables, 0)

    lane = iota((size_z, LANES), 1)
    lane3 = iota((size_y, size_z, LANES), 2)
    row3 = iota((size_y, size_z, LANES), 1)

    messages = (
        (in_yu, {"dev": 1}), (in_yd, {"dev": -1}), (in_zu, {"gz": 1}), (in_zd, {"gz": -1}),
        (in_zy, {"gz": -1, "dev": 1}), (in_yz, {"dev": -1, "gz": 1}),
        (in_xu, {"xy": 1}), (in_xd, {"xy": -1}),
        (in_yx, {"dev": 1, "xy": -1}), (in_zx, {"gz": 1, "xy": -1}), (in_xz, {"xy": 1, "gz": -1}), (in_xy, {"xy": 1, "dev": -1}),
    )

    def within(move, sign):
        inside = True
        for axis, step in move.items():
            spot = place[axis] + sign * step
            inside = jnp.logical_and(inside, jnp.logical_and(spot >= 0, spot < count[axis]))
        return inside

    def first_of(n):
        return (0, 5) if n == 0 else (5 + 3 * (n - 1), 3)

    def views(n):
        start, length = first_of(n)
        planes, pair = pl.ds(start, length), pl.ds(2 * n, 2)
        low, high = pl.ds(0, 8), pl.ds(size_z - 8, 8)
        return (
            (out_yu.at[planes], in_yu.at[planes]), (out_yd.at[pair], in_yd.at[pair]),
            (out_zu.at[planes], in_zu.at[planes]), (out_zd.at[pair], in_zd.at[pair]),
            (out_zd.at[2 * n, size_y - 1], in_zy.at[n]), (out_yd.at[2 * n, high], in_yz.at[n]),
            (out_xu.at[n], in_xu.at[n]), (out_xd.at[n], in_xd.at[n]),
            (out_xd.at[n], in_yx.at[n]), (out_xd.at[n, high], in_zx.at[n]),
            (out_xu.at[n, low], in_xz.at[n]), (out_xu.at[n], in_xy.at[n]),
        )

    def halo_copy(n, number, source, landing):
        to = {axis: (place[axis] + step + count[axis]) % count[axis] for axis, step in messages[number][1].items()}
        return pltpu.make_async_remote_copy(
            src_ref=source,
            dst_ref=landing,
            send_sem=halo_send.at[number],
            recv_sem=halo_got.at[n],
            device_id=to,
            device_id_type=MESH,
        )

    def start_halo(n, numbers):
        for number in numbers:
            @pl.when(within(messages[number][1], 1))
            def _():
                halo_copy(n, number, *views(n)[number]).start()

    def fill_halo(n):
        length = first_of(n)[1]
        planes, pair, rows, row_pair = blank.at[pl.ds(0, length)], blank.at[pl.ds(0, 2)], blank_rows.at[pl.ds(0, length)], blank_rows.at[pl.ds(0, 2)]
        plane, tile = blank.at[0], blank.at[0, pl.ds(0, 8)]
        sources = (planes, pair, rows, row_pair, blank_rows.at[0, 0], tile, plane, plane, plane, tile, tile, plane)
        for number, source in enumerate(sources):
            @pl.when(jnp.logical_not(within(messages[number][1], -1)))
            def _():
                pltpu.make_async_copy(source, views(n)[number][1], halo_got.at[n]).start()

    def wait_halo(n):
        everything = arrivals.at[pl.ds(0, arrival_rows(n, size_y, size_z))]
        pltpu.make_async_copy(everything, everything, halo_got.at[n]).wait()

    def pack(values, high):
        packed = jnp.zeros((size_z, LANES), F32)
        for k, value in enumerate(values):
            for y in range(size_y):
                spot = k * size_y + y
                amount = (spot + 1) % LANES if high else spot
                turned = pltpu.roll(value[y], amount, 1) if amount else value[y]
                packed = jnp.where(lane == spot, turned, packed)
        return packed

    def stage(n, ex, ey, ez, for_y, for_z, for_x):
        start, _ = first_of(n)
        for k, value in enumerate((ex, ey, ez) + for_y):
            out_yu[start + k] = value[size_y - 1]
        for k, value in enumerate((ez, ex)):
            out_yd[2 * n + k] = value[0]
        for k, value in enumerate((ex, ey, ez) + for_z):
            out_zu[start + k] = value[:, size_z - 1 : size_z, :]
        for k, value in enumerate((ey, ex)):
            out_zd[2 * n + k] = value[:, 0:1, :]
        yield
        out_xu[n] = pack((ex, ey, ez) + for_x, True)
        out_xd[n] = pack((ez, ey), False)
        yield

    blank[...] = jnp.zeros(blank.shape, F32)
    blank_rows[...] = jnp.zeros(blank_rows.shape, F32)

    def inner(ahead, axis, value):
        if axis == 0:
            none = jnp.zeros_like(value[:1])
            if ahead:
                return jnp.concatenate([value[1:], none], axis=0) - value
            return value - jnp.concatenate([none, value[:-1]], axis=0)
        length = value.shape[axis]
        spots = row3 if axis == 1 else lane3
        if ahead:
            return jnp.where(spots == length - 1, 0.0, pltpu.roll(value, length - 1, axis)) - value
        return value - jnp.where(spots == 0, 0.0, pltpu.roll(value, 1, axis))

    none = jnp.zeros((size_y - 1, size_z, LANES), F32)

    def at_y(plane, ahead):
        return jnp.concatenate([none, plane[None]] if ahead else [plane[None], none], axis=0)

    def at_z(rows, ahead):
        return jnp.where(row3 == (size_z - 1 if ahead else 0), rows, 0.0)

    def at_x(packed, k, ahead):
        edges = []
        for y in range(size_y):
            spot = k * size_y + y
            amount = (LANES - 1 - spot) if ahead else (LANES - spot) % LANES
            edges.append(pltpu.roll(packed, amount, 1) if amount else packed)
        return jnp.where(lane3 == (size_x - 1 if ahead else 0), jnp.stack(edges, axis=0), 0.0)

    def turn(value, by, axis):
        return pltpu.roll(value, by % value.shape[axis], axis)

    row2 = iota((size_z, LANES), 0)
    lane_row = iota((size_y, 1, LANES), 2)
    half_y = jnp.where(dev > 0, COURANT, 0.0)
    half_z = jnp.where(gz > 0, COURANT, 0.0)
    half_x = jnp.where(xy > 0, COURANT, 0.0)

    zt = pl.multiple_of(jnp.where(gz == 0, 0, size_z - 8), 8)
    depth = STEPS
    extent = size_y + 2 * depth
    quarter = 8 * size_y
    low_tile, high_tile = pl.ds(0, 8), pl.ds(size_z - 8, 8)

    regions = []
    for a in (1, -1, 0):
        for b in (1, -1, 0):
            if a or b:
                source = out_w if b == 0 else out_w.at[:, high_tile if b > 0 else low_tile]
                rows = pl.ds(8, size_z) if b == 0 else pl.ds(0 if b > 0 else size_z + 8, 8)
                landing = land_w.at[1 - a, :, rows]
                nothing = blank.at[pl.ds(0, 2)] if b == 0 else empty.at[0, pl.ds(0, 2)]
                regions.append((0, {"dev": a, "gz": b}, source, landing, landing, nothing))
    for a in (1, -1, 0):
        for flip in (0, 1):
            if a or flip:
                to = {"dev": a, "flip": flip}
                regions.append((1, to, out_x, land_x.at[1 - a, xy], land_x.at[1 - a, (xy + flip) % 2], empty.at[0, 0]))
    for at, a in enumerate((1, -1)):
        three = pl.ds(size_y - depth, depth) if a > 0 else pl.ds(0, depth)
        two = pl.ds(size_y - 2, 2) if a > 0 else pl.ds(0, 2)
        h_planes = three if a > 0 else two
        h_landing = cap_h.at[at] if a > 0 else cap_h.at[at, :, two]
        tile = pl.ds(zt, 8)
        for kind, source, landing, nothing in (
            (2, fields.at[pl.ds(0, 3), three, tile], cap_e.at[at], empty),
            (3, fields.at[pl.ds(3, 3), h_planes, tile], h_landing, empty if a > 0 else empty.at[:, two]),
            (3, permit_in.at[two, tile], cap_r.at[at], empty.at[0, pl.ds(0, 2)]),
        ):
            regions.append((kind, {"dev": a}, source, landing, landing, nothing))

    def group_of(number):
        kind, move = regions[number][:2]
        if kind:
            return len(messages) + 2 + (0 if not move["dev"] else 1 if move["dev"] > 0 else 2)
        for at, (_, other) in enumerate(messages):
            if {axis: step for axis, step in move.items() if step} == other:
                return at
        return len(messages) + (0 if move["dev"] > 0 else 1)

    def region_inside(move, sign):
        return within({axis: step for axis, step in move.items() if axis != "flip" and step}, sign)

    def region_copy(number):
        kind, move, source, landing, _, _ = regions[number]
        to = {axis: (place[axis] + step + count[axis]) % count[axis] for axis, step in move.items() if axis != "flip"}
        if move.get("flip"):
            to["xy"] = (xy + 1) % 2
        return pltpu.make_async_remote_copy(
            src_ref=source,
            dst_ref=landing,
            send_sem=halo_send.at[group_of(number)],
            recv_sem=region_got.at[min(kind, 2)],
            device_id=to,
            device_id_type=MESH,
        )

    def region_when(number, sign):
        inside = region_inside(regions[number][1], sign)
        return jnp.logical_and(inside, is_end) if regions[number][0] else inside

    def start_regions(kinds):
        for number, region in enumerate(regions):
            if region[0] in kinds:
                @pl.when(region_when(number, 1))
                def _():
                    region_copy(number).start()

    def fill_regions():
        for number, (kind, move, _, _, landing, nothing) in enumerate(regions):
            missing = jnp.logical_not(region_inside(move, -1))

            @pl.when(jnp.logical_and(missing, is_end) if kind else missing)
            def _():
                pltpu.make_async_copy(nothing, landing, region_got.at[min(kind, 2)]).start()

    def wait_region(which):
        length = (10 * size_z, 5 * 8, 2 * 9 * 8 + (9 + 6) * 8 + 2 * 2 * 8)[which]
        everything = arrivals.at[pl.ds(0, length)]
        pltpu.make_async_copy(everything, everything, region_got.at[which]).wait()

    def window(slots, amount_of):
        rows = slots[0].shape[1]
        spot = iota((rows, LANES), 1)
        packs = []
        for part in range(2):
            packed = jnp.full((rows, LANES), COURANT, F32)
            for c in range(4 * part, min(4 * part + 4, len(slots))):
                for y in range(size_y):
                    base = quarter * (c % 4) + 8 * y
                    turned = pltpu.roll(slots[c][y], amount_of(base), 1)
                    packed = jnp.where(jnp.logical_and(spot >= base, spot < base + 8), turned, packed)
            packs.append(packed)
        return packs

    empty[...] = jnp.zeros(empty.shape, F32)
    lhs[...] = jnp.zeros(lhs.shape, BF16)
    pl.semaphore_wait(barrier, beside)
    pass_on()
    loading[0].wait()
    start_regions((2,))
    loading[3].wait()
    permit[...] = COURANT / permit[...]
    own = window([fields[c] for c in range(6)] + [permit[...]], lambda base: (base - (x_wall - 4) + 2 * LANES) % LANES)
    for part in range(2):
        out_w[part] = own[part]
        land_w[1, part, pl.ds(8, size_z), :] = own[part]
    start_regions((0,))

    @pl.when(is_end)
    def _():
        tile = pl.ds(zt, 8)
        eight = iota((8, LANES), 1)
        packed = jnp.full((8, LANES), COURANT, F32)
        for c in range(7):
            values = permit[:, tile, :] if c == 6 else fields[c, :, tile, :]
            for y in range(size_y):
                base = quarter * (c % 4) + 8 * y + 4 * (c // 4)
                turned = pltpu.roll(values[y], (base + 4 * (1 - xy)) % LANES, 1)
                packed = jnp.where(jnp.logical_and(eight >= base, eight < base + 4), turned, packed)
        out_x[...] = packed
        land_x[1, xy] = packed

    @pl.when(jnp.logical_not(is_end))
    def _():
        land_x[...] = jnp.zeros(land_x.shape, F32)

    start_regions((1,))
    start_regions((3,))
    for _ in stage(0, *(fields[c] for c in range(3)), (fields[3], fields[5]), (fields[3], fields[4]), (fields[4], fields[5])):
        pass
    start_halo(0, (4, 5, 8, 11, 9, 10, 0, 1, 2, 3, 6, 7))
    fill_regions()
    for n in range(STEPS):
        fill_halo(n)
    for copy in loading[1:3]:
        copy.wait()
    geometry()
    run_s, run_c = sincos((phase[0] + 0.5 * ANGULAR_STEP * (iota((8, LANES), 0).astype(F32) + 1.0)) * (0.5 / math.pi))
    for n in range(STEPS):
        tables_of(n)

    def relay(k, carry):
        hear()
        pass_on()
        return carry

    lax.fori_loop(0, slabs - 3, relay, 0)
    for copy in loading[4:]:
        copy.wait()

    def half_of(n):
        return run_c[2 * n : 2 * n + 1, :], run_s[2 * n : 2 * n + 1, :]

    def full_of(n):
        return run_c[2 * n + 1 : 2 * n + 2, :], run_s[2 * n + 1 : 2 * n + 2, :]

    cap_sum[...] = jnp.zeros(cap_sum.shape, F32)
    own_walls = walls.at[gz]
    own_walls[...] = jnp.zeros((8, LANES), F32)
    lanes8 = iota((1, LANES), 1)
    owner_row = jnp.zeros((1, LANES), F32)
    for p in range(size_y):
        owner_row = jnp.where(lanes8 == 8 * gz + p, (wall_owner[0, p] + 1).astype(F32), owner_row)
    own_walls[pl.ds(size_y, 1), :] = owner_row
    gathered = jnp.zeros((size_z, LANES), F32)
    for y in range(size_y):
        for c in range(8):
            k = c % 4
            from_c = X_PICKS[k] + (6 if c >= 4 else 0)
            turned = pltpu.roll(spectra[from_c, y], (8 * y + c - x_wall + 2 * LANES) % LANES, 1)
            gathered = jnp.where(lane == 8 * y + c, turned, gathered)
            from_c = Z_PICKS[k] + (6 if c >= 4 else 0)
            low = spectra[from_c, y, pl.ds(ZB, 1), :]
            high = spectra[from_c, y, pl.ds(size_z - 1 - ZB, 1), :]
            cap_plane[pl.ds(8 * y + c, 1), :] = jnp.where(gz == 0, low, high)

    def spread_out(source_of, rows, shift_of, masks):
        spot = iota((rows, LANES), 1)
        values = []
        for c in range(8):
            value = jnp.zeros((rows, LANES), F32)
            first = 0
            for dy, planes in enumerate((depth, size_y, depth)):
                start = quarter * (c % 4) + (8 * (size_y - depth) if dy == 0 else 0)
                last = first + 8 * planes
                inside = jnp.logical_and(spot >= first, spot < last)
                for side in range(masks):
                    chosen = inside if masks == 1 else jnp.logical_and(inside, spot % 8 // 4 == side)
                    value = jnp.where(chosen, turn(source_of(dy, c, side), first - start + shift_of(c, side), 1), value)
                first = last
            values.append(value)
        return values

    def steps_of(values, visit):
        ex, ey, ez, hx, hy, hz, r, k = values
        for n in range(STEPS):
            before = (ez, ey)
            hx = hx - k * ((turn(ez, -8, 1) - ez) - (turn(ey, -1, 0) - ey))
            hy = hy - k * ((turn(ex, -1, 0) - ex) - (turn(ez, -1, 1) - ez))
            hz = hz - k * ((turn(ey, -1, 1) - ey) - (turn(ex, -8, 1) - ex))
            ex = ex + r * ((hz - turn(hz, 8, 1)) - (hy - turn(hy, 1, 0)))
            ey = ey + r * ((hx - turn(hx, 1, 0)) - (hz - turn(hz, 1, 1)))
            ez = ez + r * ((hy - turn(hy, 1, 1)) - (hx - turn(hx, 8, 1)))
            visit(n, before, ey, ez, hy, hz)

    wait_region(0)

    @pl.when(is_end)
    def _():
        wait_region(1)

    sums = [jnp.zeros((size_z, LANES), F32) for _ in range(8)]

    def add_up(n, before, ey, ez, hy, hz):
        for at, (value, (co, si)) in enumerate(((hz, half_of(n)), (hy, half_of(n)), (ez, full_of(n)), (ey, full_of(n)))):
            value = value[:size_z]
            sums[at] = sums[at] + value * co
            sums[4 + at] = sums[4 + at] - value * si

    folded = [
        [
            jnp.concatenate([
                land_w[dy, part, pl.ds(8, size_z), :],
                jnp.where(iota((8, LANES), 0) < 4, land_w[dy, part, pl.ds(size_z + 8, 8), :], land_w[dy, part, pl.ds(0, 8), :]),
            ], axis=0)
            for part in range(2)
        ]
        for dy in range(3)
    ]
    border_e, border_h = [], []

    def keep(n, before, ey, ez, hy, hz):
        border_e.append(before)
        border_h.append((hz, hy))

    steps_of(spread_out(lambda dy, c, side: folded[dy][c // 4], size_z + 8, lambda c, side: 0, 1), add_up)
    steps_of(spread_out(lambda dy, c, side: land_x[dy, side], 8, lambda c, side: 4 * side - 4 * (c // 4), 2), keep)
    for c in range(8):
        chosen = jnp.logical_and(lane % 8 == c, lane < 8 * size_y)
        gathered = gathered + jnp.where(chosen, turn(sums[c], c - 8 * depth - 4, 1), 0.0)
    row_sign = jnp.where(jnp.logical_and(iota((half_rows, LANES), 0) % 4 > 0, iota((half_rows, LANES), 0) % 4 < 3), 1.0, -1.0)
    wall_cells = jnp.transpose(gathered)[:half_rows] * (row_sign[:, :size_z] * facing_x)
    for at, part in enumerate(split(wall_cells * norm)):
        lhs[pl.ds(at * all_rows + half_rows, half_rows), pl.ds(size_x, size_z)] = part


    @pl.when(is_end)
    def _():
        wait_region(2)
        tile = pl.ds(zt, 8)
        eight = iota((8, LANES), 1)
        left, right = jnp.where(xy == 0, 1.0, 0.0), jnp.where(xy == 0, 0.0, 1.0)
        behind, ahead = jnp.where(dev > 0, COURANT, 0.0), jnp.where(dev < devs - 1, COURANT, 0.0)

        def rate_of(eps):
            there = eps > 0.0
            return jnp.where(there, COURANT / jnp.where(there, eps, 1.0), 0.0)

        e = [[cap_e[0, c, i] for i in range(3)] + [fields[c, y, tile, :] for y in range(size_y)] + [cap_e[1, c, i] for i in range(3)] for c in range(3)]
        h = [[cap_h[0, c, i] for i in range(3)] + [fields[3 + c, y, tile, :] for y in range(size_y)] + [cap_h[1, c, i] for i in range(2)] for c in range(3)]
        rates = [None] + [rate_of(cap_r[0, i]) for i in range(2)] + [permit[y, tile, :] for y in range(size_y)] + [rate_of(cap_r[1, i]) for i in range(2)]
        coefs = [behind] * depth + [COURANT] * size_y + [ahead] * depth

        def next_x(value, border, i):
            return jnp.where(eight == LANES - 1, turn(border, LANES - 1 - (8 * i + 4), 1), turn(value, -1, 1))

        def last_x(value, border, i):
            return jnp.where(eight == 0, turn(border, -(8 * i + 3), 1), turn(value, 1, 1))

        totals_of = [[jnp.zeros((8, LANES), F32) for _ in range(8)] for _ in range(size_y)]
        for n in range(STEPS):
            bz, by = (value * left for value in border_e[n])
            fx, fy, fz = [list(v) for v in h]
            for i in range(n, extent - 1 - n):
                xs, ys, zs = e[0][i], e[1][i], e[2][i]
                fx[i] = h[0][i] - coefs[i] * ((e[2][i + 1] - zs) - (turn(ys, -1, 0) - ys))
                fy[i] = h[1][i] - coefs[i] * ((turn(xs, -1, 0) - xs) - (next_x(zs, bz, i) - zs))
                fz[i] = h[2][i] - coefs[i] * ((next_x(ys, by, i) - ys) - (e[0][i + 1] - xs))
            h = [fx, fy, fz]
            bz, by = (value * right for value in border_h[n])
            gx, gy, gz_ = [list(v) for v in e]
            for i in range(n + 1, extent - 1 - n):
                xs, ys, zs = h[0][i], h[1][i], h[2][i]
                gx[i] = e[0][i] + rates[i] * ((zs - h[2][i - 1]) - (ys - turn(ys, 1, 0)))
                gy[i] = e[1][i] + rates[i] * ((xs - turn(xs, 1, 0)) - (zs - last_x(zs, bz, i)))
                gz_[i] = e[2][i] + rates[i] * ((ys - last_x(ys, by, i)) - (xs - h[0][i - 1]))
            e = [gx, gy, gz_]
            for y in range(size_y):
                i = depth + y
                for at, (value, (co, si)) in enumerate(((h[1][i], half_of(n)), (h[0][i], half_of(n)), (e[1][i], full_of(n)), (e[0][i], full_of(n)))):
                    totals_of[y][at] = totals_of[y][at] + value * co
                    totals_of[y][4 + at] = totals_of[y][4 + at] - value * si
        for y in range(size_y):
            for c in range(8):
                value = totals_of[y][c]
                cap_sum[pl.ds(8 * y + c, 1), :] = jnp.where(gz == 0, value[ZB : ZB + 1], value[7 - ZB : 8 - ZB])

    def advance(n, ghosts):
        fields_from, spec_from = (fields, spectra) if n == 0 else (fields_out, spectra_out)
        ex, ey, ez, hx, hy, hz = (fields_from[c] for c in range(6))
        rate = permit[...]
        hx = hx - COURANT * (inner(True, 0, ez) - inner(True, 1, ey))
        hy = hy - COURANT * (inner(True, 1, ex) - inner(True, 2, ez))
        hz = hz - COURANT * (inner(True, 2, ey) - inner(True, 0, ex))
        wait_halo(n)
        start, _ = first_of(n)
        xp = in_xd[n]
        hx = hx - COURANT * (at_y(in_yd[2 * n], True) - at_z(in_zd[2 * n], True))
        hy = hy - COURANT * (at_z(in_zd[2 * n + 1], True) - at_x(xp, 0, True))
        hz = hz - COURANT * (at_x(xp, 1, True) - at_y(in_yd[2 * n + 1], True))

        ax, ay, az = in_yu[start], in_yu[start + 1], in_yu[start + 2]
        bx, by, bz = in_zu[start], in_zu[start + 1], in_zu[start + 2]
        c_ex, own = in_xu[n], out_xd[n]
        if n == 0:
            y_hx, y_hz = in_yu[3], in_yu[4]
            z_hx, z_hy = in_zu[3], in_zu[4]
            x_hy, x_hz = turn(c_ex, -3 * size_y, 1), turn(c_ex, -4 * size_y, 1)
        else:
            y_hx, y_hz, z_hx, z_hy, x_hy, x_hz = ghosts
        ay_z = jnp.where(row2 == size_z - 1, in_zy[n], turn(ay, -1, 0))
        ay_x = jnp.where(lane == size_x - 1, turn(in_yx[n], -2 * size_y, 1), turn(ay, -1, 1))
        y_hx = y_hx - half_y * ((ez[0] - az) - (ay_z - ay))
        y_hz = y_hz - half_y * ((ay_x - ay) - (ex[0] - ax))
        bz_y = jnp.concatenate([bz[1:], in_yz[n, 7:8, :][None]], axis=0)
        corner = in_zx[n, 7:8, :]
        bz_x = jnp.stack([turn(corner, -1 - y, 1) for y in range(size_y)], axis=0)
        bz_x = jnp.where(lane_row == size_x - 1, bz_x, jnp.stack([turn(bz[y], -1, 1) for y in range(size_y)], axis=0))
        z_hx = z_hx - half_z * ((bz_y - bz) - (ey[:, 0:1, :] - by))
        z_hy = z_hy - half_z * ((ex[:, 0:1, :] - bx) - (bz_x - bz))
        c_z = jnp.where(row2 == size_z - 1, in_xz[n, 0:1, :], turn(c_ex, -1, 0))
        c_y = jnp.where(lane == size_y - 1, turn(in_xy[n], size_y - 1, 1), turn(c_ex, -1, 1))
        x_hy = x_hy - half_x * ((c_z - c_ex) - (own - turn(c_ex, -2 * size_y, 1)))
        x_hz = x_hz - half_x * ((turn(own, -size_y, 1) - turn(c_ex, -size_y, 1)) - (c_y - c_ex))

        ex = ex + rate * (inner(False, 0, hz) - inner(False, 1, hy))
        ey = ey + rate * (inner(False, 1, hx) - inner(False, 2, hz))
        ez = ez + rate * (inner(False, 2, hy) - inner(False, 0, hx))
        ex = ex - rate * (at_y(y_hz, False) - at_z(z_hy, False))
        ey = ey - rate * (at_z(z_hx, False) - at_x(x_hz, 0, False))
        ez = ez - rate * (at_x(x_hy, 0, False) - at_y(y_hx, False))
        if n < STEPS - 1:
            staging = stage(n + 1, ex, ey, ez, (), (), ())
            next(staging)
            start_halo(n + 1, (4, 5, 0, 1, 2, 3))
            next(staging)
            start_halo(n + 1, (8, 11, 9, 10, 6, 7))
        half_c, half_s = run_c[2 * n : 2 * n + 1, :], run_s[2 * n : 2 * n + 1, :]
        for c, value in enumerate((hx, hy, hz)):
            spectra_out[3 + c] = spec_from[3 + c] + value * half_c
            spectra_out[9 + c] = spec_from[9 + c] - value * half_s
        full_c, full_s = run_c[2 * n + 1 : 2 * n + 2, :], run_s[2 * n + 1 : 2 * n + 2, :]
        for c, value in enumerate((ex, ey, ez)):
            spectra_out[c] = spec_from[c] + value * full_c
            spectra_out[6 + c] = spec_from[6 + c] - value * full_s
        for c, value in enumerate((ex, ey, ez, hx, hy, hz)):
            fields_out[c] = value
        return y_hx, y_hz, z_hx, z_hy, x_hy, x_hz

    sub = iota((8, LANES), 0)
    caps_now = (cap_plane[...] + cap_sum[...]) * (row_sign * (facing_z * end_weight))
    cap_plane[...] = caps_now
    for at, part in enumerate(split(caps_now * norm)):
        lhs[pl.ds(at * all_rows, half_rows), pl.ds(0, size_x)] = part

    def wall_copy(k, ref=None):
        held = walls.at[gz] if ref is None else ref
        return pltpu.make_async_remote_copy(
            src_ref=held,
            dst_ref=held,
            send_sem=wall_send,
            recv_sem=wall_got,
            device_id={"gz": (gz + k) % slabs},
            device_id_type=MESH,
        )

    def cap_copy(k, at):
        return pltpu.make_async_remote_copy(
            src_ref=caps.at[at],
            dst_ref=caps.at[at],
            send_sem=cap_send,
            recv_sem=cap_got.at[at],
            device_id={"gz": (gz + k) % slabs},
            device_id_type=MESH,
        )

    sign = jnp.where(sub < 4, -1.0, 1.0)

    def far_of(j):
        rows = lhs[...]
        by_high = jnp.dot(rows, table_hi[j], preferred_element_type=F32)
        by_low = jnp.dot(rows[:all_rows], table_lo[j], preferred_element_type=F32)
        product = by_high[:all_rows] + by_high[all_rows:] + by_low
        theta = jnp.zeros((8, LANES), F32)
        phi = jnp.zeros((8, LANES), F32)
        for face in range(2):
            sum_c = jnp.zeros((8, LANES), F32)
            sum_s = jnp.zeros((8, LANES), F32)
            for y in range(size_y):
                g = face * size_y + y
                tile = product[8 * g : 8 * g + 8]
                tile = tile[:, :LANES] + sign * pltpu.roll(tile[:, LANES:], 4, 0)
                sum_c = sum_c + tile * phases[j, 0, pl.ds(g, 1), :]
                sum_s = sum_s + tile * phases[j, 1, pl.ds(g, 1), :]
            far = sum_c + sign * pltpu.roll(sum_s, 4, 0)
            theta = theta + weights[j, 2 * face] * far
            phi = phi + weights[j, 2 * face + 1] * far

        def four(values):
            pairs = values + pltpu.roll(values, 7, 0)
            return pairs + pltpu.roll(pairs, 6, 0)

        both = jnp.where(sub % 4 == 1, pltpu.roll(four(phi), 1, 0), four(theta))
        parts_out[j] = jnp.where(sub < 2, both, pltpu.roll(both, 6, 0))[:4]

    bunch = per * max(1, 4 // per)
    together = bunch // per
    upper = jnp.where(gz >= slabs // 2, 1, 0)
    near = (upper * across + dev * xys + xy) % owners

    def partner(number):
        other, bit = 0, 1
        while bit < owners:
            other = other + bit * ((near // bit + number // bit) % 2)
            bit *= 2
        return other

    def flat_of(owner):
        return (slabs // 2 - 1) * across + owner

    def part_copy(owner, source):
        return pltpu.make_async_remote_copy(
            src_ref=parts_out.at[pl.ds(owner * per, per)],
            dst_ref=parts_in.at[source],
            send_sem=part_send,
            recv_sem=part_got,
            device_id=ident(flat_of(owner)),
            device_id_type=MESH,
        )

    mine = me - flat_of(0)
    leads = jnp.logical_and(mine >= 0, mine < owners)

    def far_and_send(number, carry):
        several = [partner(owners - 1 - together * number - m) for m in range(together)]
        for owner in several:
            for m in range(per):
                far_of(owner * per + m)
        for owner in several:
            @pl.when(owner != mine)
            def _():
                part_copy(owner, me).start()

        return carry

    hear()
    lax.fori_loop(0, owners // together, far_and_send, 0)

    ghosts = advance(0, None)
    for y in range(size_y):
        cells = jnp.concatenate([wall_cells[8 * y : 8 * y + 8], jnp.zeros((8, LANES - size_z), F32)], axis=1)
        own_walls[pl.ds(y, 1), :] = jnp.sum(stagger(cells, PATCH), axis=0, keepdims=True)
    for k in range(1, slabs):
        wall_copy(k).start()
    for at, holder in enumerate((0, slabs - 1)):
        @pl.when(gz == holder)
        def _():
            for y in range(size_y):
                caps[at, pl.ds(8 * y, 8), :] = block_transpose(cap_plane[pl.ds(8 * y, 8), :])
            for k in range(1, slabs):
                cap_copy(k, at).start()

    def total_copy(k, owner, ref=None):
        held = totals.at[pl.ds(owner * per, per)] if ref is None else ref
        return pltpu.make_async_remote_copy(
            src_ref=held,
            dst_ref=held,
            send_sem=total_send,
            recv_sem=total_got.at[owner // together],
            device_id=ident((me + k) % peers),
            device_id_type=MESH,
        )

    @pl.when(leads)
    def _():
        everyone = parts_in.at[pl.ds(0, peers - 1)]
        pltpu.make_async_remote_copy(
            src_ref=everyone, dst_ref=everyone, send_sem=part_send, recv_sem=part_got, device_id={"gz": gz}, device_id_type=MESH
        ).wait_recv()
        parts_in[me] = parts_out[pl.ds(mine * per, per)]
        totals[pl.ds(mine * per, per)] = jnp.sum(parts_in[...], axis=0)
        for k in sorted(range(slabs), key=lambda k: -min(k, slabs - k)):
            row = (gz + k) % slabs * across

            def send(r, carry):
                to = row + (dev * xys + xy + r) % across

                @pl.when(to != me)
                def _():
                    total_copy((to - me + peers) % peers, mine).start()

                return carry

            lax.fori_loop(0, across, send, 0, unroll=across <= 4)


    def choose(mine, share, records):
        length = mine.shape[1]
        before = jnp.where(iota((length, length), 0) < iota((length, length), 1), 1.0, 0.0).astype(BF16)
        ones = jnp.broadcast_to(jnp.where(mine, 1.0, 0.0), (8, length))
        rank = jnp.dot(ones.astype(BF16), before, preferred_element_type=F32)
        wanted = iota((8, length), 0).astype(F32)
        chooser = jnp.where(rank == wanted, ones, 0.0)
        return jnp.dot(chooser, records, precision=HIGHEST, preferred_element_type=F32)[:share]

    def choose_owned():
        wall_copy(1, walls.at[pl.ds(0, slabs - 1)]).wait_recv()
        for at, holder in enumerate((0, slabs - 1)):
            @pl.when(gz != holder)
            def _():
                cap_copy(1, at).wait_recv()
        all_walls = walls[...]
        owner_all = jnp.sum(all_walls[:, size_y : size_y + 1, :], axis=0)[:, : 8 * slabs]
        cap_share = (owned_out.shape[0] - size_y) // 2
        owned_out[pl.ds(0, size_y), 0, :] = choose(
            owner_all == (gz + 1).astype(F32), size_y, all_walls.reshape(8 * slabs, LANES)
        )
        for at in range(2):
            owned_out[pl.ds(size_y + at * cap_share, cap_share), 0, :] = choose(
                cap_owner[pl.ds(at, 1), :] == gz, cap_share, caps[at]
            )

    def intensity_of(field):
        return jnp.sum(field * field, axis=0, keepdims=True)

    def slope_of(j):
        field = totals[j]
        residual = aim[pl.ds(j, 1), :].astype(F32) * (intensity_of(field) - target[pl.ds(j, 1), :])
        return 2.0 * residual * field

    def adjoint_of(j):
        slope = slope_of(j)
        by_theta = jnp.where(sub < 4, slope[0:1], slope[2:3])
        by_phi = jnp.where(sub < 4, slope[1:2], slope[3:4])
        tiles = []
        for face in range(2):
            vector = weights[j, 2 * face] * by_theta + weights[j, 2 * face + 1] * by_phi
            turned = -sign * pltpu.roll(vector, 4, 0)
            for y in range(size_y):
                g = face * size_y + y
                tile = vector * phases[j, 0, pl.ds(g, 1), :] + turned * phases[j, 1, pl.ds(g, 1), :]
                tiles.append(jnp.concatenate([tile, -sign * pltpu.roll(tile, 4, 0)], axis=1))
        rows = jnp.concatenate(tiles, axis=0)
        high, low = split(rows)
        both = jnp.concatenate([high, low], axis=0)
        across = (((1,), (1,)), ((), ()))
        by_high = lax.dot_general(both, table_hi[j], across, preferred_element_type=F32)
        by_low = lax.dot_general(high, table_lo[j], across, preferred_element_type=F32)
        return by_high[:all_rows] + by_high[all_rows:] + by_low

    def adjoint_wait(number):
        several = [partner(together * number + m) for m in range(together)]
        batch = several[0] // together
        ours = jnp.logical_and(leads, mine // together == batch)

        @pl.when(jnp.logical_not(ours))
        def _():
            total_copy(1, several[0], totals.at[pl.ds(batch * bunch, bunch)]).wait_recv()

        if together > 1:
            @pl.when(ours)
            def _():
                total_copy(1, several[0], totals.at[pl.ds(batch * bunch, bunch - per)]).wait_recv()

        return several

    def adjoint_some(numbers, total):
        several = [owner for number in numbers for owner in adjoint_wait(number)]
        for owner in several:
            for m in range(per):
                total = total + adjoint_of(owner * per + m)
        return total

    rounds = owners // together
    ghosts = advance(1, ghosts)
    choose_owned()
    gradient = adjoint_some((0,), jnp.zeros((all_rows, size_x + size_z), F32))
    gradient = adjoint_some(range(1, rounds), gradient)
    intensity_out[...] = intensity_of(totals[me // ratio])
    advance(2, ghosts)
    for y in range(size_y):
        wall = gradient[half_rows + 8 * y : half_rows + 8 * y + 8, size_x:]
        wall = jnp.concatenate([wall, jnp.zeros((8, LANES - size_z), F32)], axis=1)
        wall = stagger(wall, PATCH)
        adjoint_out[pl.ds(y, 1), 0, :] = jnp.sum(wall, axis=0, keepdims=True) * norm
        cap = block_transpose(gradient[8 * y : 8 * y + 8, :size_x] * (norm * end_weight))
        adjoint_out[pl.ds(size_y + 8 * y, 8), 0, :] = cap

    groups_sent = {}
    for number, (landing, move) in enumerate(messages):
        groups_sent[number] = [within(move, 1), math.prod(landing.shape) // LANES]
    for number, (_, _, source, _, _, _) in enumerate(regions):
        entry = groups_sent.setdefault(group_of(number), [region_when(number, 1), 0])
        entry[1] += math.prod(source.shape) // LANES
    for group, (sent, rows_sent) in groups_sent.items():
        @pl.when(sent)
        def _():
            everything = arrivals.at[pl.ds(0, rows_sent)]
            pltpu.make_async_copy(everything, everything, halo_send.at[group]).wait()

    def parts_sent(ref):
        pltpu.make_async_remote_copy(
            src_ref=ref, dst_ref=ref, send_sem=part_send, recv_sem=part_got, device_id={"gz": gz}, device_id_type=MESH
        ).wait_send()

    @pl.when(leads)
    def _():
        parts_sent(parts_out.at[pl.ds(0, (owners - 1) * per)])
        total_copy(1, 0, parts_in.at[pl.ds(0, peers - 1)]).wait_send()

    @pl.when(jnp.logical_not(leads))
    def _():
        parts_sent(parts_out)

    wall_copy(1, walls.at[pl.ds(0, slabs - 1)]).wait_send()
    for at, holder in enumerate((0, slabs - 1)):
        @pl.when(gz == holder)
        def _():
            sent = weights.at[pl.ds(0, slabs - 1)]
            pltpu.make_async_copy(sent, sent, cap_send).wait()


def write_out(*refs):
    copies = [pltpu.make_async_copy(refs[i], refs[5 + i], refs[10].at[i]) for i in range(5)]
    for copy in copies:
        copy.start()
    for copy in copies:
        copy.wait()


def local(fields, spectra, permittivity, phase_start, wall_owner, cap_owner, dir_index, target, aim_mask):
    slabs, devs, xys = (lax.axis_size(a) for a in ("gz", "dev", "xy"))
    peers = slabs * devs * xys
    size_y, size_z, size_x = permittivity.shape
    assert size_z == PATCH and size_x == LANES and size_y == 4 and xys == 2
    directions = dir_index.shape[0]
    chunks = directions // LANES
    ratio = peers // chunks
    per = max(1, chunks // (2 * devs * xys))
    owners = chunks // per
    share = directions // peers
    cap_count = size_y * size_x // PATCH
    owned = size_y + 2 * (cap_count // slabs)
    rows = 16 * size_y
    depth = size_x + size_z
    planes, pairs = 5 + 3 * (STEPS - 1), 2 * STEPS
    halos = (
        (planes, size_z, LANES), (pairs, size_z, LANES), (planes, size_y, 1, LANES), (pairs, size_y, 1, LANES),
        (STEPS, size_z, LANES), (STEPS, size_z, LANES),
        (STEPS, 1, LANES), (STEPS, 8, LANES), (STEPS, size_z, LANES), (STEPS, 8, LANES), (STEPS, 8, LANES), (STEPS, size_z, LANES),
    )
    vmem = pl.BlockSpec(memory_space=pltpu.VMEM)
    anywhere = pl.BlockSpec(memory_space=pl.ANY)
    dma = pltpu.SemaphoreType.DMA
    outs = pl.pallas_call(
        functools.partial(kernel, (slabs, devs, xys)),
        out_shape=(
            pltpu.VMEM(fields.shape, F32),
            pltpu.VMEM(spectra.shape, F32),
            pltpu.VMEM((owned, 1, LANES), F32),
            pltpu.VMEM((1, LANES), F32),
            pltpu.VMEM((size_y + cap_count, 1, LANES), F32),
        ),
        in_specs=[anywhere] * 9,
        out_specs=(vmem,) * 5,
        scratch_shapes=[
            *(pltpu.VMEM(shape, F32) for shape in halos[:6]),
            *(pltpu.VMEM(shape, F32) for shape in halos),
            pltpu.VMEM((5, size_z, LANES), F32),
            pltpu.VMEM((5, size_y, 1, LANES), F32),
            pltpu.VMEM((376, 1, LANES), F32),
            pltpu.VMEM((2, size_z, LANES), F32),
            pltpu.VMEM((8, LANES), F32),
            pltpu.VMEM((3, 2, size_z + 16, LANES), F32),
            pltpu.VMEM((3, 2, 8, LANES), F32),
            pltpu.VMEM((2, 3, 3, 8, LANES), F32),
            pltpu.VMEM((2, 3, 3, 8, LANES), F32),
            pltpu.VMEM((2, 2, 8, LANES), F32),
            pltpu.VMEM((3, 3, 8, LANES), F32),
            pltpu.VMEM((8 * size_y, LANES), F32),
            pltpu.VMEM(fields.shape, F32),
            pltpu.VMEM(spectra.shape, F32),
            pltpu.VMEM(permittivity.shape, F32),
            pltpu.SMEM((1,), F32),
            pltpu.SMEM(wall_owner.shape, jnp.int32),
            pltpu.VMEM(cap_owner.shape, jnp.int32),
            pltpu.VMEM((chunks, LANES), jnp.int32),
            pltpu.VMEM((chunks, LANES), F32),
            pltpu.VMEM((chunks, LANES), jnp.int32),
            pltpu.VMEM((8, chunks, LANES), F32),
            pltpu.VMEM((chunks, 4, 8, LANES), F32),
            pltpu.VMEM((chunks, 2, 2 * size_y, LANES), F32),
            pltpu.VMEM((chunks, depth, 2 * LANES), BF16),
            pltpu.VMEM((chunks, depth, 2 * LANES), BF16),
            pltpu.VMEM((8 * size_y, LANES), F32),
            pltpu.VMEM((2 * rows, depth), BF16),
            pltpu.VMEM((chunks, 4, LANES), F32),
            pltpu.VMEM((peers, per, 4, LANES), F32),
            pltpu.VMEM((chunks, 4, LANES), F32),
            pltpu.VMEM((slabs, 8, LANES), F32),
            pltpu.VMEM((2, cap_count, LANES), F32),
            dma((len(halos) + 5,)), dma((STEPS,)),
            dma, dma,
            dma, dma((owners // max(1, 4 // per),)),
            dma, dma,
            dma, dma((2,)),
            dma((9,)), pltpu.SemaphoreType.REGULAR((2,)), dma((3,)),
        ],
        compiler_params=pltpu.CompilerParams(collective_id=0, has_side_effects=True),
    )(
        fields, spectra, permittivity, phase_start, wall_owner, cap_owner,
        dir_index.reshape(chunks, LANES), target.reshape(chunks, LANES), aim_mask.reshape(chunks, LANES),
    )
    held = (fields.shape, spectra.shape, (owned, 1, LANES), (1, LANES), (size_y + cap_count, 1, LANES))
    fields_new, spectra_new, owned_rows, intensity, adjoint = pl.pallas_call(
        write_out,
        out_shape=tuple(jax.ShapeDtypeStruct(shape, F32) for shape in held),
        in_specs=[pl.BlockSpec(memory_space=pltpu.VMEM)] * 5,
        out_specs=(pl.BlockSpec(memory_space=pl.ANY),) * 5,
        scratch_shapes=[dma((5,))],
    )(*(pltpu.with_memory_space_constraint(out, pltpu.VMEM) for out in outs))
    owned_rows = owned_rows.reshape(1, 1, owned, 1, LANES).transpose(0, 1, 3, 2, 4)
    adjoint = adjoint.reshape(1, 1, size_y + cap_count, 1, LANES).transpose(0, 1, 3, 2, 4)
    intensity = intensity.reshape(LANES)
    if ratio > 1:
        me = (lax.axis_index("gz") * devs + lax.axis_index("dev")) * xys + lax.axis_index("xy")
        intensity = lax.dynamic_slice_in_dim(intensity, (me % ratio) * share, share, 0)
    return (fields_new, spectra_new, owned_rows, intensity, adjoint)


def solution(mesh):
    placed = (
        P("groups", "dev", "gz", "xy"),
        P("groups", "dev", "gz", "xy"),
        P(("groups", "dev"), "gz", "xy"),
        P("groups"),
        P("gz", None),
        P(),
        P(),
        P("groups"),
        P("groups"),
    )
    return jax.shard_map(
        local,
        mesh=mesh,
        in_specs=placed,
        out_specs=(
            P("groups", "dev", "gz", "xy"),
            P("groups", "dev", "gz", "xy"),
            P(("groups", "gz"), "dev", "xy", None, None),
            P(("groups", "gz", "dev", "xy")),
            P(("groups", "gz"), "dev", "xy", None, None),
        ),
        check_vma=False,
    )
```

```python
import functools
import math

import jax
import jax.numpy as jnp
from jax import lax
from jax.experimental import pallas as pl
from jax.experimental.pallas import tpu as pltpu
from jax.sharding import PartitionSpec as P

PATCH = 16
XB = 8
ZB = 4
STEPS = 3
THETAS = 64
COURANT = 0.5
ANGULAR_STEP = 0.3
WAVE_NUMBER = 0.6
LANES = 128
HIGHEST = lax.Precision.HIGHEST
CURRENT_SIGNS = (-1.0, 1.0, 1.0, -1.0)
X_PICKS = (5, 4, 2, 1)
Z_PICKS = (4, 3, 1, 0)
MESH = pl.DeviceIdType.MESH
AXES = ("dev", "gz", "xy")
F32 = jnp.float32
BF16 = jnp.bfloat16


def iota(shape, dim):
    return lax.broadcasted_iota(jnp.int32, shape, dim)


def sincos(turns):
    half = (turns - jnp.floor(turns + 0.5)) * math.pi
    sq = half * half
    sin_h = half * (1.0 + sq * (-1.0 / 6 + sq * (1.0 / 120 + sq * (-1.0 / 5040 + sq * (1.0 / 362880 - sq * (1.0 / 39916800))))))
    cos_h = 1.0 + sq * (-0.5 + sq * (1.0 / 24 + sq * (-1.0 / 720 + sq * (1.0 / 40320 + sq * (-1.0 / 3628800 + sq * (1.0 / 479001600))))))
    return 2.0 * sin_h * cos_h, 1.0 - 2.0 * sin_h * sin_h


def split(values):
    high = values.astype(BF16)
    return high, (values - high.astype(F32)).astype(BF16)


def arrival_rows(n, size_y, size_z):
    length = 5 if n == 0 else 3
    return (length + 2) * (size_z + size_y) + 1 + 3 * 8 + 4 * size_z


def stagger(tile, by):
    row = iota(tile.shape, 0)
    for bit in (1, 2, 4):
        tile = jnp.where(row // bit % 2 == 1, pltpu.roll(tile, by * bit % LANES, 1), tile)
    return tile


def block_transpose(tile):
    on_diagonal = (iota(tile.shape, 1) // PATCH) == iota(tile.shape, 0)
    total = jnp.where(on_diagonal, tile, 0.0)
    for k in range(1, 8):
        turned = pltpu.roll(tile, PATCH * k, 1)
        total = total + pltpu.roll(jnp.where(on_diagonal, turned, 0.0), 8 - k, 0)
    return total


def kernel(
    sizes,
    fields_in, spectra_in, permit_in, phase_in, wall_owner_in, cap_owner_in, dirs_in, target_in, aim_in,
    fields_out, spectra_out, owned_out, intensity_out, adjoint_out,
    out_yu, out_yd, out_zu, out_zd, out_xu, out_xd,
    in_yu, in_yd, in_zu, in_zd, in_xu, in_xd, in_zy, in_yz, in_yx, in_zx, in_xz, in_xy, blank, blank_rows, arrivals,
    out_w, out_z, out_x, land_w, land_z, land_x, tile_e, tile_h, tile_f, cap_e, cap_h, cap_f, empty, empty_half, cap_sum,
    fields, spectra, permit, phase, wall_owner, cap_owner, dirs, target, aim,
    geo, weights, phases, table_hi, table_lo, cap_plane, lhs,
    parts_out, parts_in, totals, walls, caps,
    halo_send, halo_got, part_got, total_got, wall_got, cap_send, cap_got, loads, chain, region_got,
):
    slabs, devs, xys = sizes
    peers = slabs * devs * xys
    size_y, size_z, size_x = permit.shape
    chunks = dirs.shape[0]
    ratio = peers // chunks
    across = devs * xys
    per = max(1, chunks // (2 * across))
    owners = chunks // per
    groups = 2 * size_y
    half_rows = 8 * size_y
    all_rows = 2 * half_rows
    gz, dev, xy = lax.axis_index("gz"), lax.axis_index("dev"), lax.axis_index("xy")
    me = (gz * devs + dev) * xys + xy
    place = {"dev": dev, "gz": gz, "xy": xy}
    count = {"dev": devs, "gz": slabs, "xy": xys}

    def ident(flat):
        return {"gz": flat // (devs * xys), "dev": (flat // xys) % devs, "xy": flat % xys}

    pltpu.make_async_copy(fields_in, fields, loads.at[0]).start()
    barrier = pltpu.get_barrier_semaphore()

    for away in (1, -1, 0):
        @pl.when(jnp.logical_and(gz + away >= 0, gz + away < slabs))
        def _():
            def greet(k, carry):
                spot = (dev * xys + xy + k) % across
                to = {"gz": gz + away, "dev": spot // xys, "xy": spot % xys}
                pl.semaphore_signal(barrier, inc=1, device_id=to, device_id_type=MESH)
                return carry

            lax.fori_loop(0 if away else 1, across, greet, 0)

    beside = jnp.where(gz > 0, across, 0) + jnp.where(gz < slabs - 1, across, 0) + across - 1

    def pass_on():
        for at, away in enumerate((1, -1)):
            @pl.when(jnp.logical_and(gz + away >= 0, gz + away < slabs))
            def _():
                to = {"gz": gz + away, "dev": dev, "xy": xy}
                pl.semaphore_signal(chain.at[at], inc=1, device_id=to, device_id_type=MESH)

    def hear():
        for at, away in enumerate((1, -1)):
            @pl.when(jnp.logical_and(gz - away >= 0, gz - away < slabs))
            def _():
                pl.semaphore_wait(chain.at[at], 1)

    loading = [
        pltpu.make_async_copy(source, held, loads.at[number])
        for number, (source, held) in enumerate((
            (fields_in, fields), (dirs_in, dirs), (phase_in, phase), (permit_in, permit), (spectra_in, spectra),
            (wall_owner_in, wall_owner), (cap_owner_in, cap_owner), (target_in, target), (aim_in, aim),
        ))
    ]
    for copy in loading[1:]:
        copy.start()

    def geometry():
        index = dirs[...]
        sin_t, cos_t = sincos(((index // THETAS).astype(F32) + 0.5) * (0.5 / THETAS))
        sin_f, cos_f = sincos((index % THETAS).astype(F32) * (1.0 / THETAS))
        wave = WAVE_NUMBER / (2.0 * math.pi)
        for slot, values in enumerate((
            wave * sin_t * cos_f, wave * sin_t * sin_f, wave * cos_t,
            cos_t * cos_f, cos_t * sin_f, -sin_t, -sin_f, cos_f,
        )):
            geo[slot] = values

    grid_x, grid_y, grid_z = size_x * xys, size_y * devs, size_z * slabs
    x_first = (xy * size_x).astype(F32) - (grid_x - 1) / 2.0
    y_first = (dev * size_y).astype(F32) - (grid_y - 1) / 2.0
    z_first = (gz * size_z).astype(F32) - (grid_z - 1) / 2.0
    x_wall = jnp.where(xy == 0, XB, size_x - 1 - XB)
    z_cap = jnp.where(gz == 0, ZB, size_z - 1 - ZB)
    x_face = x_first + x_wall.astype(F32)
    z_face = z_first + z_cap.astype(F32)
    facing_x = jnp.where(xy == 0, -1.0, 1.0)
    facing_z = jnp.where(gz == 0, -1.0, 1.0)
    is_end = jnp.logical_or(gz == 0, gz == slabs - 1)
    end_weight = jnp.where(is_end, 1.0, 0.0)
    norm = 1.0 / math.sqrt(2.0 * (2 * grid_y * grid_z + 2 * grid_y * grid_x))

    def make_tables(j, carry):
        def row(slot):
            return geo[slot, pl.ds(j, 1), :]

        ux, uy, uz = row(0), row(1), row(2)
        blocks = size_x // 8
        far_s, far_c = sincos((iota((blocks, LANES), 0).astype(F32) * 8.0 + x_first) * ux)
        near_s, near_c = sincos(iota((8, LANES), 0).astype(F32) * ux)
        far_s, far_c = far_s[:, None, :], far_c[:, None, :]
        near_s, near_c = near_s[None], near_c[None]
        cos_x = (far_c * near_c - far_s * near_s).reshape(size_x, LANES)
        sin_x = (far_s * near_c + far_c * near_s).reshape(size_x, LANES)
        sin_z, cos_z = sincos((iota((size_z, LANES), 0).astype(F32) + z_first) * uz)
        for at, (x_part, z_part) in enumerate(((cos_x, cos_z), (sin_x, sin_z))):
            lanes = pl.ds(at * LANES, LANES)
            x_high, x_low = split(x_part)
            z_high, z_low = split(z_part)
            table_hi[j, pl.ds(0, size_x), lanes] = x_high
            table_lo[j, pl.ds(0, size_x), lanes] = x_low
            table_hi[j, pl.ds(size_x, size_z), lanes] = z_high
            table_lo[j, pl.ds(size_x, size_z), lanes] = z_low
        which = iota((groups, LANES), 0)
        cell_y = (which % size_y).astype(F32) + y_first
        sin_g, cos_g = sincos(cell_y * uy + jnp.where(which < size_y, z_face * uz, x_face * ux))
        phases[j, 0] = cos_g
        phases[j, 1] = sin_g
        kind = iota((8, LANES), 0) % 4

        def pattern(a, b, c, d):
            return jnp.where(kind == 0, a, jnp.where(kind == 1, b, jnp.where(kind == 2, c, d)))

        tx, ty, tz, fx, fy = row(3), row(4), row(5), row(6), row(7)
        weights[j, 0] = pattern(-tx, -ty, -fx, -fy)
        weights[j, 1] = pattern(-fx, -fy, tx, ty)
        weights[j, 2] = pattern(-ty, -tz, -fy, jnp.zeros_like(fy))
        weights[j, 3] = pattern(-fy, jnp.zeros_like(fy), ty, tz)
        return carry

    windows = STEPS

    def tables_of(window):
        lax.fori_loop(window * chunks // windows, (window + 1) * chunks // windows, make_tables, 0)

    lane = iota((size_z, LANES), 1)
    lane3 = iota((size_y, size_z, LANES), 2)
    row3 = iota((size_y, size_z, LANES), 1)

    messages = (
        (in_yu, {"dev": 1}), (in_yd, {"dev": -1}), (in_zu, {"gz": 1}), (in_zd, {"gz": -1}),
        (in_zy, {"gz": -1, "dev": 1}), (in_yz, {"dev": -1, "gz": 1}),
        (in_xu, {"xy": 1}), (in_xd, {"xy": -1}),
        (in_yx, {"dev": 1, "xy": -1}), (in_zx, {"gz": 1, "xy": -1}), (in_xz, {"xy": 1, "gz": -1}), (in_xy, {"xy": 1, "dev": -1}),
    )

    def within(move, sign):
        inside = True
        for axis, step in move.items():
            spot = place[axis] + sign * step
            inside = jnp.logical_and(inside, jnp.logical_and(spot >= 0, spot < count[axis]))
        return inside

    def first_of(n):
        return (0, 5) if n == 0 else (5 + 3 * (n - 1), 3)

    def views(n):
        start, length = first_of(n)
        planes, pair = pl.ds(start, length), pl.ds(2 * n, 2)
        low, high = pl.ds(0, 8), pl.ds(size_z - 8, 8)
        return (
            (out_yu.at[planes], in_yu.at[planes]), (out_yd.at[pair], in_yd.at[pair]),
            (out_zu.at[planes], in_zu.at[planes]), (out_zd.at[pair], in_zd.at[pair]),
            (out_zd.at[2 * n, size_y - 1], in_zy.at[n]), (out_yd.at[2 * n, high], in_yz.at[n]),
            (out_xu.at[n], in_xu.at[n]), (out_xd.at[n], in_xd.at[n]),
            (out_xd.at[n], in_yx.at[n]), (out_xd.at[n, high], in_zx.at[n]),
            (out_xu.at[n, low], in_xz.at[n]), (out_xu.at[n], in_xy.at[n]),
        )

    def sent_by(group):
        if 6 <= group < 12:
            return loads.at[(1, 2, 4, 5, 6, 7)[group - 6]]
        return halo_send.at[group if group < 6 else group - 6]

    def halo_copy(n, number, source, landing):
        to = {axis: (place[axis] + step + count[axis]) % count[axis] for axis, step in messages[number][1].items()}
        return pltpu.make_async_remote_copy(
            src_ref=source,
            dst_ref=landing,
            send_sem=sent_by(number),
            recv_sem=halo_got.at[n],
            device_id=to,
            device_id_type=MESH,
        )

    def start_halo(n, numbers):
        for number in numbers:
            @pl.when(within(messages[number][1], 1))
            def _():
                halo_copy(n, number, *views(n)[number]).start()

    def fill_halo(n):
        length = first_of(n)[1]
        planes, pair, rows, row_pair = blank.at[pl.ds(0, length)], blank.at[pl.ds(0, 2)], blank_rows.at[pl.ds(0, length)], blank_rows.at[pl.ds(0, 2)]
        plane, tile = blank.at[0], blank.at[0, pl.ds(0, 8)]
        sources = (planes, pair, rows, row_pair, blank_rows.at[0, 0], tile, plane, plane, plane, tile, tile, plane)
        for number, source in enumerate(sources):
            @pl.when(jnp.logical_not(within(messages[number][1], -1)))
            def _():
                pltpu.make_async_copy(source, views(n)[number][1], halo_got.at[n]).start()

    def wait_halo(n):
        everything = arrivals.at[pl.ds(0, arrival_rows(n, size_y, size_z))]
        pltpu.make_async_copy(everything, everything, halo_got.at[n]).wait()

    def pack(values, high):
        packed = jnp.zeros((size_z, LANES), F32)
        for k, value in enumerate(values):
            for y in range(size_y):
                spot = k * size_y + y
                amount = (spot + 1) % LANES if high else spot
                turned = pltpu.roll(value[y], amount, 1) if amount else value[y]
                packed = jnp.where(lane == spot, turned, packed)
        return packed

    def stage(n, ex, ey, ez, for_y, for_z, for_x):
        start, _ = first_of(n)
        for k, value in enumerate((ex, ey, ez) + for_y):
            out_yu[start + k] = value[size_y - 1]
        for k, value in enumerate((ez, ex)):
            out_yd[2 * n + k] = value[0]
        for k, value in enumerate((ex, ey, ez) + for_z):
            out_zu[start + k] = value[:, size_z - 1 : size_z, :]
        for k, value in enumerate((ey, ex)):
            out_zd[2 * n + k] = value[:, 0:1, :]
        yield
        out_xu[n] = pack((ex, ey, ez) + for_x, True)
        out_xd[n] = pack((ez, ey), False)
        yield

    blank[...] = jnp.zeros(blank.shape, F32)
    blank_rows[...] = jnp.zeros(blank_rows.shape, F32)

    def inner(ahead, axis, value):
        if axis == 0:
            none = jnp.zeros_like(value[:1])
            if ahead:
                return jnp.concatenate([value[1:], none], axis=0) - value
            return value - jnp.concatenate([none, value[:-1]], axis=0)
        length = value.shape[axis]
        spots = row3 if axis == 1 else lane3
        if ahead:
            return jnp.where(spots == length - 1, 0.0, pltpu.roll(value, length - 1, axis)) - value
        return value - jnp.where(spots == 0, 0.0, pltpu.roll(value, 1, axis))

    none = jnp.zeros((size_y - 1, size_z, LANES), F32)

    def at_y(plane, ahead):
        return jnp.concatenate([none, plane[None]] if ahead else [plane[None], none], axis=0)

    def at_z(rows, ahead):
        return jnp.where(row3 == (size_z - 1 if ahead else 0), rows, 0.0)

    def at_x(packed, k, ahead):
        edges = []
        for y in range(size_y):
            spot = k * size_y + y
            amount = (LANES - 1 - spot) if ahead else (LANES - spot) % LANES
            edges.append(pltpu.roll(packed, amount, 1) if amount else packed)
        return jnp.where(lane3 == (size_x - 1 if ahead else 0), jnp.stack(edges, axis=0), 0.0)

    def turn(value, by, axis):
        return pltpu.roll(value, by % value.shape[axis], axis)

    row2 = iota((size_z, LANES), 0)
    lane_row = iota((size_y, 1, LANES), 2)
    half_y = jnp.where(dev > 0, COURANT, 0.0)
    half_z = jnp.where(gz > 0, COURANT, 0.0)
    half_x = jnp.where(xy > 0, COURANT, 0.0)

    zt = pl.multiple_of(jnp.where(gz == 0, 0, size_z - 8), 8)
    depth = STEPS
    extent = size_y + 2 * depth
    quarter = 8 * size_y

    regions = []
    for a in (1, -1, 0):
        for b in (1, -1, 0):
            if a or b:
                source = out_w if b == 0 else out_z.at[1 if b > 0 else 0]
                landing = land_w.at[1 - a] if b == 0 else land_z.at[1 - a, 1 if b > 0 else 0]
                nothing = blank.at[pl.ds(0, 2)] if b == 0 else empty_half.at[pl.ds(0, 2)]
                regions.append((0, {"dev": a, "gz": b}, source, landing, landing, nothing))
    for a in (1, -1, 0):
        for flip in (0, 1):
            if a or flip:
                to = {"dev": a, "flip": flip}
                regions.append((1, to, out_x, land_x.at[1 - a, xy], land_x.at[1 - a, (xy + flip) % 2], empty.at[0]))
    for at, a in enumerate((1, -1)):
        far_count = 6 if a > 0 else 3
        for kind, source, landing, nothing in (
            (2, tile_e.at[at], cap_e.at[at], empty.at[pl.ds(0, 6)]),
            (3, tile_h.at[at], cap_h.at[at], empty),
            (3, tile_f.at[at, pl.ds(0, far_count)], cap_f.at[at, pl.ds(0, far_count)], empty_half.at[pl.ds(0, far_count)]),
        ):
            regions.append((kind, {"dev": a}, source, landing, landing, nothing))

    def group_of(number):
        kind, move = regions[number][:2]
        if kind:
            return len(messages) + 2 + (0 if not move["dev"] else 1 if move["dev"] > 0 else 2)
        for at, (_, other) in enumerate(messages):
            if {axis: step for axis, step in move.items() if step} == other:
                return at
        return len(messages) + (0 if move["dev"] > 0 else 1)

    def region_inside(move, sign):
        return within({axis: step for axis, step in move.items() if axis != "flip" and step}, sign)

    def region_copy(number):
        kind, move, source, landing, _, _ = regions[number]
        to = {axis: (place[axis] + step + count[axis]) % count[axis] for axis, step in move.items() if axis != "flip"}
        if move.get("flip"):
            to["xy"] = (xy + 1) % 2
        return pltpu.make_async_remote_copy(
            src_ref=source,
            dst_ref=landing,
            send_sem=sent_by(group_of(number)),
            recv_sem=region_got.at[min(kind, 2)],
            device_id=to,
            device_id_type=MESH,
        )

    def region_when(number, sign):
        inside = region_inside(regions[number][1], sign)
        return jnp.logical_and(inside, is_end) if regions[number][0] else inside

    def start_regions(kinds):
        for number, region in enumerate(regions):
            if region[0] in kinds:
                @pl.when(region_when(number, 1))
                def _():
                    region_copy(number).start()

    def fill_regions():
        for number, (kind, move, _, _, landing, nothing) in enumerate(regions):
            missing = jnp.logical_not(region_inside(move, -1))

            @pl.when(jnp.logical_and(missing, is_end) if kind else missing)
            def _():
                pltpu.make_async_copy(nothing, landing, region_got.at[min(kind, 2)]).start()

    def wait_region(which):
        length = (4 * size_z + 6 * 8, 5 * 8, 2 * (6 + 8) * 8 + (6 + 3) * 4)[which]
        everything = arrivals.at[pl.ds(0, length)]
        pltpu.make_async_copy(everything, everything, region_got.at[which]).wait()

    def window(slots, amount_of):
        rows = slots[0].shape[1]
        spot = iota((rows, LANES), 1)
        packs = []
        for part in range(2):
            packed = jnp.full((rows, LANES), COURANT, F32)
            for c in range(4 * part, min(4 * part + 4, len(slots))):
                for y in range(size_y):
                    base = quarter * (c % 4) + 8 * y
                    turned = pltpu.roll(slots[c][y], amount_of(base), 1)
                    packed = jnp.where(jnp.logical_and(spot >= base, spot < base + 8), turned, packed)
            packs.append(packed)
        return packs

    empty[...] = jnp.zeros(empty.shape, F32)
    empty_half[...] = jnp.zeros(empty_half.shape, F32)
    lhs[...] = jnp.zeros(lhs.shape, BF16)
    pl.semaphore_wait(barrier, beside)
    pass_on()
    loading[0].wait()

    @pl.when(is_end)
    def _():
        tile = pl.ds(zt, 8)
        for c in range(3):
            for i in range(2):
                tile_e[0, 2 * c + i] = fields[c, size_y - 2 + i, tile, :]
                tile_e[1, 2 * c + i] = fields[c, i, tile, :]

    start_regions((2,))
    loading[3].wait()
    permit[...] = COURANT / permit[...]
    own = window([fields[c] for c in range(6)] + [permit[...]], lambda base: (base - (x_wall - 4) + 2 * LANES) % LANES)
    for part in range(2):
        out_w[part] = own[part]
        land_w[1, part] = own[part]
        out_z[0, part] = own[part][:4]
        out_z[1, part] = own[part][size_z - 4 :]
    start_regions((0,))

    @pl.when(is_end)
    def _():
        tile = pl.ds(zt, 8)
        for i in range(2):
            for c in range(3):
                tile_h[0, 2 * c + i] = fields[3 + c, size_y - 2 + i, tile, :]
                tile_h[1, 2 * c + i] = fields[3 + c, i, tile, :]
            tile_h[0, 6 + i] = permit[size_y - 2 + i, tile, :]
            tile_h[1, 6 + i] = permit[i, tile, :]
        for c in range(6):
            value = fields[c, size_y - 3, tile, :]
            tile_f[0, c] = jnp.where(gz == 0, value, turn(value, 1, 0))[4:]
            if c < 3:
                value = fields[c, 2, tile, :]
                tile_f[1, c] = jnp.where(gz == 0, turn(value, -1, 0), value)[:4]
        eight = iota((8, LANES), 1)
        packed = jnp.full((8, LANES), COURANT, F32)
        for c in range(7):
            values = permit[:, tile, :] if c == 6 else fields[c, :, tile, :]
            for y in range(size_y):
                base = quarter * (c % 4) + 8 * y + 4 * (c // 4)
                turned = pltpu.roll(values[y], (base + 4 * (1 - xy)) % LANES, 1)
                packed = jnp.where(jnp.logical_and(eight >= base, eight < base + 4), turned, packed)
        out_x[...] = packed
        land_x[1, xy] = packed

    @pl.when(jnp.logical_not(is_end))
    def _():
        land_x[...] = jnp.zeros(land_x.shape, F32)

    start_regions((1,))
    start_regions((3,))
    for copy in loading[1:3] + loading[4:]:
        copy.wait()
    for _ in stage(0, *(fields[c] for c in range(3)), (fields[3], fields[5]), (fields[3], fields[4]), (fields[4], fields[5])):
        pass
    start_halo(0, (4, 5, 8, 11, 9, 10, 0, 1, 2, 3, 6, 7))
    fill_regions()
    for n in range(STEPS):
        fill_halo(n)
    geometry()
    run_s, run_c = sincos((phase[0] + 0.5 * ANGULAR_STEP * (iota((8, LANES), 0).astype(F32) + 1.0)) * (0.5 / math.pi))
    for n in range(STEPS):
        tables_of(n)

    def relay(k, carry):
        hear()
        pass_on()
        return carry

    lax.fori_loop(0, slabs - 3, relay, 0)

    def half_of(n):
        return run_c[2 * n : 2 * n + 1, :], run_s[2 * n : 2 * n + 1, :]

    def full_of(n):
        return run_c[2 * n + 1 : 2 * n + 2, :], run_s[2 * n + 1 : 2 * n + 2, :]

    cap_sum[...] = jnp.zeros(cap_sum.shape, F32)
    own_walls = walls.at[gz]
    own_walls[...] = jnp.zeros((8, LANES), F32)
    lanes8 = iota((1, LANES), 1)
    owner_row = jnp.zeros((1, LANES), F32)
    for p in range(size_y):
        owner_row = jnp.where(lanes8 == 8 * gz + p, (wall_owner[0, p] + 1).astype(F32), owner_row)
    own_walls[pl.ds(size_y, 1), :] = owner_row
    gathered = jnp.zeros((size_z, LANES), F32)
    for y in range(size_y):
        for c in range(8):
            k = c % 4
            from_c = X_PICKS[k] + (6 if c >= 4 else 0)
            turned = pltpu.roll(spectra[from_c, y], (8 * y + c - x_wall + 2 * LANES) % LANES, 1)
            gathered = jnp.where(lane == 8 * y + c, turned, gathered)
            from_c = Z_PICKS[k] + (6 if c >= 4 else 0)
            low = spectra[from_c, y, pl.ds(ZB, 1), :]
            high = spectra[from_c, y, pl.ds(size_z - 1 - ZB, 1), :]
            cap_plane[pl.ds(8 * y + c, 1), :] = jnp.where(gz == 0, low, high)

    def spread_out(source_of, rows, shift_of, masks):
        spot = iota((rows, LANES), 1)
        values = []
        for c in range(8):
            value = jnp.zeros((rows, LANES), F32)
            first = 0
            for dy, planes in enumerate((depth, size_y, depth)):
                start = quarter * (c % 4) + (8 * (size_y - depth) if dy == 0 else 0)
                last = first + 8 * planes
                inside = jnp.logical_and(spot >= first, spot < last)
                for side in range(masks):
                    chosen = inside if masks == 1 else jnp.logical_and(inside, spot % 8 // 4 == side)
                    value = jnp.where(chosen, turn(source_of(dy, c, side), first - start + shift_of(c, side), 1), value)
                first = last
            values.append(value)
        return values

    def steps_of(values, visit):
        ex, ey, ez, hx, hy, hz, r, k = values
        for n in range(STEPS):
            before = (ez, ey)
            hx = hx - k * ((turn(ez, -8, 1) - ez) - (turn(ey, -1, 0) - ey))
            hy = hy - k * ((turn(ex, -1, 0) - ex) - (turn(ez, -1, 1) - ez))
            hz = hz - k * ((turn(ey, -1, 1) - ey) - (turn(ex, -8, 1) - ex))
            ex = ex + r * ((hz - turn(hz, 8, 1)) - (hy - turn(hy, 1, 0)))
            ey = ey + r * ((hx - turn(hx, 1, 0)) - (hz - turn(hz, 1, 1)))
            ez = ez + r * ((hy - turn(hy, 1, 1)) - (hx - turn(hx, 8, 1)))
            visit(n, before, ey, ez, hy, hz)

    wait_region(0)

    @pl.when(is_end)
    def _():
        wait_region(1)

    sums = [jnp.zeros((size_z, LANES), F32) for _ in range(8)]

    def add_up(n, before, ey, ez, hy, hz):
        for at, (value, (co, si)) in enumerate(((hz, half_of(n)), (hy, half_of(n)), (ez, full_of(n)), (ey, full_of(n)))):
            value = value[:size_z]
            sums[at] = sums[at] + value * co
            sums[4 + at] = sums[4 + at] - value * si

    folded = [
        [
            jnp.concatenate([
                land_w[dy, part], land_z[dy, 0, part], land_z[dy, 1, part],
            ], axis=0)
            for part in range(2)
        ]
        for dy in range(3)
    ]
    border_e, border_h = [], []

    def keep(n, before, ey, ez, hy, hz):
        border_e.append(before)
        border_h.append((hz, hy))

    steps_of(spread_out(lambda dy, c, side: folded[dy][c // 4], size_z + 8, lambda c, side: 0, 1), add_up)
    steps_of(spread_out(lambda dy, c, side: land_x[dy, side], 8, lambda c, side: 4 * side - 4 * (c // 4), 2), keep)
    for c in range(8):
        chosen = jnp.logical_and(lane % 8 == c, lane < 8 * size_y)
        gathered = gathered + jnp.where(chosen, turn(sums[c], c - 8 * depth - 4, 1), 0.0)
    row_sign = jnp.where(jnp.logical_and(iota((half_rows, LANES), 0) % 4 > 0, iota((half_rows, LANES), 0) % 4 < 3), 1.0, -1.0)
    wall_cells = jnp.transpose(gathered)[:half_rows] * (row_sign[:, :size_z] * facing_x)
    for at, part in enumerate(split(wall_cells * norm)):
        lhs[pl.ds(at * all_rows + half_rows, half_rows), pl.ds(size_x, size_z)] = part


    @pl.when(is_end)
    def _():
        wait_region(2)
        tile = pl.ds(zt, 8)
        eight = iota((8, LANES), 1)
        left, right = jnp.where(xy == 0, 1.0, 0.0), jnp.where(xy == 0, 0.0, 1.0)
        behind, ahead = jnp.where(dev > 0, COURANT, 0.0), jnp.where(dev < devs - 1, COURANT, 0.0)

        missing = jnp.zeros((4, LANES), F32)

        def behind_far(half):
            value = jnp.concatenate([missing, half], axis=0)
            return jnp.where(gz == 0, value, turn(value, -1, 0))

        def ahead_far(half):
            value = jnp.concatenate([half, missing], axis=0)
            return jnp.where(gz == 0, turn(value, 1, 0), value)

        def column(c, held_far, near, offset, ahead_too):
            planes = [behind_far(held_far)] + [near[0, 2 * offset + i] for i in range(2)]
            planes += [fields[c, y, tile, :] for y in range(size_y)] + [near[1, 2 * offset + i] for i in range(2)]
            return planes + ([ahead_far(cap_f[1, offset])] if ahead_too else [])

        e = [column(c, cap_f[0, c], cap_e, c, True) for c in range(3)]
        h = [column(3 + c, cap_f[0, 3 + c], cap_h, c, False) for c in range(3)]
        rates = [None] + [cap_h[0, 6 + i] for i in range(2)] + [permit[y, tile, :] for y in range(size_y)] + [cap_h[1, 6 + i] for i in range(2)]
        coefs = [behind] * depth + [COURANT] * size_y + [ahead] * depth

        def next_x(value, border, i):
            return jnp.where(eight == LANES - 1, turn(border, LANES - 1 - (8 * i + 4), 1), turn(value, -1, 1))

        def last_x(value, border, i):
            return jnp.where(eight == 0, turn(border, -(8 * i + 3), 1), turn(value, 1, 1))

        totals_of = [[jnp.zeros((8, LANES), F32) for _ in range(8)] for _ in range(size_y)]
        for n in range(STEPS):
            bz, by = (value * left for value in border_e[n])
            fx, fy, fz = [list(v) for v in h]
            for i in range(n, extent - 1 - n):
                xs, ys, zs = e[0][i], e[1][i], e[2][i]
                fx[i] = h[0][i] - coefs[i] * ((e[2][i + 1] - zs) - (turn(ys, -1, 0) - ys))
                fy[i] = h[1][i] - coefs[i] * ((turn(xs, -1, 0) - xs) - (next_x(zs, bz, i) - zs))
                fz[i] = h[2][i] - coefs[i] * ((next_x(ys, by, i) - ys) - (e[0][i + 1] - xs))
            h = [fx, fy, fz]
            bz, by = (value * right for value in border_h[n])
            gx, gy, gz_ = [list(v) for v in e]
            for i in range(n + 1, extent - 1 - n):
                xs, ys, zs = h[0][i], h[1][i], h[2][i]
                gx[i] = e[0][i] + rates[i] * ((zs - h[2][i - 1]) - (ys - turn(ys, 1, 0)))
                gy[i] = e[1][i] + rates[i] * ((xs - turn(xs, 1, 0)) - (zs - last_x(zs, bz, i)))
                gz_[i] = e[2][i] + rates[i] * ((ys - last_x(ys, by, i)) - (xs - h[0][i - 1]))
            e = [gx, gy, gz_]
            for y in range(size_y):
                i = depth + y
                for at, (value, (co, si)) in enumerate(((h[1][i], half_of(n)), (h[0][i], half_of(n)), (e[1][i], full_of(n)), (e[0][i], full_of(n)))):
                    totals_of[y][at] = totals_of[y][at] + value * co
                    totals_of[y][4 + at] = totals_of[y][4 + at] - value * si
        for y in range(size_y):
            for c in range(8):
                value = totals_of[y][c]
                cap_sum[pl.ds(8 * y + c, 1), :] = jnp.where(gz == 0, value[ZB : ZB + 1], value[7 - ZB : 8 - ZB])

    def advance(n, ghosts):
        fields_from, spec_from = (fields, spectra) if n == 0 else (fields_out, spectra_out)
        ex, ey, ez, hx, hy, hz = (fields_from[c] for c in range(6))
        rate = permit[...]
        hx = hx - COURANT * (inner(True, 0, ez) - inner(True, 1, ey))
        hy = hy - COURANT * (inner(True, 1, ex) - inner(True, 2, ez))
        hz = hz - COURANT * (inner(True, 2, ey) - inner(True, 0, ex))
        wait_halo(n)
        start, _ = first_of(n)
        xp = in_xd[n]
        hx = hx - COURANT * (at_y(in_yd[2 * n], True) - at_z(in_zd[2 * n], True))
        hy = hy - COURANT * (at_z(in_zd[2 * n + 1], True) - at_x(xp, 0, True))
        hz = hz - COURANT * (at_x(xp, 1, True) - at_y(in_yd[2 * n + 1], True))

        ax, ay, az = in_yu[start], in_yu[start + 1], in_yu[start + 2]
        bx, by, bz = in_zu[start], in_zu[start + 1], in_zu[start + 2]
        c_ex, own = in_xu[n], out_xd[n]
        if n == 0:
            y_hx, y_hz = in_yu[3], in_yu[4]
            z_hx, z_hy = in_zu[3], in_zu[4]
            x_hy, x_hz = turn(c_ex, -3 * size_y, 1), turn(c_ex, -4 * size_y, 1)
        else:
            y_hx, y_hz, z_hx, z_hy, x_hy, x_hz = ghosts
        ay_z = jnp.where(row2 == size_z - 1, in_zy[n], turn(ay, -1, 0))
        ay_x = jnp.where(lane == size_x - 1, turn(in_yx[n], -2 * size_y, 1), turn(ay, -1, 1))
        y_hx = y_hx - half_y * ((ez[0] - az) - (ay_z - ay))
        y_hz = y_hz - half_y * ((ay_x - ay) - (ex[0] - ax))
        bz_y = jnp.concatenate([bz[1:], in_yz[n, 7:8, :][None]], axis=0)
        corner = in_zx[n, 7:8, :]
        bz_x = jnp.stack([turn(corner, -1 - y, 1) for y in range(size_y)], axis=0)
        bz_x = jnp.where(lane_row == size_x - 1, bz_x, jnp.stack([turn(bz[y], -1, 1) for y in range(size_y)], axis=0))
        z_hx = z_hx - half_z * ((bz_y - bz) - (ey[:, 0:1, :] - by))
        z_hy = z_hy - half_z * ((ex[:, 0:1, :] - bx) - (bz_x - bz))
        c_z = jnp.where(row2 == size_z - 1, in_xz[n, 0:1, :], turn(c_ex, -1, 0))
        c_y = jnp.where(lane == size_y - 1, turn(in_xy[n], size_y - 1, 1), turn(c_ex, -1, 1))
        x_hy = x_hy - half_x * ((c_z - c_ex) - (own - turn(c_ex, -2 * size_y, 1)))
        x_hz = x_hz - half_x * ((turn(own, -size_y, 1) - turn(c_ex, -size_y, 1)) - (c_y - c_ex))

        ex = ex + rate * (inner(False, 0, hz) - inner(False, 1, hy))
        ey = ey + rate * (inner(False, 1, hx) - inner(False, 2, hz))
        ez = ez + rate * (inner(False, 2, hy) - inner(False, 0, hx))
        ex = ex - rate * (at_y(y_hz, False) - at_z(z_hy, False))
        ey = ey - rate * (at_z(z_hx, False) - at_x(x_hz, 0, False))
        ez = ez - rate * (at_x(x_hy, 0, False) - at_y(y_hx, False))
        if n < STEPS - 1:
            staging = stage(n + 1, ex, ey, ez, (), (), ())
            next(staging)
            start_halo(n + 1, (4, 5, 0, 1, 2, 3))
            next(staging)
            start_halo(n + 1, (8, 11, 9, 10, 6, 7))
        half_c, half_s = run_c[2 * n : 2 * n + 1, :], run_s[2 * n : 2 * n + 1, :]
        for c, value in enumerate((hx, hy, hz)):
            spectra_out[3 + c] = spec_from[3 + c] + value * half_c
            spectra_out[9 + c] = spec_from[9 + c] - value * half_s
        full_c, full_s = run_c[2 * n + 1 : 2 * n + 2, :], run_s[2 * n + 1 : 2 * n + 2, :]
        for c, value in enumerate((ex, ey, ez)):
            spectra_out[c] = spec_from[c] + value * full_c
            spectra_out[6 + c] = spec_from[6 + c] - value * full_s
        for c, value in enumerate((ex, ey, ez, hx, hy, hz)):
            fields_out[c] = value
        return y_hx, y_hz, z_hx, z_hy, x_hy, x_hz

    sub = iota((8, LANES), 0)
    caps_now = (cap_plane[...] + cap_sum[...]) * (row_sign * (facing_z * end_weight))
    cap_plane[...] = caps_now
    for at, part in enumerate(split(caps_now * norm)):
        lhs[pl.ds(at * all_rows, half_rows), pl.ds(0, size_x)] = part

    def wall_copy(k, ref=None):
        held = walls.at[gz] if ref is None else ref
        return pltpu.make_async_remote_copy(
            src_ref=held,
            dst_ref=held,
            send_sem=loads.at[8],
            recv_sem=wall_got,
            device_id={"gz": (gz + k) % slabs},
            device_id_type=MESH,
        )

    def cap_copy(k, at):
        return pltpu.make_async_remote_copy(
            src_ref=caps.at[at],
            dst_ref=caps.at[at],
            send_sem=cap_send,
            recv_sem=cap_got.at[at],
            device_id={"gz": (gz + k) % slabs},
            device_id_type=MESH,
        )

    sign = jnp.where(sub < 4, -1.0, 1.0)

    def far_of(j):
        rows = lhs[...]
        by_high = jnp.dot(rows, table_hi[j], preferred_element_type=F32)
        by_low = jnp.dot(rows[:all_rows], table_lo[j], preferred_element_type=F32)
        product = by_high[:all_rows] + by_high[all_rows:] + by_low
        theta = jnp.zeros((8, LANES), F32)
        phi = jnp.zeros((8, LANES), F32)
        for face in range(2):
            sum_c = jnp.zeros((8, LANES), F32)
            sum_s = jnp.zeros((8, LANES), F32)
            for y in range(size_y):
                g = face * size_y + y
                tile = product[8 * g : 8 * g + 8]
                tile = tile[:, :LANES] + sign * pltpu.roll(tile[:, LANES:], 4, 0)
                sum_c = sum_c + tile * phases[j, 0, pl.ds(g, 1), :]
                sum_s = sum_s + tile * phases[j, 1, pl.ds(g, 1), :]
            far = sum_c + sign * pltpu.roll(sum_s, 4, 0)
            theta = theta + weights[j, 2 * face] * far
            phi = phi + weights[j, 2 * face + 1] * far

        def four(values):
            pairs = values + pltpu.roll(values, 7, 0)
            return pairs + pltpu.roll(pairs, 6, 0)

        both = jnp.where(sub % 4 == 1, pltpu.roll(four(phi), 1, 0), four(theta))
        parts_out[j] = jnp.where(sub < 2, both, pltpu.roll(both, 6, 0))[:4]

    bunch = per * max(1, 4 // per)
    together = bunch // per
    upper = jnp.where(gz >= slabs // 2, 1, 0)
    near = (upper * across + dev * xys + xy) % owners

    def partner(number):
        other, bit = 0, 1
        while bit < owners:
            other = other + bit * ((near // bit + number // bit) % 2)
            bit *= 2
        return other

    def flat_of(owner):
        return (slabs // 2 - 1) * across + owner

    def part_copy(owner, source):
        return pltpu.make_async_remote_copy(
            src_ref=parts_out.at[pl.ds(owner * per, per)],
            dst_ref=parts_in.at[source],
            send_sem=loads.at[0],
            recv_sem=part_got,
            device_id=ident(flat_of(owner)),
            device_id_type=MESH,
        )

    mine = me - flat_of(0)
    leads = jnp.logical_and(mine >= 0, mine < owners)

    def far_and_send(number, carry):
        several = [partner(owners - 1 - together * number - m) for m in range(together)]
        for owner in several:
            for m in range(per):
                far_of(owner * per + m)
        for owner in several:
            @pl.when(owner != mine)
            def _():
                part_copy(owner, me).start()

        return carry

    hear()
    lax.fori_loop(0, owners // together, far_and_send, 0)

    ghosts = advance(0, None)
    for y in range(size_y):
        cells = jnp.concatenate([wall_cells[8 * y : 8 * y + 8], jnp.zeros((8, LANES - size_z), F32)], axis=1)
        own_walls[pl.ds(y, 1), :] = jnp.sum(stagger(cells, PATCH), axis=0, keepdims=True)
    for k in range(1, slabs):
        wall_copy(k).start()
    for at, holder in enumerate((0, slabs - 1)):
        @pl.when(gz == holder)
        def _():
            for y in range(size_y):
                caps[at, pl.ds(8 * y, 8), :] = block_transpose(cap_plane[pl.ds(8 * y, 8), :])
            for k in range(1, slabs):
                cap_copy(k, at).start()

    def total_copy(k, owner, ref=None):
        held = totals.at[pl.ds(owner * per, per)] if ref is None else ref
        return pltpu.make_async_remote_copy(
            src_ref=held,
            dst_ref=held,
            send_sem=loads.at[3],
            recv_sem=total_got.at[owner // together],
            device_id=ident((me + k) % peers),
            device_id_type=MESH,
        )

    @pl.when(leads)
    def _():
        everyone = parts_in.at[pl.ds(0, peers - 1)]
        pltpu.make_async_remote_copy(
            src_ref=everyone, dst_ref=everyone, send_sem=loads.at[0], recv_sem=part_got, device_id={"gz": gz}, device_id_type=MESH
        ).wait_recv()
        parts_in[me] = parts_out[pl.ds(mine * per, per)]
        totals[pl.ds(mine * per, per)] = jnp.sum(parts_in[...], axis=0)
        for k in sorted(range(slabs), key=lambda k: -min(k, slabs - k)):
            row = (gz + k) % slabs * across

            def send(r, carry):
                to = row + (dev * xys + xy + r) % across

                @pl.when(to != me)
                def _():
                    total_copy((to - me + peers) % peers, mine).start()

                return carry

            lax.fori_loop(0, across, send, 0, unroll=across <= 4)


    def choose(mine, share, records):
        length = mine.shape[1]
        before = jnp.where(iota((length, length), 0) < iota((length, length), 1), 1.0, 0.0).astype(BF16)
        ones = jnp.broadcast_to(jnp.where(mine, 1.0, 0.0), (8, length))
        rank = jnp.dot(ones.astype(BF16), before, preferred_element_type=F32)
        wanted = iota((8, length), 0).astype(F32)
        chooser = jnp.where(rank == wanted, ones, 0.0)
        return jnp.dot(chooser, records, precision=HIGHEST, preferred_element_type=F32)[:share]

    def choose_owned():
        wall_copy(1, walls.at[pl.ds(0, slabs - 1)]).wait_recv()
        for at, holder in enumerate((0, slabs - 1)):
            @pl.when(gz != holder)
            def _():
                cap_copy(1, at).wait_recv()
        all_walls = walls[...]
        owner_all = jnp.sum(all_walls[:, size_y : size_y + 1, :], axis=0)[:, : 8 * slabs]
        cap_share = (owned_out.shape[0] - size_y) // 2
        owned_out[pl.ds(0, size_y), 0, :] = choose(
            owner_all == (gz + 1).astype(F32), size_y, all_walls.reshape(8 * slabs, LANES)
        )
        for at in range(2):
            owned_out[pl.ds(size_y + at * cap_share, cap_share), 0, :] = choose(
                cap_owner[pl.ds(at, 1), :] == gz, cap_share, caps[at]
            )

    def intensity_of(field):
        return jnp.sum(field * field, axis=0, keepdims=True)

    def slope_of(j):
        field = totals[j]
        residual = aim[pl.ds(j, 1), :].astype(F32) * (intensity_of(field) - target[pl.ds(j, 1), :])
        return 2.0 * residual * field

    def adjoint_of(j):
        slope = slope_of(j)
        by_theta = jnp.where(sub < 4, slope[0:1], slope[2:3])
        by_phi = jnp.where(sub < 4, slope[1:2], slope[3:4])
        tiles = []
        for face in range(2):
            vector = weights[j, 2 * face] * by_theta + weights[j, 2 * face + 1] * by_phi
            turned = -sign * pltpu.roll(vector, 4, 0)
            for y in range(size_y):
                g = face * size_y + y
                tile = vector * phases[j, 0, pl.ds(g, 1), :] + turned * phases[j, 1, pl.ds(g, 1), :]
                tiles.append(jnp.concatenate([tile, -sign * pltpu.roll(tile, 4, 0)], axis=1))
        rows = jnp.concatenate(tiles, axis=0)
        high, low = split(rows)
        both = jnp.concatenate([high, low], axis=0)
        across = (((1,), (1,)), ((), ()))
        by_high = lax.dot_general(both, table_hi[j], across, preferred_element_type=F32)
        by_low = lax.dot_general(high, table_lo[j], across, preferred_element_type=F32)
        return by_high[:all_rows] + by_high[all_rows:] + by_low

    def adjoint_wait(number):
        several = [partner(together * number + m) for m in range(together)]
        batch = several[0] // together
        ours = jnp.logical_and(leads, mine // together == batch)

        @pl.when(jnp.logical_not(ours))
        def _():
            total_copy(1, several[0], totals.at[pl.ds(batch * bunch, bunch)]).wait_recv()

        if together > 1:
            @pl.when(ours)
            def _():
                total_copy(1, several[0], totals.at[pl.ds(batch * bunch, bunch - per)]).wait_recv()

        return several

    def adjoint_some(numbers, total):
        several = [owner for number in numbers for owner in adjoint_wait(number)]
        for owner in several:
            for m in range(per):
                total = total + adjoint_of(owner * per + m)
        return total

    rounds = owners // together
    ghosts = advance(1, ghosts)
    choose_owned()
    gradient = adjoint_some((0,), jnp.zeros((all_rows, size_x + size_z), F32))
    gradient = adjoint_some(range(1, rounds), gradient)
    intensity_out[...] = intensity_of(totals[me // ratio])
    advance(2, ghosts)
    for y in range(size_y):
        wall = gradient[half_rows + 8 * y : half_rows + 8 * y + 8, size_x:]
        wall = jnp.concatenate([wall, jnp.zeros((8, LANES - size_z), F32)], axis=1)
        wall = stagger(wall, PATCH)
        adjoint_out[pl.ds(y, 1), 0, :] = jnp.sum(wall, axis=0, keepdims=True) * norm
        cap = block_transpose(gradient[8 * y : 8 * y + 8, :size_x] * (norm * end_weight))
        adjoint_out[pl.ds(size_y + 8 * y, 8), 0, :] = cap

    groups_sent = {}
    for number, (landing, move) in enumerate(messages):
        groups_sent[number] = [within(move, 1), math.prod(landing.shape) // LANES]
    for number, (_, _, source, _, _, _) in enumerate(regions):
        entry = groups_sent.setdefault(group_of(number), [region_when(number, 1), 0])
        entry[1] += math.prod(source.shape) // LANES
    for group, (sent, rows_sent) in groups_sent.items():
        @pl.when(sent)
        def _():
            everything = arrivals.at[pl.ds(0, rows_sent)]
            pltpu.make_async_copy(everything, everything, sent_by(group)).wait()

    def parts_sent(ref):
        pltpu.make_async_remote_copy(
            src_ref=ref, dst_ref=ref, send_sem=loads.at[0], recv_sem=part_got, device_id={"gz": gz}, device_id_type=MESH
        ).wait_send()

    @pl.when(leads)
    def _():
        parts_sent(parts_out.at[pl.ds(0, (owners - 1) * per)])
        total_copy(1, 0, parts_in.at[pl.ds(0, peers - 1)]).wait_send()

    @pl.when(jnp.logical_not(leads))
    def _():
        parts_sent(parts_out)

    wall_copy(1, walls.at[pl.ds(0, slabs - 1)]).wait_send()
    for at, holder in enumerate((0, slabs - 1)):
        @pl.when(gz == holder)
        def _():
            sent = weights.at[pl.ds(0, slabs - 1)]
            pltpu.make_async_copy(sent, sent, cap_send).wait()


def write_out(*refs):
    copies = [pltpu.make_async_copy(refs[i], refs[5 + i], refs[10].at[i]) for i in range(5)]
    for copy in copies:
        copy.start()
    for copy in copies:
        copy.wait()


def local(fields, spectra, permittivity, phase_start, wall_owner, cap_owner, dir_index, target, aim_mask):
    slabs, devs, xys = (lax.axis_size(a) for a in ("gz", "dev", "xy"))
    peers = slabs * devs * xys
    size_y, size_z, size_x = permittivity.shape
    assert size_z == PATCH and size_x == LANES and size_y == 4 and xys == 2
    directions = dir_index.shape[0]
    chunks = directions // LANES
    ratio = peers // chunks
    per = max(1, chunks // (2 * devs * xys))
    owners = chunks // per
    share = directions // peers
    cap_count = size_y * size_x // PATCH
    owned = size_y + 2 * (cap_count // slabs)
    rows = 16 * size_y
    depth = size_x + size_z
    planes, pairs = 5 + 3 * (STEPS - 1), 2 * STEPS
    halos = (
        (planes, size_z, LANES), (pairs, size_z, LANES), (planes, size_y, 1, LANES), (pairs, size_y, 1, LANES),
        (STEPS, size_z, LANES), (STEPS, size_z, LANES),
        (STEPS, 1, LANES), (STEPS, 8, LANES), (STEPS, size_z, LANES), (STEPS, 8, LANES), (STEPS, 8, LANES), (STEPS, size_z, LANES),
    )
    vmem = pl.BlockSpec(memory_space=pltpu.VMEM)
    anywhere = pl.BlockSpec(memory_space=pl.ANY)
    dma = pltpu.SemaphoreType.DMA
    outs = pl.pallas_call(
        functools.partial(kernel, (slabs, devs, xys)),
        out_shape=(
            pltpu.VMEM(fields.shape, F32),
            pltpu.VMEM(spectra.shape, F32),
            pltpu.VMEM((owned, 1, LANES), F32),
            pltpu.VMEM((1, LANES), F32),
            pltpu.VMEM((size_y + cap_count, 1, LANES), F32),
        ),
        in_specs=[anywhere] * 9,
        out_specs=(vmem,) * 5,
        scratch_shapes=[
            *(pltpu.VMEM(shape, F32) for shape in halos[:6]),
            *(pltpu.VMEM(shape, F32) for shape in halos),
            pltpu.VMEM((5, size_z, LANES), F32),
            pltpu.VMEM((5, size_y, 1, LANES), F32),
            pltpu.VMEM((376, 1, LANES), F32),
            pltpu.VMEM((2, size_z, LANES), F32),
            pltpu.VMEM((2, 2, 4, LANES), F32),
            pltpu.VMEM((8, LANES), F32),
            pltpu.VMEM((3, 2, size_z, LANES), F32),
            pltpu.VMEM((3, 2, 2, 4, LANES), F32),
            pltpu.VMEM((3, 2, 8, LANES), F32),
            *(pltpu.VMEM(shape, F32) for shape in ((2, 6, 8, LANES), (2, 8, 8, LANES), (2, 6, 4, LANES)) * 2),
            pltpu.VMEM((8, 8, LANES), F32),
            pltpu.VMEM((6, 4, LANES), F32),
            pltpu.VMEM((8 * size_y, LANES), F32),
            pltpu.VMEM(fields.shape, F32),
            pltpu.VMEM(spectra.shape, F32),
            pltpu.VMEM(permittivity.shape, F32),
            pltpu.SMEM((1,), F32),
            pltpu.SMEM(wall_owner.shape, jnp.int32),
            pltpu.VMEM(cap_owner.shape, jnp.int32),
            pltpu.VMEM((chunks, LANES), jnp.int32),
            pltpu.VMEM((chunks, LANES), F32),
            pltpu.VMEM((chunks, LANES), jnp.int32),
            pltpu.VMEM((8, chunks, LANES), F32),
            pltpu.VMEM((chunks, 4, 8, LANES), F32),
            pltpu.VMEM((chunks, 2, 2 * size_y, LANES), F32),
            pltpu.VMEM((chunks, depth, 2 * LANES), BF16),
            pltpu.VMEM((chunks, depth, 2 * LANES), BF16),
            pltpu.VMEM((8 * size_y, LANES), F32),
            pltpu.VMEM((2 * rows, depth), BF16),
            pltpu.VMEM((chunks, 4, LANES), F32),
            pltpu.VMEM((peers, per, 4, LANES), F32),
            pltpu.VMEM((chunks, 4, LANES), F32),
            pltpu.VMEM((slabs, 8, LANES), F32),
            pltpu.VMEM((2, cap_count, LANES), F32),
            dma((11,)), dma((STEPS,)),
            dma, dma((owners // max(1, 4 // per),)), dma,
            dma, dma((2,)),
            dma((9,)), pltpu.SemaphoreType.REGULAR((2,)), dma((3,)),
        ],
        compiler_params=pltpu.CompilerParams(collective_id=0, has_side_effects=True),
    )(
        fields, spectra, permittivity, phase_start, wall_owner, cap_owner,
        dir_index.reshape(chunks, LANES), target.reshape(chunks, LANES), aim_mask.reshape(chunks, LANES),
    )
    held = (fields.shape, spectra.shape, (owned, 1, LANES), (1, LANES), (size_y + cap_count, 1, LANES))
    fields_new, spectra_new, owned_rows, intensity, adjoint = pl.pallas_call(
        write_out,
        out_shape=tuple(jax.ShapeDtypeStruct(shape, F32) for shape in held),
        in_specs=[pl.BlockSpec(memory_space=pltpu.VMEM)] * 5,
        out_specs=(pl.BlockSpec(memory_space=pl.ANY),) * 5,
        scratch_shapes=[dma((5,))],
    )(*(pltpu.with_memory_space_constraint(out, pltpu.VMEM) for out in outs))
    owned_rows = owned_rows.reshape(1, 1, owned, 1, LANES).transpose(0, 1, 3, 2, 4)
    adjoint = adjoint.reshape(1, 1, size_y + cap_count, 1, LANES).transpose(0, 1, 3, 2, 4)
    intensity = intensity.reshape(LANES)
    if ratio > 1:
        me = (lax.axis_index("gz") * devs + lax.axis_index("dev")) * xys + lax.axis_index("xy")
        intensity = lax.dynamic_slice_in_dim(intensity, (me % ratio) * share, share, 0)
    return (fields_new, spectra_new, owned_rows, intensity, adjoint)


def solution(mesh):
    placed = (
        P("groups", "dev", "gz", "xy"),
        P("groups", "dev", "gz", "xy"),
        P(("groups", "dev"), "gz", "xy"),
        P("groups"),
        P("gz", None),
        P(),
        P(),
        P("groups"),
        P("groups"),
    )
    return jax.shard_map(
        local,
        mesh=mesh,
        in_specs=placed,
        out_specs=(
            P("groups", "dev", "gz", "xy"),
            P("groups", "dev", "gz", "xy"),
            P(("groups", "gz"), "dev", "xy", None, None),
            P(("groups", "gz", "dev", "xy")),
            P(("groups", "gz"), "dev", "xy", None, None),
        ),
        check_vma=False,
    )
```

```python
import functools
import math

import jax
import jax.numpy as jnp
from jax import lax
from jax.experimental import pallas as pl
from jax.experimental.pallas import tpu as pltpu
from jax.sharding import PartitionSpec as P

PATCH = 16
XB = 8
ZB = 4
STEPS = 3
THETAS = 64
COURANT = 0.5
ANGULAR_STEP = 0.3
WAVE_NUMBER = 0.6
LANES = 128
HIGHEST = lax.Precision.HIGHEST
CURRENT_SIGNS = (-1.0, 1.0, 1.0, -1.0)
X_PICKS = (5, 4, 2, 1)
Z_PICKS = (4, 3, 1, 0)
MESH = pl.DeviceIdType.MESH
AXES = ("dev", "gz", "xy")
F32 = jnp.float32
BF16 = jnp.bfloat16


def iota(shape, dim):
    return lax.broadcasted_iota(jnp.int32, shape, dim)


def sincos(turns):
    half = (turns - jnp.floor(turns + 0.5)) * math.pi
    sq = half * half
    sin_h = half * (1.0 + sq * (-1.0 / 6 + sq * (1.0 / 120 + sq * (-1.0 / 5040 + sq * (1.0 / 362880 - sq * (1.0 / 39916800))))))
    cos_h = 1.0 + sq * (-0.5 + sq * (1.0 / 24 + sq * (-1.0 / 720 + sq * (1.0 / 40320 + sq * (-1.0 / 3628800 + sq * (1.0 / 479001600))))))
    return 2.0 * sin_h * cos_h, 1.0 - 2.0 * sin_h * sin_h


def split(values):
    high = values.astype(BF16)
    return high, (values - high.astype(F32)).astype(BF16)


def arrival_rows(n, size_y, size_z):
    length = 5 if n == 0 else 3
    return (length + 2) * (size_z + size_y) + 1 + 3 * 8 + 4 * size_z


def stagger(tile, by):
    row = iota(tile.shape, 0)
    for bit in (1, 2, 4):
        tile = jnp.where(row // bit % 2 == 1, pltpu.roll(tile, by * bit % LANES, 1), tile)
    return tile


def block_transpose(tile):
    on_diagonal = (iota(tile.shape, 1) // PATCH) == iota(tile.shape, 0)
    total = jnp.where(on_diagonal, tile, 0.0)
    for k in range(1, 8):
        turned = pltpu.roll(tile, PATCH * k, 1)
        total = total + pltpu.roll(jnp.where(on_diagonal, turned, 0.0), 8 - k, 0)
    return total


def kernel(
    sizes,
    fields_in, spectra_in, permit_in, phase_in, wall_owner_in, cap_owner_in, dirs_in, target_in, aim_in,
    fields_out, spectra_out, owned_out, intensity_out, adjoint_out,
    out_yu, out_yd, out_zu, out_zd, out_xu, out_xd,
    in_yu, in_yd, in_zu, in_zd, in_xu, in_xd, in_zy, in_yz, in_yx, in_zx, in_xz, in_xy, blank, blank_rows, arrivals,
    out_w, out_z, out_x, land_w, land_z, land_x, tile_e, tile_h, tile_f, cap_e, cap_h, cap_f, empty, empty_half, cap_sum,
    fields, spectra, permit, phase, wall_owner, cap_owner, dirs, target, aim,
    geo, weights, phases, table_hi, table_lo, cap_plane, lhs,
    parts_out, parts_in, totals, walls, caps,
    halo_send, halo_got, part_got, total_got, wall_got, loads, chain, region_got,
):
    slabs, devs, xys = sizes
    peers = slabs * devs * xys
    size_y, size_z, size_x = permit.shape
    chunks = dirs.shape[0]
    ratio = peers // chunks
    across = devs * xys
    per = max(1, chunks // (2 * across))
    owners = chunks // per
    groups = 2 * size_y
    half_rows = 8 * size_y
    all_rows = 2 * half_rows
    gz, dev, xy = lax.axis_index("gz"), lax.axis_index("dev"), lax.axis_index("xy")
    me = (gz * devs + dev) * xys + xy
    place = {"dev": dev, "gz": gz, "xy": xy}
    count = {"dev": devs, "gz": slabs, "xy": xys}

    def ident(flat):
        return {"gz": flat // (devs * xys), "dev": (flat // xys) % devs, "xy": flat % xys}

    pltpu.make_async_copy(fields_in, fields, loads.at[0]).start()
    barrier = pltpu.get_barrier_semaphore()

    for away in (1, -1, 0):
        @pl.when(jnp.logical_and(gz + away >= 0, gz + away < slabs))
        def _():
            def greet(k, carry):
                spot = (dev * xys + xy + k) % across
                to = {"gz": gz + away, "dev": spot // xys, "xy": spot % xys}
                pl.semaphore_signal(barrier, inc=1, device_id=to, device_id_type=MESH)
                return carry

            lax.fori_loop(0 if away else 1, across, greet, 0)

    beside = jnp.where(gz > 0, across, 0) + jnp.where(gz < slabs - 1, across, 0) + across - 1

    def pass_on():
        for at, away in enumerate((1, -1)):
            @pl.when(jnp.logical_and(gz + away >= 0, gz + away < slabs))
            def _():
                to = {"gz": gz + away, "dev": dev, "xy": xy}
                pl.semaphore_signal(chain.at[at], inc=1, device_id=to, device_id_type=MESH)

    def hear():
        for at, away in enumerate((1, -1)):
            @pl.when(jnp.logical_and(gz - away >= 0, gz - away < slabs))
            def _():
                pl.semaphore_wait(chain.at[at], 1)

    loading = [
        pltpu.make_async_copy(source, held, loads.at[number])
        for number, (source, held) in enumerate((
            (fields_in, fields), (dirs_in, dirs), (phase_in, phase), (permit_in, permit), (spectra_in, spectra),
            (wall_owner_in, wall_owner), (cap_owner_in, cap_owner), (target_in, target), (aim_in, aim),
        ))
    ]
    for copy in loading[1:]:
        copy.start()

    def geometry():
        index = dirs[...]
        sin_t, cos_t = sincos(((index // THETAS).astype(F32) + 0.5) * (0.5 / THETAS))
        sin_f, cos_f = sincos((index % THETAS).astype(F32) * (1.0 / THETAS))
        wave = WAVE_NUMBER / (2.0 * math.pi)
        for slot, values in enumerate((
            wave * sin_t * cos_f, wave * sin_t * sin_f, wave * cos_t,
            cos_t * cos_f, cos_t * sin_f, -sin_t, -sin_f, cos_f,
        )):
            geo[slot] = values

    grid_x, grid_y, grid_z = size_x * xys, size_y * devs, size_z * slabs
    x_first = (xy * size_x).astype(F32) - (grid_x - 1) / 2.0
    y_first = (dev * size_y).astype(F32) - (grid_y - 1) / 2.0
    z_first = (gz * size_z).astype(F32) - (grid_z - 1) / 2.0
    x_wall = jnp.where(xy == 0, XB, size_x - 1 - XB)
    z_cap = jnp.where(gz == 0, ZB, size_z - 1 - ZB)
    x_face = x_first + x_wall.astype(F32)
    z_face = z_first + z_cap.astype(F32)
    facing_x = jnp.where(xy == 0, -1.0, 1.0)
    facing_z = jnp.where(gz == 0, -1.0, 1.0)
    is_end = jnp.logical_or(gz == 0, gz == slabs - 1)
    end_weight = jnp.where(is_end, 1.0, 0.0)
    norm = 1.0 / math.sqrt(2.0 * (2 * grid_y * grid_z + 2 * grid_y * grid_x))

    def make_tables(j, carry):
        def row(slot):
            return geo[slot, pl.ds(j, 1), :]

        ux, uy, uz = row(0), row(1), row(2)
        blocks = size_x // 8
        far_s, far_c = sincos((iota((blocks, LANES), 0).astype(F32) * 8.0 + x_first) * ux)
        near_s, near_c = sincos(iota((8, LANES), 0).astype(F32) * ux)
        far_s, far_c = far_s[:, None, :], far_c[:, None, :]
        near_s, near_c = near_s[None], near_c[None]
        cos_x = (far_c * near_c - far_s * near_s).reshape(size_x, LANES)
        sin_x = (far_s * near_c + far_c * near_s).reshape(size_x, LANES)
        sin_z, cos_z = sincos((iota((size_z, LANES), 0).astype(F32) + z_first) * uz)
        for at, (x_part, z_part) in enumerate(((cos_x, cos_z), (sin_x, sin_z))):
            lanes = pl.ds(at * LANES, LANES)
            x_high, x_low = split(x_part)
            z_high, z_low = split(z_part)
            table_hi[j, pl.ds(0, size_x), lanes] = x_high
            table_lo[j, pl.ds(0, size_x), lanes] = x_low
            table_hi[j, pl.ds(size_x, size_z), lanes] = z_high
            table_lo[j, pl.ds(size_x, size_z), lanes] = z_low
        which = iota((groups, LANES), 0)
        cell_y = (which % size_y).astype(F32) + y_first
        sin_g, cos_g = sincos(cell_y * uy + jnp.where(which < size_y, z_face * uz, x_face * ux))
        phases[j, 0] = cos_g
        phases[j, 1] = sin_g
        kind = iota((8, LANES), 0) % 4

        def pattern(a, b, c, d):
            return jnp.where(kind == 0, a, jnp.where(kind == 1, b, jnp.where(kind == 2, c, d)))

        tx, ty, tz, fx, fy = row(3), row(4), row(5), row(6), row(7)
        weights[j, 0] = pattern(-tx, -ty, -fx, -fy)
        weights[j, 1] = pattern(-fx, -fy, tx, ty)
        weights[j, 2] = pattern(-ty, -tz, -fy, jnp.zeros_like(fy))
        weights[j, 3] = pattern(-fy, jnp.zeros_like(fy), ty, tz)
        return carry

    windows = STEPS

    def tables_of(window):
        lax.fori_loop(window * chunks // windows, (window + 1) * chunks // windows, make_tables, 0)

    lane = iota((size_z, LANES), 1)
    lane3 = iota((size_y, size_z, LANES), 2)
    row3 = iota((size_y, size_z, LANES), 1)

    messages = (
        (in_yu, {"dev": 1}), (in_yd, {"dev": -1}), (in_zu, {"gz": 1}), (in_zd, {"gz": -1}),
        (in_zy, {"gz": -1, "dev": 1}), (in_yz, {"dev": -1, "gz": 1}),
        (in_xu, {"xy": 1}), (in_xd, {"xy": -1}),
        (in_yx, {"dev": 1, "xy": -1}), (in_zx, {"gz": 1, "xy": -1}), (in_xz, {"xy": 1, "gz": -1}), (in_xy, {"xy": 1, "dev": -1}),
    )

    def within(move, sign):
        inside = True
        for axis, step in move.items():
            spot = place[axis] + sign * step
            inside = jnp.logical_and(inside, jnp.logical_and(spot >= 0, spot < count[axis]))
        return inside

    def first_of(n):
        return (0, 5) if n == 0 else (5 + 3 * (n - 1), 3)

    def views(n):
        start, length = first_of(n)
        planes, pair = pl.ds(start, length), pl.ds(2 * n, 2)
        low, high = pl.ds(0, 8), pl.ds(size_z - 8, 8)
        return (
            (out_yu.at[planes], in_yu.at[planes]), (out_yd.at[pair], in_yd.at[pair]),
            (out_zu.at[planes], in_zu.at[planes]), (out_zd.at[pair], in_zd.at[pair]),
            (out_zd.at[2 * n, size_y - 1], in_zy.at[n]), (out_yd.at[2 * n, high], in_yz.at[n]),
            (out_xu.at[n], in_xu.at[n]), (out_xd.at[n], in_xd.at[n]),
            (out_xd.at[n], in_yx.at[n]), (out_xd.at[n, high], in_zx.at[n]),
            (out_xu.at[n, low], in_xz.at[n]), (out_xu.at[n], in_xy.at[n]),
        )

    def sent_by(group):
        if 6 <= group < 12:
            return loads.at[(1, 2, 4, 5, 6, 7)[group - 6]]
        return halo_send.at[group if group < 6 else group - 6]

    def halo_copy(n, number, source, landing):
        to = {axis: (place[axis] + step + count[axis]) % count[axis] for axis, step in messages[number][1].items()}
        return pltpu.make_async_remote_copy(
            src_ref=source,
            dst_ref=landing,
            send_sem=sent_by(number),
            recv_sem=halo_got.at[n],
            device_id=to,
            device_id_type=MESH,
        )

    def start_halo(n, numbers):
        for number in numbers:
            @pl.when(within(messages[number][1], 1))
            def _():
                halo_copy(n, number, *views(n)[number]).start()

    def fill_halo(n):
        length = first_of(n)[1]
        planes, pair, rows, row_pair = blank.at[pl.ds(0, length)], blank.at[pl.ds(0, 2)], blank_rows.at[pl.ds(0, length)], blank_rows.at[pl.ds(0, 2)]
        plane, tile = blank.at[0], blank.at[0, pl.ds(0, 8)]
        sources = (planes, pair, rows, row_pair, blank_rows.at[0, 0], tile, plane, plane, plane, tile, tile, plane)
        for number, source in enumerate(sources):
            @pl.when(jnp.logical_not(within(messages[number][1], -1)))
            def _():
                pltpu.make_async_copy(source, views(n)[number][1], halo_got.at[n]).start()

    def wait_halo(n):
        everything = arrivals.at[pl.ds(0, arrival_rows(n, size_y, size_z))]
        pltpu.make_async_copy(everything, everything, halo_got.at[n]).wait()

    def pack(values, high):
        packed = jnp.zeros((size_z, LANES), F32)
        for k, value in enumerate(values):
            for y in range(size_y):
                spot = k * size_y + y
                amount = (spot + 1) % LANES if high else spot
                turned = pltpu.roll(value[y], amount, 1) if amount else value[y]
                packed = jnp.where(lane == spot, turned, packed)
        return packed

    def stage(n, ex, ey, ez, for_y, for_z, for_x):
        start, _ = first_of(n)
        for k, value in enumerate((ex, ey, ez) + for_y):
            out_yu[start + k] = value[size_y - 1]
        for k, value in enumerate((ez, ex)):
            out_yd[2 * n + k] = value[0]
        for k, value in enumerate((ex, ey, ez) + for_z):
            out_zu[start + k] = value[:, size_z - 1 : size_z, :]
        for k, value in enumerate((ey, ex)):
            out_zd[2 * n + k] = value[:, 0:1, :]
        yield
        out_xu[n] = pack((ex, ey, ez) + for_x, True)
        out_xd[n] = pack((ez, ey), False)
        yield

    blank[...] = jnp.zeros(blank.shape, F32)
    blank_rows[...] = jnp.zeros(blank_rows.shape, F32)

    def inner(ahead, axis, value):
        if axis == 0:
            none = jnp.zeros_like(value[:1])
            if ahead:
                return jnp.concatenate([value[1:], none], axis=0) - value
            return value - jnp.concatenate([none, value[:-1]], axis=0)
        length = value.shape[axis]
        spots = row3 if axis == 1 else lane3
        if ahead:
            return jnp.where(spots == length - 1, 0.0, pltpu.roll(value, length - 1, axis)) - value
        return value - jnp.where(spots == 0, 0.0, pltpu.roll(value, 1, axis))

    none = jnp.zeros((size_y - 1, size_z, LANES), F32)

    def at_y(plane, ahead):
        return jnp.concatenate([none, plane[None]] if ahead else [plane[None], none], axis=0)

    def at_z(rows, ahead):
        return jnp.where(row3 == (size_z - 1 if ahead else 0), rows, 0.0)

    def at_x(packed, k, ahead):
        edges = []
        for y in range(size_y):
            spot = k * size_y + y
            amount = (LANES - 1 - spot) if ahead else (LANES - spot) % LANES
            edges.append(pltpu.roll(packed, amount, 1) if amount else packed)
        return jnp.where(lane3 == (size_x - 1 if ahead else 0), jnp.stack(edges, axis=0), 0.0)

    def turn(value, by, axis):
        return pltpu.roll(value, by % value.shape[axis], axis)

    row2 = iota((size_z, LANES), 0)
    lane_row = iota((size_y, 1, LANES), 2)
    half_y = jnp.where(dev > 0, COURANT, 0.0)
    half_z = jnp.where(gz > 0, COURANT, 0.0)
    half_x = jnp.where(xy > 0, COURANT, 0.0)

    zt = pl.multiple_of(jnp.where(gz == 0, 0, size_z - 8), 8)
    depth = STEPS
    extent = size_y + 2 * depth
    quarter = 8 * size_y

    regions = []
    for a in (1, -1, 0):
        for b in (1, -1, 0):
            if a or b:
                source = out_w if b == 0 else out_z.at[1 if b > 0 else 0]
                landing = land_w.at[1 - a] if b == 0 else land_z.at[1 - a, 1 if b > 0 else 0]
                nothing = blank.at[pl.ds(0, 2)] if b == 0 else empty_half.at[pl.ds(0, 2)]
                regions.append((0, {"dev": a, "gz": b}, source, landing, landing, nothing))
    for a in (1, -1, 0):
        for flip in (0, 1):
            if a or flip:
                to = {"dev": a, "flip": flip}
                regions.append((1, to, out_x, land_x.at[1 - a, xy], land_x.at[1 - a, (xy + flip) % 2], empty.at[0]))
    for at, a in enumerate((1, -1)):
        far_count = 6 if a > 0 else 3
        for kind, source, landing, nothing in (
            (3, tile_e.at[at], cap_e.at[at], empty.at[pl.ds(0, 6)]),
            (3, tile_h.at[at], cap_h.at[at], empty),
            (2, tile_f.at[at, pl.ds(0, far_count)], cap_f.at[at, pl.ds(0, far_count)], empty_half.at[pl.ds(0, far_count)]),
        ):
            regions.append((kind, {"dev": a}, source, landing, landing, nothing))

    def group_of(number):
        kind, move = regions[number][:2]
        if kind:
            return len(messages) + 2 + (0 if not move["dev"] else 1 if move["dev"] > 0 else 2)
        for at, (_, other) in enumerate(messages):
            if {axis: step for axis, step in move.items() if step} == other:
                return at
        return len(messages) + (0 if move["dev"] > 0 else 1)

    def region_inside(move, sign):
        return within({axis: step for axis, step in move.items() if axis != "flip" and step}, sign)

    def region_copy(number):
        kind, move, source, landing, _, _ = regions[number]
        to = {axis: (place[axis] + step + count[axis]) % count[axis] for axis, step in move.items() if axis != "flip"}
        if move.get("flip"):
            to["xy"] = (xy + 1) % 2
        return pltpu.make_async_remote_copy(
            src_ref=source,
            dst_ref=landing,
            send_sem=sent_by(group_of(number)),
            recv_sem=region_got.at[0 if kind < 2 else 1],
            device_id=to,
            device_id_type=MESH,
        )

    def region_when(number, sign):
        inside = region_inside(regions[number][1], sign)
        return jnp.logical_and(inside, is_end) if regions[number][0] else inside

    def start_regions(kinds):
        for number, region in enumerate(regions):
            if region[0] in kinds:
                @pl.when(region_when(number, 1))
                def _():
                    region_copy(number).start()

    def fill_regions():
        for number, (kind, move, _, _, landing, nothing) in enumerate(regions):
            missing = jnp.logical_not(region_inside(move, -1))

            @pl.when(jnp.logical_and(missing, is_end) if kind else missing)
            def _():
                pltpu.make_async_copy(nothing, landing, region_got.at[0 if kind < 2 else 1]).start()

    def wait_region(which):
        length = (4 * size_z + 6 * 8, 4 * size_z + 6 * 8 + 5 * 8, 2 * (6 + 8) * 8 + (6 + 3) * 4)[which]
        everything = arrivals.at[pl.ds(0, length)]
        pltpu.make_async_copy(everything, everything, region_got.at[which // 2]).wait()

    def window(slots, amount_of):
        rows = slots[0].shape[1]
        spot = iota((rows, LANES), 1)
        packs = []
        for part in range(2):
            packed = jnp.full((rows, LANES), COURANT, F32)
            for c in range(4 * part, min(4 * part + 4, len(slots))):
                for y in range(size_y):
                    base = quarter * (c % 4) + 8 * y
                    turned = pltpu.roll(slots[c][y], amount_of(base), 1)
                    packed = jnp.where(jnp.logical_and(spot >= base, spot < base + 8), turned, packed)
            packs.append(packed)
        return packs

    empty[...] = jnp.zeros(empty.shape, F32)
    empty_half[...] = jnp.zeros(empty_half.shape, F32)
    lhs[...] = jnp.zeros(lhs.shape, BF16)
    pl.semaphore_wait(barrier, beside)
    pass_on()
    loading[0].wait()

    @pl.when(is_end)
    def _():
        tile = pl.ds(zt, 8)
        for c in range(6):
            value = fields[c, size_y - 3, tile, :]
            tile_f[0, c] = jnp.where(gz == 0, value, turn(value, 1, 0))[4:]
            if c < 3:
                value = fields[c, 2, tile, :]
                tile_f[1, c] = jnp.where(gz == 0, turn(value, -1, 0), value)[:4]

    start_regions((2,))
    loading[3].wait()
    permit[...] = COURANT / permit[...]
    own = window([fields[c] for c in range(6)] + [permit[...]], lambda base: (base - (x_wall - 4) + 2 * LANES) % LANES)
    for part in range(2):
        out_w[part] = own[part]
        land_w[1, part] = own[part]
        out_z[0, part] = own[part][:4]
        out_z[1, part] = own[part][size_z - 4 :]
    start_regions((0,))

    @pl.when(is_end)
    def _():
        tile = pl.ds(zt, 8)
        for i in range(2):
            for c in range(3):
                tile_h[0, 2 * c + i] = fields[3 + c, size_y - 2 + i, tile, :]
                tile_h[1, 2 * c + i] = fields[3 + c, i, tile, :]
            tile_h[0, 6 + i] = permit[size_y - 2 + i, tile, :]
            tile_h[1, 6 + i] = permit[i, tile, :]
        for c in range(3):
            for i in range(2):
                tile_e[0, 2 * c + i] = fields[c, size_y - 2 + i, tile, :]
                tile_e[1, 2 * c + i] = fields[c, i, tile, :]
        eight = iota((8, LANES), 1)
        packed = jnp.full((8, LANES), COURANT, F32)
        for c in range(7):
            values = permit[:, tile, :] if c == 6 else fields[c, :, tile, :]
            for y in range(size_y):
                base = quarter * (c % 4) + 8 * y + 4 * (c // 4)
                turned = pltpu.roll(values[y], (base + 4 * (1 - xy)) % LANES, 1)
                packed = jnp.where(jnp.logical_and(eight >= base, eight < base + 4), turned, packed)
        out_x[...] = packed
        land_x[1, xy] = packed

    @pl.when(jnp.logical_not(is_end))
    def _():
        land_x[...] = jnp.zeros(land_x.shape, F32)

    start_regions((1,))
    start_regions((3,))
    for copy in loading[1:3] + loading[4:]:
        copy.wait()
    for _ in stage(0, *(fields[c] for c in range(3)), (fields[3], fields[5]), (fields[3], fields[4]), (fields[4], fields[5])):
        pass
    start_halo(0, (4, 5, 8, 11, 9, 10, 0, 1, 2, 3, 6, 7))
    fill_regions()
    for n in range(STEPS):
        fill_halo(n)
    geometry()
    run_s, run_c = sincos((phase[0] + 0.5 * ANGULAR_STEP * (iota((8, LANES), 0).astype(F32) + 1.0)) * (0.5 / math.pi))
    for n in range(STEPS):
        tables_of(n)

    def relay(k, carry):
        hear()
        pass_on()
        return carry

    lax.fori_loop(0, slabs - 3, relay, 0)

    def half_of(n):
        return run_c[2 * n : 2 * n + 1, :], run_s[2 * n : 2 * n + 1, :]

    def full_of(n):
        return run_c[2 * n + 1 : 2 * n + 2, :], run_s[2 * n + 1 : 2 * n + 2, :]

    cap_sum[...] = jnp.zeros(cap_sum.shape, F32)
    own_walls = walls.at[gz]
    own_walls[...] = jnp.zeros((8, LANES), F32)
    lanes8 = iota((1, LANES), 1)
    owner_row = jnp.zeros((1, LANES), F32)
    for p in range(size_y):
        owner_row = jnp.where(lanes8 == 8 * gz + p, (wall_owner[0, p] + 1).astype(F32), owner_row)
    own_walls[pl.ds(size_y, 1), :] = owner_row
    gathered = jnp.zeros((size_z, LANES), F32)
    for y in range(size_y):
        for c in range(8):
            k = c % 4
            from_c = X_PICKS[k] + (6 if c >= 4 else 0)
            turned = pltpu.roll(spectra[from_c, y], (8 * y + c - x_wall + 2 * LANES) % LANES, 1)
            gathered = jnp.where(lane == 8 * y + c, turned, gathered)
            from_c = Z_PICKS[k] + (6 if c >= 4 else 0)
            low = spectra[from_c, y, pl.ds(ZB, 1), :]
            high = spectra[from_c, y, pl.ds(size_z - 1 - ZB, 1), :]
            cap_plane[pl.ds(8 * y + c, 1), :] = jnp.where(gz == 0, low, high)

    def spread_out(source_of, rows, shift_of, masks):
        spot = iota((rows, LANES), 1)
        values = []
        for c in range(8):
            value = jnp.zeros((rows, LANES), F32)
            first = 0
            for dy, planes in enumerate((depth, size_y, depth)):
                start = quarter * (c % 4) + (8 * (size_y - depth) if dy == 0 else 0)
                last = first + 8 * planes
                inside = jnp.logical_and(spot >= first, spot < last)
                for side in range(masks):
                    chosen = inside if masks == 1 else jnp.logical_and(inside, spot % 8 // 4 == side)
                    value = jnp.where(chosen, turn(source_of(dy, c, side), first - start + shift_of(c, side), 1), value)
                first = last
            values.append(value)
        return values

    def steps_of(values, visit):
        ex, ey, ez, hx, hy, hz, r, k = values
        for n in range(STEPS):
            before = (ez, ey)
            hx = hx - k * ((turn(ez, -8, 1) - ez) - (turn(ey, -1, 0) - ey))
            hy = hy - k * ((turn(ex, -1, 0) - ex) - (turn(ez, -1, 1) - ez))
            hz = hz - k * ((turn(ey, -1, 1) - ey) - (turn(ex, -8, 1) - ex))
            ex = ex + r * ((hz - turn(hz, 8, 1)) - (hy - turn(hy, 1, 0)))
            ey = ey + r * ((hx - turn(hx, 1, 0)) - (hz - turn(hz, 1, 1)))
            ez = ez + r * ((hy - turn(hy, 1, 1)) - (hx - turn(hx, 8, 1)))
            visit(n, before, ey, ez, hy, hz)

    @pl.when(is_end)
    def _():
        wait_region(1)

    @pl.when(jnp.logical_not(is_end))
    def _():
        wait_region(0)

    sums = [jnp.zeros((size_z, LANES), F32) for _ in range(8)]

    def add_up(n, before, ey, ez, hy, hz):
        for at, (value, (co, si)) in enumerate(((hz, half_of(n)), (hy, half_of(n)), (ez, full_of(n)), (ey, full_of(n)))):
            value = value[:size_z]
            sums[at] = sums[at] + value * co
            sums[4 + at] = sums[4 + at] - value * si

    folded = [
        [
            jnp.concatenate([
                land_w[dy, part], land_z[dy, 0, part], land_z[dy, 1, part],
            ], axis=0)
            for part in range(2)
        ]
        for dy in range(3)
    ]
    border_e, border_h = [], []

    def keep(n, before, ey, ez, hy, hz):
        border_e.append(before)
        border_h.append((hz, hy))

    steps_of(spread_out(lambda dy, c, side: folded[dy][c // 4], size_z + 8, lambda c, side: 0, 1), add_up)
    steps_of(spread_out(lambda dy, c, side: land_x[dy, side], 8, lambda c, side: 4 * side - 4 * (c // 4), 2), keep)
    for c in range(8):
        chosen = jnp.logical_and(lane % 8 == c, lane < 8 * size_y)
        gathered = gathered + jnp.where(chosen, turn(sums[c], c - 8 * depth - 4, 1), 0.0)
    row_sign = jnp.where(jnp.logical_and(iota((half_rows, LANES), 0) % 4 > 0, iota((half_rows, LANES), 0) % 4 < 3), 1.0, -1.0)
    wall_cells = jnp.transpose(gathered)[:half_rows] * (row_sign[:, :size_z] * facing_x)
    for at, part in enumerate(split(wall_cells * norm)):
        lhs[pl.ds(at * all_rows + half_rows, half_rows), pl.ds(size_x, size_z)] = part


    @pl.when(is_end)
    def _():
        wait_region(2)
        tile = pl.ds(zt, 8)
        eight = iota((8, LANES), 1)
        left, right = jnp.where(xy == 0, 1.0, 0.0), jnp.where(xy == 0, 0.0, 1.0)
        behind, ahead = jnp.where(dev > 0, COURANT, 0.0), jnp.where(dev < devs - 1, COURANT, 0.0)

        missing = jnp.zeros((4, LANES), F32)

        def behind_far(half):
            value = jnp.concatenate([missing, half], axis=0)
            return jnp.where(gz == 0, value, turn(value, -1, 0))

        def ahead_far(half):
            value = jnp.concatenate([half, missing], axis=0)
            return jnp.where(gz == 0, turn(value, 1, 0), value)

        def column(c, held_far, near, offset, ahead_too):
            planes = [behind_far(held_far)] + [near[0, 2 * offset + i] for i in range(2)]
            planes += [fields[c, y, tile, :] for y in range(size_y)] + [near[1, 2 * offset + i] for i in range(2)]
            return planes + ([ahead_far(cap_f[1, offset])] if ahead_too else [])

        e = [column(c, cap_f[0, c], cap_e, c, True) for c in range(3)]
        h = [column(3 + c, cap_f[0, 3 + c], cap_h, c, False) for c in range(3)]
        rates = [None] + [cap_h[0, 6 + i] for i in range(2)] + [permit[y, tile, :] for y in range(size_y)] + [cap_h[1, 6 + i] for i in range(2)]
        coefs = [behind] * depth + [COURANT] * size_y + [ahead] * depth

        def next_x(value, border, i):
            return jnp.where(eight == LANES - 1, turn(border, LANES - 1 - (8 * i + 4), 1), turn(value, -1, 1))

        def last_x(value, border, i):
            return jnp.where(eight == 0, turn(border, -(8 * i + 3), 1), turn(value, 1, 1))

        totals_of = [[jnp.zeros((8, LANES), F32) for _ in range(8)] for _ in range(size_y)]
        for n in range(STEPS):
            bz, by = (value * left for value in border_e[n])
            fx, fy, fz = [list(v) for v in h]
            for i in range(n, extent - 1 - n):
                xs, ys, zs = e[0][i], e[1][i], e[2][i]
                fx[i] = h[0][i] - coefs[i] * ((e[2][i + 1] - zs) - (turn(ys, -1, 0) - ys))
                fy[i] = h[1][i] - coefs[i] * ((turn(xs, -1, 0) - xs) - (next_x(zs, bz, i) - zs))
                fz[i] = h[2][i] - coefs[i] * ((next_x(ys, by, i) - ys) - (e[0][i + 1] - xs))
            h = [fx, fy, fz]
            bz, by = (value * right for value in border_h[n])
            gx, gy, gz_ = [list(v) for v in e]
            for i in range(n + 1, extent - 1 - n):
                xs, ys, zs = h[0][i], h[1][i], h[2][i]
                gx[i] = e[0][i] + rates[i] * ((zs - h[2][i - 1]) - (ys - turn(ys, 1, 0)))
                gy[i] = e[1][i] + rates[i] * ((xs - turn(xs, 1, 0)) - (zs - last_x(zs, bz, i)))
                gz_[i] = e[2][i] + rates[i] * ((ys - last_x(ys, by, i)) - (xs - h[0][i - 1]))
            e = [gx, gy, gz_]
            for y in range(size_y):
                i = depth + y
                for at, (value, (co, si)) in enumerate(((h[1][i], half_of(n)), (h[0][i], half_of(n)), (e[1][i], full_of(n)), (e[0][i], full_of(n)))):
                    totals_of[y][at] = totals_of[y][at] + value * co
                    totals_of[y][4 + at] = totals_of[y][4 + at] - value * si
        for y in range(size_y):
            for c in range(8):
                value = totals_of[y][c]
                cap_sum[pl.ds(8 * y + c, 1), :] = jnp.where(gz == 0, value[ZB : ZB + 1], value[7 - ZB : 8 - ZB])

    def advance(n, ghosts):
        fields_from, spec_from = (fields, spectra) if n == 0 else (fields_out, spectra_out)
        ex, ey, ez, hx, hy, hz = (fields_from[c] for c in range(6))
        rate = permit[...]
        hx = hx - COURANT * (inner(True, 0, ez) - inner(True, 1, ey))
        hy = hy - COURANT * (inner(True, 1, ex) - inner(True, 2, ez))
        hz = hz - COURANT * (inner(True, 2, ey) - inner(True, 0, ex))
        wait_halo(n)
        start, _ = first_of(n)
        xp = in_xd[n]
        hx = hx - COURANT * (at_y(in_yd[2 * n], True) - at_z(in_zd[2 * n], True))
        hy = hy - COURANT * (at_z(in_zd[2 * n + 1], True) - at_x(xp, 0, True))
        hz = hz - COURANT * (at_x(xp, 1, True) - at_y(in_yd[2 * n + 1], True))

        ax, ay, az = in_yu[start], in_yu[start + 1], in_yu[start + 2]
        bx, by, bz = in_zu[start], in_zu[start + 1], in_zu[start + 2]
        c_ex, own = in_xu[n], out_xd[n]
        if n == 0:
            y_hx, y_hz = in_yu[3], in_yu[4]
            z_hx, z_hy = in_zu[3], in_zu[4]
            x_hy, x_hz = turn(c_ex, -3 * size_y, 1), turn(c_ex, -4 * size_y, 1)
        else:
            y_hx, y_hz, z_hx, z_hy, x_hy, x_hz = ghosts
        ay_z = jnp.where(row2 == size_z - 1, in_zy[n], turn(ay, -1, 0))
        ay_x = jnp.where(lane == size_x - 1, turn(in_yx[n], -2 * size_y, 1), turn(ay, -1, 1))
        y_hx = y_hx - half_y * ((ez[0] - az) - (ay_z - ay))
        y_hz = y_hz - half_y * ((ay_x - ay) - (ex[0] - ax))
        bz_y = jnp.concatenate([bz[1:], in_yz[n, 7:8, :][None]], axis=0)
        corner = in_zx[n, 7:8, :]
        bz_x = jnp.stack([turn(corner, -1 - y, 1) for y in range(size_y)], axis=0)
        bz_x = jnp.where(lane_row == size_x - 1, bz_x, jnp.stack([turn(bz[y], -1, 1) for y in range(size_y)], axis=0))
        z_hx = z_hx - half_z * ((bz_y - bz) - (ey[:, 0:1, :] - by))
        z_hy = z_hy - half_z * ((ex[:, 0:1, :] - bx) - (bz_x - bz))
        c_z = jnp.where(row2 == size_z - 1, in_xz[n, 0:1, :], turn(c_ex, -1, 0))
        c_y = jnp.where(lane == size_y - 1, turn(in_xy[n], size_y - 1, 1), turn(c_ex, -1, 1))
        x_hy = x_hy - half_x * ((c_z - c_ex) - (own - turn(c_ex, -2 * size_y, 1)))
        x_hz = x_hz - half_x * ((turn(own, -size_y, 1) - turn(c_ex, -size_y, 1)) - (c_y - c_ex))

        ex = ex + rate * (inner(False, 0, hz) - inner(False, 1, hy))
        ey = ey + rate * (inner(False, 1, hx) - inner(False, 2, hz))
        ez = ez + rate * (inner(False, 2, hy) - inner(False, 0, hx))
        ex = ex - rate * (at_y(y_hz, False) - at_z(z_hy, False))
        ey = ey - rate * (at_z(z_hx, False) - at_x(x_hz, 0, False))
        ez = ez - rate * (at_x(x_hy, 0, False) - at_y(y_hx, False))
        if n < STEPS - 1:
            staging = stage(n + 1, ex, ey, ez, (), (), ())
            next(staging)
            start_halo(n + 1, (4, 5, 0, 1, 2, 3))
            next(staging)
            start_halo(n + 1, (8, 11, 9, 10, 6, 7))
        half_c, half_s = run_c[2 * n : 2 * n + 1, :], run_s[2 * n : 2 * n + 1, :]
        for c, value in enumerate((hx, hy, hz)):
            spectra_out[3 + c] = spec_from[3 + c] + value * half_c
            spectra_out[9 + c] = spec_from[9 + c] - value * half_s
        full_c, full_s = run_c[2 * n + 1 : 2 * n + 2, :], run_s[2 * n + 1 : 2 * n + 2, :]
        for c, value in enumerate((ex, ey, ez)):
            spectra_out[c] = spec_from[c] + value * full_c
            spectra_out[6 + c] = spec_from[6 + c] - value * full_s
        for c, value in enumerate((ex, ey, ez, hx, hy, hz)):
            fields_out[c] = value
        return y_hx, y_hz, z_hx, z_hy, x_hy, x_hz

    sub = iota((8, LANES), 0)
    caps_now = (cap_plane[...] + cap_sum[...]) * (row_sign * (facing_z * end_weight))
    cap_plane[...] = caps_now
    for at, part in enumerate(split(caps_now * norm)):
        lhs[pl.ds(at * all_rows, half_rows), pl.ds(0, size_x)] = part

    def wall_copy(k, ref=None):
        held = walls.at[gz] if ref is None else ref
        return pltpu.make_async_remote_copy(
            src_ref=held,
            dst_ref=held,
            send_sem=loads.at[8],
            recv_sem=wall_got,
            device_id={"gz": (gz + k) % slabs},
            device_id_type=MESH,
        )

    def cap_copy(k, at):
        return pltpu.make_async_remote_copy(
            src_ref=caps.at[at],
            dst_ref=caps.at[at],
            send_sem=loads.at[8],
            recv_sem=wall_got,
            device_id={"gz": (gz + k) % slabs},
            device_id_type=MESH,
        )

    sign = jnp.where(sub < 4, -1.0, 1.0)

    far_rows = lhs[...]

    def far_of(j):
        rows = far_rows
        by_high = jnp.dot(rows, table_hi[j], preferred_element_type=F32)
        by_low = jnp.dot(rows[:all_rows], table_lo[j], preferred_element_type=F32)
        product = by_high[:all_rows] + by_high[all_rows:] + by_low
        theta = jnp.zeros((8, LANES), F32)
        phi = jnp.zeros((8, LANES), F32)
        for face in range(2):
            sum_c = jnp.zeros((8, LANES), F32)
            sum_s = jnp.zeros((8, LANES), F32)
            for y in range(size_y):
                g = face * size_y + y
                tile = product[8 * g : 8 * g + 8]
                tile = tile[:, :LANES] + sign * pltpu.roll(tile[:, LANES:], 4, 0)
                sum_c = sum_c + tile * phases[j, 0, pl.ds(g, 1), :]
                sum_s = sum_s + tile * phases[j, 1, pl.ds(g, 1), :]
            far = sum_c + sign * pltpu.roll(sum_s, 4, 0)
            theta = theta + weights[j, 2 * face] * far
            phi = phi + weights[j, 2 * face + 1] * far

        def four(values):
            pairs = values + pltpu.roll(values, 7, 0)
            return pairs + pltpu.roll(pairs, 6, 0)

        both = jnp.where(sub % 4 == 1, pltpu.roll(four(phi), 1, 0), four(theta))
        parts_out[j] = jnp.where(sub < 2, both, pltpu.roll(both, 6, 0))[:4]

    bunch = per * max(1, 4 // per)
    together = bunch // per
    upper = jnp.where(gz >= slabs // 2, 1, 0)
    near = (upper * across + dev * xys + xy) % owners

    def partner(number):
        other, bit = 0, 1
        while bit < owners:
            other = other + bit * ((near // bit + number // bit) % 2)
            bit *= 2
        return other

    def flat_of(owner):
        return (slabs // 2 - 1) * across + owner

    def part_copy(owner, source):
        return pltpu.make_async_remote_copy(
            src_ref=parts_out.at[pl.ds(owner * per, per)],
            dst_ref=parts_in.at[source],
            send_sem=loads.at[0],
            recv_sem=part_got,
            device_id=ident(flat_of(owner)),
            device_id_type=MESH,
        )

    mine = me - flat_of(0)
    leads = jnp.logical_and(mine >= 0, mine < owners)

    def far_and_send(number, carry):
        several = [partner(owners - 1 - together * number - m) for m in range(together)]
        for owner in several:
            for m in range(per):
                far_of(owner * per + m)
        for owner in several:
            @pl.when(owner != mine)
            def _():
                part_copy(owner, me).start()

        return carry

    hear()
    lax.fori_loop(0, owners // together, far_and_send, 0, unroll=True)

    @pl.when(leads)
    def _():
        parts_in[me] = parts_out[pl.ds(mine * per, per)]

    ghosts = advance(0, None)
    for y in range(size_y):
        cells = jnp.concatenate([wall_cells[8 * y : 8 * y + 8], jnp.zeros((8, LANES - size_z), F32)], axis=1)
        own_walls[pl.ds(y, 1), :] = jnp.sum(stagger(cells, PATCH), axis=0, keepdims=True)
    for k in range(1, slabs):
        wall_copy(k).start()
    for at, holder in enumerate((0, slabs - 1)):
        @pl.when(gz == holder)
        def _():
            for y in range(size_y):
                caps[at, pl.ds(8 * y, 8), :] = block_transpose(cap_plane[pl.ds(8 * y, 8), :])
            for k in range(1, slabs):
                cap_copy(k, at).start()

    def total_copy(k, owner, ref=None):
        held = totals.at[pl.ds(owner * per, per)] if ref is None else ref
        return pltpu.make_async_remote_copy(
            src_ref=held,
            dst_ref=held,
            send_sem=loads.at[3],
            recv_sem=total_got.at[owner // together],
            device_id=ident((me + k) % peers),
            device_id_type=MESH,
        )

    @pl.when(leads)
    def _():
        everyone = parts_in.at[pl.ds(0, peers - 1)]
        pltpu.make_async_remote_copy(
            src_ref=everyone, dst_ref=everyone, send_sem=loads.at[0], recv_sem=part_got, device_id={"gz": gz}, device_id_type=MESH
        ).wait_recv()
        totals[pl.ds(mine * per, per)] = jnp.sum(parts_in[...], axis=0)
        for k in sorted(range(slabs), key=lambda k: -min(k, slabs - k)):
            row = (gz + k) % slabs * across

            def send(r, carry):
                to = row + (dev * xys + xy + r) % across

                @pl.when(to != me)
                def _():
                    total_copy((to - me + peers) % peers, mine).start()

                return carry

            lax.fori_loop(0, across, send, 0, unroll=across <= 4)


    def choose(mine, share, records):
        length = mine.shape[1]
        before = jnp.where(iota((length, length), 0) < iota((length, length), 1), 1.0, 0.0).astype(BF16)
        ones = jnp.broadcast_to(jnp.where(mine, 1.0, 0.0), (8, length))
        rank = jnp.dot(ones.astype(BF16), before, preferred_element_type=F32)
        wanted = iota((8, length), 0).astype(F32)
        chooser = jnp.where(rank == wanted, ones, 0.0)
        return jnp.dot(chooser, records, precision=HIGHEST, preferred_element_type=F32)[:share]

    def choose_owned():
        for ends, caps_due in ((is_end, 1), (jnp.logical_not(is_end), 2)):
            @pl.when(ends)
            def _():
                everything = arrivals.at[pl.ds(0, 8 * (slabs - 1) + caps_due * caps.shape[1])]
                pltpu.make_async_copy(everything, everything, wall_got).wait()

        all_walls = walls[...]
        owner_all = jnp.sum(all_walls[:, size_y : size_y + 1, :], axis=0)[:, : 8 * slabs]
        cap_share = (owned_out.shape[0] - size_y) // 2
        owned_out[pl.ds(0, size_y), 0, :] = choose(
            owner_all == (gz + 1).astype(F32), size_y, all_walls.reshape(8 * slabs, LANES)
        )
        for at in range(2):
            owned_out[pl.ds(size_y + at * cap_share, cap_share), 0, :] = choose(
                cap_owner[pl.ds(at, 1), :] == gz, cap_share, caps[at]
            )

    def intensity_of(field):
        return jnp.sum(field * field, axis=0, keepdims=True)

    def slope_of(j):
        field = totals[j]
        residual = aim[pl.ds(j, 1), :].astype(F32) * (intensity_of(field) - target[pl.ds(j, 1), :])
        return 2.0 * residual * field

    def adjoint_of(j):
        slope = slope_of(j)
        by_theta = jnp.where(sub < 4, slope[0:1], slope[2:3])
        by_phi = jnp.where(sub < 4, slope[1:2], slope[3:4])
        tiles = []
        for face in range(2):
            vector = weights[j, 2 * face] * by_theta + weights[j, 2 * face + 1] * by_phi
            turned = -sign * pltpu.roll(vector, 4, 0)
            for y in range(size_y):
                g = face * size_y + y
                tile = vector * phases[j, 0, pl.ds(g, 1), :] + turned * phases[j, 1, pl.ds(g, 1), :]
                tiles.append(jnp.concatenate([tile, -sign * pltpu.roll(tile, 4, 0)], axis=1))
        rows = jnp.concatenate(tiles, axis=0)
        high, low = split(rows)
        both = jnp.concatenate([high, low], axis=0)
        across = (((1,), (1,)), ((), ()))
        by_high = lax.dot_general(both, table_hi[j], across, preferred_element_type=F32)
        by_low = lax.dot_general(high, table_lo[j], across, preferred_element_type=F32)
        return by_high[:all_rows] + by_high[all_rows:] + by_low

    def adjoint_wait(number):
        several = [partner(together * number + m) for m in range(together)]
        batch = several[0] // together
        ours = jnp.logical_and(leads, mine // together == batch)

        @pl.when(jnp.logical_not(ours))
        def _():
            total_copy(1, several[0], totals.at[pl.ds(batch * bunch, bunch)]).wait_recv()

        if together > 1:
            @pl.when(ours)
            def _():
                total_copy(1, several[0], totals.at[pl.ds(batch * bunch, bunch - per)]).wait_recv()

        return several

    def adjoint_some(numbers, total):
        several = [owner for number in numbers for owner in adjoint_wait(number)]
        for owner in several:
            for m in range(per):
                total = total + adjoint_of(owner * per + m)
        return total

    rounds = owners // together
    ghosts = advance(1, ghosts)
    choose_owned()
    gradient = adjoint_some((0,), jnp.zeros((all_rows, size_x + size_z), F32))
    gradient = adjoint_some(range(1, rounds), gradient)
    intensity_out[...] = intensity_of(totals[me // ratio])
    advance(2, ghosts)
    for y in range(size_y):
        wall = gradient[half_rows + 8 * y : half_rows + 8 * y + 8, size_x:]
        wall = jnp.concatenate([wall, jnp.zeros((8, LANES - size_z), F32)], axis=1)
        wall = stagger(wall, PATCH)
        adjoint_out[pl.ds(y, 1), 0, :] = jnp.sum(wall, axis=0, keepdims=True) * norm
        cap = block_transpose(gradient[8 * y : 8 * y + 8, :size_x] * (norm * end_weight))
        adjoint_out[pl.ds(size_y + 8 * y, 8), 0, :] = cap

    groups_sent = {}
    for number, (landing, move) in enumerate(messages):
        groups_sent[number] = [within(move, 1), math.prod(landing.shape) // LANES]
    for number, (_, _, source, _, _, _) in enumerate(regions):
        entry = groups_sent.setdefault(group_of(number), [region_when(number, 1), 0])
        entry[1] += math.prod(source.shape) // LANES
    for group, (sent, rows_sent) in groups_sent.items():
        @pl.when(sent)
        def _():
            everything = arrivals.at[pl.ds(0, rows_sent)]
            pltpu.make_async_copy(everything, everything, sent_by(group)).wait()

    def parts_sent(ref):
        pltpu.make_async_remote_copy(
            src_ref=ref, dst_ref=ref, send_sem=loads.at[0], recv_sem=part_got, device_id={"gz": gz}, device_id_type=MESH
        ).wait_send()

    @pl.when(leads)
    def _():
        parts_sent(parts_out.at[pl.ds(0, (owners - 1) * per)])
        total_copy(1, 0, parts_in.at[pl.ds(0, peers - 1)]).wait_send()

    @pl.when(jnp.logical_not(leads))
    def _():
        parts_sent(parts_out)

    for ends, caps_sent in ((is_end, 1), (jnp.logical_not(is_end), 0)):
        @pl.when(ends)
        def _():
            everything = arrivals.at[pl.ds(0, (slabs - 1) * (8 + caps_sent * caps.shape[1]))]
            pltpu.make_async_copy(everything, everything, loads.at[8]).wait()


def write_out(*refs):
    copies = [pltpu.make_async_copy(refs[i], refs[5 + i], refs[10].at[i]) for i in range(5)]
    for copy in copies:
        copy.start()
    for copy in copies:
        copy.wait()


def local(fields, spectra, permittivity, phase_start, wall_owner, cap_owner, dir_index, target, aim_mask):
    slabs, devs, xys = (lax.axis_size(a) for a in ("gz", "dev", "xy"))
    peers = slabs * devs * xys
    size_y, size_z, size_x = permittivity.shape
    assert size_z == PATCH and size_x == LANES and size_y == 4 and xys == 2
    directions = dir_index.shape[0]
    chunks = directions // LANES
    ratio = peers // chunks
    per = max(1, chunks // (2 * devs * xys))
    owners = chunks // per
    share = directions // peers
    cap_count = size_y * size_x // PATCH
    owned = size_y + 2 * (cap_count // slabs)
    rows = 16 * size_y
    depth = size_x + size_z
    planes, pairs = 5 + 3 * (STEPS - 1), 2 * STEPS
    halos = (
        (planes, size_z, LANES), (pairs, size_z, LANES), (planes, size_y, 1, LANES), (pairs, size_y, 1, LANES),
        (STEPS, size_z, LANES), (STEPS, size_z, LANES),
        (STEPS, 1, LANES), (STEPS, 8, LANES), (STEPS, size_z, LANES), (STEPS, 8, LANES), (STEPS, 8, LANES), (STEPS, size_z, LANES),
    )
    vmem = pl.BlockSpec(memory_space=pltpu.VMEM)
    anywhere = pl.BlockSpec(memory_space=pl.ANY)
    dma = pltpu.SemaphoreType.DMA
    outs = pl.pallas_call(
        functools.partial(kernel, (slabs, devs, xys)),
        out_shape=(
            pltpu.VMEM(fields.shape, F32),
            pltpu.VMEM(spectra.shape, F32),
            pltpu.VMEM((owned, 1, LANES), F32),
            pltpu.VMEM((1, LANES), F32),
            pltpu.VMEM((size_y + cap_count, 1, LANES), F32),
        ),
        in_specs=[anywhere] * 9,
        out_specs=(vmem,) * 5,
        scratch_shapes=[
            *(pltpu.VMEM(shape, F32) for shape in halos[:6]),
            *(pltpu.VMEM(shape, F32) for shape in halos),
            pltpu.VMEM((5, size_z, LANES), F32),
            pltpu.VMEM((5, size_y, 1, LANES), F32),
            pltpu.VMEM((max(376, (slabs - 1) * (8 + cap_count)), 1, LANES), F32),
            pltpu.VMEM((2, size_z, LANES), F32),
            pltpu.VMEM((2, 2, 4, LANES), F32),
            pltpu.VMEM((8, LANES), F32),
            pltpu.VMEM((3, 2, size_z, LANES), F32),
            pltpu.VMEM((3, 2, 2, 4, LANES), F32),
            pltpu.VMEM((3, 2, 8, LANES), F32),
            *(pltpu.VMEM(shape, F32) for shape in ((2, 6, 8, LANES), (2, 8, 8, LANES), (2, 6, 4, LANES)) * 2),
            pltpu.VMEM((8, 8, LANES), F32),
            pltpu.VMEM((6, 4, LANES), F32),
            pltpu.VMEM((8 * size_y, LANES), F32),
            pltpu.VMEM(fields.shape, F32),
            pltpu.VMEM(spectra.shape, F32),
            pltpu.VMEM(permittivity.shape, F32),
            pltpu.SMEM((1,), F32),
            pltpu.SMEM(wall_owner.shape, jnp.int32),
            pltpu.VMEM(cap_owner.shape, jnp.int32),
            pltpu.VMEM((chunks, LANES), jnp.int32),
            pltpu.VMEM((chunks, LANES), F32),
            pltpu.VMEM((chunks, LANES), jnp.int32),
            pltpu.VMEM((8, chunks, LANES), F32),
            pltpu.VMEM((chunks, 4, 8, LANES), F32),
            pltpu.VMEM((chunks, 2, 2 * size_y, LANES), F32),
            pltpu.VMEM((chunks, depth, 2 * LANES), BF16),
            pltpu.VMEM((chunks, depth, 2 * LANES), BF16),
            pltpu.VMEM((8 * size_y, LANES), F32),
            pltpu.VMEM((2 * rows, depth), BF16),
            pltpu.VMEM((chunks, 4, LANES), F32),
            pltpu.VMEM((peers, per, 4, LANES), F32),
            pltpu.VMEM((chunks, 4, LANES), F32),
            pltpu.VMEM((slabs, 8, LANES), F32),
            pltpu.VMEM((2, cap_count, LANES), F32),
            dma((11,)), dma((STEPS,)),
            dma, dma((owners // max(1, 4 // per),)), dma,
            dma((9,)), pltpu.SemaphoreType.REGULAR((2,)), dma((2,)),
        ],
        compiler_params=pltpu.CompilerParams(collective_id=0, has_side_effects=True),
    )(
        fields, spectra, permittivity, phase_start, wall_owner, cap_owner,
        dir_index.reshape(chunks, LANES), target.reshape(chunks, LANES), aim_mask.reshape(chunks, LANES),
    )
    held = (fields.shape, spectra.shape, (owned, 1, LANES), (1, LANES), (size_y + cap_count, 1, LANES))
    fields_new, spectra_new, owned_rows, intensity, adjoint = pl.pallas_call(
        write_out,
        out_shape=tuple(jax.ShapeDtypeStruct(shape, F32) for shape in held),
        in_specs=[pl.BlockSpec(memory_space=pltpu.VMEM)] * 5,
        out_specs=(pl.BlockSpec(memory_space=pl.ANY),) * 5,
        scratch_shapes=[dma((5,))],
    )(*(pltpu.with_memory_space_constraint(out, pltpu.VMEM) for out in outs))
    owned_rows = owned_rows.reshape(1, 1, owned, 1, LANES).transpose(0, 1, 3, 2, 4)
    adjoint = adjoint.reshape(1, 1, size_y + cap_count, 1, LANES).transpose(0, 1, 3, 2, 4)
    intensity = intensity.reshape(LANES)
    if ratio > 1:
        me = (lax.axis_index("gz") * devs + lax.axis_index("dev")) * xys + lax.axis_index("xy")
        intensity = lax.dynamic_slice_in_dim(intensity, (me % ratio) * share, share, 0)
    return (fields_new, spectra_new, owned_rows, intensity, adjoint)


def solution(mesh):
    placed = (
        P("groups", "dev", "gz", "xy"),
        P("groups", "dev", "gz", "xy"),
        P(("groups", "dev"), "gz", "xy"),
        P("groups"),
        P("gz", None),
        P(),
        P(),
        P("groups"),
        P("groups"),
    )
    return jax.shard_map(
        local,
        mesh=mesh,
        in_specs=placed,
        out_specs=(
            P("groups", "dev", "gz", "xy"),
            P("groups", "dev", "gz", "xy"),
            P(("groups", "gz"), "dev", "xy", None, None),
            P(("groups", "gz", "dev", "xy")),
            P(("groups", "gz"), "dev", "xy", None, None),
        ),
        check_vma=False,
    )
```

```python
import functools
import math

import jax
import jax.numpy as jnp
from jax import lax
from jax.experimental import pallas as pl
from jax.experimental.pallas import tpu as pltpu
from jax.sharding import PartitionSpec as P

PATCH = 16
XB = 8
ZB = 4
STEPS = 3
THETAS = 64
COURANT = 0.5
ANGULAR_STEP = 0.3
WAVE_NUMBER = 0.6
LANES = 128
HIGHEST = lax.Precision.HIGHEST
CURRENT_SIGNS = (-1.0, 1.0, 1.0, -1.0)
X_PICKS = (5, 4, 2, 1)
Z_PICKS = (4, 3, 1, 0)
MESH = pl.DeviceIdType.MESH
AXES = ("dev", "gz", "xy")
F32 = jnp.float32
BF16 = jnp.bfloat16


def iota(shape, dim):
    return lax.broadcasted_iota(jnp.int32, shape, dim)


def sincos(turns):
    half = (turns - jnp.floor(turns + 0.5)) * math.pi
    sq = half * half
    sin_h = half * (1.0 + sq * (-1.0 / 6 + sq * (1.0 / 120 + sq * (-1.0 / 5040 + sq * (1.0 / 362880 - sq * (1.0 / 39916800))))))
    cos_h = 1.0 + sq * (-0.5 + sq * (1.0 / 24 + sq * (-1.0 / 720 + sq * (1.0 / 40320 + sq * (-1.0 / 3628800 + sq * (1.0 / 479001600))))))
    return 2.0 * sin_h * cos_h, 1.0 - 2.0 * sin_h * sin_h


def split(values):
    high = values.astype(BF16)
    return high, (values - high.astype(F32)).astype(BF16)


def arrival_rows(n, size_y, size_z):
    length = 5 if n == 0 else 3
    return (length + 2) * (size_z + size_y) + 1 + 3 * 8 + 4 * size_z


def stagger(tile, by):
    row = iota(tile.shape, 0)
    for bit in (1, 2, 4):
        tile = jnp.where(row // bit % 2 == 1, pltpu.roll(tile, by * bit % LANES, 1), tile)
    return tile


def block_transpose(tile):
    on_diagonal = (iota(tile.shape, 1) // PATCH) == iota(tile.shape, 0)
    total = jnp.where(on_diagonal, tile, 0.0)
    for k in range(1, 8):
        turned = pltpu.roll(tile, PATCH * k, 1)
        total = total + pltpu.roll(jnp.where(on_diagonal, turned, 0.0), 8 - k, 0)
    return total


def kernel(
    sizes,
    fields_in, spectra_in, permit_in, phase_in, wall_owner_in, cap_owner_in, dirs_in, target_in, aim_in,
    fields_out, spectra_out, owned_out, intensity_out, adjoint_out,
    out_yu, out_yd, out_zu, out_zd, out_xu, out_xd,
    in_yu, in_yd, in_zu, in_zd, in_xu, in_xd, in_zy, in_yz, in_yx, in_zx, in_xz, in_xy, blank, blank_rows, arrivals,
    out_w, out_z, out_x, land_w, land_z, land_x, tile_e, tile_h, tile_f, cap_e, cap_h, cap_f, empty, empty_half, cap_sum,
    fields, spectra, permit, phase, wall_owner, cap_owner, dirs, target, aim,
    geo, weights, phases, table_hi, table_lo, cap_plane, lhs,
    parts_out, parts_in, totals, walls, caps,
    halo_send, halo_got, part_got, total_got, wall_got, loads, chain, region_got,
):
    slabs, devs, xys = sizes
    peers = slabs * devs * xys
    size_y, size_z, size_x = permit.shape
    chunks = dirs.shape[0]
    ratio = peers // chunks
    across = devs * xys
    per = max(1, chunks // (2 * across))
    owners = chunks // per
    groups = 2 * size_y
    half_rows = 8 * size_y
    all_rows = 2 * half_rows
    gz, dev, xy = lax.axis_index("gz"), lax.axis_index("dev"), lax.axis_index("xy")
    me = (gz * devs + dev) * xys + xy
    place = {"dev": dev, "gz": gz, "xy": xy}
    count = {"dev": devs, "gz": slabs, "xy": xys}

    def ident(flat):
        return {"gz": flat // (devs * xys), "dev": (flat // xys) % devs, "xy": flat % xys}

    pltpu.make_async_copy(fields_in, fields, loads.at[0]).start()
    barrier = pltpu.get_barrier_semaphore()

    for away in (1, -1, 0):
        @pl.when(jnp.logical_and(gz + away >= 0, gz + away < slabs))
        def _():
            def greet(k, carry):
                spot = (dev * xys + xy + k) % across
                to = {"gz": gz + away, "dev": spot // xys, "xy": spot % xys}
                pl.semaphore_signal(barrier, inc=1, device_id=to, device_id_type=MESH)
                return carry

            lax.fori_loop(0 if away else 1, across, greet, 0)

    beside = jnp.where(gz > 0, across, 0) + jnp.where(gz < slabs - 1, across, 0) + across - 1

    def pass_on():
        for at, away in enumerate((1, -1)):
            @pl.when(jnp.logical_and(gz + away >= 0, gz + away < slabs))
            def _():
                to = {"gz": gz + away, "dev": dev, "xy": xy}
                pl.semaphore_signal(chain.at[at], inc=1, device_id=to, device_id_type=MESH)

    def hear():
        for at, away in enumerate((1, -1)):
            @pl.when(jnp.logical_and(gz - away >= 0, gz - away < slabs))
            def _():
                pl.semaphore_wait(chain.at[at], 1)

    loading = [
        pltpu.make_async_copy(source, held, loads.at[number])
        for number, (source, held) in enumerate((
            (fields_in, fields), (dirs_in, dirs), (phase_in, phase), (permit_in, permit), (spectra_in, spectra),
            (wall_owner_in, wall_owner), (cap_owner_in, cap_owner), (target_in, target), (aim_in, aim),
        ))
    ]
    for copy in loading[1:]:
        copy.start()

    def geometry():
        index = dirs[...]
        sin_t, cos_t = sincos(((index // THETAS).astype(F32) + 0.5) * (0.5 / THETAS))
        sin_f, cos_f = sincos((index % THETAS).astype(F32) * (1.0 / THETAS))
        wave = WAVE_NUMBER / (2.0 * math.pi)
        for slot, values in enumerate((
            wave * sin_t * cos_f, wave * sin_t * sin_f, wave * cos_t,
            cos_t * cos_f, cos_t * sin_f, -sin_t, -sin_f, cos_f,
        )):
            geo[slot] = values

    grid_x, grid_y, grid_z = size_x * xys, size_y * devs, size_z * slabs
    x_first = (xy * size_x).astype(F32) - (grid_x - 1) / 2.0
    y_first = (dev * size_y).astype(F32) - (grid_y - 1) / 2.0
    z_first = (gz * size_z).astype(F32) - (grid_z - 1) / 2.0
    x_wall = jnp.where(xy == 0, XB, size_x - 1 - XB)
    z_cap = jnp.where(gz == 0, ZB, size_z - 1 - ZB)
    x_face = x_first + x_wall.astype(F32)
    z_face = z_first + z_cap.astype(F32)
    facing_x = jnp.where(xy == 0, -1.0, 1.0)
    facing_z = jnp.where(gz == 0, -1.0, 1.0)
    is_end = jnp.logical_or(gz == 0, gz == slabs - 1)
    end_weight = jnp.where(is_end, 1.0, 0.0)
    norm = 1.0 / math.sqrt(2.0 * (2 * grid_y * grid_z + 2 * grid_y * grid_x))

    def make_tables(j, carry):
        def row(slot):
            return geo[slot, pl.ds(j, 1), :]

        ux, uy, uz = row(0), row(1), row(2)
        blocks = size_x // 8
        far_s, far_c = sincos((iota((blocks, LANES), 0).astype(F32) * 8.0 + x_first) * ux)
        near_s, near_c = sincos(iota((8, LANES), 0).astype(F32) * ux)
        far_s, far_c = far_s[:, None, :], far_c[:, None, :]
        near_s, near_c = near_s[None], near_c[None]
        cos_x = (far_c * near_c - far_s * near_s).reshape(size_x, LANES)
        sin_x = (far_s * near_c + far_c * near_s).reshape(size_x, LANES)
        sin_z, cos_z = sincos((iota((size_z, LANES), 0).astype(F32) + z_first) * uz)
        for at, (x_part, z_part) in enumerate(((cos_x, cos_z), (sin_x, sin_z))):
            lanes = pl.ds(at * LANES, LANES)
            x_high, x_low = split(x_part)
            z_high, z_low = split(z_part)
            table_hi[j, pl.ds(0, size_x), lanes] = x_high
            table_lo[j, pl.ds(0, size_x), lanes] = x_low
            table_hi[j, pl.ds(size_x, size_z), lanes] = z_high
            table_lo[j, pl.ds(size_x, size_z), lanes] = z_low
        which = iota((groups, LANES), 0)
        cell_y = (which % size_y).astype(F32) + y_first
        sin_g, cos_g = sincos(cell_y * uy + jnp.where(which < size_y, z_face * uz, x_face * ux))
        phases[j, 0] = cos_g
        phases[j, 1] = sin_g
        kind = iota((8, LANES), 0) % 4

        def pattern(a, b, c, d):
            return jnp.where(kind == 0, a, jnp.where(kind == 1, b, jnp.where(kind == 2, c, d)))

        tx, ty, tz, fx, fy = row(3), row(4), row(5), row(6), row(7)
        weights[j, 0] = pattern(-tx, -ty, -fx, -fy)
        weights[j, 1] = pattern(-fx, -fy, tx, ty)
        weights[j, 2] = pattern(-ty, -tz, -fy, jnp.zeros_like(fy))
        weights[j, 3] = pattern(-fy, jnp.zeros_like(fy), ty, tz)
        return carry

    windows = STEPS

    def tables_of(window):
        lax.fori_loop(window * chunks // windows, (window + 1) * chunks // windows, make_tables, 0)

    lane = iota((size_z, LANES), 1)
    lane3 = iota((size_y, size_z, LANES), 2)
    row3 = iota((size_y, size_z, LANES), 1)

    messages = (
        (in_yu, {"dev": 1}), (in_yd, {"dev": -1}), (in_zu, {"gz": 1}), (in_zd, {"gz": -1}),
        (in_zy, {"gz": -1, "dev": 1}), (in_yz, {"dev": -1, "gz": 1}),
        (in_xu, {"xy": 1}), (in_xd, {"xy": -1}),
        (in_yx, {"dev": 1, "xy": -1}), (in_zx, {"gz": 1, "xy": -1}), (in_xz, {"xy": 1, "gz": -1}), (in_xy, {"xy": 1, "dev": -1}),
    )

    def within(move, sign):
        inside = True
        for axis, step in move.items():
            spot = place[axis] + sign * step
            inside = jnp.logical_and(inside, jnp.logical_and(spot >= 0, spot < count[axis]))
        return inside

    def first_of(n):
        return (0, 5) if n == 0 else (5 + 3 * (n - 1), 3)

    def views(n):
        start, length = first_of(n)
        planes, pair = pl.ds(start, length), pl.ds(2 * n, 2)
        low, high = pl.ds(0, 8), pl.ds(size_z - 8, 8)
        return (
            (out_yu.at[planes], in_yu.at[planes]), (out_yd.at[pair], in_yd.at[pair]),
            (out_zu.at[planes], in_zu.at[planes]), (out_zd.at[pair], in_zd.at[pair]),
            (out_zd.at[2 * n, size_y - 1], in_zy.at[n]), (out_yd.at[2 * n, high], in_yz.at[n]),
            (out_xu.at[n], in_xu.at[n]), (out_xd.at[n], in_xd.at[n]),
            (out_xd.at[n], in_yx.at[n]), (out_xd.at[n, high], in_zx.at[n]),
            (out_xu.at[n, low], in_xz.at[n]), (out_xu.at[n], in_xy.at[n]),
        )

    def sent_by(group):
        if 6 <= group < 12:
            return loads.at[(1, 2, 4, 5, 6, 7)[group - 6]]
        return halo_send.at[group if group < 6 else group - 6]

    def halo_copy(n, number, source, landing):
        to = {axis: (place[axis] + step + count[axis]) % count[axis] for axis, step in messages[number][1].items()}
        return pltpu.make_async_remote_copy(
            src_ref=source,
            dst_ref=landing,
            send_sem=sent_by(number),
            recv_sem=halo_got.at[n],
            device_id=to,
            device_id_type=MESH,
        )

    def start_halo(n, numbers):
        for number in numbers:
            @pl.when(within(messages[number][1], 1))
            def _():
                halo_copy(n, number, *views(n)[number]).start()

    def fill_halo(n):
        length = first_of(n)[1]
        planes, pair, rows, row_pair = blank.at[pl.ds(0, length)], blank.at[pl.ds(0, 2)], blank_rows.at[pl.ds(0, length)], blank_rows.at[pl.ds(0, 2)]
        plane, tile = blank.at[0], blank.at[0, pl.ds(0, 8)]
        sources = (planes, pair, rows, row_pair, blank_rows.at[0, 0], tile, plane, plane, plane, tile, tile, plane)
        for number, source in enumerate(sources):
            @pl.when(jnp.logical_not(within(messages[number][1], -1)))
            def _():
                pltpu.make_async_copy(source, views(n)[number][1], halo_got.at[n]).start()

    def wait_halo(n):
        everything = arrivals.at[pl.ds(0, arrival_rows(n, size_y, size_z))]
        pltpu.make_async_copy(everything, everything, halo_got.at[n]).wait()

    def pack(values, high):
        packed = jnp.zeros((size_z, LANES), F32)
        for k, value in enumerate(values):
            for y in range(size_y):
                spot = k * size_y + y
                amount = (spot + 1) % LANES if high else spot
                turned = pltpu.roll(value[y], amount, 1) if amount else value[y]
                packed = jnp.where(lane == spot, turned, packed)
        return packed

    def stage(n, ex, ey, ez, for_y, for_z, for_x):
        start, _ = first_of(n)
        for k, value in enumerate((ex, ey, ez) + for_y):
            out_yu[start + k] = value[size_y - 1]
        for k, value in enumerate((ez, ex)):
            out_yd[2 * n + k] = value[0]
        for k, value in enumerate((ex, ey, ez) + for_z):
            out_zu[start + k] = value[:, size_z - 1 : size_z, :]
        for k, value in enumerate((ey, ex)):
            out_zd[2 * n + k] = value[:, 0:1, :]
        yield
        out_xu[n] = pack((ex, ey, ez) + for_x, True)
        out_xd[n] = pack((ez, ey), False)
        yield

    blank[...] = jnp.zeros(blank.shape, F32)
    blank_rows[...] = jnp.zeros(blank_rows.shape, F32)

    def inner(ahead, axis, value):
        if axis == 0:
            none = jnp.zeros_like(value[:1])
            if ahead:
                return jnp.concatenate([value[1:], none], axis=0) - value
            return value - jnp.concatenate([none, value[:-1]], axis=0)
        length = value.shape[axis]
        spots = row3 if axis == 1 else lane3
        if ahead:
            return jnp.where(spots == length - 1, 0.0, pltpu.roll(value, length - 1, axis)) - value
        return value - jnp.where(spots == 0, 0.0, pltpu.roll(value, 1, axis))

    none = jnp.zeros((size_y - 1, size_z, LANES), F32)

    def at_y(plane, ahead):
        return jnp.concatenate([none, plane[None]] if ahead else [plane[None], none], axis=0)

    def at_z(rows, ahead):
        return jnp.where(row3 == (size_z - 1 if ahead else 0), rows, 0.0)

    def at_x(packed, k, ahead):
        edges = []
        for y in range(size_y):
            spot = k * size_y + y
            amount = (LANES - 1 - spot) if ahead else (LANES - spot) % LANES
            edges.append(pltpu.roll(packed, amount, 1) if amount else packed)
        return jnp.where(lane3 == (size_x - 1 if ahead else 0), jnp.stack(edges, axis=0), 0.0)

    def turn(value, by, axis):
        return pltpu.roll(value, by % value.shape[axis], axis)

    row2 = iota((size_z, LANES), 0)
    lane_row = iota((size_y, 1, LANES), 2)
    half_y = jnp.where(dev > 0, COURANT, 0.0)
    half_z = jnp.where(gz > 0, COURANT, 0.0)
    half_x = jnp.where(xy > 0, COURANT, 0.0)

    zt = pl.multiple_of(jnp.where(gz == 0, 0, size_z - 8), 8)
    depth = STEPS
    extent = size_y + 2 * depth
    quarter = 8 * size_y

    regions = []
    for a in (1, -1, 0):
        for b in (1, -1, 0):
            if a or b:
                source = out_w if b == 0 else out_z.at[1 if b > 0 else 0]
                landing = land_w.at[1 - a] if b == 0 else land_z.at[1 - a, 1 if b > 0 else 0]
                nothing = blank.at[pl.ds(0, 2)] if b == 0 else empty_half.at[pl.ds(0, 2)]
                regions.append((0, {"dev": a, "gz": b}, source, landing, landing, nothing))
    for a in (1, -1, 0):
        for flip in (0, 1):
            if a or flip:
                to = {"dev": a, "flip": flip}
                regions.append((1, to, out_x, land_x.at[1 - a, xy], land_x.at[1 - a, (xy + flip) % 2], empty.at[0]))
    for at, a in enumerate((1, -1)):
        far_count = 6 if a > 0 else 3
        for kind, source, landing, nothing in (
            (3, tile_e.at[at], cap_e.at[at], empty.at[pl.ds(0, 6)]),
            (3, tile_h.at[at], cap_h.at[at], empty),
            (2, tile_f.at[at, pl.ds(0, far_count)], cap_f.at[at, pl.ds(0, far_count)], empty_half.at[pl.ds(0, far_count)]),
        ):
            regions.append((kind, {"dev": a}, source, landing, landing, nothing))

    def group_of(number):
        kind, move = regions[number][:2]
        if kind:
            return len(messages) + 2 + (0 if not move["dev"] else 1 if move["dev"] > 0 else 2)
        for at, (_, other) in enumerate(messages):
            if {axis: step for axis, step in move.items() if step} == other:
                return at
        return len(messages) + (0 if move["dev"] > 0 else 1)

    def region_inside(move, sign):
        return within({axis: step for axis, step in move.items() if axis != "flip" and step}, sign)

    def region_copy(number):
        kind, move, source, landing, _, _ = regions[number]
        to = {axis: (place[axis] + step + count[axis]) % count[axis] for axis, step in move.items() if axis != "flip"}
        if move.get("flip"):
            to["xy"] = (xy + 1) % 2
        return pltpu.make_async_remote_copy(
            src_ref=source,
            dst_ref=landing,
            send_sem=sent_by(group_of(number)),
            recv_sem=region_got.at[0 if kind < 2 else 1],
            device_id=to,
            device_id_type=MESH,
        )

    def region_when(number, sign):
        inside = region_inside(regions[number][1], sign)
        return jnp.logical_and(inside, is_end) if regions[number][0] else inside

    def start_regions(kinds):
        for number, region in enumerate(regions):
            if region[0] in kinds:
                @pl.when(region_when(number, 1))
                def _():
                    region_copy(number).start()

    def fill_regions():
        for number, (kind, move, _, _, landing, nothing) in enumerate(regions):
            missing = jnp.logical_not(region_inside(move, -1))

            @pl.when(jnp.logical_and(missing, is_end) if kind else missing)
            def _():
                pltpu.make_async_copy(nothing, landing, region_got.at[0 if kind < 2 else 1]).start()

    def wait_region(which):
        length = (4 * size_z + 6 * 8, 4 * size_z + 6 * 8 + 5 * 8, 2 * (6 + 8) * 8 + (6 + 3) * 4)[which]
        everything = arrivals.at[pl.ds(0, length)]
        pltpu.make_async_copy(everything, everything, region_got.at[which // 2]).wait()

    def window(slots, amount_of):
        rows = slots[0].shape[1]
        spot = iota((rows, LANES), 1)
        packs = []
        for part in range(2):
            packed = jnp.full((rows, LANES), COURANT, F32)
            for c in range(4 * part, min(4 * part + 4, len(slots))):
                for y in range(size_y):
                    base = quarter * (c % 4) + 8 * y
                    turned = pltpu.roll(slots[c][y], amount_of(base), 1)
                    packed = jnp.where(jnp.logical_and(spot >= base, spot < base + 8), turned, packed)
            packs.append(packed)
        return packs

    empty[...] = jnp.zeros(empty.shape, F32)
    empty_half[...] = jnp.zeros(empty_half.shape, F32)
    lhs[...] = jnp.zeros(lhs.shape, BF16)
    pl.semaphore_wait(barrier, beside)
    pass_on()
    loading[0].wait()

    @pl.when(is_end)
    def _():
        tile = pl.ds(zt, 8)
        for c in range(6):
            value = fields[c, size_y - 3, tile, :]
            tile_f[0, c] = jnp.where(gz == 0, value, turn(value, 1, 0))[4:]
            if c < 3:
                value = fields[c, 2, tile, :]
                tile_f[1, c] = jnp.where(gz == 0, turn(value, -1, 0), value)[:4]

    start_regions((2,))
    loading[3].wait()
    permit[...] = COURANT / permit[...]
    own = window([fields[c] for c in range(6)] + [permit[...]], lambda base: (base - (x_wall - 4) + 2 * LANES) % LANES)
    for part in range(2):
        out_w[part] = own[part]
        land_w[1, part] = own[part]
        out_z[0, part] = own[part][:4]
        out_z[1, part] = own[part][size_z - 4 :]
    start_regions((0,))

    @pl.when(is_end)
    def _():
        tile = pl.ds(zt, 8)
        for i in range(2):
            for c in range(3):
                tile_h[0, 2 * c + i] = fields[3 + c, size_y - 2 + i, tile, :]
                tile_h[1, 2 * c + i] = fields[3 + c, i, tile, :]
            tile_h[0, 6 + i] = permit[size_y - 2 + i, tile, :]
            tile_h[1, 6 + i] = permit[i, tile, :]
        for c in range(3):
            for i in range(2):
                tile_e[0, 2 * c + i] = fields[c, size_y - 2 + i, tile, :]
                tile_e[1, 2 * c + i] = fields[c, i, tile, :]
        eight = iota((8, LANES), 1)
        packed = jnp.full((8, LANES), COURANT, F32)
        for c in range(7):
            values = permit[:, tile, :] if c == 6 else fields[c, :, tile, :]
            for y in range(size_y):
                base = quarter * (c % 4) + 8 * y + 4 * (c // 4)
                turned = pltpu.roll(values[y], (base + 4 * (1 - xy)) % LANES, 1)
                packed = jnp.where(jnp.logical_and(eight >= base, eight < base + 4), turned, packed)
        out_x[...] = packed
        land_x[1, xy] = packed

    @pl.when(jnp.logical_not(is_end))
    def _():
        land_x[...] = jnp.zeros(land_x.shape, F32)

    start_regions((1,))
    start_regions((3,))
    for copy in loading[1:3] + loading[4:]:
        copy.wait()
    fill_regions()
    for n in range(STEPS):
        fill_halo(n)
    geometry()
    run_s, run_c = sincos((phase[0] + 0.5 * ANGULAR_STEP * (iota((8, LANES), 0).astype(F32) + 1.0)) * (0.5 / math.pi))
    for n in range(STEPS):
        tables_of(n)

    for _ in stage(0, *(fields[c] for c in range(3)), (fields[3], fields[5]), (fields[3], fields[4]), (fields[4], fields[5])):
        pass
    start_halo(0, (4, 5, 8, 11, 9, 10, 0, 1, 2, 3, 6, 7))

    def relay(k, carry):
        hear()
        pass_on()
        return carry

    lax.fori_loop(0, slabs - 3, relay, 0)

    def half_of(n):
        return run_c[2 * n : 2 * n + 1, :], run_s[2 * n : 2 * n + 1, :]

    def full_of(n):
        return run_c[2 * n + 1 : 2 * n + 2, :], run_s[2 * n + 1 : 2 * n + 2, :]

    cap_sum[...] = jnp.zeros(cap_sum.shape, F32)
    own_walls = walls.at[gz]
    own_walls[...] = jnp.zeros((8, LANES), F32)
    lanes8 = iota((1, LANES), 1)
    owner_row = jnp.zeros((1, LANES), F32)
    for p in range(size_y):
        owner_row = jnp.where(lanes8 == 8 * gz + p, (wall_owner[0, p] + 1).astype(F32), owner_row)
    own_walls[pl.ds(size_y, 1), :] = owner_row
    gathered = jnp.zeros((size_z, LANES), F32)
    for y in range(size_y):
        for c in range(8):
            k = c % 4
            from_c = X_PICKS[k] + (6 if c >= 4 else 0)
            turned = pltpu.roll(spectra[from_c, y], (8 * y + c - x_wall + 2 * LANES) % LANES, 1)
            gathered = jnp.where(lane == 8 * y + c, turned, gathered)
            from_c = Z_PICKS[k] + (6 if c >= 4 else 0)
            low = spectra[from_c, y, pl.ds(ZB, 1), :]
            high = spectra[from_c, y, pl.ds(size_z - 1 - ZB, 1), :]
            cap_plane[pl.ds(8 * y + c, 1), :] = jnp.where(gz == 0, low, high)

    def spread_out(source_of, rows, shift_of, masks):
        spot = iota((rows, LANES), 1)
        values = []
        for c in range(8):
            value = jnp.zeros((rows, LANES), F32)
            first = 0
            for dy, planes in enumerate((depth, size_y, depth)):
                start = quarter * (c % 4) + (8 * (size_y - depth) if dy == 0 else 0)
                last = first + 8 * planes
                inside = jnp.logical_and(spot >= first, spot < last)
                for side in range(masks):
                    chosen = inside if masks == 1 else jnp.logical_and(inside, spot % 8 // 4 == side)
                    value = jnp.where(chosen, turn(source_of(dy, c, side), first - start + shift_of(c, side), 1), value)
                first = last
            values.append(value)
        return values

    def steps_of(values, visit):
        ex, ey, ez, hx, hy, hz, r, k = values
        for n in range(STEPS):
            before = (ez, ey)
            hx = hx - k * ((turn(ez, -8, 1) - ez) - (turn(ey, -1, 0) - ey))
            hy = hy - k * ((turn(ex, -1, 0) - ex) - (turn(ez, -1, 1) - ez))
            hz = hz - k * ((turn(ey, -1, 1) - ey) - (turn(ex, -8, 1) - ex))
            ex = ex + r * ((hz - turn(hz, 8, 1)) - (hy - turn(hy, 1, 0)))
            ey = ey + r * ((hx - turn(hx, 1, 0)) - (hz - turn(hz, 1, 1)))
            ez = ez + r * ((hy - turn(hy, 1, 1)) - (hx - turn(hx, 8, 1)))
            visit(n, before, ey, ez, hy, hz)

    @pl.when(is_end)
    def _():
        wait_region(1)

    @pl.when(jnp.logical_not(is_end))
    def _():
        wait_region(0)

    sums = [jnp.zeros((size_z, LANES), F32) for _ in range(8)]

    def add_up(n, before, ey, ez, hy, hz):
        for at, (value, (co, si)) in enumerate(((hz, half_of(n)), (hy, half_of(n)), (ez, full_of(n)), (ey, full_of(n)))):
            value = value[:size_z]
            sums[at] = sums[at] + value * co
            sums[4 + at] = sums[4 + at] - value * si

    folded = [
        [
            jnp.concatenate([
                land_w[dy, part], land_z[dy, 0, part], land_z[dy, 1, part],
            ], axis=0)
            for part in range(2)
        ]
        for dy in range(3)
    ]
    border_e, border_h = [], []

    def keep(n, before, ey, ez, hy, hz):
        border_e.append(before)
        border_h.append((hz, hy))

    steps_of(spread_out(lambda dy, c, side: folded[dy][c // 4], size_z + 8, lambda c, side: 0, 1), add_up)
    steps_of(spread_out(lambda dy, c, side: land_x[dy, side], 8, lambda c, side: 4 * side - 4 * (c // 4), 2), keep)
    for c in range(8):
        chosen = jnp.logical_and(lane % 8 == c, lane < 8 * size_y)
        gathered = gathered + jnp.where(chosen, turn(sums[c], c - 8 * depth - 4, 1), 0.0)
    row_sign = jnp.where(jnp.logical_and(iota((half_rows, LANES), 0) % 4 > 0, iota((half_rows, LANES), 0) % 4 < 3), 1.0, -1.0)
    wall_cells = jnp.transpose(gathered)[:half_rows] * (row_sign[:, :size_z] * facing_x)
    for at, part in enumerate(split(wall_cells * norm)):
        lhs[pl.ds(at * all_rows + half_rows, half_rows), pl.ds(size_x, size_z)] = part


    @pl.when(is_end)
    def _():
        wait_region(2)
        tile = pl.ds(zt, 8)
        eight = iota((8, LANES), 1)
        left, right = jnp.where(xy == 0, 1.0, 0.0), jnp.where(xy == 0, 0.0, 1.0)
        behind, ahead = jnp.where(dev > 0, COURANT, 0.0), jnp.where(dev < devs - 1, COURANT, 0.0)

        missing = jnp.zeros((4, LANES), F32)

        def behind_far(half):
            value = jnp.concatenate([missing, half], axis=0)
            return jnp.where(gz == 0, value, turn(value, -1, 0))

        def ahead_far(half):
            value = jnp.concatenate([half, missing], axis=0)
            return jnp.where(gz == 0, turn(value, 1, 0), value)

        def column(c, held_far, near, offset, ahead_too):
            planes = [behind_far(held_far)] + [near[0, 2 * offset + i] for i in range(2)]
            planes += [fields[c, y, tile, :] for y in range(size_y)] + [near[1, 2 * offset + i] for i in range(2)]
            return planes + ([ahead_far(cap_f[1, offset])] if ahead_too else [])

        e = [column(c, cap_f[0, c], cap_e, c, True) for c in range(3)]
        h = [column(3 + c, cap_f[0, 3 + c], cap_h, c, False) for c in range(3)]
        rates = [None] + [cap_h[0, 6 + i] for i in range(2)] + [permit[y, tile, :] for y in range(size_y)] + [cap_h[1, 6 + i] for i in range(2)]
        coefs = [behind] * depth + [COURANT] * size_y + [ahead] * depth

        def next_x(value, border, i):
            return jnp.where(eight == LANES - 1, turn(border, LANES - 1 - (8 * i + 4), 1), turn(value, -1, 1))

        def last_x(value, border, i):
            return jnp.where(eight == 0, turn(border, -(8 * i + 3), 1), turn(value, 1, 1))

        totals_of = [[jnp.zeros((8, LANES), F32) for _ in range(8)] for _ in range(size_y)]
        for n in range(STEPS):
            bz, by = (value * left for value in border_e[n])
            fx, fy, fz = [list(v) for v in h]
            for i in range(n, extent - 1 - n):
                xs, ys, zs = e[0][i], e[1][i], e[2][i]
                fx[i] = h[0][i] - coefs[i] * ((e[2][i + 1] - zs) - (turn(ys, -1, 0) - ys))
                fy[i] = h[1][i] - coefs[i] * ((turn(xs, -1, 0) - xs) - (next_x(zs, bz, i) - zs))
                fz[i] = h[2][i] - coefs[i] * ((next_x(ys, by, i) - ys) - (e[0][i + 1] - xs))
            h = [fx, fy, fz]
            bz, by = (value * right for value in border_h[n])
            gx, gy, gz_ = [list(v) for v in e]
            for i in range(n + 1, extent - 1 - n):
                xs, ys, zs = h[0][i], h[1][i], h[2][i]
                gx[i] = e[0][i] + rates[i] * ((zs - h[2][i - 1]) - (ys - turn(ys, 1, 0)))
                gy[i] = e[1][i] + rates[i] * ((xs - turn(xs, 1, 0)) - (zs - last_x(zs, bz, i)))
                gz_[i] = e[2][i] + rates[i] * ((ys - last_x(ys, by, i)) - (xs - h[0][i - 1]))
            e = [gx, gy, gz_]
            for y in range(size_y):
                i = depth + y
                for at, (value, (co, si)) in enumerate(((h[1][i], half_of(n)), (h[0][i], half_of(n)), (e[1][i], full_of(n)), (e[0][i], full_of(n)))):
                    totals_of[y][at] = totals_of[y][at] + value * co
                    totals_of[y][4 + at] = totals_of[y][4 + at] - value * si
        for y in range(size_y):
            for c in range(8):
                value = totals_of[y][c]
                cap_sum[pl.ds(8 * y + c, 1), :] = jnp.where(gz == 0, value[ZB : ZB + 1], value[7 - ZB : 8 - ZB])

    def advance(n, ghosts):
        fields_from, spec_from = (fields, spectra) if n == 0 else (fields_out, spectra_out)
        ex, ey, ez, hx, hy, hz = (fields_from[c] for c in range(6))
        rate = permit[...]
        hx = hx - COURANT * (inner(True, 0, ez) - inner(True, 1, ey))
        hy = hy - COURANT * (inner(True, 1, ex) - inner(True, 2, ez))
        hz = hz - COURANT * (inner(True, 2, ey) - inner(True, 0, ex))
        wait_halo(n)
        start, _ = first_of(n)
        xp = in_xd[n]
        hx = hx - COURANT * (at_y(in_yd[2 * n], True) - at_z(in_zd[2 * n], True))
        hy = hy - COURANT * (at_z(in_zd[2 * n + 1], True) - at_x(xp, 0, True))
        hz = hz - COURANT * (at_x(xp, 1, True) - at_y(in_yd[2 * n + 1], True))

        ax, ay, az = in_yu[start], in_yu[start + 1], in_yu[start + 2]
        bx, by, bz = in_zu[start], in_zu[start + 1], in_zu[start + 2]
        c_ex, own = in_xu[n], out_xd[n]
        if n == 0:
            y_hx, y_hz = in_yu[3], in_yu[4]
            z_hx, z_hy = in_zu[3], in_zu[4]
            x_hy, x_hz = turn(c_ex, -3 * size_y, 1), turn(c_ex, -4 * size_y, 1)
        else:
            y_hx, y_hz, z_hx, z_hy, x_hy, x_hz = ghosts
        ay_z = jnp.where(row2 == size_z - 1, in_zy[n], turn(ay, -1, 0))
        ay_x = jnp.where(lane == size_x - 1, turn(in_yx[n], -2 * size_y, 1), turn(ay, -1, 1))
        y_hx = y_hx - half_y * ((ez[0] - az) - (ay_z - ay))
        y_hz = y_hz - half_y * ((ay_x - ay) - (ex[0] - ax))
        bz_y = jnp.concatenate([bz[1:], in_yz[n, 7:8, :][None]], axis=0)
        corner = in_zx[n, 7:8, :]
        bz_x = jnp.stack([turn(corner, -1 - y, 1) for y in range(size_y)], axis=0)
        bz_x = jnp.where(lane_row == size_x - 1, bz_x, jnp.stack([turn(bz[y], -1, 1) for y in range(size_y)], axis=0))
        z_hx = z_hx - half_z * ((bz_y - bz) - (ey[:, 0:1, :] - by))
        z_hy = z_hy - half_z * ((ex[:, 0:1, :] - bx) - (bz_x - bz))
        c_z = jnp.where(row2 == size_z - 1, in_xz[n, 0:1, :], turn(c_ex, -1, 0))
        c_y = jnp.where(lane == size_y - 1, turn(in_xy[n], size_y - 1, 1), turn(c_ex, -1, 1))
        x_hy = x_hy - half_x * ((c_z - c_ex) - (own - turn(c_ex, -2 * size_y, 1)))
        x_hz = x_hz - half_x * ((turn(own, -size_y, 1) - turn(c_ex, -size_y, 1)) - (c_y - c_ex))

        ex = ex + rate * (inner(False, 0, hz) - inner(False, 1, hy))
        ey = ey + rate * (inner(False, 1, hx) - inner(False, 2, hz))
        ez = ez + rate * (inner(False, 2, hy) - inner(False, 0, hx))
        ex = ex - rate * (at_y(y_hz, False) - at_z(z_hy, False))
        ey = ey - rate * (at_z(z_hx, False) - at_x(x_hz, 0, False))
        ez = ez - rate * (at_x(x_hy, 0, False) - at_y(y_hx, False))
        if n < STEPS - 1:
            staging = stage(n + 1, ex, ey, ez, (), (), ())
            next(staging)
            start_halo(n + 1, (4, 5, 0, 1, 2, 3))
            next(staging)
            start_halo(n + 1, (8, 11, 9, 10, 6, 7))
        half_c, half_s = run_c[2 * n : 2 * n + 1, :], run_s[2 * n : 2 * n + 1, :]
        for c, value in enumerate((hx, hy, hz)):
            spectra_out[3 + c] = spec_from[3 + c] + value * half_c
            spectra_out[9 + c] = spec_from[9 + c] - value * half_s
        full_c, full_s = run_c[2 * n + 1 : 2 * n + 2, :], run_s[2 * n + 1 : 2 * n + 2, :]
        for c, value in enumerate((ex, ey, ez)):
            spectra_out[c] = spec_from[c] + value * full_c
            spectra_out[6 + c] = spec_from[6 + c] - value * full_s
        for c, value in enumerate((ex, ey, ez, hx, hy, hz)):
            fields_out[c] = value
        return y_hx, y_hz, z_hx, z_hy, x_hy, x_hz

    sub = iota((8, LANES), 0)
    caps_now = (cap_plane[...] + cap_sum[...]) * (row_sign * (facing_z * end_weight))
    cap_plane[...] = caps_now
    for at, part in enumerate(split(caps_now * norm)):
        lhs[pl.ds(at * all_rows, half_rows), pl.ds(0, size_x)] = part

    def wall_copy(k, ref=None):
        held = walls.at[gz] if ref is None else ref
        return pltpu.make_async_remote_copy(
            src_ref=held,
            dst_ref=held,
            send_sem=loads.at[8],
            recv_sem=wall_got,
            device_id={"gz": (gz + k) % slabs},
            device_id_type=MESH,
        )

    def cap_copy(k, at):
        return pltpu.make_async_remote_copy(
            src_ref=caps.at[at],
            dst_ref=caps.at[at],
            send_sem=loads.at[8],
            recv_sem=wall_got,
            device_id={"gz": (gz + k) % slabs},
            device_id_type=MESH,
        )

    sign = jnp.where(sub < 4, -1.0, 1.0)

    far_rows = lhs[...]

    def far_of(j):
        rows = far_rows
        by_high = jnp.dot(rows, table_hi[j], preferred_element_type=F32)
        by_low = jnp.dot(rows[:all_rows], table_lo[j], preferred_element_type=F32)
        product = by_high[:all_rows] + by_high[all_rows:] + by_low
        theta = jnp.zeros((8, LANES), F32)
        phi = jnp.zeros((8, LANES), F32)
        for face in range(2):
            sum_c = jnp.zeros((8, LANES), F32)
            sum_s = jnp.zeros((8, LANES), F32)
            for y in range(size_y):
                g = face * size_y + y
                tile = product[8 * g : 8 * g + 8]
                tile = tile[:, :LANES] + sign * pltpu.roll(tile[:, LANES:], 4, 0)
                sum_c = sum_c + tile * phases[j, 0, pl.ds(g, 1), :]
                sum_s = sum_s + tile * phases[j, 1, pl.ds(g, 1), :]
            far = sum_c + sign * pltpu.roll(sum_s, 4, 0)
            theta = theta + weights[j, 2 * face] * far
            phi = phi + weights[j, 2 * face + 1] * far

        def four(values):
            pairs = values + pltpu.roll(values, 7, 0)
            return pairs + pltpu.roll(pairs, 6, 0)

        both = jnp.where(sub % 4 == 1, pltpu.roll(four(phi), 1, 0), four(theta))
        parts_out[j] = jnp.where(sub < 2, both, pltpu.roll(both, 6, 0))[:4]

    bunch = per * max(1, 4 // per)
    together = bunch // per
    upper = jnp.where(gz >= slabs // 2, 1, 0)
    near = (upper * across + dev * xys + xy) % owners

    def partner(number):
        other, bit = 0, 1
        while bit < owners:
            other = other + bit * ((near // bit + number // bit) % 2)
            bit *= 2
        return other

    def flat_of(owner):
        return (slabs // 2 - 1) * across + owner

    def part_copy(owner, source):
        return pltpu.make_async_remote_copy(
            src_ref=parts_out.at[pl.ds(owner * per, per)],
            dst_ref=parts_in.at[source],
            send_sem=loads.at[0],
            recv_sem=part_got,
            device_id=ident(flat_of(owner)),
            device_id_type=MESH,
        )

    mine = me - flat_of(0)
    leads = jnp.logical_and(mine >= 0, mine < owners)

    def far_and_send(number, carry):
        several = [partner(owners - 1 - together * number - m) for m in range(together)]
        for owner in several:
            for m in range(per):
                far_of(owner * per + m)
        for owner in several:
            @pl.when(owner != mine)
            def _():
                part_copy(owner, me).start()

        return carry

    hear()
    lax.fori_loop(0, owners // together, far_and_send, 0, unroll=True)

    @pl.when(leads)
    def _():
        parts_in[me] = parts_out[pl.ds(mine * per, per)]

    ghosts = advance(0, None)
    for y in range(size_y):
        cells = jnp.concatenate([wall_cells[8 * y : 8 * y + 8], jnp.zeros((8, LANES - size_z), F32)], axis=1)
        own_walls[pl.ds(y, 1), :] = jnp.sum(stagger(cells, PATCH), axis=0, keepdims=True)
    for k in range(1, slabs):
        wall_copy(k).start()
    for at, holder in enumerate((0, slabs - 1)):
        @pl.when(gz == holder)
        def _():
            for y in range(size_y):
                caps[at, pl.ds(8 * y, 8), :] = block_transpose(cap_plane[pl.ds(8 * y, 8), :])
            for k in range(1, slabs):
                cap_copy(k, at).start()

    def total_copy(k, owner, ref=None):
        held = totals.at[pl.ds(owner * per, per)] if ref is None else ref
        return pltpu.make_async_remote_copy(
            src_ref=held,
            dst_ref=held,
            send_sem=loads.at[3],
            recv_sem=total_got.at[owner // together],
            device_id=ident((me + k) % peers),
            device_id_type=MESH,
        )

    @pl.when(leads)
    def _():
        everyone = parts_in.at[pl.ds(0, peers - 1)]
        pltpu.make_async_remote_copy(
            src_ref=everyone, dst_ref=everyone, send_sem=loads.at[0], recv_sem=part_got, device_id={"gz": gz}, device_id_type=MESH
        ).wait_recv()
        totals[pl.ds(mine * per, per)] = jnp.sum(parts_in[...], axis=0)
        for k in sorted(range(slabs), key=lambda k: -min(k, slabs - k)):
            row = (gz + k) % slabs * across

            def send(r, carry):
                to = row + (dev * xys + xy + r) % across

                @pl.when(to != me)
                def _():
                    total_copy((to - me + peers) % peers, mine).start()

                return carry

            lax.fori_loop(0, across, send, 0, unroll=across <= 4)


    def choose(mine, share, records):
        length = mine.shape[1]
        before = jnp.where(iota((length, length), 0) < iota((length, length), 1), 1.0, 0.0).astype(BF16)
        ones = jnp.broadcast_to(jnp.where(mine, 1.0, 0.0), (8, length))
        rank = jnp.dot(ones.astype(BF16), before, preferred_element_type=F32)
        wanted = iota((8, length), 0).astype(F32)
        chooser = jnp.where(rank == wanted, ones, 0.0)
        return jnp.dot(chooser, records, precision=HIGHEST, preferred_element_type=F32)[:share]

    def choose_owned():
        for ends, caps_due in ((is_end, 1), (jnp.logical_not(is_end), 2)):
            @pl.when(ends)
            def _():
                everything = arrivals.at[pl.ds(0, 8 * (slabs - 1) + caps_due * caps.shape[1])]
                pltpu.make_async_copy(everything, everything, wall_got).wait()

        all_walls = walls[...]
        owner_all = jnp.sum(all_walls[:, size_y : size_y + 1, :], axis=0)[:, : 8 * slabs]
        cap_share = (owned_out.shape[0] - size_y) // 2
        owned_out[pl.ds(0, size_y), 0, :] = choose(
            owner_all == (gz + 1).astype(F32), size_y, all_walls.reshape(8 * slabs, LANES)
        )
        for at in range(2):
            owned_out[pl.ds(size_y + at * cap_share, cap_share), 0, :] = choose(
                cap_owner[pl.ds(at, 1), :] == gz, cap_share, caps[at]
            )

    def intensity_of(field):
        return jnp.sum(field * field, axis=0, keepdims=True)

    def slope_of(j):
        field = totals[j]
        residual = aim[pl.ds(j, 1), :].astype(F32) * (intensity_of(field) - target[pl.ds(j, 1), :])
        return 2.0 * residual * field

    def adjoint_of(j):
        slope = slope_of(j)
        by_theta = jnp.where(sub < 4, slope[0:1], slope[2:3])
        by_phi = jnp.where(sub < 4, slope[1:2], slope[3:4])
        tiles = []
        for face in range(2):
            vector = weights[j, 2 * face] * by_theta + weights[j, 2 * face + 1] * by_phi
            turned = -sign * pltpu.roll(vector, 4, 0)
            for y in range(size_y):
                g = face * size_y + y
                tile = vector * phases[j, 0, pl.ds(g, 1), :] + turned * phases[j, 1, pl.ds(g, 1), :]
                tiles.append(jnp.concatenate([tile, -sign * pltpu.roll(tile, 4, 0)], axis=1))
        rows = jnp.concatenate(tiles, axis=0)
        high, low = split(rows)
        both = jnp.concatenate([high, low], axis=0)
        across = (((1,), (1,)), ((), ()))
        by_high = lax.dot_general(both, table_hi[j], across, preferred_element_type=F32)
        by_low = lax.dot_general(high, table_lo[j], across, preferred_element_type=F32)
        return by_high[:all_rows] + by_high[all_rows:] + by_low

    def adjoint_wait(number):
        several = [partner(together * number + m) for m in range(together)]
        batch = several[0] // together
        ours = jnp.logical_and(leads, mine // together == batch)

        @pl.when(jnp.logical_not(ours))
        def _():
            total_copy(1, several[0], totals.at[pl.ds(batch * bunch, bunch)]).wait_recv()

        if together > 1:
            @pl.when(ours)
            def _():
                total_copy(1, several[0], totals.at[pl.ds(batch * bunch, bunch - per)]).wait_recv()

        return several

    def adjoint_some(numbers, total):
        several = [owner for number in numbers for owner in adjoint_wait(number)]
        for owner in several:
            for m in range(per):
                total = total + adjoint_of(owner * per + m)
        return total

    rounds = owners // together
    ghosts = advance(1, ghosts)
    choose_owned()
    gradient = adjoint_some((0,), jnp.zeros((all_rows, size_x + size_z), F32))
    gradient = adjoint_some(range(1, rounds), gradient)
    intensity_out[...] = intensity_of(totals[me // ratio])
    advance(2, ghosts)
    for y in range(size_y):
        wall = gradient[half_rows + 8 * y : half_rows + 8 * y + 8, size_x:]
        wall = jnp.concatenate([wall, jnp.zeros((8, LANES - size_z), F32)], axis=1)
        wall = stagger(wall, PATCH)
        adjoint_out[pl.ds(y, 1), 0, :] = jnp.sum(wall, axis=0, keepdims=True) * norm
        cap = block_transpose(gradient[8 * y : 8 * y + 8, :size_x] * (norm * end_weight))
        adjoint_out[pl.ds(size_y + 8 * y, 8), 0, :] = cap

    groups_sent = {}
    for number, (landing, move) in enumerate(messages):
        groups_sent[number] = [within(move, 1), math.prod(landing.shape) // LANES]
    for number, (_, _, source, _, _, _) in enumerate(regions):
        entry = groups_sent.setdefault(group_of(number), [region_when(number, 1), 0])
        entry[1] += math.prod(source.shape) // LANES
    for group, (sent, rows_sent) in groups_sent.items():
        @pl.when(sent)
        def _():
            everything = arrivals.at[pl.ds(0, rows_sent)]
            pltpu.make_async_copy(everything, everything, sent_by(group)).wait()

    def parts_sent(ref):
        pltpu.make_async_remote_copy(
            src_ref=ref, dst_ref=ref, send_sem=loads.at[0], recv_sem=part_got, device_id={"gz": gz}, device_id_type=MESH
        ).wait_send()

    @pl.when(leads)
    def _():
        parts_sent(parts_out.at[pl.ds(0, (owners - 1) * per)])
        total_copy(1, 0, parts_in.at[pl.ds(0, peers - 1)]).wait_send()

    @pl.when(jnp.logical_not(leads))
    def _():
        parts_sent(parts_out)

    for ends, caps_sent in ((is_end, 1), (jnp.logical_not(is_end), 0)):
        @pl.when(ends)
        def _():
            everything = arrivals.at[pl.ds(0, (slabs - 1) * (8 + caps_sent * caps.shape[1]))]
            pltpu.make_async_copy(everything, everything, loads.at[8]).wait()


def write_out(*refs):
    copies = [pltpu.make_async_copy(refs[i], refs[5 + i], refs[10].at[i]) for i in range(5)]
    for copy in copies:
        copy.start()
    for copy in copies:
        copy.wait()


def local(fields, spectra, permittivity, phase_start, wall_owner, cap_owner, dir_index, target, aim_mask):
    slabs, devs, xys = (lax.axis_size(a) for a in ("gz", "dev", "xy"))
    peers = slabs * devs * xys
    size_y, size_z, size_x = permittivity.shape
    assert size_z == PATCH and size_x == LANES and size_y == 4 and xys == 2
    directions = dir_index.shape[0]
    chunks = directions // LANES
    ratio = peers // chunks
    per = max(1, chunks // (2 * devs * xys))
    owners = chunks // per
    share = directions // peers
    cap_count = size_y * size_x // PATCH
    owned = size_y + 2 * (cap_count // slabs)
    rows = 16 * size_y
    depth = size_x + size_z
    planes, pairs = 5 + 3 * (STEPS - 1), 2 * STEPS
    halos = (
        (planes, size_z, LANES), (pairs, size_z, LANES), (planes, size_y, 1, LANES), (pairs, size_y, 1, LANES),
        (STEPS, size_z, LANES), (STEPS, size_z, LANES),
        (STEPS, 1, LANES), (STEPS, 8, LANES), (STEPS, size_z, LANES), (STEPS, 8, LANES), (STEPS, 8, LANES), (STEPS, size_z, LANES),
    )
    vmem = pl.BlockSpec(memory_space=pltpu.VMEM)
    anywhere = pl.BlockSpec(memory_space=pl.ANY)
    dma = pltpu.SemaphoreType.DMA
    outs = pl.pallas_call(
        functools.partial(kernel, (slabs, devs, xys)),
        out_shape=(
            pltpu.VMEM(fields.shape, F32),
            pltpu.VMEM(spectra.shape, F32),
            pltpu.VMEM((owned, 1, LANES), F32),
            pltpu.VMEM((1, LANES), F32),
            pltpu.VMEM((size_y + cap_count, 1, LANES), F32),
        ),
        in_specs=[anywhere] * 9,
        out_specs=(vmem,) * 5,
        scratch_shapes=[
            *(pltpu.VMEM(shape, F32) for shape in halos[:6]),
            *(pltpu.VMEM(shape, F32) for shape in halos),
            pltpu.VMEM((5, size_z, LANES), F32),
            pltpu.VMEM((5, size_y, 1, LANES), F32),
            pltpu.VMEM((max(376, (slabs - 1) * (8 + cap_count)), 1, LANES), F32),
            pltpu.VMEM((2, size_z, LANES), F32),
            pltpu.VMEM((2, 2, 4, LANES), F32),
            pltpu.VMEM((8, LANES), F32),
            pltpu.VMEM((3, 2, size_z, LANES), F32),
            pltpu.VMEM((3, 2, 2, 4, LANES), F32),
            pltpu.VMEM((3, 2, 8, LANES), F32),
            *(pltpu.VMEM(shape, F32) for shape in ((2, 6, 8, LANES), (2, 8, 8, LANES), (2, 6, 4, LANES)) * 2),
            pltpu.VMEM((8, 8, LANES), F32),
            pltpu.VMEM((6, 4, LANES), F32),
            pltpu.VMEM((8 * size_y, LANES), F32),
            pltpu.VMEM(fields.shape, F32),
            pltpu.VMEM(spectra.shape, F32),
            pltpu.VMEM(permittivity.shape, F32),
            pltpu.SMEM((1,), F32),
            pltpu.SMEM(wall_owner.shape, jnp.int32),
            pltpu.VMEM(cap_owner.shape, jnp.int32),
            pltpu.VMEM((chunks, LANES), jnp.int32),
            pltpu.VMEM((chunks, LANES), F32),
            pltpu.VMEM((chunks, LANES), jnp.int32),
            pltpu.VMEM((8, chunks, LANES), F32),
            pltpu.VMEM((chunks, 4, 8, LANES), F32),
            pltpu.VMEM((chunks, 2, 2 * size_y, LANES), F32),
            pltpu.VMEM((chunks, depth, 2 * LANES), BF16),
            pltpu.VMEM((chunks, depth, 2 * LANES), BF16),
            pltpu.VMEM((8 * size_y, LANES), F32),
            pltpu.VMEM((2 * rows, depth), BF16),
            pltpu.VMEM((chunks, 4, LANES), F32),
            pltpu.VMEM((peers, per, 4, LANES), F32),
            pltpu.VMEM((chunks, 4, LANES), F32),
            pltpu.VMEM((slabs, 8, LANES), F32),
            pltpu.VMEM((2, cap_count, LANES), F32),
            dma((11,)), dma((STEPS,)),
            dma, dma((owners // max(1, 4 // per),)), dma,
            dma((9,)), pltpu.SemaphoreType.REGULAR((2,)), dma((2,)),
        ],
        compiler_params=pltpu.CompilerParams(collective_id=0, has_side_effects=True),
    )(
        fields, spectra, permittivity, phase_start, wall_owner, cap_owner,
        dir_index.reshape(chunks, LANES), target.reshape(chunks, LANES), aim_mask.reshape(chunks, LANES),
    )
    held = (fields.shape, spectra.shape, (owned, 1, LANES), (1, LANES), (size_y + cap_count, 1, LANES))
    fields_new, spectra_new, owned_rows, intensity, adjoint = pl.pallas_call(
        write_out,
        out_shape=tuple(jax.ShapeDtypeStruct(shape, F32) for shape in held),
        in_specs=[pl.BlockSpec(memory_space=pltpu.VMEM)] * 5,
        out_specs=(pl.BlockSpec(memory_space=pl.ANY),) * 5,
        scratch_shapes=[dma((5,))],
    )(*(pltpu.with_memory_space_constraint(out, pltpu.VMEM) for out in outs))
    owned_rows = owned_rows.reshape(1, 1, owned, 1, LANES).transpose(0, 1, 3, 2, 4)
    adjoint = adjoint.reshape(1, 1, size_y + cap_count, 1, LANES).transpose(0, 1, 3, 2, 4)
    intensity = intensity.reshape(LANES)
    if ratio > 1:
        me = (lax.axis_index("gz") * devs + lax.axis_index("dev")) * xys + lax.axis_index("xy")
        intensity = lax.dynamic_slice_in_dim(intensity, (me % ratio) * share, share, 0)
    return (fields_new, spectra_new, owned_rows, intensity, adjoint)


def solution(mesh):
    placed = (
        P("groups", "dev", "gz", "xy"),
        P("groups", "dev", "gz", "xy"),
        P(("groups", "dev"), "gz", "xy"),
        P("groups"),
        P("gz", None),
        P(),
        P(),
        P("groups"),
        P("groups"),
    )
    return jax.shard_map(
        local,
        mesh=mesh,
        in_specs=placed,
        out_specs=(
            P("groups", "dev", "gz", "xy"),
            P("groups", "dev", "gz", "xy"),
            P(("groups", "gz"), "dev", "xy", None, None),
            P(("groups", "gz", "dev", "xy")),
            P(("groups", "gz"), "dev", "xy", None, None),
        ),
        check_vma=False,
    )
```
